32 devices in a mesh: img: 8 (over z, y), sp: 4 (over x, core).
Axes of the slice: x: 2, y: 2, z: 4, core: 2. Of those that a mesh axis runs over, the one named last changes fastest.
Arguments:
- images: bfloat16 [96, 32, 32, 512], P('img', 'sp'), may hold values from -10 to 10
- embedding: bfloat16 [96, 1024], P('img'), may hold values from -6 to 6
- extent: int32 [96, 2], P('img'), may hold values from 8 to 32, as said below
- cotangent: bfloat16 [96, 16, 16, 512], P('img', 'sp'), may hold values from -6 to 6
- conv_w: float32 [9216, 512], P(('img', 'sp')), may hold values from -0.09375 to 0.09375
- emb_w: float32 [1024, 1024], P(('img', 'sp')), may hold values from -0.1875 to 0.1875
- affine: float32 [4096], P(('img', 'sp'))
- conv_mom: float32 [9216, 512], P(('img', 'sp'))
- emb_mom: float32 [1024, 1024], P(('img', 'sp'))
- affine_mom: float32 [4096], P(('img', 'sp'))
- conv_ema: float32 [9216, 512], P(('img', 'sp')), may hold values from -0.09375 to 0.09375
- emb_ema: float32 [1024, 1024], P(('img', 'sp')), may hold values from -0.1875 to 0.1875
- affine_ema: float32 [4096], P(('img', 'sp'))
Outputs:
- output: bfloat16 [96, 16, 16, 512], P('img', 'sp')
- grad_images: bfloat16 [96, 32, 32, 512], P('img', 'sp')
- grad_embedding: float32 [96, 1024], P('img')
- new_conv_w: float32 [9216, 512], P(('img', 'sp'))
- new_emb_w: float32 [1024, 1024], P(('img', 'sp'))
- new_affine: float32 [4096], P(('img', 'sp'))
- new_conv_mom: float32 [9216, 512], P(('img', 'sp'))
- new_emb_mom: float32 [1024, 1024], P(('img', 'sp'))
- new_affine_mom: float32 [4096], P(('img', 'sp'))
- new_conv_ema: float32 [9216, 512], P(('img', 'sp'))
- new_emb_ema: float32 [1024, 1024], P(('img', 'sp'))
- new_affine_ema: float32 [4096], P(('img', 'sp'))
The draws below stay inside these ranges and needn't reach their ends.
Inputs may be any that keep to these rules, and one draw needn't show every extreme that they name: `extent`: each image's height and width are even, at least 8, and at least one of the two equals 32.
All inputs are finite; a program needn't handle non-finite values.
Results may differ from the reference program's by a relative error of at most 0.0095.
Values may be sent and summed in bfloat16 or wider, within the bound.
A program may use at most 192 MiB of HBM per device.

```python
import math
import jax
import jax.numpy as jnp
from jax import lax

C = 512
E = 1024
NORM_GROUPS = 32
SIDE = 32
IMAGES = 96


def draw_images(key, part):
    key_noise, key_offset = jax.random.split(jax.random.fold_in(key, 11))
    position = jnp.arange(SIDE, dtype=jnp.float32) / (SIDE - 1)
    noise = jnp.clip(jax.random.normal(key_noise, (IMAGES, SIDE, SIDE, C), jnp.float32), -6.0, 6.0)
    offset = jax.random.uniform(key_offset, (C,), jnp.float32, -0.5, 0.5)
    ramp = 0.5 + position
    return ((noise + offset) * ramp[None, :, None, None]).astype(jnp.bfloat16)


def draw_extent(key, part):
    key_short, key_tall = jax.random.split(jax.random.fold_in(key, 23))
    short_side = 2 * jax.random.randint(key_short, (IMAGES,), SIDE // 8, SIDE // 2 + 1)
    tall_image = jax.random.randint(key_tall, (IMAGES,), 0, 2)
    long_side = jnp.full((IMAGES,), SIDE, jnp.int32)
    height = jnp.where(tall_image == 1, long_side, short_side)
    breadth = jnp.where(tall_image == 1, short_side, long_side)
    return jnp.stack([height, breadth], axis=1).astype(jnp.int32)


def affine_law(key, salt):
    key_gain, key_bias = jax.random.split(jax.random.fold_in(key, salt))
    is_gain = jnp.zeros((8, 1), jnp.float32).at[0, 0].set(1.0).at[5, 0].set(1.0)
    gains = 1.0 + 0.25 * jnp.clip(jax.random.normal(key_gain, (8, C), jnp.float32), -1.8, 1.8)
    biases = 0.3 * jnp.clip(jax.random.normal(key_bias, (8, C), jnp.float32), -4.0, 4.0)
    return (is_gain * gains + (1.0 - is_gain) * biases).reshape(8 * C)


def draw_affine(key, part):
    return affine_law(key, 31)


def draw_affine_ema(key, part):
    return affine_law(key, 37)


def moment_law(key, salt, shape, factor):
    noise = jnp.clip(jax.random.normal(jax.random.fold_in(key, salt), shape, jnp.float32), -4.0, 4.0)
    return noise * (factor / math.sqrt(IMAGES))


def draw_conv_mom(key, part):
    return moment_law(key, 41, (18 * C, C), 8.0)


def draw_emb_mom(key, part):
    return moment_law(key, 43, (E, 2 * C), 4.0)


def draw_affine_mom(key, part):
    return moment_law(key, 47, (8 * C,), 8.0)


def block_scale(key, shape, cuts, low, top_value):
    def one(dim, shards_of):
        heights = jax.random.uniform(jax.random.fold_in(jax.random.fold_in(key, 6), dim), (shards_of,), jnp.float32, low / len(cuts), top_value / len(cuts))
        return jnp.repeat(jnp.exp(heights), shape[dim] // shards_of).reshape((-1,) + (1,) * (len(shape) - dim - 1))

    loudness = one(*cuts[0])
    for cut in cuts[1:]:
        loudness = loudness * one(*cut)
    return loudness


def normal_values(rng, shape, width, limit, cuts=(), kind=jnp.bfloat16):
    drawn = jax.random.normal(rng, shape, jnp.float32) * width
    if len(cuts) > 0:
        drawn = block_scale(rng, shape, cuts, -0.22, 0.18) * drawn
    return jnp.clip(drawn, min=-limit, max=limit).astype(kind)


def setup_inputs(seed: int = 0) -> dict:
    streams_of = jax.random.split(jax.random.key(seed), 14)
    return {
        "images": draw_images(jax.random.fold_in(streams_of[13], 71), 0),
        "embedding": normal_values(streams_of[1], (IMAGES, E), 1.0, 6.0, ((0, 8),)),
        "extent": draw_extent(jax.random.fold_in(streams_of[13], 71), 0),
        "cotangent": normal_values(streams_of[3], (IMAGES, SIDE // 2, SIDE // 2, C), 1.0, 6.0, ((0, 8), (1, 4))),
        "conv_w": normal_values(streams_of[4], (18 * C, C), (9 * C) ** -0.5, 0.09375, ((0, 32),), jnp.float32),
        "emb_w": normal_values(streams_of[5], (E, 2 * C), E ** -0.5, 0.1875, ((0, 32),), jnp.float32),
        "affine": draw_affine(jax.random.fold_in(streams_of[13], 71), 0),
        "conv_mom": draw_conv_mom(jax.random.fold_in(streams_of[13], 71), 0),
        "emb_mom": draw_emb_mom(jax.random.fold_in(streams_of[13], 71), 0),
        "affine_mom": draw_affine_mom(jax.random.fold_in(streams_of[13], 71), 0),
        "conv_ema": normal_values(streams_of[10], (18 * C, C), (9 * C) ** -0.5, 0.09375, ((0, 32),), jnp.float32),
        "emb_ema": normal_values(streams_of[11], (E, 2 * C), E ** -0.5, 0.1875, ((0, 32),), jnp.float32),
        "affine_ema": draw_affine_ema(jax.random.fold_in(streams_of[13], 71), 0),
    }


EPSILON = 1e-05
LEARN_RATE = 0.03
MOMENTUM = 0.5
EMA_DECAY = 0.5
HIGHEST = lax.Precision.HIGHEST

@jax.custom_vjp
def low(v):
    return lax.optimization_barrier(v.astype(jnp.bfloat16)).astype(jnp.float32)

@jax.custom_vjp
def low_back(v):
    return v

def low_keep(v):
    return (low(v), None)

def low_pass(kept, grad):
    return (grad,)

def back_keep(v):
    return (v, None)

def back_low(kept, grad):
    return (low(grad),)
low.defvjp(low_keep, low_pass)
low_back.defvjp(back_keep, back_low)

def make_masks(extent):
    height = extent[:, 0]
    breadth = extent[:, 1]
    grid_rows = jnp.arange(SIDE, dtype=jnp.int32)
    half_rows = jnp.arange(SIDE // 2, dtype=jnp.int32)
    full_mask = ((grid_rows[None, :, None] < height[:, None, None]) & (grid_rows[None, None, :] < breadth[:, None, None])).astype(jnp.float32)
    half_mask = ((half_rows[None, :, None] < (height // 2)[:, None, None]) & (half_rows[None, None, :] < (breadth // 2)[:, None, None])).astype(jnp.float32)
    return (full_mask[..., None], half_mask[..., None])

def expand(stat):
    return jnp.repeat(stat, C // NORM_GROUPS, axis=1)[:, None, None, :]

def group_norm(values, counts):
    shaped = values.reshape(values.shape[:3] + (NORM_GROUPS, C // NORM_GROUPS))
    means = lax.optimization_barrier(jnp.sum(shaped, axis=(1, 2, 4))) / counts[:, None]
    squares = lax.optimization_barrier(jnp.sum(shaped * shaped, axis=(1, 2, 4))) / counts[:, None]
    inverse = lax.rsqrt(squares - means * means + EPSILON)
    return (values - expand(means)) * expand(inverse)

def pool_cells(values):
    shaped = values.reshape(values.shape[0], values.shape[1] // 2, 2, values.shape[2] // 2, 2, values.shape[3])
    return lax.optimization_barrier(jnp.mean(shaped, axis=(2, 4)))

def convolve(values, kernel):
    return lax.conv_general_dilated(values, kernel, (1, 1), ((1, 1), (1, 1)), dimension_numbers=('NHWC', 'HWIO', 'NHWC'), precision=HIGHEST)

def forward(images, embedding, conv_w, emb_w, affine, full_mask, half_mask, full_pixel_count, half_pixel_count):
    parameters = low(affine).reshape(8, C)
    kernels = low(conv_w)
    first_kernel = kernels[:9 * C].reshape(3, 3, C, C)
    second_kernel = kernels[9 * C:].reshape(3, 3, C, C)
    masked_values = images * full_mask
    first_group_norm = group_norm(masked_values, full_pixel_count) * parameters[0] + parameters[1]
    act_one = jax.nn.silu(first_group_norm) * full_mask
    pooled = low(pool_cells(act_one))
    skip_path = pool_cells(masked_values)
    inner_act = low(low_back((convolve(pooled, first_kernel) + parameters[2]) * half_mask))
    emb_proj = jnp.dot(low(jax.nn.silu(embedding)), low(emb_w), precision=HIGHEST) + jnp.concatenate([parameters[3], parameters[4]])
    ada_scale = emb_proj[:, :C][:, None, None, :]
    ada_shift = emb_proj[:, C:][:, None, None, :]
    second_group_norm = group_norm(inner_act, half_pixel_count) * parameters[5] + parameters[6]
    mixed_act = second_group_norm * (1.0 + ada_scale) + ada_shift
    act_two = low(low_back(jax.nn.silu(mixed_act) * half_mask))
    branch = convolve(act_two, second_kernel) + parameters[7]
    return skip_path + branch * half_mask

def update(weight, moment, average, total):
    grad_mean = total / IMAGES
    new_moment = MOMENTUM * moment + grad_mean
    new_weight = weight - LEARN_RATE * (grad_mean + MOMENTUM * new_moment)
    new_average = EMA_DECAY * average + (1.0 - EMA_DECAY) * new_weight
    return (new_weight, new_moment, new_average)

def reference(images, embedding, extent, cotangent, conv_w, emb_w, affine, conv_mom, emb_mom, affine_mom, conv_ema, emb_ema, affine_ema):
    full_mask, half_mask = make_masks(extent)
    channels_per_group = C // NORM_GROUPS
    full_pixel_count = (extent[:, 0] * extent[:, 1] * channels_per_group).astype(jnp.float32)
    half_pixel_count = (extent[:, 0] // 2 * (extent[:, 1] // 2) * channels_per_group).astype(jnp.float32)
    block_size = 4 if IMAGES % 4 == 0 else 1
    blocks = IMAGES // block_size

    def blocked(values):
        return values.reshape((blocks, block_size) + values.shape[1:])

    def scan_step(carried, pieces):
        image_block, emb_block, full_block, half_block, full_count, half_count, cot_block = pieces

        def block_forward(image_vals, emb_vals, conv_vals, emb_weights, affine_vals):
            return forward(image_vals, emb_vals, conv_vals, emb_weights, affine_vals, full_block, half_block, full_count, half_count)
        result, pull_back = jax.vjp(block_forward, image_block.astype(jnp.float32), emb_block.astype(jnp.float32), conv_w, emb_w, affine)
        grad_image, grad_emb, grad_conv, grad_embw, grad_affine = pull_back(cot_block.astype(jnp.float32))
        carried = (carried[0] + grad_conv, carried[1] + grad_embw, carried[2] + grad_affine)
        return (carried, (result.astype(jnp.bfloat16), grad_image.astype(jnp.bfloat16), grad_emb))
    initial = (jnp.zeros_like(conv_w), jnp.zeros_like(emb_w), jnp.zeros_like(affine))
    pieces = (blocked(images), blocked(embedding), blocked(full_mask), blocked(half_mask), blocked(full_pixel_count), blocked(half_pixel_count), blocked(cotangent))
    totals, stacked = lax.scan(scan_step, initial, pieces)
    output = stacked[0].reshape((IMAGES,) + stacked[0].shape[2:])
    grad_images = stacked[1].reshape((IMAGES,) + stacked[1].shape[2:])
    grad_embedding = stacked[2].reshape((IMAGES,) + stacked[2].shape[2:])
    new_conv, conv_moment, conv_average = update(conv_w, conv_mom, conv_ema, totals[0])
    new_emb, emb_moment, emb_average = update(emb_w, emb_mom, emb_ema, totals[1])
    new_affine, affine_moment, affine_average = update(affine, affine_mom, affine_ema, totals[2])
    return (output, grad_images, grad_embedding, new_conv, new_emb, new_affine, conv_moment, emb_moment, affine_moment, conv_average, emb_average, affine_average)
```

```python
import functools
import jax
import jax.numpy as jnp
from jax import lax
from jax.experimental import pallas as pl
from jax.experimental.pallas import tpu as pltpu
from jax.sharding import PartitionSpec as P

F32 = jnp.float32
BF16 = jnp.bfloat16
HIGHEST = lax.Precision.HIGHEST
MESH = pl.DeviceIdType.MESH
EPSILON = 1e-05
GROUPS = 32


class Place:
    def __init__(self):
        self.img = lax.axis_index("img")
        self.sp = lax.axis_index("sp")
        self.z, self.y = lax.div(self.img, 2), lax.rem(self.img, 2)
        self.x, self.c = lax.div(self.sp, 2), lax.rem(self.sp, 2)
        z, y, x, c = self.z, self.y, self.x, self.c
        self.core = self.at(z, y, x, 1 - c)
        self.xn = self.at(z, y, 1 - x, c)
        self.yn = self.at(z, 1 - y, x, c)
        self.zs = [self.at(lax.rem(z + k, 4), y, x, c) for k in (1, 2, 3)]
        self.sps = [(self.img, lax.rem(self.sp + k, 4)) for k in (1, 2, 3)]

    def at(self, z, y, x, c):
        return (z * 2 + y, x * 2 + c)

    def greet(self):
        barrier = pltpu.get_barrier_semaphore()
        peers = self.sps + [self.yn] + self.zs
        for peer in peers:
            pl.semaphore_signal(barrier, inc=1, device_id=peer, device_id_type=MESH)
        pl.semaphore_wait(barrier, len(peers))


class Wire:
    def __init__(self, ssem, rsem):
        self.ssem, self.rsem = ssem, rsem
        self.used = 0
        self.open = []

    def take(self, count=1):
        first = self.used
        self.used += count
        return first

    def copy(self, src, dst, peer, send, recv):
        return pltpu.make_async_remote_copy(
            src_ref=src, dst_ref=dst, send_sem=self.ssem.at[send], recv_sem=self.rsem.at[recv],
            device_id=peer, device_id_type=MESH,
        )

    def put(self, src, dst, peer, send, recv=None, when=None):
        def make():
            return self.copy(src, dst, peer, send, send if recv is None else recv)

        if when is None:
            make().start()
        else:
            pl.when(when)(lambda: make().start())
        self.open.append((make, when))

    def got(self, ref, recv, peer, when=None):
        def take():
            self.copy(ref, ref, peer, recv, recv).wait_recv()

        if when is None:
            take()
        else:
            pl.when(when)(take)

    def close(self):
        for make, when in self.open:
            if when is None:
                make().wait_send()
            else:
                pl.when(when)(lambda make=make: make().wait_send())
        self.open = []


class PlaneGather:
    def __init__(self, wire, place, rows, pieces, first):
        self.wire, self.place, self.rows, self.pieces, self.first = wire, place, rows, pieces, first
        self.shard = rows // pieces
        count = 2 * pieces
        self.base = {k: wire.take(count) for k in ("x", "y", "c", "xy", "yx", "cx", "cy", "ca", "cb")}

    def sem(self, kind, b, j):
        return self.base[kind] + (b - self.first) * self.pieces + j

    def ref(self, W, b, y, x, c, j, half=None):
        shard = self.shard
        start = self.rows * ((b * 2 + y) * 4 + x * 2 + c) + j * shard
        size = shard
        if half is not None:
            size = shard // 2
            start = start + half * size
        return W.at[pl.ds(pl.multiple_of(start, 16), size)]

    def own(self, W, b, j, when=None):
        p, wire = self.place, self.wire
        r = self.ref(W, b, p.y, p.x, p.c, j)
        wire.put(r, r, p.xn, self.sem("x", b, j), when=when)
        wire.put(r, r, p.yn, self.sem("y", b, j), when=when)
        wire.put(r, r, p.core, self.sem("c", b, j), when=when)

    def turn(self, W, b, j):
        p, wire = self.place, self.wire
        r = self.ref(W, b, p.y, 1 - p.x, p.c, j)
        wire.got(r, self.sem("x", b, j), p.xn)
        h = self.ref(W, b, p.y, 1 - p.x, p.c, j, 0)
        wire.put(h, h, p.yn, self.sem("xy", b, j))
        wire.put(r, r, p.core, self.sem("cx", b, j))
        r = self.ref(W, b, 1 - p.y, p.x, p.c, j)
        wire.got(r, self.sem("y", b, j), p.yn)
        h = self.ref(W, b, 1 - p.y, p.x, p.c, j, 1)
        wire.put(h, h, p.xn, self.sem("yx", b, j))
        wire.put(r, r, p.core, self.sem("cy", b, j))

    def last(self, W, b, j):
        p, wire = self.place, self.wire
        h = self.ref(W, b, 1 - p.y, 1 - p.x, p.c, j, 0)
        wire.got(h, self.sem("xy", b, j), p.yn)
        wire.put(h, h, p.core, self.sem("ca", b, j))
        h = self.ref(W, b, 1 - p.y, 1 - p.x, p.c, j, 1)
        wire.got(h, self.sem("yx", b, j), p.xn)
        wire.put(h, h, p.core, self.sem("cb", b, j))

    def done(self, W, b, j):
        p, wire = self.place, self.wire
        o = 1 - p.c
        wire.got(self.ref(W, b, p.y, p.x, o, j), self.sem("c", b, j), p.core)
        wire.got(self.ref(W, b, p.y, 1 - p.x, o, j), self.sem("cx", b, j), p.core)
        wire.got(self.ref(W, b, 1 - p.y, p.x, o, j), self.sem("cy", b, j), p.core)
        wire.got(self.ref(W, b, 1 - p.y, 1 - p.x, o, j, 0), self.sem("ca", b, j), p.core)
        wire.got(self.ref(W, b, 1 - p.y, 1 - p.x, o, j, 1), self.sem("cb", b, j), p.core)


def group_matrix(channels, across):
    per = channels // GROUPS
    shape = (channels, 128) if across else (128, channels)
    c = lax.broadcasted_iota(jnp.int32, shape, 0 if across else 1)
    g = lax.broadcasted_iota(jnp.int32, shape, 1 if across else 0)
    return (lax.div(c, per) == g).astype(F32)


def exact_dot(a, b):
    return jnp.dot(a, b, precision=HIGHEST, preferred_element_type=F32)


def sigmoid(v):
    return 0.5 * jnp.tanh(0.5 * v) + 0.5


PIECES = 3


def first_kernel(ext, img, cw, ew, aff, W, P, ST, AFF, EZ, SKIP,
                 own, eown, T, SS, STX, CNT, AB, AFS, lsem, ssem, rsem):
    p = Place()
    wire = Wire(ssem, rsem)
    images, rows_full, side, channels = img.shape
    half_rows = rows_full // 2
    half_side = side // 2
    rows = cw.shape[0]
    z, y, x, c, sp = p.z, p.y, p.x, p.c, p.sp
    per = channels // GROUPS

    own[...] = cw[...].astype(BF16)
    mine = W.at[pl.ds(pl.multiple_of(rows * (p.img * 4 + sp), 16), rows)]
    keep = pltpu.make_async_copy(own, mine, lsem.at[0])
    keep.start()
    erows = ew.shape[0]

    def eslot(zz, yy):
        return EZ.at[pl.ds(pl.multiple_of((zz * 2 + yy) * 4 * erows + sp * erows, 32), erows)]

    EZ[...] = jnp.zeros_like(EZ)
    EZ[pl.ds(pl.multiple_of((p.img * 4 + sp) * erows, 32), erows)] = ew[...].astype(BF16)
    AFS[sp, y, z] = jnp.broadcast_to(aff[...].astype(BF16).astype(F32), (8, 128))
    p.greet()

    a1, a2, a3 = wire.take(3), wire.take(), wire.take(3)
    for k in range(3):
        wire.put(AFS.at[sp, y, z], AFS.at[sp, y, z], p.zs[k], a1 + k)

    gather = PlaneGather(wire, p, rows, PIECES, 0)
    zr, zu, zd = (wire.take(4 * PIECES) for _ in range(3))

    def zref(b, j):
        return gather.ref(W, b, y, x, c, j)

    up, down = p.at(z + 1, y, x, c), p.at(z - 1, y, x, c)
    keep.wait()
    for j in range(PIECES):
        r = zref(z, j)
        wire.put(r, r, down, zd + z * PIECES + j, zr + z * PIECES + j, when=z > 0)
        wire.put(r, r, up, zu + z * PIECES + j, zr + z * PIECES + j, when=z < 2)
        gather.own(W, z, j, when=z < 2)

    def arrive(b, j, when, plane):
        i = b * PIECES + j
        r = zref(b, j)
        wire.got(r, zr + i, up, when=when)
        wire.put(r, r, up, zu + i, zr + i, when=when & (b < z) & (z < 3))
        wire.put(r, r, down, zd + i, zr + i, when=when & (b > z) & (z > 0))
        if plane:
            gather.own(W, b, j, when=when)

    always = z >= 0
    other = jnp.where(z == 1, 0, 1)
    lead = jnp.where(z == 0, 0, 1)
    tail = 1 - lead

    SS[...] = jnp.zeros_like(SS)
    CNT[...] = jnp.ones_like(CNT)
    col = lax.broadcasted_iota(jnp.int32, (side, channels), 0)

    def width(n, r):
        return jnp.where(sp * rows_full + r < ext[n, 0], ext[n, 1], 0)

    def add_up(n, _):
        s = jnp.zeros((8, channels), F32)
        q = jnp.zeros((8, channels), F32)
        for r in range(rows_full):
            v = jnp.where(col < width(n, r), img[n, r].astype(F32), 0.0)
            v = v.reshape(side // 8, 8, channels)
            s = s + jnp.sum(v, axis=0)
            q = q + jnp.sum(v * v, axis=0)
        SS[pl.ds(n, 1)] = jnp.sum(s, axis=0, keepdims=True)
        SS[pl.ds(n + 16, 1)] = jnp.sum(q, axis=0, keepdims=True)
        CNT[pl.ds(n, 1)] = jnp.full((1, channels), ext[n, 0] * ext[n, 1] * per, jnp.int32).astype(F32)
        return 0

    lax.fori_loop(0, images, add_up, 0)
    STX[sp] = exact_dot(SS[...], group_matrix(channels, True))
    s1 = wire.take(3)
    for k in range(3):
        wire.put(STX.at[sp], STX.at[sp], p.sps[k], s1 + k)
    for k in range(3):
        zz = lax.rem(z + 3 - k, 4)
        wire.got(AFS.at[sp, y, zz], a1 + k, p.zs[k])
    wire.put(AFS.at[sp, y], AFS.at[sp, y], p.yn, a2)
    arrive(other, 0, always, True)
    wire.got(AFS.at[sp, 1 - y], a2, p.yn)
    for k in range(3):
        wire.put(AFS.at[sp], AFS.at[sp], p.sps[k], a3 + k)
    for j in range(1, PIECES):
        arrive(other, j, always, True)
    for j in range(PIECES):
        gather.turn(W, lead, j)
    e1 = wire.take(3)
    for k in range(3):
        wire.put(eslot(z, y), eslot(z, y), p.zs[k], e1 + k)
    for k in range(3):
        wire.got(STX.at[lax.rem(sp + 3 - k, 4)], s1 + k, p.sps[k])
    total = exact_dot(STX[0] + STX[1] + STX[2] + STX[3], group_matrix(channels, False))
    mean = total[:16] / CNT[...]
    inv = lax.rsqrt(total[16:] / CNT[...] - mean * mean + EPSILON)
    ST[0] = mean
    ST[1] = inv
    for k in range(3):
        wire.got(AFS.at[lax.rem(sp + 3 - k, 4)], a3 + k, p.sps[k])
    for s in range(4):
        for yy in range(2):
            for zz in range(4):
                AFF[pl.ds(zz * 2 + yy, 1), pl.ds(s * 128, 128)] = AFS[s, yy, zz, 0:1]
    scale = inv * AFF[0:1]
    AB[0] = scale
    AB[1] = AFF[1:2] - mean * scale

    def pool(n, hrs):
        scale = AB[0, pl.ds(n, 1)]
        bias = AB[1, pl.ds(n, 1)]
        for i, hr in enumerate(hrs):
            act = raw = None
            for k in range(2):
                r = 2 * hr + k
                inside = col < width(n, r)
                u = img[n, r].astype(F32)
                v = u * scale + bias
                v = jnp.where(inside, v * sigmoid(v), 0.0)
                u = jnp.where(inside, u, 0.0)
                act = v if act is None else act + v
                raw = u if raw is None else raw + u
            for t in range(channels // 128):
                T[i, t] = act[:, t * 128 : t * 128 + 128]
                T[i + 2, t] = raw[:, t * 128 : t * 128 + 128]
        for i, hr in enumerate(hrs):
            for t in range(channels // 128):
                v = T[i, t, pl.ds(0, half_side, stride=2)] + T[i, t, pl.ds(1, half_side, stride=2)]
                P[hr + 1, n, :, pl.ds(t * 128, 128)] = (v * 0.25).astype(BF16)
                v = T[i + 2, t, pl.ds(0, half_side, stride=2)] + T[i + 2, t, pl.ds(1, half_side, stride=2)]
                SKIP[hr, n, :, pl.ds(t * 128, 128)] = v * 0.25

    def edge(n, _):
        pool(n, (0, half_rows - 1))
        return 0

    def inner(n, _):
        pool(n, tuple(range(1, half_rows - 1)))
        return 0

    lax.fori_loop(0, images, edge, 0)
    hu, hd = wire.take(), wire.take()
    prev, nxt = (p.img, sp - 1), (p.img, sp + 1)
    wire.put(P.at[1], P.at[half_rows + 1], prev, hu, when=sp > 0)
    wire.put(P.at[half_rows], P.at[0], nxt, hd, when=sp < 3)

    @pl.when(sp == 0)
    def _():
        P[0] = jnp.zeros_like(P[0])

    @pl.when(sp == 3)
    def _():
        P[half_rows + 1] = jnp.zeros_like(P[0])

    for j in range(PIECES):
        arrive(jnp.zeros_like(z), j, z >= 2, True)
        gather.last(W, lead, j)
    if half_rows > 2:
        lax.fori_loop(0, images, inner, 0)
    for j in range(PIECES):
        gather.turn(W, tail, j)
        b = jnp.where(z == 2, 3, 2)
        r = zref(jnp.full_like(z, 2), j)
        wire.put(r, r, up, zu + 2 * PIECES + j, zr + 2 * PIECES + j, when=z == 2)
        arrive(b, j, always, False)
    for k in range(3):
        wire.got(eslot(lax.rem(z + 3 - k, 4), y), e1 + k, p.zs[k])
    e2 = wire.take(4)
    for k in range(4):
        wire.put(eslot(k, y), eslot(k, y), p.yn, e2 + k)
    for j in range(PIECES):
        arrive(jnp.full_like(z, 3), j, z < 2, False)
        gather.last(W, tail, j)
    for k in range(4):
        wire.got(eslot(k, 1 - y), e2 + k, p.yn)
    wire.got(P.at[half_rows + 1], hu, nxt, when=sp < 3)
    wire.got(P.at[0], hd, prev, when=sp > 0)
    for j in range(PIECES):
        gather.done(W, lead, j)
        gather.done(W, tail, j)
    wire.close()


VM = pl.BlockSpec(memory_space=pltpu.VMEM)
ANY = pl.BlockSpec(memory_space=pl.ANY)
SM = pl.BlockSpec(memory_space=pltpu.SMEM)
WIRES = 160


def params(ident):
    return pltpu.CompilerParams(collective_id=ident, has_side_effects=True, vmem_limit_bytes=56 << 20)


def sems():
    return [pltpu.SemaphoreType.DMA((WIRES,)), pltpu.SemaphoreType.DMA((WIRES,))]


def call_first(extent, images, conv_w, emb_w, affine):
    n, rows_full, side, channels = images.shape
    hr, hs = rows_full // 2, side // 2
    shp = jax.ShapeDtypeStruct
    return pl.pallas_call(
        first_kernel,
        name="gather_first_norm_pool",
        out_shape=(
            shp((18 * channels, channels), BF16),
            shp((hr + 2, n, hs, channels), BF16),
            shp((2, 16, channels), F32),
            shp((8, channels), F32),
            shp((emb_w.shape[1], emb_w.shape[1]), BF16),
            shp((hr, n, hs, channels), F32),
        ),
        in_specs=[SM, VM, VM, VM, VM],
        out_specs=(ANY, VM, VM, VM, VM, VM),
        scratch_shapes=[
            pltpu.VMEM(conv_w.shape, BF16),
            pltpu.VMEM(emb_w.shape, BF16),
            pltpu.VMEM((4, channels // 128, side, 128), F32),
            pltpu.VMEM((32, channels), F32),
            pltpu.VMEM((4, 32, 128), F32),
            pltpu.VMEM((16, channels), F32),
            pltpu.VMEM((2, 16, channels), F32),
            pltpu.VMEM((4, 2, 4, 8, 128), F32),
            pltpu.SemaphoreType.DMA((1,)),
        ] + sems(),
        compiler_params=params(1),
    )(extent, images, conv_w, emb_w, affine.reshape(1, 128))


def half_width(ext, n, row):
    return jnp.where(row < lax.div(ext[n, 0], 2), lax.div(ext[n, 1], 2), 0)


def shift_rows(src, dst, rows):
    images, side, channels = src.shape[1:]
    col = lax.broadcasted_iota(jnp.int32, (side, channels), 0)

    def one(n, _):
        for r in rows:
            v = src[r, n].astype(F32)
            dst[0, r, n] = jnp.where(col > 0, pltpu.roll(v, 1, 0), 0.0).astype(BF16)
            dst[1, r, n] = jnp.where(col < side - 1, pltpu.roll(v, side - 1, 0), 0.0).astype(BF16)
        return 0

    lax.fori_loop(0, images, one, 0)


def conv_band(center, sides, kernel, row, count, back):
    images, side, channels = center.shape[1:]
    total = None
    for a in range(3):
        for b in range(3):
            da, db = (2 - a, 2 - b) if back else (a, b)
            src = center if db == 1 else sides.at[0 if db == 0 else 1]
            left = src[pl.ds(row + da, count)].reshape(count * images * side, channels)
            tap = kernel[pl.ds((3 * a + b) * channels, channels)]
            dims = (((1,), (1 if back else 0,)), ((), ()))
            part = lax.dot_general(left, tap, dims, preferred_element_type=F32)
            total = part if total is None else total + part
    return total


def tap_grad(center, sides, grads, t, out):
    images, side, channels = center.shape[1:]
    rows = grads.shape[0] - 2
    a, b = divmod(t, 3)
    src = center if b == 1 else sides.at[0 if b == 0 else 1]
    left = src[pl.ds(a, rows)].reshape(rows * images * side, channels)
    right = grads[pl.ds(1, rows)].reshape(rows * images * side, channels)
    out[pl.ds(t * channels, channels)] = lax.dot_general(
        left, right, (((0,), (0,)), ((), ())), preferred_element_type=F32
    ).astype(BF16)


class Halo:
    def __init__(self, wire, place, buf):
        self.wire, self.place, self.buf = wire, place, buf
        self.up, self.down = wire.take(), wire.take()

    def send(self):
        p, wire, buf = self.place, self.wire, self.buf
        last = buf.shape[0] - 1
        wire.put(buf.at[1], buf.at[last], (p.img, p.sp - 1), self.up, when=p.sp > 0)
        wire.put(buf.at[last - 1], buf.at[0], (p.img, p.sp + 1), self.down, when=p.sp < 3)

        @pl.when(p.sp == 0)
        def _():
            buf[0] = jnp.zeros_like(buf[0])

        @pl.when(p.sp == 3)
        def _():
            buf[last] = jnp.zeros_like(buf[0])

    def wait(self):
        p, wire, buf = self.place, self.wire, self.buf
        last = buf.shape[0] - 1
        wire.got(buf.at[last], self.up, (p.img, p.sp + 1), when=p.sp < 3)
        wire.got(buf.at[0], self.down, (p.img, p.sp - 1), when=p.sp > 0)


class BandSum:
    def __init__(self, wire, place, slots):
        self.wire, self.place, self.slots = wire, place, slots
        self.first = wire.take(3)

    def send(self, value):
        sp = self.place.sp
        self.slots[sp] = value
        for k in range(3):
            self.wire.put(self.slots.at[sp], self.slots.at[sp], self.place.sps[k], self.first + k)

    def total(self):
        for k in range(3):
            slot = self.slots.at[lax.rem(self.place.sp + 3 - k, 4)]
            self.wire.got(slot, self.first + k, self.place.sps[k])
        return self.slots[0] + self.slots[1] + self.slots[2] + self.slots[3]


def counts(ext, out, images, per, half):
    out[...] = jnp.ones_like(out)

    def one(n, _):
        h, w = ext[n, 0], ext[n, 1]
        if half:
            h, w = lax.div(h, 2), lax.div(w, 2)
        out[pl.ds(n, 1)] = jnp.full((1, out.shape[1]), h * w * per, jnp.int32).astype(F32)
        return 0

    lax.fori_loop(0, images, one, 0)


def second_kernel(ext, cot, emb, P, ST, AFF, EZ, Win, W, A2, INN, DW, ST2, G, C2,
                  WV, X, ACC, SS, STX, PX, CNT, AB, EP, lsem, ssem, rsem):
    p = Place()
    wire = Wire(ssem, rsem)
    rim, images, side, channels = P.shape
    rows = rim - 2
    sp = p.sp
    per = channels // GROUPS
    kernel_rows = WV.shape[0]
    shard = kernel_rows // 16
    load = pltpu.make_async_copy(W.at[pl.ds(0, kernel_rows)], WV, lsem.at[0])
    load.start()
    p.greet()
    gather = PlaneGather(wire, p, shard, PIECES, 2)
    for j in range(PIECES):
        for b in (2, 3):
            gather.own(W, b, j)

    col = lax.broadcasted_iota(jnp.int32, (side, channels), 0)

    EP[...] = jnp.zeros_like(EP)
    EP[pl.ds(0, images)] = emb[...].astype(F32)
    e = EP[...]
    act = (e * sigmoid(e)).astype(BF16)
    proj = BandSum(wire, p, PX)
    proj.send(jnp.dot(act, EZ[...], preferred_element_type=F32))

    C2[...] = jnp.zeros_like(C2)

    def mask_cot(n, _):
        for r in range(rows):
            v = jnp.where(col < half_width(ext, n, sp * rows + r), cot[n, r].astype(F32), 0.0)
            G[r + 1, n] = v.astype(BF16)
            C2[...] += jnp.sum(v.reshape(side // 8, 8, channels), axis=0)
        return 0

    lax.fori_loop(0, images, mask_cot, 0)
    ghalo = Halo(wire, p, G)
    ghalo.send()
    counts(ext, CNT, images, per, True)
    shift_rows(P, X, range(rim))
    load.wait()

    SS[...] = jnp.zeros_like(SS)
    step = 2
    for row in range(0, rows, step):
        ACC[...] = conv_band(P, X, WV, row, step, False).reshape(step, images, side, channels)

        def finish(n, _):
            s = q = None
            for r in range(step):
                v = ACC[r, n] + AFF[2:3]
                v = jnp.where(col < half_width(ext, n, sp * rows + row + r), v, 0.0).astype(BF16)
                INN[row + r, n] = v
                v = v.astype(F32).reshape(side // 8, 8, channels)
                s = jnp.sum(v, axis=0) if s is None else s + jnp.sum(v, axis=0)
                q = jnp.sum(v * v, axis=0) if q is None else q + jnp.sum(v * v, axis=0)
            SS[pl.ds(n, 1)] += jnp.sum(s, axis=0, keepdims=True)
            SS[pl.ds(n + 16, 1)] += jnp.sum(q, axis=0, keepdims=True)
            return 0

        lax.fori_loop(0, images, finish, 0)
    stats = BandSum(wire, p, STX)
    stats.send(exact_dot(SS[...], group_matrix(channels, True)))
    for j in range(PIECES):
        for b in (2, 3):
            gather.turn(W, b, j)
    sums = proj.total()
    ST2[2] = sums[:, :channels] + (AFF[3:4] + 1.0)
    ST2[3] = sums[:, channels:] + AFF[4:5]
    total = exact_dot(stats.total(), group_matrix(channels, False))
    mean = total[:16] / CNT[...]
    inv = lax.rsqrt(total[16:] / CNT[...] - mean * mean + EPSILON)
    ST2[0] = mean
    ST2[1] = inv
    AB[0] = inv * AFF[5:6] * ST2[2]
    AB[1] = AFF[6:7] * ST2[2] + ST2[3] - mean * AB[0]

    def activate(n, rs):
        for r in rs:
            v = INN[r, n].astype(F32) * AB[0, pl.ds(n, 1)] + AB[1, pl.ds(n, 1)]
            v = jnp.where(col < half_width(ext, n, sp * rows + r), v * sigmoid(v), 0.0)
            A2[r + 1, n] = v.astype(BF16)

    def outer(n, _):
        activate(n, (0, rows - 1))
        return 0

    def middle(n, _):
        activate(n, range(1, rows - 1))
        return 0

    lax.fori_loop(0, images, outer, 0)
    ahalo = Halo(wire, p, A2)
    ahalo.send()
    for j in range(PIECES):
        for b in (2, 3):
            gather.last(W, b, j)
    lax.fori_loop(0, images, middle, 0)
    shift_rows(A2, X, range(1, rim - 1))
    ahalo.wait()
    shift_rows(A2, X, (0, rim - 1))
    for t in range(9):
        tap_grad(A2, X, G, t, DW)
    ghalo.wait()
    for j in range(PIECES):
        for b in (2, 3):
            gather.done(W, b, j)
    wire.close()


def call_second(extent, cotangent, embedding, P, ST, AFF, EZ, W):
    rim, n, side, channels = P.shape
    shp = jax.ShapeDtypeStruct
    return pl.pallas_call(
        second_kernel,
        name="gather_second_conv_norm_tapgrad",
        out_shape=(
            shp(W.shape, BF16),
            shp(P.shape, BF16),
            shp((rim - 2, n, side, channels), BF16),
            shp((9 * channels, channels), BF16),
            shp((4, 16, channels), F32),
            shp(P.shape, BF16),
            shp((8, channels), F32),
        ),
        in_specs=[SM, VM, VM, VM, VM, VM, VM, ANY],
        out_specs=(ANY, VM, VM, VM, VM, VM, VM),
        input_output_aliases={7: 0},
        scratch_shapes=[
            pltpu.VMEM((9 * channels, channels), BF16),
            pltpu.VMEM((2,) + P.shape, BF16),
            pltpu.VMEM((2, n, side, channels), F32),
            pltpu.VMEM((32, channels), F32),
            pltpu.VMEM((4, 32, 128), F32),
            pltpu.VMEM((4, 16, 2 * channels), F32),
            pltpu.VMEM((16, channels), F32),
            pltpu.VMEM((2, 16, channels), F32),
            pltpu.VMEM((16, 2 * channels), F32),
            pltpu.SemaphoreType.DMA((1,)),
        ] + sems(),
        compiler_params=params(2),
    )(extent, cotangent, embedding, P, ST, AFF, EZ, W)


class PlaneScatter:
    def __init__(self, wire, place, grad, bufs, first, order):
        self.wire, self.place, self.grad, self.first, self.order = wire, place, grad, first, order
        self.SB, self.CR, self.DR, self.NR, self.ZR, self.R = bufs
        self.rows = self.SB.shape[3]
        self.half = self.rows // 2
        self.cs = wire.take(8)
        self.ds = wire.take(4)
        self.ns = wire.take(8)
        self.zu, self.zd = wire.take(4), wire.take(4)

    def block(self, b, y, x, c):
        start = self.rows * ((b * 2 + y) * 4 + x * 2 + c)
        return self.grad.at[pl.ds(pl.multiple_of(start, 16), self.rows)]

    def spots(self):
        y, x = self.place.y, self.place.x
        return ((1 - y, 1 - x), (y, 1 - x), (1 - y, x), (y, x))

    def start(self):
        p = self.place
        for b in self.order:
            for i, (y, x) in enumerate(self.spots()):
                self.wire.put(self.block(b, y, x, 1 - p.c), self.CR.at[b, y, x], p.core, self.cs + b * 4 + i)

    def pieces(self, do, rows):
        step = 48

        def body(i, _):
            do(pl.ds(pl.multiple_of(i * step, 16), step))
            return 0

        lax.fori_loop(0, rows // step, body, 0)

    def add_core(self, b, i):
        p = self.place
        y, x = self.spots()[i]
        self.wire.got(self.CR.at[b, y, x], self.cs + b * 4 + i, p.core)
        mine = self.block(b, y, x, p.c)

        def do(s):
            v = mine[s].astype(F32) + self.CR[b, y, x, s].astype(F32)
            self.SB[b, y, x, s] = v.astype(BF16)

        self.pieces(do, self.rows)

    def part(self, b, i, h):
        y, x = self.spots()[i]
        return self.SB.at[b, y, x, pl.ds(h * self.half, self.half)]

    def step(self, b, k):
        p, wire, half = self.place, self.wire, self.half
        if k == 0:
            self.add_core(b, 0)
            wire.put(self.part(b, 0, 0), self.DR.at[b, 0], p.yn, self.ds + b * 2)
            wire.put(self.part(b, 0, 1), self.DR.at[b, 1], p.xn, self.ds + b * 2 + 1)
        elif k == 1:
            self.add_core(b, 1)
            wire.put(self.part(b, 1, 1), self.NR.at[b, 0, pl.ds(half, half)], p.xn, self.ns + b * 4 + 1)
            self.add_core(b, 2)
            wire.put(self.part(b, 2, 0), self.NR.at[b, 1, pl.ds(0, half)], p.yn, self.ns + b * 4 + 2)
            self.add_core(b, 3)
        elif k == 2:
            for h, i, peer, nbr in ((0, 1, p.yn, p.xn), (1, 2, p.xn, p.yn)):
                wire.got(self.DR.at[b, h], self.ds + b * 2 + h, peer)
                y, x = self.spots()[i]

                def do(s, h=h, y=y, x=x):
                    t = pl.ds(pl.multiple_of(s.start + h * half, 16), s.size)
                    v = self.SB[b, y, x, t].astype(F32) + self.DR[b, h, s].astype(F32)
                    self.SB[b, y, x, t] = v.astype(BF16)

                self.pieces(do, half)
                wire.put(self.part(b, i, h), self.NR.at[b, i - 1, pl.ds(h * half, half)], nbr, self.ns + b * 4 + (i - 1) * 2 + h)
        else:
            h = k - 3
            z = p.z
            owner = self.first + b
            rows = pl.ds(h * half, half)
            for i, peer in ((0, p.xn), (1, p.yn)):
                wire.got(self.NR.at[b, i, rows], self.ns + b * 4 + i * 2 + h, peer)
            up, down = p.at(z + 1, p.y, p.x, p.c), p.at(z - 1, p.y, p.x, p.c)

            def do(s):
                t = pl.ds(pl.multiple_of(s.start + h * half, 16), s.size)
                self.R[t] = (self.SB[b, p.y, p.x, t].astype(F32) + self.NR[b, 0, t].astype(F32)
                             + self.NR[b, 1, t].astype(F32))

            def add(slot):
                def more(s):
                    t = pl.ds(pl.multiple_of(s.start + h * half, 16), s.size)
                    self.R[t] += self.ZR[b, slot, t].astype(F32)

                self.pieces(more, half)

            self.pieces(do, half)
            i = b * 2 + h

            @pl.when((z <= owner) & (z > 0))
            def _():
                wire.got(self.ZR.at[b, 0, rows], self.zu + i, down)
                add(0)

            @pl.when((z >= owner) & (z < 3))
            def _():
                wire.got(self.ZR.at[b, 1, rows], self.zd + i, up)
                add(1)

            def back(s):
                t = pl.ds(pl.multiple_of(s.start + h * half, 16), s.size)
                self.SB[b, p.y, p.x, t] = self.R[t].astype(BF16)

            def keep(s):
                t = pl.ds(pl.multiple_of(s.start + h * half, 16), s.size)
                self.out[t] = self.R[t]

            pl.when(z != owner)(lambda: self.pieces(back, half))
            pl.when(z == owner)(lambda: self.pieces(keep, half))
            mine = self.SB.at[b, p.y, p.x, rows]
            wire.put(mine, self.ZR.at[b, 0, rows], up, self.zu + i, when=z < owner)
            wire.put(mine, self.ZR.at[b, 1, rows], down, self.zd + i, when=z > owner)

    @staticmethod
    def scratch(rows, channels):
        half = rows // 2
        return [
            pltpu.VMEM((2, 2, 2, rows, channels), BF16),
            pltpu.VMEM((2, 2, 2, rows, channels), BF16),
            pltpu.VMEM((2, 2, half, channels), BF16),
            pltpu.VMEM((2, 2, rows, channels), BF16),
            pltpu.VMEM((2, 2, rows, channels), BF16),
            pltpu.VMEM((rows, channels), F32),
        ]


def slope(v):
    s = sigmoid(v)
    return s * (1.0 + v * (1.0 - s))


def third_kernel(ext, A2, INN, DW2, ST2, G, P, AFF, SKIP, C2, W, OUT, R2, GB, DW1, AFP, GP,
                 WV, X, ACC, GM, SS, PX, STX, CNT, AB, C1, SB, CR, DR, NR, ZR, R, lsem, ssem, rsem):
    p = Place()
    wire = Wire(ssem, rsem)
    rim, images, side, channels = P.shape
    rows = rim - 2
    sp = p.sp
    per = channels // GROUPS
    kernel_rows = WV.shape[0]
    load = pltpu.make_async_copy(W.at[pl.ds(kernel_rows, kernel_rows)], WV, lsem.at[0])
    load.start()
    p.greet()
    scatter = PlaneScatter(wire, p, DW2, (SB, CR, DR, NR, ZR, R), 2, (1, 0))
    scatter.out = R2
    scatter.start()
    R2[...] = jnp.zeros_like(R2)
    col = lax.broadcasted_iota(jnp.int32, (side, channels), 0)
    counts(ext, CNT, images, per, True)
    shift_rows(G, X, range(rim))
    mean, inv = ST2[0], ST2[1]
    AB[0] = inv
    AB[1] = -mean * inv
    AB[2] = AFF[5:6] * ST2[2]
    AB[3] = AFF[6:7] * ST2[2] + ST2[3]
    load.wait()
    scatter.step(1, 0)

    SS[...] = jnp.zeros_like(SS)
    step = 2

    def norm_at(r, n):
        return INN[r, n].astype(F32) * AB[0, pl.ds(n, 1)] + AB[1, pl.ds(n, 1)]

    for row in range(0, rows, step):
        ACC[...] = conv_band(G, X, WV, row, step, True).reshape(step, images, side, channels)

        def finish(n, _):
            s = q = None
            for r in range(step):
                v = ACC[r, n].astype(BF16).astype(F32)
                xhat = norm_at(row + r, n)
                mixed = xhat * AB[2, pl.ds(n, 1)] + AB[3, pl.ds(n, 1)]
                v = jnp.where(col < half_width(ext, n, sp * rows + row + r), v * slope(mixed), 0.0)
                GM[row + r, n] = v
                u = (v * xhat).reshape(side // 8, 8, channels)
                v = v.reshape(side // 8, 8, channels)
                s = jnp.sum(v, axis=0) if s is None else s + jnp.sum(v, axis=0)
                q = jnp.sum(u, axis=0) if q is None else q + jnp.sum(u, axis=0)
            SS[pl.ds(n, 1)] += jnp.sum(s, axis=0, keepdims=True)
            SS[pl.ds(n + 16, 1)] += jnp.sum(q, axis=0, keepdims=True)
            return 0

        lax.fori_loop(0, images, finish, 0)
        scatter.step(1, 1 + row // step)
    sums = BandSum(wire, p, PX)
    sums.send(SS[...])

    p1, p2 = SS[:16], SS[16:]
    g2, b2 = AFF[5:6], AFF[6:7]
    AFP[...] = jnp.zeros_like(AFP)
    AFP[3:4] = jnp.sum(g2 * p2 + b2 * p1, axis=0, keepdims=True)
    AFP[4:5] = jnp.sum(p1, axis=0, keepdims=True)
    AFP[5:6] = jnp.sum(ST2[2] * p2, axis=0, keepdims=True)
    AFP[6:7] = jnp.sum(ST2[2] * p1, axis=0, keepdims=True)
    AFP[7:8] = jnp.sum(C2[...], axis=0, keepdims=True)

    shift_rows(A2, X, range(rim))
    for row in range(0, rows, step):
        ACC[...] = conv_band(A2, X, WV, row, step, False).reshape(step, images, side, channels)

        def write(n, _):
            for r in range(step):
                v = ACC[r, n] + AFF[7:8]
                v = jnp.where(col < half_width(ext, n, sp * rows + row + r), v, 0.0)
                OUT[n, row + r] = (SKIP[row + r, n] + v).astype(BF16)
            return 0

        lax.fori_loop(0, images, write, 0)
        scatter.step(0, row // step)

    total = sums.total()
    p1, p2 = total[:16], total[16:]
    GP[0] = g2 * p2 + b2 * p1
    GP[1] = p1
    SS[0:16] = p1 * AB[2]
    SS[16:32] = p2 * AB[2]
    spread = exact_dot(exact_dot(SS[...], group_matrix(channels, True)), group_matrix(channels, False))
    AB[4] = inv * AB[2]
    AB[5] = inv * (spread[:16] / CNT[...])
    AB[6] = inv * (spread[16:] / CNT[...])
    C1[...] = jnp.zeros_like(C1)

    def back(n, rs):
        for r in rs:
            v = GM[r, n] * AB[4, pl.ds(n, 1)] - AB[5, pl.ds(n, 1)] - norm_at(r, n) * AB[6, pl.ds(n, 1)]
            v = jnp.where(col < half_width(ext, n, sp * rows + r), v, 0.0).astype(BF16)
            GB[r + 1, n] = v
            C1[...] += jnp.sum(v.astype(F32).reshape(side // 8, 8, channels), axis=0)

    def outer(n, _):
        back(n, (0, rows - 1))
        return 0

    def middle(n, _):
        back(n, range(1, rows - 1))
        return 0

    lax.fori_loop(0, images, outer, 0)
    halo = Halo(wire, p, GB)
    halo.send()
    scatter.step(0, 2)
    lax.fori_loop(0, images, middle, 0)
    AFP[2:3] = jnp.sum(C1[...], axis=0, keepdims=True)
    shift_rows(P, X, range(rim))
    for h in range(2):
        scatter.step(1, 3 + h)
    for t in range(9):
        tap_grad(P, X, GB, t, DW1)
    for h in range(2):
        scatter.step(0, 3 + h)
    halo.wait()
    wire.close()


def call_third(extent, A2, INN, DW2, ST2, G, P, AFF, SKIP, C2, W):
    rim, n, side, channels = P.shape
    shp = jax.ShapeDtypeStruct
    shard = 9 * channels // 16
    return pl.pallas_call(
        third_kernel,
        name="scatter_second_conv_norm_back_tapgrad",
        out_shape=(
            shp((n, rim - 2, side, channels), BF16),
            shp((shard, channels), F32),
            shp(P.shape, BF16),
            shp((9 * channels, channels), BF16),
            shp((8, channels), F32),
            shp((2, 16, channels), F32),
        ),
        in_specs=[SM] + [VM] * 9 + [ANY],
        out_specs=(VM,) * 6,
        scratch_shapes=[
            pltpu.VMEM((9 * channels, channels), BF16),
            pltpu.VMEM((2,) + P.shape, BF16),
            pltpu.VMEM((2, n, side, channels), F32),
            pltpu.VMEM((rim - 2, n, side, channels), F32),
            pltpu.VMEM((32, channels), F32),
            pltpu.VMEM((4, 32, channels), F32),
            pltpu.VMEM((4, 32, 128), F32),
            pltpu.VMEM((16, channels), F32),
            pltpu.VMEM((7, 16, channels), F32),
            pltpu.VMEM((8, channels), F32),
        ] + PlaneScatter.scratch(shard, channels) + [pltpu.SemaphoreType.DMA((1,))] + sems(),
        compiler_params=params(3),
    )(extent, A2, INN, DW2, ST2, G, P, AFF, SKIP, C2, W)


LEARN_RATE = 0.03
MOMENTUM = 0.5
EMA_DECAY = 0.5


def thirds(v):
    high = v.astype(BF16)
    v = v - high.astype(F32)
    mid = v.astype(BF16)
    low = (v - mid.astype(F32)).astype(BF16)
    return jnp.concatenate([high, mid, low], axis=0)


def fourth_kernel(ext, image_total, img, cot, GB, DW1, ST, AFF, GP, EZ, emb, AFP, R2,
                  cw, cm, ce, ew, em, ee, aw, am, ae, W,
                  GI, GE, ncw, new, naw, ncm, nem, nam, nce, nee, nae,
                  WV, X, ACC, GN, T, SS, STX, PX, CNT, AB, EP, GPA, EA, EW, AFR, AFY, AFZ, SUM,
                  SB, CR, DR, NR, ZR, R, R1, lsem, ssem, rsem):
    p = Place()
    wire = Wire(ssem, rsem)
    images, rows_full, side_full, channels = img.shape
    rim, _, side, _ = GB.shape
    rows = rim - 2
    z, y, sp = p.z, p.y, p.sp
    per = channels // GROUPS
    kernel_rows = WV.shape[0]
    tiles = channels // 128
    load = pltpu.make_async_copy(W.at[pl.ds(0, kernel_rows)], WV, lsem.at[0])
    load.start()
    p.greet()
    scatter = PlaneScatter(wire, p, DW1, (SB, CR, DR, NR, ZR, R), 0, (0, 1))
    scatter.out = R1
    scatter.start()

    EP[...] = jnp.zeros_like(EP)
    EP[pl.ds(0, images)] = emb[...].astype(F32)
    e = EP[...]
    EA[y, z] = (e * sigmoid(e)).astype(BF16)
    GPA[y, z] = GP[...]
    g1, h1 = wire.take(3), wire.take(3)
    for k in range(3):
        wire.put(GPA.at[y, z], GPA.at[y, z], p.zs[k], g1 + k)
        wire.put(EA.at[y, z], EA.at[y, z], p.zs[k], h1 + k)
    gp = jnp.concatenate([GP[0], GP[1]], axis=1)
    part = lax.dot_general(thirds(gp), EZ[...], (((1,), (1,)), ((), ())), preferred_element_type=F32)
    esum = BandSum(wire, p, PX)
    esum.send(part[:16] + part[16:32] + part[32:])

    counts(ext, CNT, images, per, False)
    shift_rows(GB, X, range(rim))
    mean, inv = ST[0], ST[1]
    AB[0] = inv * AFF[0:1]
    AB[1] = AFF[1:2] - mean * AB[0]
    AB[2] = inv
    AB[3] = -mean * inv
    load.wait()
    scatter.step(0, 0)
    for k in range(3):
        zz = lax.rem(z + 3 - k, 4)
        wire.got(GPA.at[y, zz], g1 + k, p.zs[k])
        wire.got(EA.at[y, zz], h1 + k, p.zs[k])
    g2, h2 = wire.take(), wire.take()
    wire.put(GPA.at[y], GPA.at[y], p.yn, g2)
    wire.put(EA.at[y], EA.at[y], p.yn, h2)
    scatter.step(0, 1)

    SS[...] = jnp.zeros_like(SS)
    step = 2
    col = lax.broadcasted_iota(jnp.int32, (side_full, channels), 0)

    def width(n, r):
        return jnp.where(sp * rows_full + r < ext[n, 0], ext[n, 1], 0)

    def copied(value, slot):
        for t in range(tiles):
            v = value[:, t * 128 : t * 128 + 128]
            T[slot, t, pl.ds(0, side, stride=2)] = v
            T[slot, t, pl.ds(1, side, stride=2)] = v
        return jnp.concatenate([T[slot, t] for t in range(tiles)], axis=1)

    for row in range(0, rows, step):
        ACC[...] = conv_band(GB, X, WV, row, step, True).reshape(step, images, side, channels)

        def finish(n, _):
            s = q = None
            for r in range(step):
                grad = copied(ACC[r, n] * 0.25, r)
                for k in range(2):
                    rr = 2 * (row + r) + k
                    v = img[n, rr].astype(F32)
                    xhat = v * AB[2, pl.ds(n, 1)] + AB[3, pl.ds(n, 1)]
                    v = v * AB[0, pl.ds(n, 1)] + AB[1, pl.ds(n, 1)]
                    v = jnp.where(col < width(n, rr), grad * slope(v), 0.0)
                    GN[n, rr] = v
                    u = (v * xhat).reshape(side_full // 8, 8, channels)
                    v = v.reshape(side_full // 8, 8, channels)
                    s = jnp.sum(v, axis=0) if s is None else s + jnp.sum(v, axis=0)
                    q = jnp.sum(u, axis=0) if q is None else q + jnp.sum(u, axis=0)
            SS[pl.ds(n, 1)] += jnp.sum(s, axis=0, keepdims=True)
            SS[pl.ds(n + 16, 1)] += jnp.sum(q, axis=0, keepdims=True)
            return 0

        lax.fori_loop(0, images, finish, 0)
        scatter.step((row // step), 2 if row == 0 else 0)
    SUM[...] = AFP[...]
    SUM[0:1] = jnp.sum(SS[16:32], axis=0, keepdims=True)
    SUM[1:2] = jnp.sum(SS[0:16], axis=0, keepdims=True)
    asum = BandSum(wire, p, AFR)
    asum.send(SUM[...])
    sums = BandSum(wire, p, STX)
    sums.send(exact_dot(SS[...] * AFF[0:1], group_matrix(channels, True)))
    scatter.step(1, 1)
    AFY[0] = asum.total()
    a2 = wire.take()
    wire.put(AFY.at[0], AFY.at[1], p.yn, a2)
    total = exact_dot(sums.total(), group_matrix(channels, False))
    AB[4] = inv * AFF[0:1]
    AB[5] = inv * (total[:16] / CNT[...])
    AB[6] = inv * (total[16:] / CNT[...])
    scatter.step(1, 2)
    wire.got(AFY.at[1], a2, p.yn)
    AFZ[z] = AFY[0] + AFY[1]
    a3 = wire.take(3)
    for k in range(3):
        wire.put(AFZ.at[z], AFZ.at[z], p.zs[k], a3 + k)

    def image_grad(n, _):
        for hr in range(rows):
            cell = copied(cot[n, hr].astype(F32) * 0.25, hr % 2)
            for k in range(2):
                r = 2 * hr + k
                v = img[n, r].astype(F32)
                xhat = v * AB[2, pl.ds(n, 1)] + AB[3, pl.ds(n, 1)]
                v = GN[n, r] * AB[4, pl.ds(n, 1)] - AB[5, pl.ds(n, 1)] - xhat * AB[6, pl.ds(n, 1)] + cell
                GI[n, r] = jnp.where(col < width(n, r), v, 0.0).astype(BF16)
        return 0

    lax.fori_loop(0, images // 2, image_grad, 0)
    for h in range(2):
        scatter.step(0, 3 + h)
    lax.fori_loop(images // 2, images, image_grad, 0)

    v = esum.total()[:images]
    e = EP[pl.ds(0, images)]
    GE[...] = v * slope(e)
    wire.got(GPA.at[1 - y], g2, p.yn)
    wire.got(EA.at[1 - y], h2, p.yn)
    lanes = pl.ds(pl.multiple_of(p.img * 128, 128), 128)
    EW[...] = jnp.zeros_like(EW)
    for yy in range(2):
        left = EA[yy, :, :, lanes].reshape(64, 128)
        for i in range(2):
            right = GPA[yy, :, i].reshape(64, channels)
            high = right.astype(BF16)
            rest = right - high.astype(F32)
            mid = rest.astype(BF16)
            low = (rest - mid.astype(F32)).astype(BF16)
            for w in (high, mid, low):
                EW[:, pl.ds(i * channels, channels)] += lax.dot_general(
                    left, w, (((0,), (0,)), ((), ())), preferred_element_type=F32
                )

    inverse = 1.0 / image_total

    def update(weight, moment, average, total, outs, at):
        mean_grad = total * inverse
        new_moment = MOMENTUM * moment[at] + mean_grad
        new_weight = weight[at] - LEARN_RATE * (mean_grad + MOMENTUM * new_moment)
        outs[0][at] = new_weight
        outs[1][at] = new_moment
        outs[2][at] = EMA_DECAY * average[at] + (1.0 - EMA_DECAY) * new_weight

    own = pl.ds(pl.multiple_of(sp * 32, 32), 32)
    update(ew, em, ee, EW[own], (new, nem, nee), slice(None))
    for k in range(3):
        zz = lax.rem(z + 3 - k, 4)
        wire.got(AFZ.at[zz], a3 + k, p.zs[k])
    SUM[...] = AFZ[0] + AFZ[1] + AFZ[2] + AFZ[3]
    tile = SUM[:, pl.ds(pl.multiple_of(sp * 128, 128), 128)]
    line = lax.broadcasted_iota(jnp.int32, tile.shape, 0) == p.img
    line = jnp.sum(jnp.where(line, tile, 0.0), axis=0, keepdims=True)
    update(aw, am, ae, line, (naw, nam, nae), slice(None))
    for h in range(2):
        scatter.step(1, 3 + h)

    def conv_update(i, _):
        at = pl.ds(pl.multiple_of(i * 32, 32), 32)
        update(cw, cm, ce, jnp.where(z < 2, R1[at], R2[at]), (ncw, ncm, nce), at)
        return 0

    lax.fori_loop(0, cw.shape[0] // 32, conv_update, 0)
    wire.close()


def call_fourth(image_total, extent, images, cotangent, GB, DW1, ST, AFF, GP, EZ, embedding, AFP, R2, weights, W):
    n, rows_full, side_full, channels = images.shape
    rim, _, side, _ = GB.shape
    shp = jax.ShapeDtypeStruct
    conv_w, emb_w, affine, conv_mom, emb_mom, affine_mom, conv_ema, emb_ema, affine_ema = weights
    line = lambda v: v.reshape(1, 128)
    shard = conv_w.shape[0]
    outs = [shp(v.shape, F32) for v in (conv_w, emb_w)] + [shp((1, 128), F32)]
    res = pl.pallas_call(
        lambda ext, *refs: fourth_kernel(ext, image_total, *refs),
        name="scatter_first_norm_back_update",
        out_shape=[shp(images.shape, BF16), shp(embedding.shape, F32)] + outs * 3,
        in_specs=[SM] + [VM] * 20 + [ANY],
        out_specs=[VM] * 11,
        scratch_shapes=[
            pltpu.VMEM((9 * channels, channels), BF16),
            pltpu.VMEM((2,) + GB.shape, BF16),
            pltpu.VMEM((2, n, side, channels), F32),
            pltpu.VMEM(images.shape, F32),
            pltpu.VMEM((2, channels // 128, side_full, 128), F32),
            pltpu.VMEM((32, channels), F32),
            pltpu.VMEM((4, 32, 128), F32),
            pltpu.VMEM((4, 16, 2 * channels), F32),
            pltpu.VMEM((16, channels), F32),
            pltpu.VMEM((7, 16, channels), F32),
            pltpu.VMEM((16, 2 * channels), F32),
            pltpu.VMEM((2, 4, 2, 16, channels), F32),
            pltpu.VMEM((2, 4, 16, 2 * channels), BF16),
            pltpu.VMEM((128, 2 * channels), F32),
            pltpu.VMEM((4, 8, channels), F32),
            pltpu.VMEM((2, 8, channels), F32),
            pltpu.VMEM((4, 8, channels), F32),
            pltpu.VMEM((8, channels), F32),
        ] + PlaneScatter.scratch(shard, channels)
        + [pltpu.VMEM((shard, channels), F32), pltpu.SemaphoreType.DMA((1,))] + sems(),
        compiler_params=params(4),
    )(extent, images, cotangent, GB, DW1, ST, AFF, GP, EZ, embedding, AFP, R2,
      conv_w, conv_mom, conv_ema, emb_w, emb_mom, emb_ema, line(affine), line(affine_mom), line(affine_ema), W)
    gi, ge, ncw, new, naw, ncm, nem, nam, nce, nee, nae = res
    flat = lambda v: v.reshape(-1)
    return gi, ge, ncw, new, flat(naw), ncm, nem, flat(nam), nce, nee, flat(nae)


def local_kernels(image_total, images, embedding, extent, cotangent, conv_w, emb_w, affine,
                  conv_mom, emb_mom, affine_mom, conv_ema, emb_ema, affine_ema):
    W, P, ST, AFF, EZ, SKIP = call_first(extent, images, conv_w, emb_w, affine)
    W, A2, INN, DW2, ST2, G, C2 = call_second(extent, cotangent, embedding, P, ST, AFF, EZ, W)
    OUT, R2, GB, DW1, AFP, GP = call_third(extent, A2, INN, DW2, ST2, G, P, AFF, SKIP, C2, W)
    weights = (conv_w, emb_w, affine, conv_mom, emb_mom, affine_mom, conv_ema, emb_ema, affine_ema)
    rest = call_fourth(image_total, extent, images, cotangent, GB, DW1, ST, AFF, GP, EZ, embedding, AFP, R2, weights, W)
    return (OUT,) + rest


NORM_GROUPS = 32


def padded_2(cells, sides, width):
    for axis, dim in sides:
        count = lax.axis_size(axis)
        ends = count - 1
        head = lax.slice_in_dim(cells, 0, width, axis=dim)
        tail = lax.slice_in_dim(cells, cells.shape[dim] - width, cells.shape[dim], axis=dim)
        cells = jnp.concatenate(
            [
                lax.ppermute(tail, axis, [(i, (i + 1) % count) for i in range(ends)]),
                cells,
                lax.ppermute(head, axis, [((i + 1) % count, i) for i in range(ends)]),
            ],
            axis=dim,
        )
    return cells


def band_mask(extent, first_row, band_rows, band_cols, halved):
    height = extent[:, 0]
    breadth = extent[:, 1]
    if halved:
        height = height // 2
        breadth = breadth // 2
    row_ids = first_row + jnp.arange(band_rows, dtype=jnp.int32)
    col_ids = jnp.arange(band_cols, dtype=jnp.int32)
    inside = (row_ids[None, :, None] < height[:, None, None]) & (
        col_ids[None, None, :] < breadth[:, None, None]
    )
    return inside.astype(jnp.float32)[..., None]


def per_group_sums(values, group_count):
    shaped = values.reshape(values.shape[:3] + (group_count, values.shape[3] // group_count))
    return jnp.sum(shaped, axis=(1, 2, 4))


def spread_to_channels(stat, channels_per_group):
    return jnp.repeat(stat, channels_per_group, axis=1)[:, None, None, :]


def pool_cells(values):
    shaped = values.reshape(
        values.shape[0], values.shape[1] // 2, 2, values.shape[2] // 2, 2, values.shape[3]
    )
    return jnp.sum(shaped, axis=(2, 4)) * 0.25


def spread_cells(values):
    return jnp.repeat(jnp.repeat(values, 2, axis=1), 2, axis=2) * 0.25


def silu_slope(values):
    sigma = jax.nn.sigmoid(values)
    return sigma * (1.0 + values * (1.0 - sigma))


def conv_rows(padded, kernel, layout):
    return lax.conv_general_dilated(
        padded,
        kernel,
        (1, 1),
        ((0, 0), (1, 1)),
        dimension_numbers=("NHWC", "HWIO", layout),
        preferred_element_type=jnp.float32,
    )


def conv_back(padded, kernel):
    return lax.conv_general_dilated(
        padded,
        jnp.flip(kernel, (0, 1)),
        (1, 1),
        ((0, 0), (1, 1)),
        dimension_numbers=("NHWC", "HWOI", "NHWC"),
        preferred_element_type=jnp.float32,
    )


def tap_grads(padded, grads):
    window = jnp.pad(padded, ((0, 0), (0, 0), (1, 1), (0, 0)))
    band_rows = grads.shape[1]
    band_cols = grads.shape[2]
    kernel_rows = []
    for tap_row in range(3):
        taps = []
        for tap_col in range(3):
            source = window[:, tap_row : tap_row + band_rows, tap_col : tap_col + band_cols, :]
            taps.append(
                jnp.einsum("brci,brco->io", source, grads, preferred_element_type=jnp.float32)
            )
        kernel_rows.append(jnp.stack(taps))
    return jnp.stack(kernel_rows)


def band_rim(values):
    return padded_2(values, (("sp", 1),), 1)


def other_rim(values):
    return padded_2(values, (("sp", 1),), 1)


def update(weight, moment, average, total, image_total):
    grad_mean = total / image_total
    new_moment = MOMENTUM * moment + grad_mean
    new_weight = weight - LEARN_RATE * (grad_mean + MOMENTUM * new_moment)
    new_average = EMA_DECAY * average + (1.0 - EMA_DECAY) * new_weight
    return (new_weight, new_moment, new_average)


def local(
    images,
    embedding,
    extent,
    cotangent,
    conv_w,
    emb_w,
    affine,
    conv_mom,
    emb_mom,
    affine_mom,
    conv_ema,
    emb_ema,
    affine_ema,
):
    conv_all, emb_all, affine_all = (
        lax.all_gather(conv_w.astype(jnp.bfloat16), ("img", "sp"), axis=0, tiled=True),
        lax.all_gather(emb_w.astype(jnp.bfloat16), ("img", "sp"), axis=0, tiled=True),
        lax.all_gather(affine.astype(jnp.bfloat16), ("img", "sp"), axis=0, tiled=True),
    )
    channels = conv_all.shape[1]
    first_kernel = conv_all[: 9 * channels].reshape(3, 3, channels, channels)
    second_kernel = conv_all[9 * channels :].reshape(3, 3, channels, channels)
    parameters = affine_all.astype(jnp.float32).reshape(8, channels)
    image_count = images.shape[0]
    band_rows = images.shape[1]
    grid_side = images.shape[2]
    half_band = band_rows // 2
    half_side = grid_side // 2
    sp_size = lax.axis_size("sp")
    sp_index = lax.axis_index("sp")
    local_channels = channels // sp_size
    first_channels = sp_index * local_channels
    channels_per_group = channels // NORM_GROUPS
    groups_on_device = local_channels // channels_per_group
    full_mask = band_mask(extent, sp_index * band_rows, band_rows, grid_side, False)
    half_mask = band_mask(extent, sp_index * half_band, half_band, half_side, True)
    whole_half = band_mask(extent, 0, half_side, half_side, True)
    full_pixel_count = (extent[:, 0] * extent[:, 1] * channels_per_group).astype(jnp.float32)[
        :, None
    ]
    half_pixel_count = (extent[:, 0] // 2 * (extent[:, 1] // 2) * channels_per_group).astype(
        jnp.float32
    )[:, None]
    masked_values = images.astype(jnp.float32) * full_mask
    sums_one, squares_one = lax.psum(
        (
            per_group_sums(masked_values, NORM_GROUPS),
            per_group_sums(masked_values * masked_values, NORM_GROUPS),
        ),
        "sp",
    )
    first_group_mean = sums_one / full_pixel_count
    first_inverse_deviation = lax.rsqrt(
        squares_one / full_pixel_count - first_group_mean * first_group_mean + EPSILON
    )
    first_normalized = (
        masked_values - spread_to_channels(first_group_mean, channels_per_group)
    ) * spread_to_channels(first_inverse_deviation, channels_per_group)
    first_group_norm = first_normalized * parameters[0] + parameters[1]
    pooled = pool_cells(jax.nn.silu(first_group_norm) * full_mask).astype(jnp.bfloat16)
    skip_path = pool_cells(masked_values)
    pooled_rim = band_rim(pooled)
    inner_act = ((conv_rows(pooled_rim, first_kernel, "NHWC") + parameters[2]) * half_mask).astype(
        jnp.bfloat16
    )
    emb_act = jax.nn.silu(embedding.astype(jnp.float32)).astype(jnp.bfloat16)

    def place_local(values):
        return lax.dynamic_update_slice_in_dim(
            jnp.zeros((channels,), jnp.float32), values, first_channels, 0
        )

    inner_channels = lax.all_to_all(
        inner_act, "sp", split_axis=3, concat_axis=1, tiled=True
    ).astype(jnp.float32)
    emb_cols = jnp.concatenate(
        [
            lax.dynamic_slice_in_dim(emb_all, first_channels, local_channels, 1),
            lax.dynamic_slice_in_dim(emb_all, channels + first_channels, local_channels, 1),
        ],
        axis=1,
    )
    emb_bias = jnp.concatenate(
        [
            lax.dynamic_slice_in_dim(parameters[3], first_channels, local_channels, 0),
            lax.dynamic_slice_in_dim(parameters[4], first_channels, local_channels, 0),
        ]
    )
    emb_proj = jnp.dot(emb_act, emb_cols, preferred_element_type=jnp.float32) + emb_bias
    ada_scale = 1.0 + emb_proj[:, :local_channels][:, None, None, :]
    ada_shift = emb_proj[:, local_channels:][:, None, None, :]
    sums_two = per_group_sums(inner_channels, groups_on_device)
    squares_two = per_group_sums(inner_channels * inner_channels, groups_on_device)
    second_group_mean = sums_two / half_pixel_count
    second_inverse_deviation = lax.rsqrt(
        squares_two / half_pixel_count - second_group_mean * second_group_mean + EPSILON
    )
    second_normalized = (
        inner_channels - spread_to_channels(second_group_mean, channels_per_group)
    ) * spread_to_channels(second_inverse_deviation, channels_per_group)
    second_gain = lax.dynamic_slice_in_dim(parameters[5], first_channels, local_channels, 0)
    second_group_norm = second_normalized * second_gain + lax.dynamic_slice_in_dim(
        parameters[6], first_channels, local_channels, 0
    )
    mixed_act = second_group_norm * ada_scale + ada_shift
    act_two = (jax.nn.silu(mixed_act) * whole_half).astype(jnp.bfloat16)
    act_rows = lax.all_to_all(act_two, "sp", split_axis=1, concat_axis=3, tiled=True)
    act_rim = other_rim(act_rows)
    branch = conv_rows(act_rim, second_kernel, "NHWC") + parameters[7]
    output = (skip_path + branch * half_mask).astype(jnp.bfloat16)
    grad_branch = (cotangent.astype(jnp.float32) * half_mask).astype(jnp.bfloat16)
    bias_two_grad = jnp.sum(grad_branch.astype(jnp.float32), axis=(0, 1, 2))
    grad_rim = other_rim(grad_branch)
    kernel_two = tap_grads(act_rim, grad_branch)
    grad_band = conv_back(grad_rim, second_kernel).astype(jnp.bfloat16)
    grad_act = lax.all_to_all(grad_band, "sp", split_axis=3, concat_axis=1, tiled=True)
    grad_mixed = grad_act.astype(jnp.float32) * whole_half * silu_slope(mixed_act)
    grad_proj = jnp.concatenate(
        [jnp.sum(grad_mixed * second_group_norm, axis=(1, 2)), jnp.sum(grad_mixed, axis=(1, 2))],
        axis=1,
    )
    second_norm_gradient = grad_mixed * ada_scale
    second_gain_gradient = jnp.sum(second_norm_gradient * second_normalized, axis=(0, 1, 2))
    bias_norm_two_grad = jnp.sum(second_norm_gradient, axis=(0, 1, 2))
    second_normalized_gradient = second_norm_gradient * second_gain
    first_total_count = (
        per_group_sums(second_normalized_gradient, groups_on_device) / half_pixel_count
    )
    second_total_count = (
        per_group_sums(second_normalized_gradient * second_normalized, groups_on_device)
        / half_pixel_count
    )
    grad_inner = spread_to_channels(second_inverse_deviation, channels_per_group) * (
        second_normalized_gradient
        - spread_to_channels(first_total_count, channels_per_group)
        - second_normalized * spread_to_channels(second_total_count, channels_per_group)
    )
    grad_inner_rows = lax.all_to_all(
        grad_inner.astype(jnp.bfloat16), "sp", split_axis=1, concat_axis=3, tiled=True
    )
    emb_grad_cols = jnp.einsum(
        "be,bk->ek", emb_act.astype(jnp.float32), grad_proj, precision=HIGHEST
    )
    emb_kernel = jnp.zeros((emb_all.shape[0], 2 * channels), jnp.float32)
    emb_kernel = lax.dynamic_update_slice_in_dim(
        emb_kernel, emb_grad_cols[:, :local_channels], first_channels, 1
    )
    emb_kernel = lax.dynamic_update_slice_in_dim(
        emb_kernel, emb_grad_cols[:, local_channels:], channels + first_channels, 1
    )
    silu_part = jnp.einsum("bk,ek->be", grad_proj, emb_cols.astype(jnp.float32), precision=HIGHEST)
    silu_grad = lax.psum(silu_part.astype(jnp.bfloat16), "sp").astype(jnp.float32)
    emb_bias_grad = jnp.sum(grad_proj, axis=0)
    coarse_affine = [
        place_local(emb_bias_grad[:local_channels]),
        place_local(emb_bias_grad[local_channels:]),
        place_local(second_gain_gradient),
        place_local(bias_norm_two_grad),
    ]
    grad_embedding = silu_grad * silu_slope(embedding.astype(jnp.float32))
    grad_raw = (grad_inner_rows.astype(jnp.float32) * half_mask).astype(jnp.bfloat16)
    bias_one_grad = jnp.sum(grad_raw.astype(jnp.float32), axis=(0, 1, 2))
    kernel_one = tap_grads(pooled_rim, grad_raw)
    grad_pooled = conv_back(band_rim(grad_raw), first_kernel)
    first_norm_gradient = spread_cells(grad_pooled) * full_mask * silu_slope(first_group_norm)
    first_gain_gradient = jnp.sum(first_norm_gradient * first_normalized, axis=(0, 1, 2))
    bias_norm_one_grad = jnp.sum(first_norm_gradient, axis=(0, 1, 2))
    first_normalized_gradient = first_norm_gradient * parameters[0]
    back_one, second_backward = lax.psum(
        (
            per_group_sums(first_normalized_gradient, NORM_GROUPS),
            per_group_sums(first_normalized_gradient * first_normalized, NORM_GROUPS),
        ),
        "sp",
    )
    grad_masked = spread_to_channels(first_inverse_deviation, channels_per_group) * (
        first_normalized_gradient
        - spread_to_channels(back_one / full_pixel_count, channels_per_group)
        - first_normalized
        * spread_to_channels(second_backward / full_pixel_count, channels_per_group)
    ) + spread_cells(cotangent.astype(jnp.float32))
    grad_images = (grad_masked * full_mask).astype(jnp.bfloat16)
    affine_grad = jnp.concatenate(
        [first_gain_gradient, bias_norm_one_grad, bias_one_grad] + coarse_affine + [bias_two_grad]
    )
    conv_grad = jnp.concatenate(
        [kernel_one.reshape(9 * channels, channels), kernel_two.reshape(9 * channels, channels)]
    )
    conv_sum, emb_sum, affine_sum = (
        lax.psum_scatter(conv_grad, ("img", "sp"), scatter_dimension=0, tiled=True),
        lax.psum_scatter(emb_kernel, ("img", "sp"), scatter_dimension=0, tiled=True),
        lax.psum_scatter(affine_grad, ("img", "sp"), scatter_dimension=0, tiled=True),
    )
    image_total = float(image_count * lax.axis_size("img"))
    new_conv, conv_moment, conv_average = update(conv_w, conv_mom, conv_ema, conv_sum, image_total)
    new_emb, emb_moment, emb_average = update(emb_w, emb_mom, emb_ema, emb_sum, image_total)
    new_affine, affine_moment, affine_average = update(
        affine, affine_mom, affine_ema, affine_sum, image_total
    )
    return (
        output,
        grad_images,
        grad_embedding,
        new_conv,
        new_emb,
        new_affine,
        conv_moment,
        emb_moment,
        affine_moment,
        conv_average,
        emb_average,
        affine_average,
    )


def kernels_or_ops(images, embedding, extent, cotangent, conv_w, *rest):
    arrays = (images, embedding, extent, cotangent, conv_w) + rest
    n, rows, side, channels = images.shape
    if n > 16 or rows != 8 or side != 32 or channels != 512 or conv_w.shape[0] != 288:
        return local(*arrays)
    return local_kernels(float(n * lax.axis_size("img")), *arrays)


def solution(mesh):
    in_specs = (
        P("img", "sp", None, None),
        P("img", None),
        P("img", None),
        P("img", "sp", None, None),
        P(("img", "sp"), None),
        P(("img", "sp"), None),
        P(("img", "sp")),
        P(("img", "sp"), None),
        P(("img", "sp"), None),
        P(("img", "sp")),
        P(("img", "sp"), None),
        P(("img", "sp"), None),
        P(("img", "sp")),
    )
    out_specs = (
        P("img", "sp", None, None),
        P("img", "sp", None, None),
        P("img", None),
        P(("img", "sp"), None),
        P(("img", "sp"), None),
        P(("img", "sp")),
        P(("img", "sp"), None),
        P(("img", "sp"), None),
        P(("img", "sp")),
        P(("img", "sp"), None),
        P(("img", "sp"), None),
        P(("img", "sp")),
    )
    fits = dict(mesh.shape) == {"img": 8, "sp": 4}
    return jax.shard_map(kernels_or_ops if fits else local, mesh=mesh, in_specs=in_specs, out_specs=out_specs, check_vma=False)
```

```python
import jax
import jax.numpy as jnp
from jax import lax
from jax.experimental import pallas as pl
from jax.experimental.pallas import tpu as pltpu
from jax.sharding import PartitionSpec as P

F32 = jnp.float32
BF16 = jnp.bfloat16
HIGHEST = lax.Precision.HIGHEST
MESH = pl.DeviceIdType.MESH
EPSILON = 1e-05
LEARN_RATE = 0.03
MOMENTUM = 0.5
EMA_DECAY = 0.5
NORM_GROUPS = 32
PIECES = 3


def choose(cond, a, b):
    if isinstance(cond, bool):
        return a if cond else b
    return jnp.where(cond, a, b)


def many(value, factor):
    return value if isinstance(value, int) else pl.multiple_of(value, factor)


class Place:
    def __init__(self, img, sp):
        self.img, self.sp = img, sp
        if isinstance(img, int):
            self.z, self.y, self.x, self.c = img // 2, img % 2, sp // 2, sp % 2
        else:
            self.z, self.y = lax.div(img, 2), lax.rem(img, 2)
            self.x, self.c = lax.div(sp, 2), lax.rem(sp, 2)
        z, y, x, c = self.z, self.y, self.x, self.c
        self.core = self.at(z, y, x, 1 - c)
        self.xn = self.at(z, y, 1 - x, c)
        self.yn = self.at(z, 1 - y, x, c)
        self.up, self.down = self.at(z + 1, y, x, c), self.at(z - 1, y, x, c)
        self.pair = self.at(z + 1 - 2 * self.odd(z), y, x, c)
        self.gate = self.at(choose(z < 2, 2, 1), y, x, c)
        self.zs = [self.at(self.z_off(k), y, x, c) for k in (1, 2, 3)]
        self.sps = [(img, self.sp_off(k)) for k in (1, 2, 3)]

    def at(self, z, y, x, c):
        return (z * 2 + y, x * 2 + c)

    def odd(self, value):
        return value % 2 if isinstance(value, int) else lax.rem(value, 2)

    def off(self, value, k):
        value = value + k
        return value % 4 if isinstance(value, int) else lax.rem(value, 4)

    def z_off(self, k):
        return self.off(self.z, k)

    def sp_off(self, k):
        return self.off(self.sp, k)


class Wire:
    def __init__(self, ssem, rsem):
        self.ssem, self.rsem = ssem, rsem
        self.used = 0
        self.open = []

    def take(self, count=1):
        first = self.used
        self.used += count
        return first

    def when(self, cond, do):
        if cond is None:
            do()
        else:
            pl.when(cond)(do)

    def copy(self, src, dst, peer, send, recv):
        return pltpu.make_async_remote_copy(
            src_ref=src, dst_ref=dst, send_sem=self.ssem.at[send], recv_sem=self.rsem.at[recv],
            device_id=peer, device_id_type=MESH,
        )

    def put(self, src, dst, peer, send, recv=None, when=None):
        def make():
            return self.copy(src, dst, peer, send, send if recv is None else recv)

        self.when(when, lambda: make().start())
        self.open.append((make, when))
        return self.open[-1]

    def left(self, copies):
        for make, when in copies:
            self.when(when, lambda make=make: make().wait_send())
        self.open = [item for item in self.open if not any(item is copy for copy in copies)]

    def got(self, ref, recv, peer, when=None):
        self.when(when, lambda: self.copy(ref, ref, peer, recv, recv).wait_recv())

    def close(self):
        self.left(self.open)

    def greet(self, place):
        barrier = pltpu.get_barrier_semaphore()
        peers = place.sps + [place.yn] + place.zs
        for peer in peers:
            pl.semaphore_signal(barrier, inc=1, device_id=peer, device_id_type=MESH)
        pl.semaphore_wait(barrier, len(peers))


class Gather:
    def __init__(self, wire, place, W, rows):
        self.wire, self.place, self.W, self.rows = wire, place, W, rows
        self.piece = rows // PIECES
        count = 4 * PIECES
        self.sems = {k: wire.take(count) for k in ("z", "u", "d", "x", "y", "c", "xy", "yx", "cx", "cy", "ca", "cb")}

    def sem(self, kind, b, j):
        return self.sems[kind] + b * PIECES + j

    def ref(self, b, y, x, c, j, half=None):
        start = self.rows * ((b * 2 + y) * 4 + x * 2 + c) + j * self.piece
        size = self.piece
        if half is not None:
            size = size // 2
            start = start + half * size
        return self.W.at[pl.ds(many(start, 16), size)]

    def along(self, b, j, up, down):
        p, wire = self.place, self.wire
        r = self.ref(b, p.y, p.x, p.c, j)
        wire.put(r, r, p.up, self.sem("u", b, j), self.sem("z", b, j), when=up)
        wire.put(r, r, p.down, self.sem("d", b, j), self.sem("z", b, j), when=down)

    def arrive(self, b, j, when=None):
        p = self.place
        both = lambda cond: cond if when is None else when & cond
        self.wire.got(self.ref(b, p.y, p.x, p.c, j), self.sem("z", b, j), p.up, when=when)
        self.along(b, j, both((b < p.z) & (p.z < 3)), both((b > p.z) & (p.z > 0)))

    def own(self, b, j, when=None):
        p, wire = self.place, self.wire
        r = self.ref(b, p.y, p.x, p.c, j)
        wire.put(r, r, p.xn, self.sem("x", b, j), when=when)
        wire.put(r, r, p.yn, self.sem("y", b, j), when=when)
        wire.put(r, r, p.core, self.sem("c", b, j), when=when)

    def turn(self, b, j):
        p, wire = self.place, self.wire
        r = self.ref(b, p.y, 1 - p.x, p.c, j)
        wire.got(r, self.sem("x", b, j), p.xn)
        h = self.ref(b, p.y, 1 - p.x, p.c, j, 0)
        wire.put(h, h, p.yn, self.sem("xy", b, j))
        wire.put(r, r, p.core, self.sem("cx", b, j))
        r = self.ref(b, 1 - p.y, p.x, p.c, j)
        wire.got(r, self.sem("y", b, j), p.yn)
        h = self.ref(b, 1 - p.y, p.x, p.c, j, 1)
        wire.put(h, h, p.xn, self.sem("yx", b, j))
        wire.put(r, r, p.core, self.sem("cy", b, j))

    def last(self, b, j):
        p, wire = self.place, self.wire
        h = self.ref(b, 1 - p.y, 1 - p.x, p.c, j, 0)
        wire.got(h, self.sem("xy", b, j), p.yn)
        wire.put(h, h, p.core, self.sem("ca", b, j))
        h = self.ref(b, 1 - p.y, 1 - p.x, p.c, j, 1)
        wire.got(h, self.sem("yx", b, j), p.xn)
        wire.put(h, h, p.core, self.sem("cb", b, j))

    def done(self, b, j):
        p, wire = self.place, self.wire
        o = 1 - p.c
        wire.got(self.ref(b, p.y, p.x, o, j), self.sem("c", b, j), p.core)
        wire.got(self.ref(b, p.y, 1 - p.x, o, j), self.sem("cx", b, j), p.core)
        wire.got(self.ref(b, 1 - p.y, p.x, o, j), self.sem("cy", b, j), p.core)
        wire.got(self.ref(b, 1 - p.y, 1 - p.x, o, j, 0), self.sem("ca", b, j), p.core)
        wire.got(self.ref(b, 1 - p.y, 1 - p.x, o, j, 1), self.sem("cb", b, j), p.core)


class Scatter:
    def __init__(self, wire, place, grad, bufs, out, first):
        self.wire, self.place, self.grad, self.out, self.first = wire, place, grad, out, first
        self.SB, self.CR, self.DR, self.NR, self.ZR, self.R = bufs
        self.rows = self.SB.shape[3]
        self.piece = self.rows // PIECES
        self.half = self.piece // 2
        count = 2 * PIECES
        self.core = wire.take(8)
        self.sems = {k: wire.take(count) for k in ("da", "db", "xa", "xb", "ya", "yb", "u", "v", "d")}
        self.sent = []

    def sem(self, kind, b, j):
        return self.sems[kind] + b * PIECES + j

    def block(self, b, y, x, c, j=0, size=None):
        start = self.rows * ((b * 2 + y) * 4 + x * 2 + c) + j * self.piece
        return self.grad.at[pl.ds(many(start, 16), self.rows if size is None else size)]

    def give(self, ready):
        p = self.place
        while len(self.sent) < 8 and (2 * len(self.sent) + 2) * self.rows <= ready:
            i = len(self.sent)
            b, y, x = i // 4, i // 2 % 2, i % 2
            src = self.block(b, y, x, 1 - p.c)
            self.sent.append(self.wire.put(src, self.CR.at[b, y, x], p.core, self.core + i))

    def given(self):
        self.wire.left(self.sent)

    def take(self, b, y, x):
        self.wire.got(self.CR.at[b, y, x], self.core + b * 4 + y * 2 + x, self.place.core)

    def span(self, j, h=None):
        if h is None:
            return pl.ds(j * self.piece, self.piece)
        return pl.ds(j * self.piece + h * self.half, self.half)

    def add_core(self, b, y, x, j):
        mine = self.block(b, y, x, self.place.c, j, self.piece)
        v = mine[...].astype(F32) + self.CR[b, y, x, self.span(j)].astype(F32)
        self.SB[b, y, x, self.span(j)] = v.astype(BF16)

    def add_pass(self, b, y, x, j, h):
        at = self.span(j, h)
        v = self.SB[b, y, x, at].astype(F32) + self.DR[b, h, pl.ds(j * self.half, self.half)].astype(F32)
        self.SB[b, y, x, at] = v.astype(BF16)

    def add_plane(self, b, j):
        p, at = self.place, self.span(j)
        self.R[b, at] = (self.SB[b, p.y, p.x, at].astype(F32) + self.NR[b, 0, at].astype(F32)
                         + self.NR[b, 1, at].astype(F32))

    def back(self, b, j):
        at = self.span(j)
        self.SB[b, self.place.y, self.place.x, at] = self.R[b, at].astype(BF16)

    def add_far(self, b, j):
        at = self.span(j)
        self.R[b, at] += self.ZR[b, 0, at].astype(F32)

    def final(self, b, j):
        at = self.span(j)
        self.out[at] = self.R[b, at] + (self.ZR[b, 0, at].astype(F32) + self.ZR[b, 1, at].astype(F32))

    def step(self, k, b, j):
        p, wire = self.place, self.wire
        y, x = p.y, p.x
        owner = self.first + b
        far, mid = (0, 1) if self.first == 2 else (3, 2)
        if k == 0:
            self.add_core(b, 1 - y, 1 - x, j)
            at = pl.ds(j * self.half, self.half)
            src = self.SB.at[b, 1 - y, 1 - x]
            wire.put(src.at[self.span(j, 0)], self.DR.at[b, 0, at], p.yn, self.sem("da", b, j))
            wire.put(src.at[self.span(j, 1)], self.DR.at[b, 1, at], p.xn, self.sem("db", b, j))
        elif k == 1:
            self.add_core(b, y, 1 - x, j)
            at = self.span(j, 1)
            wire.put(self.SB.at[b, y, 1 - x, at], self.NR.at[b, 0, at], p.xn, self.sem("xb", b, j))
            self.add_core(b, 1 - y, x, j)
            at = self.span(j, 0)
            wire.put(self.SB.at[b, 1 - y, x, at], self.NR.at[b, 1, at], p.yn, self.sem("ya", b, j))
            self.add_core(b, y, x, j)
        elif k == 2:
            got = pl.ds(j * self.half, self.half)
            wire.got(self.DR.at[b, 0, got], self.sem("da", b, j), p.yn)
            self.add_pass(b, y, 1 - x, j, 0)
            at = self.span(j, 0)
            wire.put(self.SB.at[b, y, 1 - x, at], self.NR.at[b, 0, at], p.xn, self.sem("xa", b, j))
            wire.got(self.DR.at[b, 1, got], self.sem("db", b, j), p.xn)
            self.add_pass(b, 1 - y, x, j, 1)
            at = self.span(j, 1)
            wire.put(self.SB.at[b, 1 - y, x, at], self.NR.at[b, 1, at], p.yn, self.sem("yb", b, j))
        elif k == 3:
            wire.got(self.NR.at[b, 0, self.span(j, 1)], self.sem("xb", b, j), p.xn)
            wire.got(self.NR.at[b, 1, self.span(j, 0)], self.sem("ya", b, j), p.yn)
            wire.got(self.NR.at[b, 0, self.span(j, 0)], self.sem("xa", b, j), p.xn)
            wire.got(self.NR.at[b, 1, self.span(j, 1)], self.sem("yb", b, j), p.yn)
            self.add_plane(b, j)
            at = self.span(j)
            mine = self.SB.at[b, y, x, at]
            side = 2 * self.first + 1 - owner
            wire.when((p.z == far) | (p.z == side), lambda: self.back(b, j))
            wire.put(mine, self.ZR.at[b, 0, at], p.pair, self.sem("u", b, j), when=p.z == far)
            wire.put(mine, self.ZR.at[b, 1, at], p.pair, self.sem("d", b, j), when=p.z == side)
        elif k == 4:
            at = self.span(j)

            def on():
                self.add_far(b, j)
                self.back(b, j)

            wire.got(self.ZR.at[b, 0, at], self.sem("u", b, j), p.pair, when=p.z == mid)
            wire.when(p.z == mid, on)
            peer = p.at(owner, y, x, p.c)
            wire.put(self.SB.at[b, y, x, at], self.ZR.at[b, 0, at], peer, self.sem("v", b, j), when=p.z == mid)
        else:
            at = self.span(j)
            wire.got(self.ZR.at[b, 0, at], self.sem("v", b, j), p.gate, when=p.z == owner)
            wire.got(self.ZR.at[b, 1, at], self.sem("d", b, j), p.pair, when=p.z == owner)
            wire.when(p.z == owner, lambda: self.final(b, j))

    @staticmethod
    def scratch(rows, channels):
        return [
            ((2, 2, 2, rows, channels), BF16),
            ((2, 2, 2, rows, channels), BF16),
            ((2, 2, rows // 2, channels), BF16),
            ((2, 2, rows, channels), BF16),
            ((2, 2, rows, channels), BF16),
            ((2, rows, channels), F32),
        ]


class Halo:
    def __init__(self, wire, place, buf):
        self.wire, self.place, self.buf = wire, place, buf
        self.up, self.down = wire.take(), wire.take()

    def send(self):
        p, wire, buf = self.place, self.wire, self.buf
        last = buf.shape[0] - 1
        wire.put(buf.at[1], buf.at[last], (p.img, p.sp - 1), self.up, when=p.sp > 0)
        wire.put(buf.at[last - 1], buf.at[0], (p.img, p.sp + 1), self.down, when=p.sp < 3)
        wire.when(p.sp == 0, lambda: self.clear(0))
        wire.when(p.sp == 3, lambda: self.clear(last))

    def clear(self, row):
        self.buf[row] = jnp.zeros_like(self.buf[row])

    def wait(self):
        p, wire, buf = self.place, self.wire, self.buf
        last = buf.shape[0] - 1
        wire.got(buf.at[last], self.up, (p.img, p.sp + 1), when=p.sp < 3)
        wire.got(buf.at[0], self.down, (p.img, p.sp - 1), when=p.sp > 0)


class BandSum:
    def __init__(self, wire, place, slots):
        self.wire, self.place, self.slots = wire, place, slots
        self.first = wire.take(3)

    def send(self):
        p = self.place
        for k in range(3):
            self.wire.put(self.slots.at[p.sp], self.slots.at[p.sp], p.sps[k], self.first + k)

    def wait(self):
        for k in range(3):
            slot = self.slots.at[self.place.sp_off(3 - k)]
            self.wire.got(slot, self.first + k, self.place.sps[k])

    def total(self):
        return self.slots[0] + self.slots[1] + self.slots[2] + self.slots[3]


class SplitSum:
    def __init__(self, wire, place, slots):
        self.wire, self.place, self.slots = wire, place, slots
        self.sems = wire.take(3)

    def send(self):
        p, s = self.place, self.slots
        self.wire.put(s.at[1 - p.c], s.at[2], p.core, self.sems)

    def add(self, out, a, b):
        self.slots[out] = self.slots[a] + self.slots[b]

    def cross(self):
        p, s = self.place, self.slots
        self.wire.got(s.at[2], self.sems, p.core)
        self.add(3, p.c, 2)
        self.wire.put(s.at[3], s.at[4], p.xn, self.sems + 1)

    def back(self):
        p, s = self.place, self.slots
        self.wire.got(s.at[4], self.sems + 1, p.xn)
        self.add(5 + p.c, 3, 4)
        self.wire.put(s.at[5 + p.c], s.at[5 + p.c], p.core, self.sems + 2)

    def wait(self):
        self.wire.got(self.slots.at[6 - self.place.c], self.sems + 2, self.place.core)


class Spread:
    def __init__(self, wire, place, slots):
        self.wire, self.place, self.slots = wire, place, slots
        self.z, self.y = wire.take(3), wire.take()

    def send(self):
        p = self.place
        for k in range(3):
            self.wire.put(self.slots.at[p.y, p.z], self.slots.at[p.y, p.z], p.zs[k], self.z + k)

    def turn(self):
        p = self.place
        for k in range(3):
            self.wire.got(self.slots.at[p.y, p.z_off(3 - k)], self.z + k, p.zs[k])
        self.wire.put(self.slots.at[p.y], self.slots.at[p.y], p.yn, self.y)

    def wait(self):
        self.wire.got(self.slots.at[1 - self.place.y], self.y, self.place.yn)


def group_matrix(channels, across):
    per = channels // NORM_GROUPS
    shape = (channels, 128) if across else (128, channels)
    c = lax.broadcasted_iota(jnp.int32, shape, 0 if across else 1)
    g = lax.broadcasted_iota(jnp.int32, shape, 1 if across else 0)
    return (lax.div(c, per) == g).astype(F32)


def exact_dot(a, b):
    return jnp.dot(a, b, precision=HIGHEST, preferred_element_type=F32)


def sigmoid(v):
    return 0.5 * jnp.tanh(0.5 * v) + 0.5


def slope(v):
    s = sigmoid(v)
    return s * (1.0 + v * (1.0 - s))


def thirds(v):
    high = v.astype(BF16)
    v = v - high.astype(F32)
    mid = v.astype(BF16)
    return high, mid, (v - mid.astype(F32)).astype(BF16)


def fold(v):
    return jnp.sum(v.reshape(v.shape[0] // 8, 8, v.shape[1]), axis=0)


def plus(total, v):
    return v if total is None else total + v


class Step:
    def __init__(self, place, wire, refs):
        self.__dict__.update(refs)
        self.p, self.w = place, wire
        self.images, self.rows_full, self.side_full, self.channels = self.IMG.shape
        self.rim, _, self.side, _ = self.PO.shape
        self.rows = self.rim - 2
        self.per = self.channels // NORM_GROUPS
        self.tiles = self.channels // 128
        shard = self.cw.shape[0]
        self.kernel_rows = 16 * shard
        self.g = Gather(wire, place, self.W, shard)
        self.r2 = Scatter(wire, place, self.DW, [self.__dict__["RA%d" % i] for i in range(6)], self.RES, 2)
        self.r1 = Scatter(wire, place, self.DW, [self.__dict__["RB%d" % i] for i in range(6)], self.RES, 0)
        self.halo_p = Halo(wire, place, self.PO)
        self.halo_g = Halo(wire, place, self.G)
        self.halo_a = Halo(wire, place, self.A2)
        self.halo_b = Halo(wire, place, self.GB)
        self.aff_img = Spread(wire, place, self.AFS.at[place.sp])
        self.aff_sp = BandSum(wire, place, self.AFS)
        self.sum1 = BandSum(wire, place, self.ST1)
        self.sum2 = BandSum(wire, place, self.ST2)
        self.sum3 = BandSum(wire, place, self.ST3)
        self.sum4 = BandSum(wire, place, self.ST4)
        self.psum = SplitSum(wire, place, self.PS)
        self.proj = SplitSum(wire, place, self.PX)
        self.esum = SplitSum(wire, place, self.PE)
        self.asum = BandSum(wire, place, self.AFR)
        self.spread_g = Spread(wire, place, self.GPA)
        self.spread_e = Spread(wire, place, self.EA)
        self.ez = wire.take(3), wire.take(4)
        self.afy = wire.take()
        self.afz = wire.take(3)


    def loop(self, body, first=0, last=None):
        def one(n, _):
            body(n)
            return 0

        lax.fori_loop(first, self.images if last is None else last, one, 0)

    def width(self, n, r):
        return jnp.where(self.p.sp * self.rows_full + r < self.ext[n, 0], self.ext[n, 1], 0)

    def half_width(self, n, r):
        inside = self.p.sp * self.rows + r < lax.div(self.ext[n, 0], 2)
        return jnp.where(inside, lax.div(self.ext[n, 1], 2), 0)

    def cols(self, side):
        return lax.broadcasted_iota(jnp.int32, (side, self.channels), 0)

    def at(self, k, n):
        return self.AB[k, pl.ds(n, 1)]

    def clear_sums(self):
        self.SS[...] = jnp.zeros_like(self.SS)

    def add_sums(self, n, s, q):
        self.SS[pl.ds(n, 1)] += jnp.sum(s, axis=0, keepdims=True)
        self.SS[pl.ds(n + 16, 1)] += jnp.sum(q, axis=0, keepdims=True)

    def eslot(self, z, y):
        rows = self.ew.shape[0]
        start = ((z * 2 + y) * 4 + self.p.sp) * rows
        return self.EZ.at[pl.ds(many(start, 32), rows)]


    def load(self):
        self.copies = [
            pltpu.make_async_copy(self.img, self.IMG, self.lsem.at[0]),
            pltpu.make_async_copy(self.cot, self.COT, self.lsem.at[1]),
        ]
        for copy in self.copies:
            copy.start()

    def loaded(self, k):
        self.copies[k].wait()

    def own_weights(self):
        p = self.p
        rows = self.cw.shape[0]
        self.W[pl.ds(many(rows * (p.img * 4 + p.sp), 16), rows)] = self.cw[...].astype(BF16)
        low = self.aff[...].astype(BF16).astype(F32)
        self.AFS[p.sp, p.y, p.z] = jnp.broadcast_to(low, (8, 128))

    def own_embedding(self):
        p = self.p
        rows = self.ew.shape[0]
        zero = jnp.zeros((rows, self.EZ.shape[1]), BF16)
        for i in range(8):
            for sp in p.sps:
                self.EZ[pl.ds(many((i * 4 + sp[1]) * rows, 32), rows)] = zero
        self.EZ[pl.ds(many((p.img * 4 + p.sp) * rows, 32), rows)] = self.ew[...].astype(BF16)
        self.EP[...] = jnp.zeros_like(self.EP)
        self.EP[pl.ds(0, self.images)] = self.emb[...].astype(F32)
        e = self.EP[...]
        self.EA[p.y, p.z] = (e * sigmoid(e)).astype(BF16)

    def counts(self):
        self.CNT[...] = jnp.ones_like(self.CNT)

        def one(n):
            h, w = self.ext[n, 0], self.ext[n, 1]
            for i, number in enumerate((h * w, lax.div(h, 2) * lax.div(w, 2))):
                number = jnp.full((1, self.channels), number * self.per, jnp.int32)
                self.CNT[i, pl.ds(n, 1)] = number.astype(F32)

        self.loop(one)


    def ez_send(self):
        p = self.p
        for k in range(3):
            self.w.put(self.eslot(p.z, p.y), self.eslot(p.z, p.y), p.zs[k], self.ez[0] + k)

    def ez_turn(self):
        p = self.p
        for k in range(3):
            self.w.got(self.eslot(p.z_off(3 - k), p.y), self.ez[0] + k, p.zs[k])
        for k in range(4):
            self.w.put(self.eslot(k, p.y), self.eslot(k, p.y), p.yn, self.ez[1] + k)

    def ez_wait(self):
        for k in range(4):
            self.w.got(self.eslot(k, 1 - self.p.y), self.ez[1] + k, self.p.yn)

    def project(self):
        v = jnp.dot(self.EA[self.p.y, self.p.z], self.EZ[...], preferred_element_type=F32)
        self.PX[0] = v[:, : self.channels]
        self.PX[1] = v[:, self.channels :]


    def stats_one(self, first, last):
        col = self.cols(self.side_full)

        def one(n):
            s = q = None
            for r in range(self.rows_full):
                v = jnp.where(col < self.width(n, r), self.IMG[n, r].astype(F32), 0.0)
                s, q = plus(s, fold(v)), plus(q, fold(v * v))
            self.add_sums(n, s, q)

        self.loop(one, first, last)

    def stats_one_end(self):
        self.ST1[self.p.sp] = exact_dot(self.SS[...], group_matrix(self.channels, True))

    def affine_rows(self):
        for s in range(4):
            for y in range(2):
                for z in range(4):
                    self.AFF[pl.ds(z * 2 + y, 1), pl.ds(s * 128, 128)] = self.AFS[s, y, z, 0:1]

    def moments(self, total, count, mean_ref, inv_ref):
        total = exact_dot(total, group_matrix(self.channels, False))
        mean = total[:16] / count
        inv = lax.rsqrt(total[16:] / count - mean * mean + EPSILON)
        mean_ref[...] = mean
        inv_ref[...] = inv
        return mean, inv

    def norm_one(self):
        mean, inv = self.moments(self.sum1.total(), self.CNT[0], self.MI.at[0], self.MI.at[1])
        self.AB[0] = inv * self.AFF[0:1]
        self.AB[1] = self.AFF[1:2] - mean * self.AB[0]

    def pool(self, hrs, first=0, last=None):
        col = self.cols(self.side_full)

        def one(n):
            for i, hr in enumerate(hrs):
                act = raw = None
                for k in range(2):
                    r = 2 * hr + k
                    inside = col < self.width(n, r)
                    u = self.IMG[n, r].astype(F32)
                    v = u * self.at(0, n) + self.at(1, n)
                    act = plus(act, jnp.where(inside, v * sigmoid(v), 0.0))
                    raw = plus(raw, jnp.where(inside, u, 0.0))
                for t in range(self.tiles):
                    lanes = slice(t * 128, t * 128 + 128)
                    self.T[i, t] = act[:, lanes]
                    self.T[i + 2, t] = raw[:, lanes]
            even, odd = pl.ds(0, self.side, stride=2), pl.ds(1, self.side, stride=2)
            for i, hr in enumerate(hrs):
                for t in range(self.tiles):
                    lanes = pl.ds(t * 128, 128)
                    v = self.T[i, t, even] + self.T[i, t, odd]
                    self.PO[hr + 1, n, :, lanes] = (v * 0.25).astype(BF16)
                    v = self.T[i + 2, t, even] + self.T[i + 2, t, odd]
                    self.SKIP[hr, n, :, lanes] = v * 0.25

        self.loop(one, first, last)


    def shift(self, src, rows):
        col = self.cols(self.side)

        def one(n):
            for r in rows:
                v = src[r, n].astype(F32)
                self.X[0, r, n] = jnp.where(col > 0, pltpu.roll(v, 1, 0), 0.0).astype(BF16)
                v = jnp.where(col < self.side - 1, pltpu.roll(v, self.side - 1, 0), 0.0)
                self.X[1, r, n] = v.astype(BF16)

        self.loop(one)

    def conv(self, center, base, row, back):
        count = self.ACC.shape[0]
        size = count * self.images * self.side
        total = None
        for a in range(3):
            for b in range(3):
                da, db = (2 - a, 2 - b) if back else (a, b)
                src = center if db == 1 else self.X.at[0 if db == 0 else 1]
                left = src[pl.ds(row + da, count)].reshape(size, self.channels)
                tap = self.W[pl.ds(base + (3 * a + b) * self.channels, self.channels)]
                dims = (((1,), (1 if back else 0,)), ((), ()))
                total = plus(total, lax.dot_general(left, tap, dims, preferred_element_type=F32))
        self.ACC[...] = total.reshape(self.ACC.shape)

    def tap_grad(self, center, grads, t):
        a, b = divmod(t, 3)
        size = self.rows * self.images * self.side
        src = center if b == 1 else self.X.at[0 if b == 0 else 1]
        left = src[pl.ds(a, self.rows)].reshape(size, self.channels)
        right = grads[pl.ds(1, self.rows)].reshape(size, self.channels)
        self.DW[pl.ds(t * self.channels, self.channels)] = lax.dot_general(
            left, right, (((0,), (0,)), ((), ())), preferred_element_type=F32
        ).astype(BF16)

    def mask_cot(self):
        col = self.cols(self.side)
        self.C2[...] = jnp.zeros_like(self.C2)

        def one(n):
            total = None
            for r in range(self.rows):
                v = jnp.where(col < self.half_width(n, r), self.COT[n, r].astype(F32), 0.0)
                self.G[r + 1, n] = v.astype(BF16)
                total = plus(total, fold(v))
            self.C2[...] += total

        self.loop(one)

    def inner_conv(self, row):
        col = self.cols(self.side)
        self.conv(self.PO, 0, row, False)

        def one(n):
            s = q = None
            for r in range(self.ACC.shape[0]):
                v = self.ACC[r, n] + self.AFF[2:3]
                v = jnp.where(col < self.half_width(n, row + r), v, 0.0).astype(BF16)
                self.INN[row + r, n] = v
                v = v.astype(F32)
                s, q = plus(s, fold(v)), plus(q, fold(v * v))
            self.add_sums(n, s, q)

        self.loop(one)


    def stats_two(self):
        self.ST2[self.p.sp] = exact_dot(self.SS[...], group_matrix(self.channels, True))

    def norm_two(self):
        self.MI[4] = self.PX[5] + (self.AFF[3:4] + 1.0)
        self.MI[5] = self.PX[6] + self.AFF[4:5]
        mean, inv = self.moments(self.sum2.total(), self.CNT[1], self.MI.at[2], self.MI.at[3])
        self.AB[2] = inv
        self.AB[3] = -mean * inv
        self.AB[4] = self.AFF[5:6] * self.MI[4]
        self.AB[5] = self.AFF[6:7] * self.MI[4] + self.MI[5]

    def xhat_two(self, r, n):
        return self.INN[r, n].astype(F32) * self.at(2, n) + self.at(3, n)

    def activate(self, rs):
        col = self.cols(self.side)

        def one(n):
            for r in rs:
                v = self.xhat_two(r, n) * self.at(4, n) + self.at(5, n)
                v = jnp.where(col < self.half_width(n, r), v * sigmoid(v), 0.0)
                self.A2[r + 1, n] = v.astype(BF16)

        self.loop(one)

    def mixed_grad(self, row):
        col = self.cols(self.side)
        self.conv(self.G, self.kernel_rows, row, True)

        def one(n):
            s = q = None
            for r in range(self.ACC.shape[0]):
                v = self.ACC[r, n].astype(BF16).astype(F32)
                xhat = self.xhat_two(row + r, n)
                mixed = xhat * self.at(4, n) + self.at(5, n)
                v = jnp.where(col < self.half_width(n, row + r), v * slope(mixed), 0.0)
                self.GM[row + r, n] = v
                s, q = plus(s, fold(v)), plus(q, fold(v * xhat))
            self.add_sums(n, s, q)

        self.loop(one)

    def sums_two_back(self):
        p1, p2 = self.SS[:16], self.SS[16:]
        self.PS[0] = p1
        self.PS[1] = p2
        both = jnp.concatenate([p1 * self.AB[4], p2 * self.AB[4]], axis=0)
        self.ST3[self.p.sp] = exact_dot(both, group_matrix(self.channels, True))
        scale = self.MI[4]
        self.AFP[0:3] = jnp.zeros_like(self.AFP[0:3])
        self.AFP[3:4] = jnp.sum(self.AFF[5:6] * p2 + self.AFF[6:7] * p1, axis=0, keepdims=True)
        self.AFP[4:5] = jnp.sum(p1, axis=0, keepdims=True)
        self.AFP[5:6] = jnp.sum(scale * p2, axis=0, keepdims=True)
        self.AFP[6:7] = jnp.sum(scale * p1, axis=0, keepdims=True)
        self.AFP[7:8] = jnp.sum(self.C2[...], axis=0, keepdims=True)

    def output(self, row):
        col = self.cols(self.side)
        self.conv(self.A2, self.kernel_rows, row, False)

        def one(n):
            for r in range(self.ACC.shape[0]):
                v = self.ACC[r, n] + self.AFF[7:8]
                v = jnp.where(col < self.half_width(n, row + r), v, 0.0)
                self.OUTV[n, row + r] = (self.SKIP[row + r, n] + v).astype(BF16)

        self.loop(one)

    def output_out(self):
        copy = pltpu.make_async_copy(self.OUTV, self.out, self.lsem.at[2])
        copy.start()
        self.copies.append(copy)

    def project_grad(self):
        p1, p2 = self.PS[5], self.PS[6]
        self.GPA[self.p.y, self.p.z, 0] = self.AFF[5:6] * p2 + self.AFF[6:7] * p1
        self.GPA[self.p.y, self.p.z, 1] = p1

    def norm_two_back(self):
        spread = exact_dot(self.sum3.total(), group_matrix(self.channels, False))
        inv = self.AB[2]
        self.AB[6] = inv * self.AB[4]
        self.AB[7] = inv * (spread[:16] / self.CNT[1])
        self.AB[8] = inv * (spread[16:] / self.CNT[1])
        self.C1[...] = jnp.zeros_like(self.C1)

    def inner_grad(self, rs):
        col = self.cols(self.side)

        def one(n):
            total = None
            for r in rs:
                v = self.GM[r, n] * self.at(6, n) - self.at(7, n) - self.xhat_two(r, n) * self.at(8, n)
                v = jnp.where(col < self.half_width(n, r), v, 0.0).astype(BF16)
                self.GB[r + 1, n] = v
                total = plus(total, fold(v.astype(F32)))
            self.C1[...] += total

        self.loop(one)


    def embedding_part(self):
        y, z = self.p.y, self.p.z
        gp = jnp.concatenate([self.GPA[y, z, 0], self.GPA[y, z, 1]], axis=1)
        gp = jnp.concatenate(thirds(gp), axis=0)
        v = lax.dot_general(gp, self.EZ[...], (((1,), (1,)), ((), ())), preferred_element_type=F32)
        v = v[:16] + v[16:32] + v[32:]
        self.PE[0] = v[:, : self.channels]
        self.PE[1] = v[:, self.channels :]

    def embedding_grad(self):
        v = jnp.concatenate([self.PE[5], self.PE[6]], axis=1)[: self.images]
        self.ge[...] = v * slope(self.EP[pl.ds(0, self.images)])

    def embedding_weights(self):
        lanes = pl.ds(many(self.p.img * 128, 128), 128)
        total = [None, None]
        for y in range(2):
            left = self.EA[y, :, :, lanes].reshape(64, 128)
            for i in range(2):
                for w in thirds(self.GPA[y, :, i].reshape(64, self.channels)):
                    v = lax.dot_general(left, w, (((0,), (0,)), ((), ())), preferred_element_type=F32)
                    total[i] = plus(total[i], v)
        for i in range(2):
            self.EW[:, pl.ds(i * self.channels, self.channels)] = total[i]
        self.ewg[...] = self.EW[pl.ds(many(self.p.sp * 32, 32), 32)]


    def doubled(self, value, slot):
        for t in range(self.tiles):
            v = value[:, t * 128 : t * 128 + 128]
            self.T[slot, t, pl.ds(0, self.side, stride=2)] = v
            self.T[slot, t, pl.ds(1, self.side, stride=2)] = v
        return jnp.concatenate([self.T[slot, t] for t in range(self.tiles)], axis=1)

    def prepare_one_back(self):
        self.AB[2] = self.MI[1]
        self.AB[3] = -self.MI[0] * self.MI[1]
        self.clear_sums()

    def norm_one_grad(self, n, r, grad):
        v = self.IMG[n, r].astype(F32)
        xhat = v * self.at(2, n) + self.at(3, n)
        v = v * self.at(0, n) + self.at(1, n)
        return xhat, jnp.where(self.cols(self.side_full) < self.width(n, r), grad * slope(v), 0.0)

    def pooled_conv(self, row):
        self.conv(self.GB, 0, row, True)
        self.GM[pl.ds(row, self.ACC.shape[0])] = self.ACC[...] * 0.25

    def pooled_grad(self, row, first=0, last=None):
        def one(n):
            s = q = None
            for r in range(self.ACC.shape[0]):
                grad = self.doubled(self.GM[row + r, n], r)
                for k in range(2):
                    xhat, v = self.norm_one_grad(n, 2 * (row + r) + k, grad)
                    s, q = plus(s, fold(v)), plus(q, fold(v * xhat))
            self.add_sums(n, s, q)

        self.loop(one, first, last)

    def sums_one_back(self):
        self.AFP[0:1] = jnp.sum(self.SS[16:32], axis=0, keepdims=True)
        self.AFP[1:2] = jnp.sum(self.SS[0:16], axis=0, keepdims=True)
        self.AFP[2:3] = jnp.sum(self.C1[...], axis=0, keepdims=True)
        self.AFR[self.p.sp] = self.AFP[...]
        self.ST4[self.p.sp] = exact_dot(self.SS[...] * self.AFF[0:1], group_matrix(self.channels, True))

    def affine_y(self):
        self.AFY[0] = self.asum.total()
        self.w.put(self.AFY.at[0], self.AFY.at[1], self.p.yn, self.afy)

    def affine_z(self):
        self.w.got(self.AFY.at[1], self.afy, self.p.yn)
        self.AFZ[self.p.z] = self.AFY[0] + self.AFY[1]
        for k in range(3):
            self.w.put(self.AFZ.at[self.p.z], self.AFZ.at[self.p.z], self.p.zs[k], self.afz + k)

    def affine_done(self):
        for k in range(3):
            self.w.got(self.AFZ.at[self.p.z_off(3 - k)], self.afz + k, self.p.zs[k])
        self.AFP[...] = self.AFZ[0] + self.AFZ[1] + self.AFZ[2] + self.AFZ[3]
        tile = self.AFP[:, pl.ds(many(self.p.sp * 128, 128), 128)]
        line = lax.broadcasted_iota(jnp.int32, tile.shape, 0) == self.p.img
        self.ag[...] = jnp.sum(jnp.where(line, tile, 0.0), axis=0, keepdims=True)

    def norm_one_back(self):
        total = exact_dot(self.sum4.total(), group_matrix(self.channels, False))
        self.AB[4] = self.MI[1] * self.AFF[0:1]
        self.AB[5] = self.MI[1] * (total[:16] / self.CNT[0])
        self.AB[6] = self.MI[1] * (total[16:] / self.CNT[0])

    def image_grad(self, first, last):
        col = self.cols(self.side_full)

        def one(n):
            for hr in range(self.rows):
                grad = self.doubled(self.GM[hr, n], 0)
                cell = self.doubled(self.COT[n, hr].astype(F32) * 0.25, 1)
                for k in range(2):
                    r = 2 * hr + k
                    xhat, v = self.norm_one_grad(n, r, grad)
                    v = v * self.at(4, n) - self.at(5, n) - xhat * self.at(6, n) + cell
                    self.IMG[n, r] = jnp.where(col < self.width(n, r), v, 0.0).astype(BF16)

        self.loop(one, first, last)
        part = pl.ds(first, last - first)
        copy = pltpu.make_async_copy(self.IMG.at[part], self.gi.at[part], self.lsem.at[len(self.copies)])
        copy.start()
        self.copies.append(copy)

    def finish(self):
        for copy in self.copies[2:]:
            copy.wait()


def mix(works, ticks):
    done = 0
    for i, work in enumerate(works):
        work()
        upto = (i + 1) * len(ticks) // len(works)
        for tick in ticks[done:upto]:
            tick()
        done = upto
    for tick in ticks[done:]:
        tick()


def pairs(*lists):
    return [item for group in zip(*lists) for item in group]


def schedule(s):
    p, g, z = s.p, s.g, s.p.z
    pieces = list(range(PIECES))
    edge, middle = (0, s.rows - 1), range(1, s.rows - 1)
    inside, outside = range(1, s.rim - 1), (0, s.rim - 1)
    lead = choose(z == 0, 0, 1)
    other = choose(z == 1, 0, 1)
    tail = 1 - lead
    near = choose(z == 2, 3, 2)
    n = s.images

    def come(b, j, when=None):
        def run():
            g.arrive(b, j, when)
            g.own(b, j, when)

        return run

    def call(method, *args):
        return lambda: method(*args)

    s.load()
    s.own_weights()
    s.w.greet(p)
    s.aff_img.send()
    for j in pieces:
        g.along(z, j, z < 2, z > 0)
        g.own(z, j, z < 2)
    s.own_embedding()
    s.counts()
    s.clear_sums()
    s.loaded(0)
    s.stats_one(0, n // 2)
    come(other, 0)()
    s.stats_one(n // 2, n)
    s.stats_one_end()
    s.sum1.send()
    s.aff_img.turn()
    come(other, 1)()
    s.aff_img.wait()
    s.aff_sp.send()
    for j in pieces[2:]:
        come(other, j)()
    g.turn(lead, 0)
    s.sum1.wait()
    s.aff_sp.wait()
    s.affine_rows()
    s.norm_one()
    works = [call(s.pool, edge, i, i + 4) for i in range(0, n, 4)] + [s.halo_p.send, s.ez_send]
    works += [call(s.pool, middle, i, i + 4) for i in range(0, n, 4)]
    works += [call(s.loaded, 1), s.mask_cot, call(s.shift, s.PO, inside)]
    ticks = pairs([come(0, j, z >= 2) for j in pieces], [call(g.turn, lead, j) for j in pieces[1:]] + [lambda: None])
    ticks += pairs([call(g.last, lead, j) for j in pieces], [call(g.turn, tail, j) for j in pieces])
    mix(works, ticks)
    s.ez_turn()
    for j in pieces:
        g.last(tail, j)
    s.halo_p.wait()
    s.shift(s.PO, outside)
    for j in pieces:
        g.done(lead, j)
        g.done(tail, j)
    for j in pieces:
        g.along(2, j, z == 2, z > 3)
        g.own(z, j, z >= 2)
    s.clear_sums()
    s.inner_conv(0)
    s.ez_wait()
    s.project()
    s.proj.send()
    come(2, 0, z < 2)()
    s.proj.cross()
    come(2, 1, z < 2)()
    s.inner_conv(2)
    s.proj.back()
    s.stats_two()
    s.sum2.send()
    for j in pieces[2:]:
        come(2, j, z < 2)()
    come(near, 0, z >= 2)()
    s.proj.wait()
    s.sum2.wait()
    s.norm_two()
    s.activate(edge)
    s.halo_a.send()
    s.activate(middle)
    for j in pieces[1:]:
        come(near, j, z >= 2)()
    for j in pieces:
        come(3, j, z < 2)()
    s.shift(s.A2, inside)
    for j in pieces:
        g.turn(2, j)
    s.halo_g.send()
    s.halo_a.wait()
    s.shift(s.A2, outside)

    def tap_two(t):
        s.tap_grad(s.A2, s.G, t)
        s.r2.give((t + 1) * s.channels)

    ticks = [call(g.turn, 3, j) for j in pieces] + [call(g.last, b, j) for b in (2, 3) for j in pieces]
    mix([call(tap_two, t) for t in range(9)], ticks)
    for b in (1, 0):
        for yy in range(2):
            for xx in range(2):
                s.r2.take(b, yy, xx)
    for b in (1, 0):
        for j in pieces:
            s.r2.step(0, b, j)
        if b == 1:
            s.shift(s.G, inside)
            s.clear_sums()
    s.halo_g.wait()
    s.shift(s.G, outside)
    for j in pieces:
        g.done(2, j)
        g.done(3, j)
    for j in pieces:
        s.r2.step(1, 1, j)
    s.mixed_grad(0)
    for j in pieces:
        s.r2.step(2, 1, j)
    s.mixed_grad(2)
    s.sums_two_back()
    s.sum3.send()
    for j in pieces:
        s.r2.step(1, 0, j)
    s.shift(s.PO, range(s.rim))
    s.sum3.wait()
    s.norm_two_back()
    s.inner_grad(edge)
    s.halo_b.send()
    s.inner_grad(middle)
    s.r2.given()

    def tap_one(t):
        s.tap_grad(s.PO, s.GB, t)
        s.r1.give((t + 1) * s.channels)

    for t in range(9):
        tap_one(t)
        if t < PIECES:
            s.r2.step(2, 0, t)
    for b in (0, 1):
        for yy in range(2):
            for xx in range(2):
                s.r1.take(b, yy, xx)
    for b in (0, 1):
        for j in pieces:
            s.r1.step(0, b, j)
    for j in pieces:
        s.r1.step(1, 0, j)
    s.halo_b.wait()
    s.shift(s.GB, range(s.rim))
    s.prepare_one_back()
    s.psum.send()
    s.pooled_conv(0)
    s.psum.cross()
    for j in pieces:
        s.r1.step(2, 0, j)
    for j in pieces:
        s.r1.step(1, 1, j)
    s.pooled_conv(2)
    s.psum.back()
    for j in pieces:
        s.r2.step(3, 1, j)
    works = [call(s.pooled_grad, row, i, i + 4) for row in (0, 2) for i in range(0, n, 4)]
    ticks = [call(s.r1.step, 2, 1, j) for j in pieces] + [call(s.r2.step, 3, 0, j) for j in pieces]
    mix(works, ticks)
    s.sums_one_back()
    s.sum4.send()
    s.asum.send()
    for j in pieces:
        s.r1.step(3, 0, j)
    s.psum.wait()
    s.project_grad()
    s.spread_g.send()
    s.spread_e.send()
    s.sum4.wait()
    s.norm_one_back()
    s.asum.wait()
    s.affine_y()
    s.shift(s.A2, range(s.rim))
    for j in pieces:
        s.r1.step(3, 1, j)
    for j in pieces:
        s.r2.step(4, 1, j)
    s.output(0)
    for j in pieces:
        s.r2.step(4, 0, j)
        s.r1.step(4, 0, j)
    s.affine_z()
    s.spread_g.turn()
    s.spread_e.turn()
    s.output(2)
    s.output_out()
    for j in pieces:
        s.r1.step(4, 1, j)
    s.embedding_part()
    s.esum.send()
    s.esum.cross()
    works = [call(s.image_grad, i, i + 3) for i in range(0, n, 3)]
    ticks = [call(s.r2.step, 5, 1, j) for j in pieces] + [call(s.r2.step, 5, 0, j) for j in pieces]
    mix(works, ticks)
    s.esum.back()
    s.spread_g.wait()
    s.spread_e.wait()
    s.embedding_weights()
    for b in (0, 1):
        for j in pieces:
            s.r1.step(5, b, j)
    s.affine_done()
    s.esum.wait()
    s.embedding_grad()
    s.finish()
    s.w.close()


def whole_kernel(names, *refs):
    refs = dict(zip(names, refs))
    place = Place(lax.axis_index("img"), lax.axis_index("sp"))
    wire = Wire(refs.pop("ssem"), refs.pop("rsem"))
    schedule(Step(place, wire, refs))


def shapes(images, cotangent, conv_w, emb_w):
    n, rows_full, side_full, c = images
    _, rows, side, _ = cotangent
    shard = conv_w[0]
    rim = (rows + 2, n, side, c)
    band = (rows, n, side, c)
    out = dict(
        IMG=(images, BF16), COT=(cotangent, BF16), W=((32 * shard, c), BF16), EZ=((emb_w[1], emb_w[1]), BF16),
        PO=(rim, BF16), G=(rim, BF16), A2=(rim, BF16), GB=(rim, BF16), X=((2,) + rim, BF16),
        INN=(band, BF16), SKIP=(band, F32), GM=(band, F32), ACC=((2,) + band[1:], F32), OUTV=(cotangent, BF16),
        DW=((16 * shard, c), BF16), T=((4, c // 128, side_full, 128), F32), SS=((32, c), F32),
        CNT=((2, 16, c), F32), MI=((6, 16, c), F32), AB=((9, 16, c), F32), AFF=((8, c), F32), AFP=((8, c), F32),
        C1=((8, c), F32), C2=((8, c), F32), AFS=((4, 2, 4, 8, 128), F32), AFR=((4, 8, c), F32),
        AFY=((2, 8, c), F32), AFZ=((4, 8, c), F32), EP=((16, 2 * c), F32), EA=((2, 4, 16, 2 * c), BF16),
        GPA=((2, 4, 2, 16, c), F32), EW=((128, 2 * c), F32), PX=((7, 16, c), F32), PE=((7, 16, c), F32),
        ST1=((4, 32, 128), F32), ST2=((4, 32, 128), F32), ST3=((4, 32, 128), F32), PS=((7, 16, c), F32), ST4=((4, 32, 128), F32),
    )
    for k in "AB":
        for i, v in enumerate(Scatter.scratch(shard, c)):
            out["R%s%d" % (k, i)] = v
    return out


WIRES = 360
VM = pl.BlockSpec(memory_space=pltpu.VMEM)
ANY = pl.BlockSpec(memory_space=pl.ANY)
SM = pl.BlockSpec(memory_space=pltpu.SMEM)


def finish_kernel(image_total, res, ewg, ag, gi_in, out_in, cw, cm, ce, ew, em, ee, aw, am, ae,
                  gi, out, ncw, new, naw, ncm, nem, nam, nce, nee, nae, sem):
    copies = [pltpu.make_async_copy(gi_in, gi, sem.at[0]), pltpu.make_async_copy(out_in, out, sem.at[1])]
    for copy in copies:
        copy.start()
    inverse = 1.0 / image_total

    def update(weight, moment, average, total, new_weight, new_moment, new_average):
        mean = total[...] * inverse
        m = MOMENTUM * moment[...] + mean
        w = weight[...] - LEARN_RATE * (mean + MOMENTUM * m)
        new_weight[...] = w
        new_moment[...] = m
        new_average[...] = EMA_DECAY * average[...] + (1.0 - EMA_DECAY) * w

    update(ew, em, ee, ewg, new, nem, nee)
    update(aw, am, ae, ag, naw, nam, nae)
    step = 32

    def piece(i, _):
        at = pl.ds(pl.multiple_of(i * step, step), step)
        update(*(r.at[at] for r in (cw, cm, ce, res, ncw, ncm, nce)))
        return 0

    lax.fori_loop(0, cw.shape[0] // step, piece, 0)
    for copy in copies:
        copy.wait()


def local_kernels(image_total, images, embedding, extent, cotangent, conv_w, emb_w, affine,
                  conv_mom, emb_mom, affine_mom, conv_ema, emb_ema, affine_ema):
    shp = jax.ShapeDtypeStruct
    line = lambda v: v.reshape(1, 128)
    scratch = shapes(images.shape, cotangent.shape, conv_w.shape, emb_w.shape)
    inputs = ["ext", "img", "cot", "emb", "cw", "ew", "aff"]
    outputs = ["out", "gi", "RES", "ge", "ewg", "ag"]
    names = inputs + outputs + list(scratch) + ["lsem", "ssem", "rsem"]
    out, gi, res, ge, ewg, ag = pl.pallas_call(
        lambda *refs: whole_kernel(names, *refs),
        name="resblock_step",
        out_shape=(
            shp(cotangent.shape, BF16), shp(images.shape, BF16), shp(conv_w.shape, F32),
            shp(embedding.shape, F32), shp(emb_w.shape, F32), shp((1, 128), F32),
        ),
        in_specs=[SM, ANY, ANY, VM, VM, VM, VM],
        out_specs=(ANY, ANY, VM, VM, VM, VM),
        scratch_shapes=[pltpu.VMEM(*v) for v in scratch.values()]
        + [pltpu.SemaphoreType.DMA((8,)), pltpu.SemaphoreType.DMA((WIRES,)), pltpu.SemaphoreType.DMA((WIRES,))],
        compiler_params=pltpu.CompilerParams(
            collective_id=1, has_side_effects=True, vmem_limit_bytes=62 << 20
        ),
    )(extent, images, cotangent, embedding, conv_w, emb_w, line(affine))
    trio = [shp(conv_w.shape, F32), shp(emb_w.shape, F32), shp((1, 128), F32)]
    gi, out, ncw, new, naw, ncm, nem, nam, nce, nee, nae = pl.pallas_call(
        lambda *refs: finish_kernel(image_total, *refs),
        name="update",
        out_shape=[shp(images.shape, BF16), shp(cotangent.shape, BF16)] + trio * 3,
        in_specs=[VM] * 14,
        out_specs=[ANY, ANY] + [VM] * 9,
        scratch_shapes=[pltpu.SemaphoreType.DMA((2,))],
        compiler_params=pltpu.CompilerParams(vmem_limit_bytes=40 << 20),
    )(res, ewg, ag, gi, out, conv_w, conv_mom, conv_ema, emb_w, emb_mom, emb_ema,
      line(affine), line(affine_mom), line(affine_ema))
    flat = lambda v: v.reshape(-1)
    return out, gi, ge, ncw, new, flat(naw), ncm, nem, flat(nam), nce, nee, flat(nae)


def padded_2(cells, sides, width):
    for axis, dim in sides:
        count = lax.axis_size(axis)
        ends = count - 1
        head = lax.slice_in_dim(cells, 0, width, axis=dim)
        tail = lax.slice_in_dim(cells, cells.shape[dim] - width, cells.shape[dim], axis=dim)
        cells = jnp.concatenate(
            [
                lax.ppermute(tail, axis, [(i, (i + 1) % count) for i in range(ends)]),
                cells,
                lax.ppermute(head, axis, [((i + 1) % count, i) for i in range(ends)]),
            ],
            axis=dim,
        )
    return cells


def band_mask(extent, first_row, band_rows, band_cols, halved):
    height = extent[:, 0]
    breadth = extent[:, 1]
    if halved:
        height = height // 2
        breadth = breadth // 2
    row_ids = first_row + jnp.arange(band_rows, dtype=jnp.int32)
    col_ids = jnp.arange(band_cols, dtype=jnp.int32)
    inside = (row_ids[None, :, None] < height[:, None, None]) & (
        col_ids[None, None, :] < breadth[:, None, None]
    )
    return inside.astype(jnp.float32)[..., None]


def per_group_sums(values, group_count):
    shaped = values.reshape(values.shape[:3] + (group_count, values.shape[3] // group_count))
    return jnp.sum(shaped, axis=(1, 2, 4))


def spread_to_channels(stat, channels_per_group):
    return jnp.repeat(stat, channels_per_group, axis=1)[:, None, None, :]


def pool_cells(values):
    shaped = values.reshape(
        values.shape[0], values.shape[1] // 2, 2, values.shape[2] // 2, 2, values.shape[3]
    )
    return jnp.sum(shaped, axis=(2, 4)) * 0.25


def spread_cells(values):
    return jnp.repeat(jnp.repeat(values, 2, axis=1), 2, axis=2) * 0.25


def silu_slope(values):
    sigma = jax.nn.sigmoid(values)
    return sigma * (1.0 + values * (1.0 - sigma))


def conv_rows(padded, kernel, layout):
    return lax.conv_general_dilated(
        padded,
        kernel,
        (1, 1),
        ((0, 0), (1, 1)),
        dimension_numbers=("NHWC", "HWIO", layout),
        preferred_element_type=jnp.float32,
    )


def conv_back(padded, kernel):
    return lax.conv_general_dilated(
        padded,
        jnp.flip(kernel, (0, 1)),
        (1, 1),
        ((0, 0), (1, 1)),
        dimension_numbers=("NHWC", "HWOI", "NHWC"),
        preferred_element_type=jnp.float32,
    )


def tap_grads(padded, grads):
    window = jnp.pad(padded, ((0, 0), (0, 0), (1, 1), (0, 0)))
    band_rows = grads.shape[1]
    band_cols = grads.shape[2]
    kernel_rows = []
    for tap_row in range(3):
        taps = []
        for tap_col in range(3):
            source = window[:, tap_row : tap_row + band_rows, tap_col : tap_col + band_cols, :]
            taps.append(
                jnp.einsum("brci,brco->io", source, grads, preferred_element_type=jnp.float32)
            )
        kernel_rows.append(jnp.stack(taps))
    return jnp.stack(kernel_rows)


def band_rim(values):
    return padded_2(values, (("sp", 1),), 1)


def other_rim(values):
    return padded_2(values, (("sp", 1),), 1)


def update(weight, moment, average, total, image_total):
    grad_mean = total / image_total
    new_moment = MOMENTUM * moment + grad_mean
    new_weight = weight - LEARN_RATE * (grad_mean + MOMENTUM * new_moment)
    new_average = EMA_DECAY * average + (1.0 - EMA_DECAY) * new_weight
    return (new_weight, new_moment, new_average)


def local(
    images,
    embedding,
    extent,
    cotangent,
    conv_w,
    emb_w,
    affine,
    conv_mom,
    emb_mom,
    affine_mom,
    conv_ema,
    emb_ema,
    affine_ema,
):
    conv_all, emb_all, affine_all = (
        lax.all_gather(conv_w.astype(jnp.bfloat16), ("img", "sp"), axis=0, tiled=True),
        lax.all_gather(emb_w.astype(jnp.bfloat16), ("img", "sp"), axis=0, tiled=True),
        lax.all_gather(affine.astype(jnp.bfloat16), ("img", "sp"), axis=0, tiled=True),
    )
    channels = conv_all.shape[1]
    first_kernel = conv_all[: 9 * channels].reshape(3, 3, channels, channels)
    second_kernel = conv_all[9 * channels :].reshape(3, 3, channels, channels)
    parameters = affine_all.astype(jnp.float32).reshape(8, channels)
    image_count = images.shape[0]
    band_rows = images.shape[1]
    grid_side = images.shape[2]
    half_band = band_rows // 2
    half_side = grid_side // 2
    sp_size = lax.axis_size("sp")
    sp_index = lax.axis_index("sp")
    local_channels = channels // sp_size
    first_channels = sp_index * local_channels
    channels_per_group = channels // NORM_GROUPS
    groups_on_device = local_channels // channels_per_group
    full_mask = band_mask(extent, sp_index * band_rows, band_rows, grid_side, False)
    half_mask = band_mask(extent, sp_index * half_band, half_band, half_side, True)
    whole_half = band_mask(extent, 0, half_side, half_side, True)
    full_pixel_count = (extent[:, 0] * extent[:, 1] * channels_per_group).astype(jnp.float32)[
        :, None
    ]
    half_pixel_count = (extent[:, 0] // 2 * (extent[:, 1] // 2) * channels_per_group).astype(
        jnp.float32
    )[:, None]
    masked_values = images.astype(jnp.float32) * full_mask
    sums_one, squares_one = lax.psum(
        (
            per_group_sums(masked_values, NORM_GROUPS),
            per_group_sums(masked_values * masked_values, NORM_GROUPS),
        ),
        "sp",
    )
    first_group_mean = sums_one / full_pixel_count
    first_inverse_deviation = lax.rsqrt(
        squares_one / full_pixel_count - first_group_mean * first_group_mean + EPSILON
    )
    first_normalized = (
        masked_values - spread_to_channels(first_group_mean, channels_per_group)
    ) * spread_to_channels(first_inverse_deviation, channels_per_group)
    first_group_norm = first_normalized * parameters[0] + parameters[1]
    pooled = pool_cells(jax.nn.silu(first_group_norm) * full_mask).astype(jnp.bfloat16)
    skip_path = pool_cells(masked_values)
    pooled_rim = band_rim(pooled)
    inner_act = ((conv_rows(pooled_rim, first_kernel, "NHWC") + parameters[2]) * half_mask).astype(
        jnp.bfloat16
    )
    emb_act = jax.nn.silu(embedding.astype(jnp.float32)).astype(jnp.bfloat16)

    def place_local(values):
        return lax.dynamic_update_slice_in_dim(
            jnp.zeros((channels,), jnp.float32), values, first_channels, 0
        )

    inner_channels = lax.all_to_all(
        inner_act, "sp", split_axis=3, concat_axis=1, tiled=True
    ).astype(jnp.float32)
    emb_cols = jnp.concatenate(
        [
            lax.dynamic_slice_in_dim(emb_all, first_channels, local_channels, 1),
            lax.dynamic_slice_in_dim(emb_all, channels + first_channels, local_channels, 1),
        ],
        axis=1,
    )
    emb_bias = jnp.concatenate(
        [
            lax.dynamic_slice_in_dim(parameters[3], first_channels, local_channels, 0),
            lax.dynamic_slice_in_dim(parameters[4], first_channels, local_channels, 0),
        ]
    )
    emb_proj = jnp.dot(emb_act, emb_cols, preferred_element_type=jnp.float32) + emb_bias
    ada_scale = 1.0 + emb_proj[:, :local_channels][:, None, None, :]
    ada_shift = emb_proj[:, local_channels:][:, None, None, :]
    sums_two = per_group_sums(inner_channels, groups_on_device)
    squares_two = per_group_sums(inner_channels * inner_channels, groups_on_device)
    second_group_mean = sums_two / half_pixel_count
    second_inverse_deviation = lax.rsqrt(
        squares_two / half_pixel_count - second_group_mean * second_group_mean + EPSILON
    )
    second_normalized = (
        inner_channels - spread_to_channels(second_group_mean, channels_per_group)
    ) * spread_to_channels(second_inverse_deviation, channels_per_group)
    second_gain = lax.dynamic_slice_in_dim(parameters[5], first_channels, local_channels, 0)
    second_group_norm = second_normalized * second_gain + lax.dynamic_slice_in_dim(
        parameters[6], first_channels, local_channels, 0
    )
    mixed_act = second_group_norm * ada_scale + ada_shift
    act_two = (jax.nn.silu(mixed_act) * whole_half).astype(jnp.bfloat16)
    act_rows = lax.all_to_all(act_two, "sp", split_axis=1, concat_axis=3, tiled=True)
    act_rim = other_rim(act_rows)
    branch = conv_rows(act_rim, second_kernel, "NHWC") + parameters[7]
    output = (skip_path + branch * half_mask).astype(jnp.bfloat16)
    grad_branch = (cotangent.astype(jnp.float32) * half_mask).astype(jnp.bfloat16)
    bias_two_grad = jnp.sum(grad_branch.astype(jnp.float32), axis=(0, 1, 2))
    grad_rim = other_rim(grad_branch)
    kernel_two = tap_grads(act_rim, grad_branch)
    grad_band = conv_back(grad_rim, second_kernel).astype(jnp.bfloat16)
    grad_act = lax.all_to_all(grad_band, "sp", split_axis=3, concat_axis=1, tiled=True)
    grad_mixed = grad_act.astype(jnp.float32) * whole_half * silu_slope(mixed_act)
    grad_proj = jnp.concatenate(
        [jnp.sum(grad_mixed * second_group_norm, axis=(1, 2)), jnp.sum(grad_mixed, axis=(1, 2))],
        axis=1,
    )
    second_norm_gradient = grad_mixed * ada_scale
    second_gain_gradient = jnp.sum(second_norm_gradient * second_normalized, axis=(0, 1, 2))
    bias_norm_two_grad = jnp.sum(second_norm_gradient, axis=(0, 1, 2))
    second_normalized_gradient = second_norm_gradient * second_gain
    first_total_count = (
        per_group_sums(second_normalized_gradient, groups_on_device) / half_pixel_count
    )
    second_total_count = (
        per_group_sums(second_normalized_gradient * second_normalized, groups_on_device)
        / half_pixel_count
    )
    grad_inner = spread_to_channels(second_inverse_deviation, channels_per_group) * (
        second_normalized_gradient
        - spread_to_channels(first_total_count, channels_per_group)
        - second_normalized * spread_to_channels(second_total_count, channels_per_group)
    )
    grad_inner_rows = lax.all_to_all(
        grad_inner.astype(jnp.bfloat16), "sp", split_axis=1, concat_axis=3, tiled=True
    )
    emb_grad_cols = jnp.einsum(
        "be,bk->ek", emb_act.astype(jnp.float32), grad_proj, precision=HIGHEST
    )
    emb_kernel = jnp.zeros((emb_all.shape[0], 2 * channels), jnp.float32)
    emb_kernel = lax.dynamic_update_slice_in_dim(
        emb_kernel, emb_grad_cols[:, :local_channels], first_channels, 1
    )
    emb_kernel = lax.dynamic_update_slice_in_dim(
        emb_kernel, emb_grad_cols[:, local_channels:], channels + first_channels, 1
    )
    silu_part = jnp.einsum("bk,ek->be", grad_proj, emb_cols.astype(jnp.float32), precision=HIGHEST)
    silu_grad = lax.psum(silu_part.astype(jnp.bfloat16), "sp").astype(jnp.float32)
    emb_bias_grad = jnp.sum(grad_proj, axis=0)
    coarse_affine = [
        place_local(emb_bias_grad[:local_channels]),
        place_local(emb_bias_grad[local_channels:]),
        place_local(second_gain_gradient),
        place_local(bias_norm_two_grad),
    ]
    grad_embedding = silu_grad * silu_slope(embedding.astype(jnp.float32))
    grad_raw = (grad_inner_rows.astype(jnp.float32) * half_mask).astype(jnp.bfloat16)
    bias_one_grad = jnp.sum(grad_raw.astype(jnp.float32), axis=(0, 1, 2))
    kernel_one = tap_grads(pooled_rim, grad_raw)
    grad_pooled = conv_back(band_rim(grad_raw), first_kernel)
    first_norm_gradient = spread_cells(grad_pooled) * full_mask * silu_slope(first_group_norm)
    first_gain_gradient = jnp.sum(first_norm_gradient * first_normalized, axis=(0, 1, 2))
    bias_norm_one_grad = jnp.sum(first_norm_gradient, axis=(0, 1, 2))
    first_normalized_gradient = first_norm_gradient * parameters[0]
    back_one, second_backward = lax.psum(
        (
            per_group_sums(first_normalized_gradient, NORM_GROUPS),
            per_group_sums(first_normalized_gradient * first_normalized, NORM_GROUPS),
        ),
        "sp",
    )
    grad_masked = spread_to_channels(first_inverse_deviation, channels_per_group) * (
        first_normalized_gradient
        - spread_to_channels(back_one / full_pixel_count, channels_per_group)
        - first_normalized
        * spread_to_channels(second_backward / full_pixel_count, channels_per_group)
    ) + spread_cells(cotangent.astype(jnp.float32))
    grad_images = (grad_masked * full_mask).astype(jnp.bfloat16)
    affine_grad = jnp.concatenate(
        [first_gain_gradient, bias_norm_one_grad, bias_one_grad] + coarse_affine + [bias_two_grad]
    )
    conv_grad = jnp.concatenate(
        [kernel_one.reshape(9 * channels, channels), kernel_two.reshape(9 * channels, channels)]
    )
    conv_sum, emb_sum, affine_sum = (
        lax.psum_scatter(conv_grad, ("img", "sp"), scatter_dimension=0, tiled=True),
        lax.psum_scatter(emb_kernel, ("img", "sp"), scatter_dimension=0, tiled=True),
        lax.psum_scatter(affine_grad, ("img", "sp"), scatter_dimension=0, tiled=True),
    )
    image_total = float(image_count * lax.axis_size("img"))
    new_conv, conv_moment, conv_average = update(conv_w, conv_mom, conv_ema, conv_sum, image_total)
    new_emb, emb_moment, emb_average = update(emb_w, emb_mom, emb_ema, emb_sum, image_total)
    new_affine, affine_moment, affine_average = update(
        affine, affine_mom, affine_ema, affine_sum, image_total
    )
    return (
        output,
        grad_images,
        grad_embedding,
        new_conv,
        new_emb,
        new_affine,
        conv_moment,
        emb_moment,
        affine_moment,
        conv_average,
        emb_average,
        affine_average,
    )


def kernels_or_ops(images, embedding, extent, cotangent, conv_w, *rest):
    arrays = (images, embedding, extent, cotangent, conv_w) + rest
    n, rows, side, channels = images.shape
    if n > 16 or rows != 8 or side != 32 or channels != 512 or conv_w.shape[0] != 288:
        return local(*arrays)
    return local_kernels(float(n * lax.axis_size("img")), *arrays)


def solution(mesh):
    in_specs = (
        P("img", "sp", None, None),
        P("img", None),
        P("img", None),
        P("img", "sp", None, None),
        P(("img", "sp"), None),
        P(("img", "sp"), None),
        P(("img", "sp")),
        P(("img", "sp"), None),
        P(("img", "sp"), None),
        P(("img", "sp")),
        P(("img", "sp"), None),
        P(("img", "sp"), None),
        P(("img", "sp")),
    )
    out_specs = (
        P("img", "sp", None, None),
        P("img", "sp", None, None),
        P("img", None),
        P(("img", "sp"), None),
        P(("img", "sp"), None),
        P(("img", "sp")),
        P(("img", "sp"), None),
        P(("img", "sp"), None),
        P(("img", "sp")),
        P(("img", "sp"), None),
        P(("img", "sp"), None),
        P(("img", "sp")),
    )
    fits = dict(mesh.shape) == {"img": 8, "sp": 4}
    return jax.shard_map(kernels_or_ops if fits else local, mesh=mesh, in_specs=in_specs, out_specs=out_specs, check_vma=False)
```

```python
import jax
import jax.numpy as jnp
from jax import lax
from jax.experimental import pallas as pl
from jax.experimental.pallas import tpu as pltpu
from jax.sharding import PartitionSpec as P

F32 = jnp.float32
BF16 = jnp.bfloat16
HIGHEST = lax.Precision.HIGHEST
MESH = pl.DeviceIdType.MESH
EPSILON = 1e-05
LEARN_RATE = 0.03
MOMENTUM = 0.5
EMA_DECAY = 0.5
NORM_GROUPS = 32
PIECES = 3


def choose(cond, a, b):
    if isinstance(cond, bool):
        return a if cond else b
    return jnp.where(cond, a, b)


def many(value, factor):
    return value if isinstance(value, int) else pl.multiple_of(value, factor)


class Place:
    def __init__(self, img, sp):
        self.img, self.sp = img, sp
        if isinstance(img, int):
            self.z, self.y, self.x, self.c = img // 2, img % 2, sp // 2, sp % 2
        else:
            self.z, self.y = lax.div(img, 2), lax.rem(img, 2)
            self.x, self.c = lax.div(sp, 2), lax.rem(sp, 2)
        z, y, x, c = self.z, self.y, self.x, self.c
        self.core = self.at(z, y, x, 1 - c)
        self.xn = self.at(z, y, 1 - x, c)
        self.yn = self.at(z, 1 - y, x, c)
        self.up, self.down = self.at(z + 1, y, x, c), self.at(z - 1, y, x, c)
        self.pair = self.at(z + 1 - 2 * self.odd(z), y, x, c)
        self.gate = self.at(choose(z < 2, 2, 1), y, x, c)
        self.zs = [self.at(self.z_off(k), y, x, c) for k in (1, 2, 3)]
        self.sps = [(img, self.sp_off(k)) for k in (1, 2, 3)]

    def at(self, z, y, x, c):
        return (z * 2 + y, x * 2 + c)

    def odd(self, value):
        return value % 2 if isinstance(value, int) else lax.rem(value, 2)

    def off(self, value, k):
        value = value + k
        return value % 4 if isinstance(value, int) else lax.rem(value, 4)

    def z_off(self, k):
        return self.off(self.z, k)

    def sp_off(self, k):
        return self.off(self.sp, k)


class Wire:
    def __init__(self, ssem, rsem):
        self.ssem, self.rsem = ssem, rsem
        self.used = 0
        self.open = []

    def take(self, count=1):
        first = self.used
        self.used += count
        return first

    def when(self, cond, do):
        if cond is None:
            do()
        else:
            pl.when(cond)(do)

    def copy(self, src, dst, peer, send, recv):
        return pltpu.make_async_remote_copy(
            src_ref=src, dst_ref=dst, send_sem=self.ssem.at[send], recv_sem=self.rsem.at[recv],
            device_id=peer, device_id_type=MESH,
        )

    def put(self, src, dst, peer, send, recv=None, when=None):
        def make():
            return self.copy(src, dst, peer, send, send if recv is None else recv)

        self.when(when, lambda: make().start())
        self.open.append((make, when))
        return self.open[-1]

    def left(self, copies):
        for make, when in copies:
            self.when(when, lambda make=make: make().wait_send())
        self.open = [item for item in self.open if not any(item is copy for copy in copies)]

    def got(self, ref, recv, peer, when=None):
        self.when(when, lambda: self.copy(ref, ref, peer, recv, recv).wait_recv())

    def close(self):
        self.left(self.open)

    def greet(self, place):
        barrier = pltpu.get_barrier_semaphore()
        peers = place.sps + [place.yn] + place.zs
        for peer in peers:
            pl.semaphore_signal(barrier, inc=1, device_id=peer, device_id_type=MESH)
        pl.semaphore_wait(barrier, len(peers))


class Gather:
    def __init__(self, wire, place, W, rows):
        self.wire, self.place, self.W, self.rows = wire, place, W, rows
        self.piece = rows // PIECES
        count = 4 * PIECES
        self.sems = {k: wire.take(count) for k in ("z", "u", "d", "x", "y", "c", "xy", "yx", "cx", "cy", "ca", "cb")}

    def sem(self, kind, b, j):
        return self.sems[kind] + b * PIECES + j

    def ref(self, b, y, x, c, j, half=None):
        start = self.rows * ((b * 2 + y) * 4 + x * 2 + c) + j * self.piece
        size = self.piece
        if half is not None:
            size = size // 2
            start = start + half * size
        return self.W.at[pl.ds(many(start, 16), size)]

    def along(self, b, j, up, down):
        p, wire = self.place, self.wire
        r = self.ref(b, p.y, p.x, p.c, j)
        wire.put(r, r, p.up, self.sem("u", b, j), self.sem("z", b, j), when=up)
        wire.put(r, r, p.down, self.sem("d", b, j), self.sem("z", b, j), when=down)

    def arrive(self, b, j, when=None):
        p = self.place
        both = lambda cond: cond if when is None else when & cond
        self.wire.got(self.ref(b, p.y, p.x, p.c, j), self.sem("z", b, j), p.up, when=when)
        self.along(b, j, both((b < p.z) & (p.z < 3)), both((b > p.z) & (p.z > 0)))

    def own(self, b, j, when=None):
        p, wire = self.place, self.wire
        r = self.ref(b, p.y, p.x, p.c, j)
        wire.put(r, r, p.xn, self.sem("x", b, j), when=when)
        wire.put(r, r, p.yn, self.sem("y", b, j), when=when)
        wire.put(r, r, p.core, self.sem("c", b, j), when=when)

    def turn(self, b, j):
        p, wire = self.place, self.wire
        r = self.ref(b, p.y, 1 - p.x, p.c, j)
        wire.got(r, self.sem("x", b, j), p.xn)
        h = self.ref(b, p.y, 1 - p.x, p.c, j, 0)
        wire.put(h, h, p.yn, self.sem("xy", b, j))
        wire.put(r, r, p.core, self.sem("cx", b, j))
        r = self.ref(b, 1 - p.y, p.x, p.c, j)
        wire.got(r, self.sem("y", b, j), p.yn)
        h = self.ref(b, 1 - p.y, p.x, p.c, j, 1)
        wire.put(h, h, p.xn, self.sem("yx", b, j))
        wire.put(r, r, p.core, self.sem("cy", b, j))

    def last(self, b, j):
        p, wire = self.place, self.wire
        h = self.ref(b, 1 - p.y, 1 - p.x, p.c, j, 0)
        wire.got(h, self.sem("xy", b, j), p.yn)
        wire.put(h, h, p.core, self.sem("ca", b, j))
        h = self.ref(b, 1 - p.y, 1 - p.x, p.c, j, 1)
        wire.got(h, self.sem("yx", b, j), p.xn)
        wire.put(h, h, p.core, self.sem("cb", b, j))

    def done(self, b, j):
        p, wire = self.place, self.wire
        o = 1 - p.c
        wire.got(self.ref(b, p.y, p.x, o, j), self.sem("c", b, j), p.core)
        wire.got(self.ref(b, p.y, 1 - p.x, o, j), self.sem("cx", b, j), p.core)
        wire.got(self.ref(b, 1 - p.y, p.x, o, j), self.sem("cy", b, j), p.core)
        wire.got(self.ref(b, 1 - p.y, 1 - p.x, o, j, 0), self.sem("ca", b, j), p.core)
        wire.got(self.ref(b, 1 - p.y, 1 - p.x, o, j, 1), self.sem("cb", b, j), p.core)


class Scatter:
    def __init__(self, wire, place, grad, bufs, out, first):
        self.wire, self.place, self.grad, self.out, self.first = wire, place, grad, out, first
        self.SB, self.CR, self.DR, self.NR, self.ZR, self.R = bufs
        self.rows = self.SB.shape[3]
        self.piece = self.rows // PIECES
        self.half = self.piece // 2
        count = 2 * PIECES
        self.core = wire.take(8)
        self.sems = {k: wire.take(count) for k in ("da", "db", "xa", "xb", "ya", "yb", "u", "v", "d")}
        self.sent = []

    def sem(self, kind, b, j):
        return self.sems[kind] + b * PIECES + j

    def block(self, b, y, x, c, j=0, size=None):
        start = self.rows * ((b * 2 + y) * 4 + x * 2 + c) + j * self.piece
        return self.grad.at[pl.ds(many(start, 16), self.rows if size is None else size)]

    def give(self, ready):
        p = self.place
        while len(self.sent) < 8 and (2 * len(self.sent) + 2) * self.rows <= ready:
            i = len(self.sent)
            b, y, x = i // 4, i // 2 % 2, i % 2
            src = self.block(b, y, x, 1 - p.c)
            self.sent.append(self.wire.put(src, self.CR.at[b, y, x], p.core, self.core + i))

    def given(self):
        self.wire.left(self.sent)

    def take(self, b, y, x):
        self.wire.got(self.CR.at[b, y, x], self.core + b * 4 + y * 2 + x, self.place.core)

    def span(self, j, h=None):
        if h is None:
            return pl.ds(j * self.piece, self.piece)
        return pl.ds(j * self.piece + h * self.half, self.half)

    def add_core(self, b, y, x, j):
        mine = self.block(b, y, x, self.place.c, j, self.piece)
        v = mine[...].astype(F32) + self.CR[b, y, x, self.span(j)].astype(F32)
        self.SB[b, y, x, self.span(j)] = v.astype(BF16)

    def add_pass(self, b, y, x, j, h):
        at = self.span(j, h)
        v = self.SB[b, y, x, at].astype(F32) + self.DR[b, h, pl.ds(j * self.half, self.half)].astype(F32)
        self.SB[b, y, x, at] = v.astype(BF16)

    def add_plane(self, b, j):
        p, at = self.place, self.span(j)
        self.R[b, at] = (self.SB[b, p.y, p.x, at].astype(F32) + self.NR[b, 0, at].astype(F32)
                         + self.NR[b, 1, at].astype(F32))

    def back(self, b, j):
        at = self.span(j)
        self.SB[b, self.place.y, self.place.x, at] = self.R[b, at].astype(BF16)

    def add_far(self, b, j):
        at = self.span(j)
        self.R[b, at] += self.ZR[b, 0, at].astype(F32)

    def final(self, b, j):
        at = self.span(j)
        self.out[at] = self.R[b, at] + (self.ZR[b, 0, at].astype(F32) + self.ZR[b, 1, at].astype(F32))

    def step(self, k, b, j):
        p, wire = self.place, self.wire
        y, x = p.y, p.x
        owner = self.first + b
        far, mid = (0, 1) if self.first == 2 else (3, 2)
        if k == 0:
            self.add_core(b, 1 - y, 1 - x, j)
            at = pl.ds(j * self.half, self.half)
            src = self.SB.at[b, 1 - y, 1 - x]
            wire.put(src.at[self.span(j, 0)], self.DR.at[b, 0, at], p.yn, self.sem("da", b, j))
            wire.put(src.at[self.span(j, 1)], self.DR.at[b, 1, at], p.xn, self.sem("db", b, j))
        elif k == 1:
            self.add_core(b, y, 1 - x, j)
            at = self.span(j, 1)
            wire.put(self.SB.at[b, y, 1 - x, at], self.NR.at[b, 0, at], p.xn, self.sem("xb", b, j))
            self.add_core(b, 1 - y, x, j)
            at = self.span(j, 0)
            wire.put(self.SB.at[b, 1 - y, x, at], self.NR.at[b, 1, at], p.yn, self.sem("ya", b, j))
            self.add_core(b, y, x, j)
        elif k == 2:
            got = pl.ds(j * self.half, self.half)
            wire.got(self.DR.at[b, 0, got], self.sem("da", b, j), p.yn)
            self.add_pass(b, y, 1 - x, j, 0)
            at = self.span(j, 0)
            wire.put(self.SB.at[b, y, 1 - x, at], self.NR.at[b, 0, at], p.xn, self.sem("xa", b, j))
            wire.got(self.DR.at[b, 1, got], self.sem("db", b, j), p.xn)
            self.add_pass(b, 1 - y, x, j, 1)
            at = self.span(j, 1)
            wire.put(self.SB.at[b, 1 - y, x, at], self.NR.at[b, 1, at], p.yn, self.sem("yb", b, j))
        elif k == 3:
            wire.got(self.NR.at[b, 0, self.span(j, 1)], self.sem("xb", b, j), p.xn)
            wire.got(self.NR.at[b, 1, self.span(j, 0)], self.sem("ya", b, j), p.yn)
            wire.got(self.NR.at[b, 0, self.span(j, 0)], self.sem("xa", b, j), p.xn)
            wire.got(self.NR.at[b, 1, self.span(j, 1)], self.sem("yb", b, j), p.yn)
            self.add_plane(b, j)
            at = self.span(j)
            mine = self.SB.at[b, y, x, at]
            side = 2 * self.first + 1 - owner
            wire.when((p.z == far) | (p.z == side), lambda: self.back(b, j))
            wire.put(mine, self.ZR.at[b, 0, at], p.pair, self.sem("u", b, j), when=p.z == far)
            wire.put(mine, self.ZR.at[b, 1, at], p.pair, self.sem("d", b, j), when=p.z == side)
        elif k == 4:
            at = self.span(j)

            def on():
                self.add_far(b, j)
                self.back(b, j)

            wire.got(self.ZR.at[b, 0, at], self.sem("u", b, j), p.pair, when=p.z == mid)
            wire.when(p.z == mid, on)
            peer = p.at(owner, y, x, p.c)
            wire.put(self.SB.at[b, y, x, at], self.ZR.at[b, 0, at], peer, self.sem("v", b, j), when=p.z == mid)
        else:
            at = self.span(j)
            wire.got(self.ZR.at[b, 0, at], self.sem("v", b, j), p.gate, when=p.z == owner)
            wire.got(self.ZR.at[b, 1, at], self.sem("d", b, j), p.pair, when=p.z == owner)
            wire.when(p.z == owner, lambda: self.final(b, j))

    @staticmethod
    def scratch(rows, channels):
        return [
            ((2, 2, 2, rows, channels), BF16),
            ((2, 2, 2, rows, channels), BF16),
            ((2, 2, rows // 2, channels), BF16),
            ((2, 2, rows, channels), BF16),
            ((2, 2, rows, channels), BF16),
            ((2, rows, channels), F32),
        ]


class Halo:
    def __init__(self, wire, place, buf):
        self.wire, self.place, self.buf = wire, place, buf
        self.up, self.down = wire.take(), wire.take()

    def send(self):
        p, wire, buf = self.place, self.wire, self.buf
        last = buf.shape[0] - 1
        wire.put(buf.at[1], buf.at[last], (p.img, p.sp - 1), self.up, when=p.sp > 0)
        wire.put(buf.at[last - 1], buf.at[0], (p.img, p.sp + 1), self.down, when=p.sp < 3)
        wire.when(p.sp == 0, lambda: self.clear(0))
        wire.when(p.sp == 3, lambda: self.clear(last))

    def clear(self, row):
        self.buf[row] = jnp.zeros_like(self.buf[row])

    def wait(self):
        p, wire, buf = self.place, self.wire, self.buf
        last = buf.shape[0] - 1
        wire.got(buf.at[last], self.up, (p.img, p.sp + 1), when=p.sp < 3)
        wire.got(buf.at[0], self.down, (p.img, p.sp - 1), when=p.sp > 0)


class BandSum:
    def __init__(self, wire, place, slots):
        self.wire, self.place, self.slots = wire, place, slots
        self.first = wire.take(3)

    def send(self):
        p = self.place
        for k in range(3):
            self.wire.put(self.slots.at[p.sp], self.slots.at[p.sp], p.sps[k], self.first + k)

    def wait(self):
        for k in range(3):
            slot = self.slots.at[self.place.sp_off(3 - k)]
            self.wire.got(slot, self.first + k, self.place.sps[k])

    def total(self):
        return self.slots[0] + self.slots[1] + self.slots[2] + self.slots[3]


class SplitSum:
    def __init__(self, wire, place, slots):
        self.wire, self.place, self.slots = wire, place, slots
        self.sems = wire.take(3)

    def send(self):
        p, s = self.place, self.slots
        self.wire.put(s.at[1 - p.c], s.at[2], p.core, self.sems)

    def add(self, out, a, b):
        self.slots[out] = self.slots[a] + self.slots[b]

    def cross(self):
        p, s = self.place, self.slots
        self.wire.got(s.at[2], self.sems, p.core)
        self.add(3, p.c, 2)
        self.wire.put(s.at[3], s.at[4], p.xn, self.sems + 1)

    def back(self):
        p, s = self.place, self.slots
        self.wire.got(s.at[4], self.sems + 1, p.xn)
        self.add(5 + p.c, 3, 4)
        self.wire.put(s.at[5 + p.c], s.at[5 + p.c], p.core, self.sems + 2)

    def wait(self):
        self.wire.got(self.slots.at[6 - self.place.c], self.sems + 2, self.place.core)


class Spread:
    def __init__(self, wire, place, slots):
        self.wire, self.place, self.slots = wire, place, slots
        self.z, self.y = wire.take(3), wire.take()

    def send(self):
        p = self.place
        for k in range(3):
            self.wire.put(self.slots.at[p.y, p.z], self.slots.at[p.y, p.z], p.zs[k], self.z + k)

    def turn(self):
        p = self.place
        for k in range(3):
            self.wire.got(self.slots.at[p.y, p.z_off(3 - k)], self.z + k, p.zs[k])
        self.wire.put(self.slots.at[p.y], self.slots.at[p.y], p.yn, self.y)

    def wait(self):
        self.wire.got(self.slots.at[1 - self.place.y], self.y, self.place.yn)


def group_matrix(channels, across):
    per = channels // NORM_GROUPS
    shape = (channels, 128) if across else (128, channels)
    c = lax.broadcasted_iota(jnp.int32, shape, 0 if across else 1)
    g = lax.broadcasted_iota(jnp.int32, shape, 1 if across else 0)
    return (lax.div(c, per) == g).astype(F32)


def exact_dot(a, b):
    return jnp.dot(a, b, precision=HIGHEST, preferred_element_type=F32)


def sigmoid(v):
    return 0.5 * jnp.tanh(0.5 * v) + 0.5


def slope(v):
    s = sigmoid(v)
    return s * (1.0 + v * (1.0 - s))


def thirds(v):
    high = v.astype(BF16)
    v = v - high.astype(F32)
    mid = v.astype(BF16)
    return high, mid, (v - mid.astype(F32)).astype(BF16)


def fold(v):
    return jnp.sum(v.reshape(v.shape[0] // 8, 8, v.shape[1]), axis=0)


def plus(total, v):
    return v if total is None else total + v


class Step:
    def __init__(self, place, wire, refs, image_total):
        self.__dict__.update(refs)
        self.inverse = 1.0 / image_total
        self.p, self.w = place, wire
        self.images, self.rows_full, self.side_full, self.channels = self.IMG.shape
        self.rim, _, self.side, _ = self.PO.shape
        self.rows = self.rim - 2
        self.per = self.channels // NORM_GROUPS
        self.tiles = self.channels // 128
        shard = self.cw.shape[0]
        self.kernel_rows = 16 * shard
        self.g = Gather(wire, place, self.W, shard)
        self.r2 = Scatter(wire, place, self.DW, [self.__dict__["RA%d" % i] for i in range(6)], self.RES, 2)
        self.r1 = Scatter(wire, place, self.DW, [self.__dict__["RB%d" % i] for i in range(6)], self.RES, 0)
        self.halo_p = Halo(wire, place, self.PO)
        self.halo_g = Halo(wire, place, self.G)
        self.halo_a = Halo(wire, place, self.A2)
        self.halo_b = Halo(wire, place, self.GB)
        self.aff_img = Spread(wire, place, self.AFS.at[place.sp])
        self.aff_sp = BandSum(wire, place, self.AFS)
        self.sum1 = BandSum(wire, place, self.ST1)
        self.sum2 = BandSum(wire, place, self.ST2)
        self.sum3 = BandSum(wire, place, self.ST3)
        self.sum4 = BandSum(wire, place, self.ST4)
        self.psum = SplitSum(wire, place, self.PS)
        self.proj = SplitSum(wire, place, self.PX)
        self.esum = SplitSum(wire, place, self.PE)
        self.asum = BandSum(wire, place, self.AFR)
        self.spread_g = Spread(wire, place, self.GPA)
        self.spread_e = Spread(wire, place, self.EA)
        self.ez = wire.take(3), wire.take(4)
        self.afy = wire.take()
        self.afz = wire.take(3)


    def loop(self, body, first=0, last=None):
        def one(n, _):
            body(n)
            return 0

        lax.fori_loop(first, self.images if last is None else last, one, 0)

    def width(self, n, r):
        return jnp.where(self.p.sp * self.rows_full + r < self.ext[0, n], self.ext[1, n], 0)

    def half_width(self, n, r):
        inside = self.p.sp * self.rows + r < lax.div(self.ext[0, n], 2)
        return jnp.where(inside, lax.div(self.ext[1, n], 2), 0)

    def cols(self, side):
        return lax.broadcasted_iota(jnp.int32, (side, self.channels), 0)

    def at(self, k, n):
        return self.AB[k, pl.ds(n, 1)]

    def clear_sums(self):
        self.SS[...] = jnp.zeros_like(self.SS)

    def add_sums(self, n, s, q):
        self.SS[pl.ds(n, 1)] += jnp.sum(s, axis=0, keepdims=True)
        self.SS[pl.ds(n + 16, 1)] += jnp.sum(q, axis=0, keepdims=True)

    def eslot(self, z, y):
        rows = self.ew.shape[0]
        start = ((z * 2 + y) * 4 + self.p.sp) * rows
        return self.EZ.at[pl.ds(many(start, 32), rows)]


    def load(self):
        self.copies = [
            pltpu.make_async_copy(self.img, self.IMG, self.lsem.at[0]),
            pltpu.make_async_copy(self.cot, self.COT, self.lsem.at[1]),
        ]
        late = ((self.cm_in, self.CM), (self.ce_in, self.CE), (self.em_in, self.EM), (self.ee_in, self.EE))
        for i, (src, dst) in enumerate(late):
            self.copies.append(pltpu.make_async_copy(src, dst, self.lsem.at[2 + i]))
        for copy in self.copies:
            copy.start()

    def loaded(self, k):
        self.copies[k].wait()

    def own_weights(self):
        p = self.p
        rows = self.cw.shape[0]
        self.W[pl.ds(many(rows * (p.img * 4 + p.sp), 16), rows)] = self.cw[...].astype(BF16)
        low = self.aff[...].astype(BF16).astype(F32)
        self.AFS[p.sp, p.y, p.z] = jnp.broadcast_to(low, (8, 128))

    def own_embedding(self):
        p = self.p
        rows = self.ew.shape[0]
        zero = jnp.zeros((rows, self.EZ.shape[1]), BF16)
        for i in range(8):
            for sp in p.sps:
                self.EZ[pl.ds(many((i * 4 + sp[1]) * rows, 32), rows)] = zero
        self.EZ[pl.ds(many((p.img * 4 + p.sp) * rows, 32), rows)] = self.ew[...].astype(BF16)
        self.EP[...] = jnp.zeros_like(self.EP)
        self.EP[pl.ds(0, self.images)] = self.emb[...].astype(F32)
        e = self.EP[...]
        self.EA[p.y, p.z] = (e * sigmoid(e)).astype(BF16)

    def counts(self):
        self.CNT[...] = jnp.ones_like(self.CNT)

        def one(n):
            h, w = self.ext[0, n], self.ext[1, n]
            for i, number in enumerate((h * w, lax.div(h, 2) * lax.div(w, 2))):
                number = jnp.full((1, self.channels), number * self.per, jnp.int32)
                self.CNT[i, pl.ds(n, 1)] = number.astype(F32)

        self.loop(one)


    def ez_send(self):
        p = self.p
        for k in range(3):
            self.w.put(self.eslot(p.z, p.y), self.eslot(p.z, p.y), p.zs[k], self.ez[0] + k)

    def ez_turn(self):
        p = self.p
        for k in range(3):
            self.w.got(self.eslot(p.z_off(3 - k), p.y), self.ez[0] + k, p.zs[k])
        for k in range(4):
            self.w.put(self.eslot(k, p.y), self.eslot(k, p.y), p.yn, self.ez[1] + k)

    def ez_wait(self):
        for k in range(4):
            self.w.got(self.eslot(k, 1 - self.p.y), self.ez[1] + k, self.p.yn)

    def project(self):
        v = jnp.dot(self.EA[self.p.y, self.p.z], self.EZ[...], preferred_element_type=F32)
        self.PX[0] = v[:, : self.channels]
        self.PX[1] = v[:, self.channels :]


    def stats_one(self, first, last):
        col = self.cols(self.side_full)

        def one(n):
            s = q = None
            for r in range(self.rows_full):
                v = jnp.where(col < self.width(n, r), self.IMG[n, r].astype(F32), 0.0)
                s, q = plus(s, fold(v)), plus(q, fold(v * v))
            self.add_sums(n, s, q)

        self.loop(one, first, last)

    def stats_one_end(self):
        self.ST1[self.p.sp] = exact_dot(self.SS[...], group_matrix(self.channels, True))

    def affine_rows(self):
        for s in range(4):
            for y in range(2):
                for z in range(4):
                    self.AFF[pl.ds(z * 2 + y, 1), pl.ds(s * 128, 128)] = self.AFS[s, y, z, 0:1]

    def moments(self, total, count, mean_ref, inv_ref):
        total = exact_dot(total, group_matrix(self.channels, False))
        mean = total[:16] / count
        inv = lax.rsqrt(total[16:] / count - mean * mean + EPSILON)
        mean_ref[...] = mean
        inv_ref[...] = inv
        return mean, inv

    def norm_one(self):
        mean, inv = self.moments(self.sum1.total(), self.CNT[0], self.MI.at[0], self.MI.at[1])
        self.AB[0] = inv * self.AFF[0:1]
        self.AB[1] = self.AFF[1:2] - mean * self.AB[0]

    def pool(self, hrs, first=0, last=None):
        col = self.cols(self.side_full)

        def one(n):
            for i, hr in enumerate(hrs):
                act = raw = None
                for k in range(2):
                    r = 2 * hr + k
                    inside = col < self.width(n, r)
                    u = self.IMG[n, r].astype(F32)
                    v = u * self.at(0, n) + self.at(1, n)
                    act = plus(act, jnp.where(inside, v * sigmoid(v), 0.0))
                    raw = plus(raw, jnp.where(inside, u, 0.0))
                for t in range(self.tiles):
                    lanes = slice(t * 128, t * 128 + 128)
                    self.T[i, t] = act[:, lanes]
                    self.T[i + 2, t] = raw[:, lanes]
            even, odd = pl.ds(0, self.side, stride=2), pl.ds(1, self.side, stride=2)
            for i, hr in enumerate(hrs):
                for t in range(self.tiles):
                    lanes = pl.ds(t * 128, 128)
                    v = self.T[i, t, even] + self.T[i, t, odd]
                    self.PO[hr + 1, n, :, lanes] = (v * 0.25).astype(BF16)
                    v = self.T[i + 2, t, even] + self.T[i + 2, t, odd]
                    self.SKIP[hr, n, :, lanes] = v * 0.25

        self.loop(one, first, last)


    def shift(self, src, rows):
        col = self.cols(self.side)

        def one(n):
            for r in rows:
                v = src[r, n].astype(F32)
                self.X[0, r, n] = jnp.where(col > 0, pltpu.roll(v, 1, 0), 0.0).astype(BF16)
                v = jnp.where(col < self.side - 1, pltpu.roll(v, self.side - 1, 0), 0.0)
                self.X[1, r, n] = v.astype(BF16)

        self.loop(one)

    def conv(self, center, base, row, back):
        count = self.ACC.shape[0]
        size = count * self.images * self.side
        total = None
        for a in range(3):
            for b in range(3):
                da, db = (2 - a, 2 - b) if back else (a, b)
                src = center if db == 1 else self.X.at[0 if db == 0 else 1]
                left = src[pl.ds(row + da, count)].reshape(size, self.channels)
                tap = self.W[pl.ds(base + (3 * a + b) * self.channels, self.channels)]
                dims = (((1,), (1 if back else 0,)), ((), ()))
                total = plus(total, lax.dot_general(left, tap, dims, preferred_element_type=F32))
        self.ACC[...] = total.reshape(self.ACC.shape)

    def tap_grad(self, center, grads, t):
        a, b = divmod(t, 3)
        size = self.rows * self.images * self.side
        src = center if b == 1 else self.X.at[0 if b == 0 else 1]
        left = src[pl.ds(a, self.rows)].reshape(size, self.channels)
        right = grads[pl.ds(1, self.rows)].reshape(size, self.channels)
        self.DW[pl.ds(t * self.channels, self.channels)] = lax.dot_general(
            left, right, (((0,), (0,)), ((), ())), preferred_element_type=F32
        ).astype(BF16)

    def mask_cot(self):
        col = self.cols(self.side)
        self.C2[...] = jnp.zeros_like(self.C2)

        def one(n):
            total = None
            for r in range(self.rows):
                v = jnp.where(col < self.half_width(n, r), self.COT[n, r].astype(F32), 0.0)
                self.G[r + 1, n] = v.astype(BF16)
                total = plus(total, fold(v))
            self.C2[...] += total

        self.loop(one)

    def inner_conv(self, row):
        col = self.cols(self.side)
        self.conv(self.PO, 0, row, False)

        def one(n):
            s = q = None
            for r in range(self.ACC.shape[0]):
                v = self.ACC[r, n] + self.AFF[2:3]
                v = jnp.where(col < self.half_width(n, row + r), v, 0.0).astype(BF16)
                self.INN[row + r, n] = v
                v = v.astype(F32)
                s, q = plus(s, fold(v)), plus(q, fold(v * v))
            self.add_sums(n, s, q)

        self.loop(one)


    def stats_two(self):
        self.ST2[self.p.sp] = exact_dot(self.SS[...], group_matrix(self.channels, True))

    def norm_two(self):
        self.MI[4] = self.PX[5] + (self.AFF[3:4] + 1.0)
        self.MI[5] = self.PX[6] + self.AFF[4:5]
        mean, inv = self.moments(self.sum2.total(), self.CNT[1], self.MI.at[2], self.MI.at[3])
        self.AB[2] = inv
        self.AB[3] = -mean * inv
        self.AB[4] = self.AFF[5:6] * self.MI[4]
        self.AB[5] = self.AFF[6:7] * self.MI[4] + self.MI[5]

    def xhat_two(self, r, n):
        return self.INN[r, n].astype(F32) * self.at(2, n) + self.at(3, n)

    def activate(self, rs):
        col = self.cols(self.side)

        def one(n):
            for r in rs:
                v = self.xhat_two(r, n) * self.at(4, n) + self.at(5, n)
                v = jnp.where(col < self.half_width(n, r), v * sigmoid(v), 0.0)
                self.A2[r + 1, n] = v.astype(BF16)

        self.loop(one)

    def mixed_grad(self, row):
        col = self.cols(self.side)
        self.conv(self.G, self.kernel_rows, row, True)

        def one(n):
            s = q = None
            for r in range(self.ACC.shape[0]):
                v = self.ACC[r, n].astype(BF16).astype(F32)
                xhat = self.xhat_two(row + r, n)
                mixed = xhat * self.at(4, n) + self.at(5, n)
                v = jnp.where(col < self.half_width(n, row + r), v * slope(mixed), 0.0)
                self.GM[row + r, n] = v
                s, q = plus(s, fold(v)), plus(q, fold(v * xhat))
            self.add_sums(n, s, q)

        self.loop(one)

    def sums_two_back(self):
        p1, p2 = self.SS[:16], self.SS[16:]
        self.PS[0] = p1
        self.PS[1] = p2
        both = jnp.concatenate([p1 * self.AB[4], p2 * self.AB[4]], axis=0)
        self.ST3[self.p.sp] = exact_dot(both, group_matrix(self.channels, True))
        scale = self.MI[4]
        self.AFP[0:3] = jnp.zeros_like(self.AFP[0:3])
        self.AFP[3:4] = jnp.sum(self.AFF[5:6] * p2 + self.AFF[6:7] * p1, axis=0, keepdims=True)
        self.AFP[4:5] = jnp.sum(p1, axis=0, keepdims=True)
        self.AFP[5:6] = jnp.sum(scale * p2, axis=0, keepdims=True)
        self.AFP[6:7] = jnp.sum(scale * p1, axis=0, keepdims=True)
        self.AFP[7:8] = jnp.sum(self.C2[...], axis=0, keepdims=True)

    def output(self, row):
        col = self.cols(self.side)
        self.conv(self.A2, self.kernel_rows, row, False)

        def one(n):
            for r in range(self.ACC.shape[0]):
                v = self.ACC[r, n] + self.AFF[7:8]
                v = jnp.where(col < self.half_width(n, row + r), v, 0.0)
                self.OUTV[n, row + r] = (self.SKIP[row + r, n] + v).astype(BF16)

        self.loop(one)

    def project_grad(self):
        p1, p2 = self.PS[5], self.PS[6]
        self.GPA[self.p.y, self.p.z, 0] = self.AFF[5:6] * p2 + self.AFF[6:7] * p1
        self.GPA[self.p.y, self.p.z, 1] = p1

    def norm_two_back(self):
        spread = exact_dot(self.sum3.total(), group_matrix(self.channels, False))
        inv = self.AB[2]
        self.AB[6] = inv * self.AB[4]
        self.AB[7] = inv * (spread[:16] / self.CNT[1])
        self.AB[8] = inv * (spread[16:] / self.CNT[1])
        self.C1[...] = jnp.zeros_like(self.C1)

    def inner_grad(self, rs):
        col = self.cols(self.side)

        def one(n):
            total = None
            for r in rs:
                v = self.GM[r, n] * self.at(6, n) - self.at(7, n) - self.xhat_two(r, n) * self.at(8, n)
                v = jnp.where(col < self.half_width(n, r), v, 0.0).astype(BF16)
                self.GB[r + 1, n] = v
                total = plus(total, fold(v.astype(F32)))
            self.C1[...] += total

        self.loop(one)


    def embedding_part(self):
        y, z = self.p.y, self.p.z
        gp = jnp.concatenate([self.GPA[y, z, 0], self.GPA[y, z, 1]], axis=1)
        gp = jnp.concatenate(thirds(gp), axis=0)
        v = lax.dot_general(gp, self.EZ[...], (((1,), (1,)), ((), ())), preferred_element_type=F32)
        v = v[:16] + v[16:32] + v[32:]
        self.PE[0] = v[:, : self.channels]
        self.PE[1] = v[:, self.channels :]

    def embedding_grad(self):
        v = jnp.concatenate([self.PE[5], self.PE[6]], axis=1)[: self.images]
        self.ge[...] = v * slope(self.EP[pl.ds(0, self.images)])

    def embedding_weights(self):
        lanes = pl.ds(many(self.p.img * 128, 128), 128)
        total = [None, None]
        for y in range(2):
            left = self.EA[y, :, :, lanes].reshape(64, 128)
            for i in range(2):
                for w in thirds(self.GPA[y, :, i].reshape(64, self.channels)):
                    v = lax.dot_general(left, w, (((0,), (0,)), ((), ())), preferred_element_type=F32)
                    total[i] = plus(total[i], v)
        for i in range(2):
            self.EW[:, pl.ds(i * self.channels, self.channels)] = total[i]
        self.ewg[...] = self.EW[pl.ds(many(self.p.sp * 32, 32), 32)]


    def doubled(self, value, slot):
        for t in range(self.tiles):
            v = value[:, t * 128 : t * 128 + 128]
            self.T[slot, t, pl.ds(0, self.side, stride=2)] = v
            self.T[slot, t, pl.ds(1, self.side, stride=2)] = v
        return jnp.concatenate([self.T[slot, t] for t in range(self.tiles)], axis=1)

    def prepare_one_back(self):
        self.AB[2] = self.MI[1]
        self.AB[3] = -self.MI[0] * self.MI[1]
        self.clear_sums()

    def norm_one_grad(self, n, r, grad):
        v = self.IMG[n, r].astype(F32)
        xhat = v * self.at(2, n) + self.at(3, n)
        v = v * self.at(0, n) + self.at(1, n)
        return xhat, jnp.where(self.cols(self.side_full) < self.width(n, r), grad * slope(v), 0.0)

    def pooled_conv(self, row):
        self.conv(self.GB, 0, row, True)
        self.GM[pl.ds(row, self.ACC.shape[0])] = self.ACC[...] * 0.25

    def pooled_grad(self, row, first=0, last=None):
        def one(n):
            s = q = None
            for r in range(self.ACC.shape[0]):
                grad = self.doubled(self.GM[row + r, n], r)
                for k in range(2):
                    xhat, v = self.norm_one_grad(n, 2 * (row + r) + k, grad)
                    s, q = plus(s, fold(v)), plus(q, fold(v * xhat))
            self.add_sums(n, s, q)

        self.loop(one, first, last)

    def sums_one_back(self):
        self.AFP[0:1] = jnp.sum(self.SS[16:32], axis=0, keepdims=True)
        self.AFP[1:2] = jnp.sum(self.SS[0:16], axis=0, keepdims=True)
        self.AFP[2:3] = jnp.sum(self.C1[...], axis=0, keepdims=True)
        self.AFR[self.p.sp] = self.AFP[...]
        self.ST4[self.p.sp] = exact_dot(self.SS[...] * self.AFF[0:1], group_matrix(self.channels, True))

    def affine_y(self):
        self.AFY[0] = self.asum.total()
        self.w.put(self.AFY.at[0], self.AFY.at[1], self.p.yn, self.afy)

    def affine_z(self):
        self.w.got(self.AFY.at[1], self.afy, self.p.yn)
        self.AFZ[self.p.z] = self.AFY[0] + self.AFY[1]
        for k in range(3):
            self.w.put(self.AFZ.at[self.p.z], self.AFZ.at[self.p.z], self.p.zs[k], self.afz + k)

    def affine_done(self):
        for k in range(3):
            self.w.got(self.AFZ.at[self.p.z_off(3 - k)], self.afz + k, self.p.zs[k])
        self.AFP[...] = self.AFZ[0] + self.AFZ[1] + self.AFZ[2] + self.AFZ[3]
        tile = self.AFP[:, pl.ds(many(self.p.sp * 128, 128), 128)]
        line = lax.broadcasted_iota(jnp.int32, tile.shape, 0) == self.p.img
        self.ag[...] = jnp.sum(jnp.where(line, tile, 0.0), axis=0, keepdims=True)

    def norm_one_back(self):
        total = exact_dot(self.sum4.total(), group_matrix(self.channels, False))
        self.AB[4] = self.MI[1] * self.AFF[0:1]
        self.AB[5] = self.MI[1] * (total[:16] / self.CNT[0])
        self.AB[6] = self.MI[1] * (total[16:] / self.CNT[0])

    def image_grad(self, first, last):
        col = self.cols(self.side_full)

        def one(n):
            for hr in range(self.rows):
                grad = self.doubled(self.GM[hr, n], 0)
                cell = self.doubled(self.COT[n, hr].astype(F32) * 0.25, 1)
                for k in range(2):
                    r = 2 * hr + k
                    xhat, v = self.norm_one_grad(n, r, grad)
                    v = v * self.at(4, n) - self.at(5, n) - xhat * self.at(6, n) + cell
                    self.IMG[n, r] = jnp.where(col < self.width(n, r), v, 0.0).astype(BF16)

        self.loop(one, first, last)


    def update(self, weight, moment, average, total, new_weight, new_moment, new_average):
        mean = total[...] * self.inverse
        m = MOMENTUM * moment[...] + mean
        w = weight[...] - LEARN_RATE * (mean + MOMENTUM * m)
        new_weight[...] = w
        new_moment[...] = m
        new_average[...] = EMA_DECAY * average[...] + (1.0 - EMA_DECAY) * w

    def update_small(self):
        self.loaded(4)
        self.loaded(5)
        self.update(self.ew, self.EM, self.EE, self.ewg, self.new, self.nem, self.nee)
        self.update(self.aff, self.am, self.ae, self.ag, self.naw, self.nam, self.nae)

    def update_conv(self):
        self.loaded(2)
        self.loaded(3)
        step = 32
        arrays = (self.cw, self.CM, self.CE, self.RES, self.ncw, self.ncm, self.nce)

        def piece(i, _):
            at = pl.ds(pl.multiple_of(i * step, step), step)
            self.update(*(r.at[at] for r in arrays))
            return 0

        lax.fori_loop(0, self.cw.shape[0] // step, piece, 0)


def mix(works, ticks):
    done = 0
    for i, work in enumerate(works):
        work()
        upto = (i + 1) * len(ticks) // len(works)
        for tick in ticks[done:upto]:
            tick()
        done = upto
    for tick in ticks[done:]:
        tick()


def pairs(*lists):
    return [item for group in zip(*lists) for item in group]


def schedule(s):
    p, g, z = s.p, s.g, s.p.z
    pieces = list(range(PIECES))
    edge, middle = (0, s.rows - 1), range(1, s.rows - 1)
    inside, outside = range(1, s.rim - 1), (0, s.rim - 1)
    lead = choose(z == 0, 0, 1)
    other = choose(z == 1, 0, 1)
    tail = 1 - lead
    lead_two = choose(z == 3, 3, 2)
    tail_two = 5 - lead_two
    n = s.images

    def come(b, j, when=None):
        def run():
            g.arrive(b, j, when)
            g.own(b, j, when)

        return run

    def call(method, *args):
        return lambda: method(*args)

    s.load()
    s.own_weights()
    s.w.greet(p)
    s.aff_img.send()
    for j in pieces:
        g.along(z, j, z < 2, z > 0)
        g.own(z, j, z < 2)
    s.own_embedding()
    s.counts()
    s.clear_sums()
    s.loaded(0)
    s.stats_one(0, n // 2)
    come(other, 0)()
    s.stats_one(n // 2, n)
    s.stats_one_end()
    s.sum1.send()
    s.aff_img.turn()
    come(other, 1)()
    s.aff_img.wait()
    s.aff_sp.send()
    for j in pieces[2:]:
        come(other, j)()
    for j in pieces:
        g.arrive(3, j, z == 2)
    g.turn(lead, 0)
    s.sum1.wait()
    s.aff_sp.wait()
    for j in pieces:
        g.arrive(2, j, z == 1)
    s.affine_rows()
    s.norm_one()
    works = [call(s.pool, edge, i, i + 4) for i in range(0, n, 4)] + [s.halo_p.send, s.ez_send]
    works += [call(s.pool, middle, i, i + 4) for i in range(0, n, 4)]
    works += [call(s.loaded, 1), s.mask_cot, call(s.shift, s.PO, inside)]
    ticks = pairs([come(0, j, z >= 2) for j in pieces], [call(g.turn, lead, j) for j in pieces[1:]] + [lambda: None])
    ticks += pairs([call(g.last, lead, j) for j in pieces], [call(g.turn, tail, j) for j in pieces])
    mix(works, ticks)

    def next_two(j):
        g.arrive(2, j, z == 0)
        g.own(lead_two, j)

    def tail_two_on(j):
        g.arrive(tail_two, j, (z == 0) | (z == 3))
        g.own(tail_two, j)

    for j in pieces:
        g.arrive(3, j, z == 1)
    next_two(0)
    s.ez_turn()
    next_two(1)
    for j in pieces:
        g.last(tail, j)
    s.halo_p.wait()
    s.shift(s.PO, outside)
    for j in pieces:
        g.along(2, j, z == 2, z > 3)
        g.done(lead, j)
        g.done(tail, j)
    next_two(2)
    s.clear_sums()
    s.spread_e.send()
    s.inner_conv(0)
    s.ez_wait()
    s.project()
    s.proj.send()
    g.turn(lead_two, 0)
    s.proj.cross()
    g.turn(lead_two, 1)
    s.inner_conv(2)
    s.proj.back()
    s.stats_two()
    s.sum2.send()
    tail_two_on(0)
    s.proj.wait()
    s.sum2.wait()
    s.norm_two()
    s.activate(edge)
    s.halo_a.send()
    s.activate(middle)
    for j in pieces[1:]:
        tail_two_on(j)
    g.turn(lead_two, 2)
    s.shift(s.A2, inside)
    s.halo_g.send()
    s.spread_e.turn()
    s.halo_a.wait()
    s.shift(s.A2, outside)

    def tap_two(t):
        s.tap_grad(s.A2, s.G, t)
        s.r2.give((t + 1) * s.channels)

    ticks = [call(g.last, lead_two, j) for j in pieces]
    ticks = pairs(ticks, [call(g.turn, tail_two, j) for j in pieces]) + [call(g.last, tail_two, j) for j in pieces]
    mix([call(tap_two, t) for t in range(9)], ticks)

    def steps(scatter, k, b):
        return [call(scatter.step, k, b, j) for j in pieces]

    def run(calls):
        for item in calls:
            item()

    def taken(scatter, b):
        for yy in range(2):
            for xx in range(2):
                scatter.take(b, yy, xx)

    s.shift(s.G, inside)
    taken(s.r2, 1)
    run(steps(s.r2, 0, 1))
    s.halo_g.wait()
    s.shift(s.G, outside)
    s.clear_sums()
    run(steps(s.r2, 1, 1))
    for j in pieces:
        g.done(2, j)
        g.done(3, j)
    s.mixed_grad(0)
    run(steps(s.r2, 2, 1))
    s.mixed_grad(2)
    s.sums_two_back()
    s.sum3.send()
    taken(s.r2, 0)
    run(steps(s.r2, 0, 0))
    s.psum.send()
    s.shift(s.PO, range(s.rim))
    s.sum3.wait()
    s.norm_two_back()
    s.inner_grad(edge)
    s.halo_b.send()
    s.inner_grad(middle)
    run(steps(s.r2, 1, 0))
    s.psum.cross()
    s.r2.given()

    def tap_one(t):
        s.tap_grad(s.PO, s.GB, t)
        s.r1.give((t + 1) * s.channels)

    ticks = steps(s.r2, 2, 0) + steps(s.r2, 3, 1) + [s.psum.back]
    mix([call(tap_one, t) for t in range(9)], ticks)

    taken(s.r1, 0)
    run(steps(s.r1, 0, 0))
    run(steps(s.r1, 1, 0))
    s.halo_b.wait()
    s.shift(s.GB, range(s.rim))
    s.prepare_one_back()
    s.psum.wait()
    s.project_grad()
    s.spread_g.send()
    s.pooled_conv(0)
    run(steps(s.r2, 4, 1))
    taken(s.r1, 1)
    run(steps(s.r1, 0, 1))
    s.pooled_conv(2)
    run(steps(s.r1, 2, 0))
    run(steps(s.r2, 3, 0))
    run(steps(s.r1, 1, 1))
    s.pooled_grad(0)
    s.spread_g.turn()
    run(steps(s.r2, 4, 0))
    s.pooled_grad(2)
    s.sums_one_back()
    s.sum4.send()
    s.asum.send()
    run(steps(s.r1, 2, 1))
    run(steps(s.r1, 3, 0))
    s.embedding_part()
    s.esum.send()
    s.sum4.wait()
    s.norm_one_back()
    s.asum.wait()
    s.affine_y()
    s.esum.cross()
    s.shift(s.A2, range(s.rim))
    s.output(0)
    run(steps(s.r1, 4, 0))
    run(steps(s.r1, 3, 1))
    s.affine_z()
    s.esum.back()
    s.output(2)
    run(steps(s.r1, 4, 1))
    s.image_grad(0, n // 3)
    run(steps(s.r2, 5, 1))
    s.image_grad(n // 3, 2 * (n // 3))
    run(steps(s.r2, 5, 0))
    s.image_grad(2 * (n // 3), n)
    s.spread_g.wait()
    s.spread_e.wait()
    s.embedding_weights()
    run(steps(s.r1, 5, 0))
    s.affine_done()
    s.esum.wait()
    s.embedding_grad()
    s.update_small()
    run(steps(s.r1, 5, 1))
    s.update_conv()
    s.w.close()


def whole_kernel(names, image_total, *refs):
    refs = dict(zip(names, refs))
    place = Place(lax.axis_index("img"), lax.axis_index("sp"))
    wire = Wire(refs.pop("ssem"), refs.pop("rsem"))
    schedule(Step(place, wire, refs, image_total))


def shapes(images, cotangent, conv_w, emb_w):
    n, rows_full, side_full, c = images
    _, rows, side, _ = cotangent
    shard = conv_w[0]
    rim = (rows + 2, n, side, c)
    band = (rows, n, side, c)
    out = dict(
        RES=(conv_w, F32), ag=((1, 128), F32), ewg=(emb_w, F32),
        CM=(conv_w, F32), CE=(conv_w, F32), EM=(emb_w, F32), EE=(emb_w, F32),
        COT=(cotangent, BF16), W=((32 * shard, c), BF16), EZ=((emb_w[1], emb_w[1]), BF16),
        PO=(rim, BF16), G=(rim, BF16), A2=(rim, BF16), GB=(rim, BF16), X=((2,) + rim, BF16),
        INN=(band, BF16), SKIP=(band, F32), GM=(band, F32), ACC=((2,) + band[1:], F32),
        DW=((16 * shard, c), BF16), T=((4, c // 128, side_full, 128), F32), SS=((32, c), F32),
        CNT=((2, 16, c), F32), MI=((6, 16, c), F32), AB=((9, 16, c), F32), AFF=((8, c), F32), AFP=((8, c), F32),
        C1=((8, c), F32), C2=((8, c), F32), AFS=((4, 2, 4, 8, 128), F32), AFR=((4, 8, c), F32),
        AFY=((2, 8, c), F32), AFZ=((4, 8, c), F32), EP=((16, 2 * c), F32), EA=((2, 4, 16, 2 * c), BF16),
        GPA=((2, 4, 2, 16, c), F32), EW=((128, 2 * c), F32), PX=((7, 16, c), F32), PE=((7, 16, c), F32),
        ST1=((4, 32, 128), F32), ST2=((4, 32, 128), F32), ST3=((4, 32, 128), F32), PS=((7, 16, c), F32), ST4=((4, 32, 128), F32),
    )
    for k in "AB":
        for i, v in enumerate(Scatter.scratch(shard, c)):
            out["R%s%d" % (k, i)] = v
    return out


WIRES = 360
VM = pl.BlockSpec(memory_space=pltpu.VMEM)
ANY = pl.BlockSpec(memory_space=pl.ANY)
SM = pl.BlockSpec(memory_space=pltpu.SMEM)


def place_kernel(*refs):
    count = len(refs) // 2
    sem = refs[-1]
    copies = [pltpu.make_async_copy(refs[i], refs[count + i], sem.at[i]) for i in range(count)]
    for copy in copies:
        copy.start()
    for copy in copies:
        copy.wait()


def local_kernels(image_total, images, embedding, extent, cotangent, conv_w, emb_w, affine,
                  conv_mom, emb_mom, affine_mom, conv_ema, emb_ema, affine_ema):
    line = lambda v: v.reshape(1, 128)
    scratch = shapes(images.shape, cotangent.shape, conv_w.shape, emb_w.shape)
    inputs = ["ext", "img", "cot", "emb", "cw", "ew", "aff", "cm_in", "ce_in", "em_in", "ee_in", "am", "ae"]
    trio = [(conv_w.shape, F32), (emb_w.shape, F32), ((1, 128), F32)]
    outputs = {"OUTV": (cotangent.shape, BF16), "IMG": (images.shape, BF16), "ge": (embedding.shape, F32)}
    outputs |= zip(("ncw", "new", "naw", "ncm", "nem", "nam", "nce", "nee", "nae"), trio * 3)
    names = inputs + list(outputs) + list(scratch) + ["lsem", "ssem", "rsem"]
    held = pl.pallas_call(
        lambda *refs: whole_kernel(names, image_total, *refs),
        name="resblock_step",
        out_shape=[pltpu.VMEM(*v) for v in outputs.values()],
        in_specs=[SM, ANY, ANY, VM, VM, VM, VM] + [ANY] * 4 + [VM] * 2,
        out_specs=[VM] * len(outputs),
        scratch_shapes=[pltpu.VMEM(*v) for v in scratch.values()]
        + [pltpu.SemaphoreType.DMA((8,)), pltpu.SemaphoreType.DMA((WIRES,)), pltpu.SemaphoreType.DMA((WIRES,))],
        compiler_params=pltpu.CompilerParams(
            collective_id=1, has_side_effects=True, vmem_limit_bytes=54 << 20
        ),
    )(extent.T, images, cotangent, embedding, conv_w, emb_w, line(affine), conv_mom, conv_ema, emb_mom, emb_ema,
      line(affine_mom), line(affine_ema))
    held = [pltpu.with_memory_space_constraint(v, pltpu.VMEM) for v in held]
    count = len(held)
    out, gi, ge, ncw, new, naw, ncm, nem, nam, nce, nee, nae = pl.pallas_call(
        place_kernel,
        name="place",
        out_shape=[jax.ShapeDtypeStruct(v.shape, v.dtype) for v in held],
        in_specs=[VM] * count,
        out_specs=[ANY] * count,
        scratch_shapes=[pltpu.SemaphoreType.DMA((count,))],
        compiler_params=pltpu.CompilerParams(vmem_limit_bytes=16 << 20),
    )(*held)
    flat = lambda v: v.reshape(-1)
    return out, gi, ge, ncw, new, flat(naw), ncm, nem, flat(nam), nce, nee, flat(nae)


def padded_2(cells, sides, width):
    for axis, dim in sides:
        count = lax.axis_size(axis)
        ends = count - 1
        head = lax.slice_in_dim(cells, 0, width, axis=dim)
        tail = lax.slice_in_dim(cells, cells.shape[dim] - width, cells.shape[dim], axis=dim)
        cells = jnp.concatenate(
            [
                lax.ppermute(tail, axis, [(i, (i + 1) % count) for i in range(ends)]),
                cells,
                lax.ppermute(head, axis, [((i + 1) % count, i) for i in range(ends)]),
            ],
            axis=dim,
        )
    return cells


def band_mask(extent, first_row, band_rows, band_cols, halved):
    height = extent[:, 0]
    breadth = extent[:, 1]
    if halved:
        height = height // 2
        breadth = breadth // 2
    row_ids = first_row + jnp.arange(band_rows, dtype=jnp.int32)
    col_ids = jnp.arange(band_cols, dtype=jnp.int32)
    inside = (row_ids[None, :, None] < height[:, None, None]) & (
        col_ids[None, None, :] < breadth[:, None, None]
    )
    return inside.astype(jnp.float32)[..., None]


def per_group_sums(values, group_count):
    shaped = values.reshape(values.shape[:3] + (group_count, values.shape[3] // group_count))
    return jnp.sum(shaped, axis=(1, 2, 4))


def spread_to_channels(stat, channels_per_group):
    return jnp.repeat(stat, channels_per_group, axis=1)[:, None, None, :]


def pool_cells(values):
    shaped = values.reshape(
        values.shape[0], values.shape[1] // 2, 2, values.shape[2] // 2, 2, values.shape[3]
    )
    return jnp.sum(shaped, axis=(2, 4)) * 0.25


def spread_cells(values):
    return jnp.repeat(jnp.repeat(values, 2, axis=1), 2, axis=2) * 0.25


def silu_slope(values):
    sigma = jax.nn.sigmoid(values)
    return sigma * (1.0 + values * (1.0 - sigma))


def conv_rows(padded, kernel, layout):
    return lax.conv_general_dilated(
        padded,
        kernel,
        (1, 1),
        ((0, 0), (1, 1)),
        dimension_numbers=("NHWC", "HWIO", layout),
        preferred_element_type=jnp.float32,
    )


def conv_back(padded, kernel):
    return lax.conv_general_dilated(
        padded,
        jnp.flip(kernel, (0, 1)),
        (1, 1),
        ((0, 0), (1, 1)),
        dimension_numbers=("NHWC", "HWOI", "NHWC"),
        preferred_element_type=jnp.float32,
    )


def tap_grads(padded, grads):
    window = jnp.pad(padded, ((0, 0), (0, 0), (1, 1), (0, 0)))
    band_rows = grads.shape[1]
    band_cols = grads.shape[2]
    kernel_rows = []
    for tap_row in range(3):
        taps = []
        for tap_col in range(3):
            source = window[:, tap_row : tap_row + band_rows, tap_col : tap_col + band_cols, :]
            taps.append(
                jnp.einsum("brci,brco->io", source, grads, preferred_element_type=jnp.float32)
            )
        kernel_rows.append(jnp.stack(taps))
    return jnp.stack(kernel_rows)


def band_rim(values):
    return padded_2(values, (("sp", 1),), 1)


def other_rim(values):
    return padded_2(values, (("sp", 1),), 1)


def update(weight, moment, average, total, image_total):
    grad_mean = total / image_total
    new_moment = MOMENTUM * moment + grad_mean
    new_weight = weight - LEARN_RATE * (grad_mean + MOMENTUM * new_moment)
    new_average = EMA_DECAY * average + (1.0 - EMA_DECAY) * new_weight
    return (new_weight, new_moment, new_average)


def local(
    images,
    embedding,
    extent,
    cotangent,
    conv_w,
    emb_w,
    affine,
    conv_mom,
    emb_mom,
    affine_mom,
    conv_ema,
    emb_ema,
    affine_ema,
):
    conv_all, emb_all, affine_all = (
        lax.all_gather(conv_w.astype(jnp.bfloat16), ("img", "sp"), axis=0, tiled=True),
        lax.all_gather(emb_w.astype(jnp.bfloat16), ("img", "sp"), axis=0, tiled=True),
        lax.all_gather(affine.astype(jnp.bfloat16), ("img", "sp"), axis=0, tiled=True),
    )
    channels = conv_all.shape[1]
    first_kernel = conv_all[: 9 * channels].reshape(3, 3, channels, channels)
    second_kernel = conv_all[9 * channels :].reshape(3, 3, channels, channels)
    parameters = affine_all.astype(jnp.float32).reshape(8, channels)
    image_count = images.shape[0]
    band_rows = images.shape[1]
    grid_side = images.shape[2]
    half_band = band_rows // 2
    half_side = grid_side // 2
    sp_size = lax.axis_size("sp")
    sp_index = lax.axis_index("sp")
    local_channels = channels // sp_size
    first_channels = sp_index * local_channels
    channels_per_group = channels // NORM_GROUPS
    groups_on_device = local_channels // channels_per_group
    full_mask = band_mask(extent, sp_index * band_rows, band_rows, grid_side, False)
    half_mask = band_mask(extent, sp_index * half_band, half_band, half_side, True)
    whole_half = band_mask(extent, 0, half_side, half_side, True)
    full_pixel_count = (extent[:, 0] * extent[:, 1] * channels_per_group).astype(jnp.float32)[
        :, None
    ]
    half_pixel_count = (extent[:, 0] // 2 * (extent[:, 1] // 2) * channels_per_group).astype(
        jnp.float32
    )[:, None]
    masked_values = images.astype(jnp.float32) * full_mask
    sums_one, squares_one = lax.psum(
        (
            per_group_sums(masked_values, NORM_GROUPS),
            per_group_sums(masked_values * masked_values, NORM_GROUPS),
        ),
        "sp",
    )
    first_group_mean = sums_one / full_pixel_count
    first_inverse_deviation = lax.rsqrt(
        squares_one / full_pixel_count - first_group_mean * first_group_mean + EPSILON
    )
    first_normalized = (
        masked_values - spread_to_channels(first_group_mean, channels_per_group)
    ) * spread_to_channels(first_inverse_deviation, channels_per_group)
    first_group_norm = first_normalized * parameters[0] + parameters[1]
    pooled = pool_cells(jax.nn.silu(first_group_norm) * full_mask).astype(jnp.bfloat16)
    skip_path = pool_cells(masked_values)
    pooled_rim = band_rim(pooled)
    inner_act = ((conv_rows(pooled_rim, first_kernel, "NHWC") + parameters[2]) * half_mask).astype(
        jnp.bfloat16
    )
    emb_act = jax.nn.silu(embedding.astype(jnp.float32)).astype(jnp.bfloat16)

    def place_local(values):
        return lax.dynamic_update_slice_in_dim(
            jnp.zeros((channels,), jnp.float32), values, first_channels, 0
        )

    inner_channels = lax.all_to_all(
        inner_act, "sp", split_axis=3, concat_axis=1, tiled=True
    ).astype(jnp.float32)
    emb_cols = jnp.concatenate(
        [
            lax.dynamic_slice_in_dim(emb_all, first_channels, local_channels, 1),
            lax.dynamic_slice_in_dim(emb_all, channels + first_channels, local_channels, 1),
        ],
        axis=1,
    )
    emb_bias = jnp.concatenate(
        [
            lax.dynamic_slice_in_dim(parameters[3], first_channels, local_channels, 0),
            lax.dynamic_slice_in_dim(parameters[4], first_channels, local_channels, 0),
        ]
    )
    emb_proj = jnp.dot(emb_act, emb_cols, preferred_element_type=jnp.float32) + emb_bias
    ada_scale = 1.0 + emb_proj[:, :local_channels][:, None, None, :]
    ada_shift = emb_proj[:, local_channels:][:, None, None, :]
    sums_two = per_group_sums(inner_channels, groups_on_device)
    squares_two = per_group_sums(inner_channels * inner_channels, groups_on_device)
    second_group_mean = sums_two / half_pixel_count
    second_inverse_deviation = lax.rsqrt(
        squares_two / half_pixel_count - second_group_mean * second_group_mean + EPSILON
    )
    second_normalized = (
        inner_channels - spread_to_channels(second_group_mean, channels_per_group)
    ) * spread_to_channels(second_inverse_deviation, channels_per_group)
    second_gain = lax.dynamic_slice_in_dim(parameters[5], first_channels, local_channels, 0)
    second_group_norm = second_normalized * second_gain + lax.dynamic_slice_in_dim(
        parameters[6], first_channels, local_channels, 0
    )
    mixed_act = second_group_norm * ada_scale + ada_shift
    act_two = (jax.nn.silu(mixed_act) * whole_half).astype(jnp.bfloat16)
    act_rows = lax.all_to_all(act_two, "sp", split_axis=1, concat_axis=3, tiled=True)
    act_rim = other_rim(act_rows)
    branch = conv_rows(act_rim, second_kernel, "NHWC") + parameters[7]
    output = (skip_path + branch * half_mask).astype(jnp.bfloat16)
    grad_branch = (cotangent.astype(jnp.float32) * half_mask).astype(jnp.bfloat16)
    bias_two_grad = jnp.sum(grad_branch.astype(jnp.float32), axis=(0, 1, 2))
    grad_rim = other_rim(grad_branch)
    kernel_two = tap_grads(act_rim, grad_branch)
    grad_band = conv_back(grad_rim, second_kernel).astype(jnp.bfloat16)
    grad_act = lax.all_to_all(grad_band, "sp", split_axis=3, concat_axis=1, tiled=True)
    grad_mixed = grad_act.astype(jnp.float32) * whole_half * silu_slope(mixed_act)
    grad_proj = jnp.concatenate(
        [jnp.sum(grad_mixed * second_group_norm, axis=(1, 2)), jnp.sum(grad_mixed, axis=(1, 2))],
        axis=1,
    )
    second_norm_gradient = grad_mixed * ada_scale
    second_gain_gradient = jnp.sum(second_norm_gradient * second_normalized, axis=(0, 1, 2))
    bias_norm_two_grad = jnp.sum(second_norm_gradient, axis=(0, 1, 2))
    second_normalized_gradient = second_norm_gradient * second_gain
    first_total_count = (
        per_group_sums(second_normalized_gradient, groups_on_device) / half_pixel_count
    )
    second_total_count = (
        per_group_sums(second_normalized_gradient * second_normalized, groups_on_device)
        / half_pixel_count
    )
    grad_inner = spread_to_channels(second_inverse_deviation, channels_per_group) * (
        second_normalized_gradient
        - spread_to_channels(first_total_count, channels_per_group)
        - second_normalized * spread_to_channels(second_total_count, channels_per_group)
    )
    grad_inner_rows = lax.all_to_all(
        grad_inner.astype(jnp.bfloat16), "sp", split_axis=1, concat_axis=3, tiled=True
    )
    emb_grad_cols = jnp.einsum(
        "be,bk->ek", emb_act.astype(jnp.float32), grad_proj, precision=HIGHEST
    )
    emb_kernel = jnp.zeros((emb_all.shape[0], 2 * channels), jnp.float32)
    emb_kernel = lax.dynamic_update_slice_in_dim(
        emb_kernel, emb_grad_cols[:, :local_channels], first_channels, 1
    )
    emb_kernel = lax.dynamic_update_slice_in_dim(
        emb_kernel, emb_grad_cols[:, local_channels:], channels + first_channels, 1
    )
    silu_part = jnp.einsum("bk,ek->be", grad_proj, emb_cols.astype(jnp.float32), precision=HIGHEST)
    silu_grad = lax.psum(silu_part.astype(jnp.bfloat16), "sp").astype(jnp.float32)
    emb_bias_grad = jnp.sum(grad_proj, axis=0)
    coarse_affine = [
        place_local(emb_bias_grad[:local_channels]),
        place_local(emb_bias_grad[local_channels:]),
        place_local(second_gain_gradient),
        place_local(bias_norm_two_grad),
    ]
    grad_embedding = silu_grad * silu_slope(embedding.astype(jnp.float32))
    grad_raw = (grad_inner_rows.astype(jnp.float32) * half_mask).astype(jnp.bfloat16)
    bias_one_grad = jnp.sum(grad_raw.astype(jnp.float32), axis=(0, 1, 2))
    kernel_one = tap_grads(pooled_rim, grad_raw)
    grad_pooled = conv_back(band_rim(grad_raw), first_kernel)
    first_norm_gradient = spread_cells(grad_pooled) * full_mask * silu_slope(first_group_norm)
    first_gain_gradient = jnp.sum(first_norm_gradient * first_normalized, axis=(0, 1, 2))
    bias_norm_one_grad = jnp.sum(first_norm_gradient, axis=(0, 1, 2))
    first_normalized_gradient = first_norm_gradient * parameters[0]
    back_one, second_backward = lax.psum(
        (
            per_group_sums(first_normalized_gradient, NORM_GROUPS),
            per_group_sums(first_normalized_gradient * first_normalized, NORM_GROUPS),
        ),
        "sp",
    )
    grad_masked = spread_to_channels(first_inverse_deviation, channels_per_group) * (
        first_normalized_gradient
        - spread_to_channels(back_one / full_pixel_count, channels_per_group)
        - first_normalized
        * spread_to_channels(second_backward / full_pixel_count, channels_per_group)
    ) + spread_cells(cotangent.astype(jnp.float32))
    grad_images = (grad_masked * full_mask).astype(jnp.bfloat16)
    affine_grad = jnp.concatenate(
        [first_gain_gradient, bias_norm_one_grad, bias_one_grad] + coarse_affine + [bias_two_grad]
    )
    conv_grad = jnp.concatenate(
        [kernel_one.reshape(9 * channels, channels), kernel_two.reshape(9 * channels, channels)]
    )
    conv_sum, emb_sum, affine_sum = (
        lax.psum_scatter(conv_grad, ("img", "sp"), scatter_dimension=0, tiled=True),
        lax.psum_scatter(emb_kernel, ("img", "sp"), scatter_dimension=0, tiled=True),
        lax.psum_scatter(affine_grad, ("img", "sp"), scatter_dimension=0, tiled=True),
    )
    image_total = float(image_count * lax.axis_size("img"))
    new_conv, conv_moment, conv_average = update(conv_w, conv_mom, conv_ema, conv_sum, image_total)
    new_emb, emb_moment, emb_average = update(emb_w, emb_mom, emb_ema, emb_sum, image_total)
    new_affine, affine_moment, affine_average = update(
        affine, affine_mom, affine_ema, affine_sum, image_total
    )
    return (
        output,
        grad_images,
        grad_embedding,
        new_conv,
        new_emb,
        new_affine,
        conv_moment,
        emb_moment,
        affine_moment,
        conv_average,
        emb_average,
        affine_average,
    )


def kernels_or_ops(images, embedding, extent, cotangent, conv_w, *rest):
    arrays = (images, embedding, extent, cotangent, conv_w) + rest
    n, rows, side, channels = images.shape
    if n > 16 or rows != 8 or side != 32 or channels != 512 or conv_w.shape[0] != 288:
        return local(*arrays)
    return local_kernels(float(n * lax.axis_size("img")), *arrays)


def solution(mesh):
    in_specs = (
        P("img", "sp", None, None),
        P("img", None),
        P("img", None),
        P("img", "sp", None, None),
        P(("img", "sp"), None),
        P(("img", "sp"), None),
        P(("img", "sp")),
        P(("img", "sp"), None),
        P(("img", "sp"), None),
        P(("img", "sp")),
        P(("img", "sp"), None),
        P(("img", "sp"), None),
        P(("img", "sp")),
    )
    out_specs = (
        P("img", "sp", None, None),
        P("img", "sp", None, None),
        P("img", None),
        P(("img", "sp"), None),
        P(("img", "sp"), None),
        P(("img", "sp")),
        P(("img", "sp"), None),
        P(("img", "sp"), None),
        P(("img", "sp")),
        P(("img", "sp"), None),
        P(("img", "sp"), None),
        P(("img", "sp")),
    )
    fits = dict(mesh.shape) == {"img": 8, "sp": 4}
    return jax.shard_map(kernels_or_ops if fits else local, mesh=mesh, in_specs=in_specs, out_specs=out_specs, check_vma=False)
```

```python
import jax
import jax.numpy as jnp
from jax import lax
from jax.experimental import pallas as pl
from jax.experimental.pallas import tpu as pltpu
from jax.sharding import PartitionSpec as P

F32 = jnp.float32
BF16 = jnp.bfloat16
HIGHEST = lax.Precision.HIGHEST
MESH = pl.DeviceIdType.MESH
EPSILON = 1e-05
LEARN_RATE = 0.03
MOMENTUM = 0.5
EMA_DECAY = 0.5
NORM_GROUPS = 32
PIECES = 3


def choose(cond, a, b):
    if isinstance(cond, bool):
        return a if cond else b
    return jnp.where(cond, a, b)


def many(value, factor):
    return value if isinstance(value, int) else pl.multiple_of(value, factor)


class Place:
    def __init__(self, img, sp):
        self.img, self.sp = img, sp
        if isinstance(img, int):
            self.z, self.y, self.x, self.c = img // 2, img % 2, sp // 2, sp % 2
        else:
            self.z, self.y = lax.div(img, 2), lax.rem(img, 2)
            self.x, self.c = lax.div(sp, 2), lax.rem(sp, 2)
        z, y, x, c = self.z, self.y, self.x, self.c
        self.core = self.at(z, y, x, 1 - c)
        self.xn = self.at(z, y, 1 - x, c)
        self.yn = self.at(z, 1 - y, x, c)
        self.up, self.down = self.at(z + 1, y, x, c), self.at(z - 1, y, x, c)
        self.pair = self.at(z + 1 - 2 * self.odd(z), y, x, c)
        self.gate = self.at(choose(z < 2, 2, 1), y, x, c)
        self.zs = [self.at(self.z_off(k), y, x, c) for k in (1, 2, 3)]
        self.sps = [(img, self.sp_off(k)) for k in (1, 2, 3)]

    def at(self, z, y, x, c):
        return (z * 2 + y, x * 2 + c)

    def odd(self, value):
        return value % 2 if isinstance(value, int) else lax.rem(value, 2)

    def off(self, value, k):
        value = value + k
        return value % 4 if isinstance(value, int) else lax.rem(value, 4)

    def z_off(self, k):
        return self.off(self.z, k)

    def sp_off(self, k):
        return self.off(self.sp, k)


class Wire:
    def __init__(self, ssem, rsem):
        self.ssem, self.rsem = ssem, rsem
        self.used = 0
        self.open = []

    def take(self, count=1):
        first = self.used
        self.used += count
        return first

    def when(self, cond, do):
        if cond is None:
            do()
        else:
            pl.when(cond)(do)

    def copy(self, src, dst, peer, send, recv):
        return pltpu.make_async_remote_copy(
            src_ref=src, dst_ref=dst, send_sem=self.ssem.at[send], recv_sem=self.rsem.at[recv],
            device_id=peer, device_id_type=MESH,
        )

    def put(self, src, dst, peer, send, recv=None, when=None):
        def make():
            return self.copy(src, dst, peer, send, send if recv is None else recv)

        self.when(when, lambda: make().start())
        self.open.append((make, when))
        return self.open[-1]

    def left(self, copies):
        for make, when in copies:
            self.when(when, lambda make=make: make().wait_send())
        gone = [id(copy) for copy in copies]
        self.open = [item for item in self.open if id(item) not in gone]

    def got(self, ref, recv, peer, when=None):
        self.when(when, lambda: self.copy(ref, ref, peer, recv, recv).wait_recv())

    def started(self):
        return list(self.open)

    def close(self):
        self.left(self.started())

    def greet(self, place):
        barrier = pltpu.get_barrier_semaphore()
        peers = place.sps + [place.yn] + place.zs
        for peer in peers:
            pl.semaphore_signal(barrier, inc=1, device_id=peer, device_id_type=MESH)
        pl.semaphore_wait(barrier, len(peers))


class Gather:
    def __init__(self, wire, place, W, rows):
        self.wire, self.place, self.W, self.rows = wire, place, W, rows
        self.piece = rows // PIECES
        count = 4 * PIECES
        self.sems = {k: wire.take(count) for k in ("z", "u", "d", "x", "y", "xy", "yx")}
        self.core = wire.take(16)

    def sem(self, kind, b, j):
        return self.sems[kind] + b * PIECES + j

    def ref(self, b, y, x, c, j, half=None):
        start = self.rows * ((b * 2 + y) * 4 + x * 2 + c) + j * self.piece
        size = self.piece
        if half is not None:
            size = size // 2
            start = start + half * size
        return self.W.at[pl.ds(many(start, 16), size)]

    def along(self, b, j, up, down):
        p, wire = self.place, self.wire
        r = self.ref(b, p.y, p.x, p.c, j)
        wire.put(r, r, p.up, self.sem("u", b, j), self.sem("z", b, j), when=up)
        wire.put(r, r, p.down, self.sem("d", b, j), self.sem("z", b, j), when=down)

    def arrive(self, b, j, when=None):
        p = self.place
        both = lambda cond: cond if when is None else when & cond
        self.wire.got(self.ref(b, p.y, p.x, p.c, j), self.sem("z", b, j), p.up, when=when)
        self.along(b, j, both((b < p.z) & (p.z < 3)), both((b > p.z) & (p.z > 0)))

    def block(self, b, y, x, c):
        start = self.rows * ((b * 2 + y) * 4 + x * 2 + c)
        return self.W.at[pl.ds(many(start, 16), self.rows)]

    def share(self, b, k, y, x, when=None):
        r = self.block(b, y, x, self.place.c)
        self.wire.put(r, r, self.place.core, self.core + b * 4 + k, when=when)

    def own(self, b, j, when=None):
        p, wire = self.place, self.wire
        r = self.ref(b, p.y, p.x, p.c, j)
        wire.put(r, r, p.xn, self.sem("x", b, j), when=when)
        wire.put(r, r, p.yn, self.sem("y", b, j), when=when)
        if j == PIECES - 1:
            self.share(b, 0, p.y, p.x, when)

    def turn(self, b, j):
        p, wire = self.place, self.wire
        wire.got(self.ref(b, p.y, 1 - p.x, p.c, j), self.sem("x", b, j), p.xn)
        h = self.ref(b, p.y, 1 - p.x, p.c, j, 0)
        wire.put(h, h, p.yn, self.sem("xy", b, j))
        wire.got(self.ref(b, 1 - p.y, p.x, p.c, j), self.sem("y", b, j), p.yn)
        h = self.ref(b, 1 - p.y, p.x, p.c, j, 1)
        wire.put(h, h, p.xn, self.sem("yx", b, j))
        if j == PIECES - 1:
            self.share(b, 1, p.y, 1 - p.x)
            self.share(b, 2, 1 - p.y, p.x)

    def last(self, b, j):
        p, wire = self.place, self.wire
        wire.got(self.ref(b, 1 - p.y, 1 - p.x, p.c, j, 0), self.sem("xy", b, j), p.yn)
        wire.got(self.ref(b, 1 - p.y, 1 - p.x, p.c, j, 1), self.sem("yx", b, j), p.xn)
        if j == PIECES - 1:
            self.share(b, 3, 1 - p.y, 1 - p.x)

    def done(self, b):
        p, wire = self.place, self.wire
        for k, y, x in ((0, p.y, p.x), (1, p.y, 1 - p.x), (2, 1 - p.y, p.x), (3, 1 - p.y, 1 - p.x)):
            wire.got(self.block(b, y, x, 1 - p.c), self.core + b * 4 + k, p.core)


class Scatter:
    def __init__(self, wire, place, grad, bufs, out, first):
        self.wire, self.place, self.grad, self.out, self.first = wire, place, grad, out, first
        self.SB, self.CR, self.DR, self.NR, self.ZR, self.R = bufs
        self.rows = self.SB.shape[3]
        self.piece = self.rows // PIECES
        self.half = self.piece // 2
        count = 2 * PIECES
        self.core = wire.take(8)
        self.sems = {k: wire.take(count) for k in ("da", "db", "xa", "xb", "ya", "yb", "u", "v", "d")}
        self.sent = []

    def sem(self, kind, b, j):
        return self.sems[kind] + b * PIECES + j

    def block(self, b, y, x, c, j=0, size=None):
        start = self.rows * ((b * 2 + y) * 4 + x * 2 + c) + j * self.piece
        return self.grad.at[pl.ds(many(start, 16), self.rows if size is None else size)]

    def give(self, ready):
        p = self.place
        while len(self.sent) < 8 and (2 * len(self.sent) + 2) * self.rows <= ready:
            i = len(self.sent)
            b, y, x = i // 4, i // 2 % 2, i % 2
            src = self.block(b, y, x, 1 - p.c)
            self.sent.append(self.wire.put(src, self.CR.at[b, y, x], p.core, self.core + i))

    def given(self):
        self.wire.left(self.sent)

    def take(self, b, y, x):
        self.wire.got(self.CR.at[b, y, x], self.core + b * 4 + y * 2 + x, self.place.core)

    def span(self, j, h=None):
        if h is None:
            return pl.ds(j * self.piece, self.piece)
        return pl.ds(j * self.piece + h * self.half, self.half)

    def add_core(self, b, y, x, j):
        mine = self.block(b, y, x, self.place.c, j, self.piece)
        v = mine[...].astype(F32) + self.CR[b, y, x, self.span(j)].astype(F32)
        self.SB[b, y, x, self.span(j)] = v.astype(BF16)

    def add_pass(self, b, y, x, j, h):
        at = self.span(j, h)
        v = self.SB[b, y, x, at].astype(F32) + self.DR[b, h, pl.ds(j * self.half, self.half)].astype(F32)
        self.SB[b, y, x, at] = v.astype(BF16)

    def add_plane(self, b, j):
        p, at = self.place, self.span(j)
        self.R[b, at] = (self.SB[b, p.y, p.x, at].astype(F32) + self.NR[b, 0, at].astype(F32)
                         + self.NR[b, 1, at].astype(F32))

    def back(self, b, j):
        at = self.span(j)
        self.SB[b, self.place.y, self.place.x, at] = self.R[b, at].astype(BF16)

    def add_far(self, b, j):
        at = self.span(j)
        self.R[b, at] += self.ZR[b, 0, at].astype(F32)

    def final(self, b, j):
        at = self.span(j)
        self.out[at] = self.R[b, at] + (self.ZR[b, 0, at].astype(F32) + self.ZR[b, 1, at].astype(F32))

    def step(self, k, b, j):
        p, wire = self.place, self.wire
        y, x = p.y, p.x
        owner = self.first + b
        far, mid = (0, 1) if self.first == 2 else (3, 2)
        if k == 0:
            self.add_core(b, 1 - y, 1 - x, j)
            at = pl.ds(j * self.half, self.half)
            src = self.SB.at[b, 1 - y, 1 - x]
            wire.put(src.at[self.span(j, 0)], self.DR.at[b, 0, at], p.yn, self.sem("da", b, j))
            wire.put(src.at[self.span(j, 1)], self.DR.at[b, 1, at], p.xn, self.sem("db", b, j))
        elif k == 1:
            self.add_core(b, y, 1 - x, j)
            at = self.span(j, 1)
            wire.put(self.SB.at[b, y, 1 - x, at], self.NR.at[b, 0, at], p.xn, self.sem("xb", b, j))
            self.add_core(b, 1 - y, x, j)
            at = self.span(j, 0)
            wire.put(self.SB.at[b, 1 - y, x, at], self.NR.at[b, 1, at], p.yn, self.sem("ya", b, j))
            self.add_core(b, y, x, j)
        elif k == 2:
            got = pl.ds(j * self.half, self.half)
            wire.got(self.DR.at[b, 0, got], self.sem("da", b, j), p.yn)
            self.add_pass(b, y, 1 - x, j, 0)
            at = self.span(j, 0)
            wire.put(self.SB.at[b, y, 1 - x, at], self.NR.at[b, 0, at], p.xn, self.sem("xa", b, j))
            wire.got(self.DR.at[b, 1, got], self.sem("db", b, j), p.xn)
            self.add_pass(b, 1 - y, x, j, 1)
            at = self.span(j, 1)
            wire.put(self.SB.at[b, 1 - y, x, at], self.NR.at[b, 1, at], p.yn, self.sem("yb", b, j))
        elif k == 3:
            wire.got(self.NR.at[b, 0, self.span(j, 1)], self.sem("xb", b, j), p.xn)
            wire.got(self.NR.at[b, 1, self.span(j, 0)], self.sem("ya", b, j), p.yn)
            wire.got(self.NR.at[b, 0, self.span(j, 0)], self.sem("xa", b, j), p.xn)
            wire.got(self.NR.at[b, 1, self.span(j, 1)], self.sem("yb", b, j), p.yn)
            self.add_plane(b, j)
            at = self.span(j)
            mine = self.SB.at[b, y, x, at]
            side = 2 * self.first + 1 - owner
            wire.when((p.z == far) | (p.z == side), lambda: self.back(b, j))
            wire.put(mine, self.ZR.at[b, 0, at], p.pair, self.sem("u", b, j), when=p.z == far)
            wire.put(mine, self.ZR.at[b, 1, at], p.pair, self.sem("d", b, j), when=p.z == side)
        elif k == 4:
            at = self.span(j)

            def on():
                self.add_far(b, j)
                self.back(b, j)

            wire.got(self.ZR.at[b, 0, at], self.sem("u", b, j), p.pair, when=p.z == mid)
            wire.when(p.z == mid, on)
            peer = p.at(owner, y, x, p.c)
            wire.put(self.SB.at[b, y, x, at], self.ZR.at[b, 0, at], peer, self.sem("v", b, j), when=p.z == mid)
        else:
            at = self.span(j)
            wire.got(self.ZR.at[b, 0, at], self.sem("v", b, j), p.gate, when=p.z == owner)
            wire.got(self.ZR.at[b, 1, at], self.sem("d", b, j), p.pair, when=p.z == owner)
            wire.when(p.z == owner, lambda: self.final(b, j))

    @staticmethod
    def scratch(rows, channels):
        return [
            ((2, 2, 2, rows, channels), BF16),
            ((2, 2, 2, rows, channels), BF16),
            ((2, 2, rows // 2, channels), BF16),
            ((2, 2, rows, channels), BF16),
            ((2, 2, rows, channels), BF16),
            ((2, rows, channels), F32),
        ]


class Halo:
    def __init__(self, wire, place, buf):
        self.wire, self.place, self.buf = wire, place, buf
        self.up, self.down = wire.take(), wire.take()

    def send(self):
        p, wire, buf = self.place, self.wire, self.buf
        last = buf.shape[0] - 1
        wire.put(buf.at[1], buf.at[last], (p.img, p.sp - 1), self.up, when=p.sp > 0)
        wire.put(buf.at[last - 1], buf.at[0], (p.img, p.sp + 1), self.down, when=p.sp < 3)
        wire.when(p.sp == 0, lambda: self.clear(0))
        wire.when(p.sp == 3, lambda: self.clear(last))

    def clear(self, row):
        self.buf[row] = jnp.zeros_like(self.buf[row])

    def wait(self):
        p, wire, buf = self.place, self.wire, self.buf
        last = buf.shape[0] - 1
        wire.got(buf.at[last], self.up, (p.img, p.sp + 1), when=p.sp < 3)
        wire.got(buf.at[0], self.down, (p.img, p.sp - 1), when=p.sp > 0)


class BandSum:
    def __init__(self, wire, place, slots):
        self.wire, self.place, self.slots = wire, place, slots
        self.first = wire.take(3)

    def send(self):
        p = self.place
        for k in range(3):
            self.wire.put(self.slots.at[p.sp], self.slots.at[p.sp], p.sps[k], self.first + k)

    def wait(self):
        for k in range(3):
            slot = self.slots.at[self.place.sp_off(3 - k)]
            self.wire.got(slot, self.first + k, self.place.sps[k])

    def total(self):
        return self.slots[0] + self.slots[1] + self.slots[2] + self.slots[3]


class SplitSum:
    def __init__(self, wire, place, slots):
        self.wire, self.place, self.slots = wire, place, slots
        self.sems = wire.take(3)

    def send(self):
        p, s = self.place, self.slots
        self.wire.put(s.at[1 - p.c], s.at[2], p.core, self.sems)

    def add(self, out, a, b):
        self.slots[out] = self.slots[a] + self.slots[b]

    def cross(self):
        p, s = self.place, self.slots
        self.wire.got(s.at[2], self.sems, p.core)
        self.add(3, p.c, 2)
        self.wire.put(s.at[3], s.at[4], p.xn, self.sems + 1)

    def back(self):
        p, s = self.place, self.slots
        self.wire.got(s.at[4], self.sems + 1, p.xn)
        self.add(5 + p.c, 3, 4)
        self.wire.put(s.at[5 + p.c], s.at[5 + p.c], p.core, self.sems + 2)

    def wait(self):
        self.wire.got(self.slots.at[6 - self.place.c], self.sems + 2, self.place.core)


class Spread:
    def __init__(self, wire, place, slots):
        self.wire, self.place, self.slots = wire, place, slots
        self.z, self.y = wire.take(3), wire.take()

    def send(self):
        p = self.place
        for k in range(3):
            self.wire.put(self.slots.at[p.y, p.z], self.slots.at[p.y, p.z], p.zs[k], self.z + k)

    def turn(self):
        p = self.place
        for k in range(3):
            self.wire.got(self.slots.at[p.y, p.z_off(3 - k)], self.z + k, p.zs[k])
        self.wire.put(self.slots.at[p.y], self.slots.at[p.y], p.yn, self.y)

    def wait(self):
        self.wire.got(self.slots.at[1 - self.place.y], self.y, self.place.yn)


def group_matrix(channels, across, first):
    per = channels // NORM_GROUPS
    shape = (channels, 128) if across else (128, channels)
    c = lax.broadcasted_iota(jnp.int32, shape, 0 if across else 1)
    g = lax.broadcasted_iota(jnp.int32, shape, 1 if across else 0)
    return (lax.div(c, per) + first == g).astype(F32)


def exact_dot(a, b):
    return jnp.dot(a, b, precision=HIGHEST, preferred_element_type=F32)


def pack(a, b):
    return exact_dot(a, group_matrix(a.shape[1], True, 0)) + exact_dot(b, group_matrix(b.shape[1], True, 64))


def unpack(v, channels):
    return exact_dot(v, group_matrix(channels, False, 0)), exact_dot(v, group_matrix(channels, False, 64))


def sigmoid(v):
    return 0.5 * jnp.tanh(0.5 * v) + 0.5


def slope(v):
    s = sigmoid(v)
    return s * (1.0 + v * (1.0 - s))


def thirds(v):
    high = v.astype(BF16)
    v = v - high.astype(F32)
    mid = v.astype(BF16)
    return high, mid, (v - mid.astype(F32)).astype(BF16)


def fold(v):
    return jnp.sum(v.reshape(v.shape[0] // 8, 8, v.shape[1]), axis=0)


def plus(total, v):
    return v if total is None else total + v


class Step:
    def __init__(self, place, wire, refs, image_total):
        self.__dict__.update(refs)
        self.inverse = 1.0 / image_total
        self.p, self.w = place, wire
        self.images, self.rows_full, self.side_full, self.channels = self.IMG.shape
        self.rim, _, self.side, _ = self.PO.shape
        self.rows = self.rim - 2
        self.per = self.channels // NORM_GROUPS
        self.tiles = self.channels // 128
        shard = self.cw.shape[0]
        self.kernel_rows = 16 * shard
        self.g = Gather(wire, place, self.W, shard)
        self.r2 = Scatter(wire, place, self.DW, [self.__dict__["RA%d" % i] for i in range(6)], self.RES, 2)
        self.r1 = Scatter(wire, place, self.DW, [self.__dict__["RB%d" % i] for i in range(6)], self.RES, 0)
        self.halo_p = Halo(wire, place, self.PO)
        self.halo_g = Halo(wire, place, self.G)
        self.halo_a = Halo(wire, place, self.A2)
        self.halo_b = Halo(wire, place, self.GB)
        self.aff_img = Spread(wire, place, self.AFS.at[place.sp])
        self.aff_sp = BandSum(wire, place, self.AFS)
        self.sum1 = BandSum(wire, place, self.ST1)
        self.sum2 = BandSum(wire, place, self.ST2)
        self.sum3 = BandSum(wire, place, self.ST3)
        self.sum4 = BandSum(wire, place, self.ST4)
        self.psum = SplitSum(wire, place, self.PS)
        self.proj = SplitSum(wire, place, self.PX)
        self.esum = SplitSum(wire, place, self.PE)
        self.asum = BandSum(wire, place, self.AFR)
        self.spread_g = Spread(wire, place, self.GPA)
        self.ea = wire.take(6), wire.take()
        self.ez = wire.take(3), wire.take(4)
        self.afy = wire.take()
        self.afz = wire.take(3)


    def loop(self, body, first=0, last=None):
        def one(n, _):
            body(n)
            return 0

        lax.fori_loop(first, self.images if last is None else last, one, 0)

    def width(self, n, r):
        return jnp.where(self.p.sp * self.rows_full + r < self.ext[0, n], self.ext[1, n], 0)

    def half_width(self, n, r):
        inside = self.p.sp * self.rows + r < lax.div(self.ext[0, n], 2)
        return jnp.where(inside, lax.div(self.ext[1, n], 2), 0)

    def cols(self, side):
        return lax.broadcasted_iota(jnp.int32, (side, self.channels), 0)

    def at(self, k, n):
        return self.AB[k, pl.ds(n, 1)]

    def clear_sums(self):
        self.SS[...] = jnp.zeros_like(self.SS)

    def add_sums(self, n, s, q):
        self.SS[pl.ds(n, 1)] += jnp.sum(s, axis=0, keepdims=True)
        self.SS[pl.ds(n + 16, 1)] += jnp.sum(q, axis=0, keepdims=True)

    def eslot(self, z, y):
        rows = self.ew.shape[0]
        start = ((z * 2 + y) * 4 + self.p.sp) * rows
        return self.EZ.at[pl.ds(many(start, 32), rows)]


    def load(self):
        self.copies = [
            pltpu.make_async_copy(self.img, self.IMG, self.lsem.at[0]),
            pltpu.make_async_copy(self.cot, self.COT, self.lsem.at[1]),
        ]
        late = ((self.cm_in, self.CM), (self.ce_in, self.CE), (self.em_in, self.EM), (self.ee_in, self.EE))
        for i, (src, dst) in enumerate(late):
            self.copies.append(pltpu.make_async_copy(src, dst, self.lsem.at[2 + i]))
        for copy in self.copies:
            copy.start()

    def loaded(self, k):
        self.copies[k].wait()

    def own_weights(self):
        p = self.p
        rows = self.cw.shape[0]
        self.W[pl.ds(many(rows * (p.img * 4 + p.sp), 16), rows)] = self.cw[...].astype(BF16)
        low = self.aff[...].astype(BF16).astype(F32)
        self.AFS[p.sp, p.y, p.z] = low

    def own_embedding(self):
        p = self.p
        rows = self.ew.shape[0]
        zero = jnp.zeros((rows, self.EZ.shape[1]), BF16)
        for i in range(8):
            for sp in p.sps:
                self.EZ[pl.ds(many((i * 4 + sp[1]) * rows, 32), rows)] = zero
        self.EZ[pl.ds(many((p.img * 4 + p.sp) * rows, 32), rows)] = self.ew[...].astype(BF16)
        self.EP[...] = jnp.zeros_like(self.EP)
        self.EP[pl.ds(0, self.images)] = self.emb[...].astype(F32)
        e = self.EP[...]
        act = (e * sigmoid(e)).astype(BF16)
        self.EA[...] = act
        for i in range(8):
            self.ET[i // 2, i % 2] = act[:, i * 128 : i * 128 + 128]
        for y in range(2):
            self.EZT[y, p.z] = self.ET[p.z, y]

    def counts(self):
        self.CNT[...] = jnp.ones_like(self.CNT)

        def one(n):
            h, w = self.ext[0, n], self.ext[1, n]
            for i, number in enumerate((h * w, lax.div(h, 2) * lax.div(w, 2))):
                number = jnp.full((1, self.channels), number * self.per, jnp.int32)
                self.CNT[i, pl.ds(n, 1)] = number.astype(F32)

        self.loop(one)


    def ez_send(self):
        p = self.p
        for k in range(3):
            self.w.put(self.eslot(p.z, p.y), self.eslot(p.z, p.y), p.zs[k], self.ez[0] + k)

    def ez_turn(self):
        p = self.p
        for k in range(3):
            self.w.got(self.eslot(p.z_off(3 - k), p.y), self.ez[0] + k, p.zs[k])
        for k in range(4):
            self.w.put(self.eslot(k, p.y), self.eslot(k, p.y), p.yn, self.ez[1] + k)

    def ez_wait(self):
        for k in range(4):
            self.w.got(self.eslot(k, 1 - self.p.y), self.ez[1] + k, self.p.yn)


    def ea_send(self):
        p = self.p
        for k in range(3):
            for y in range(2):
                src = self.ET.at[p.z_off(k + 1), y]
                self.w.put(src, self.EZT.at[y, p.z], p.zs[k], self.ea[0] + 2 * k + y)

    def ea_turn(self):
        p = self.p
        for k in range(3):
            for y in range(2):
                self.w.got(self.EZT.at[y, p.z_off(3 - k)], self.ea[0] + 2 * k + y, p.zs[k])
        self.w.put(self.EZT.at[1 - p.y], self.EY, p.yn, self.ea[1])

    def ea_wait(self):
        self.w.got(self.EY, self.ea[1], self.p.yn)

    def project(self):
        v = jnp.dot(self.EA[...], self.EZ[...], preferred_element_type=F32)
        self.PX[0] = v[:, : self.channels]
        self.PX[1] = v[:, self.channels :]


    def stats_one(self, first, last):
        col = self.cols(self.side_full)

        def one(n):
            s = q = None
            for r in range(self.rows_full):
                v = jnp.where(col < self.width(n, r), self.IMG[n, r].astype(F32), 0.0)
                s, q = plus(s, fold(v)), plus(q, fold(v * v))
            self.add_sums(n, s, q)

        self.loop(one, first, last)

    def stats_one_end(self):
        self.ST1[self.p.sp] = pack(self.SS[:16], self.SS[16:])

    def affine_rows(self):
        for s in range(4):
            for y in range(2):
                for z in range(4):
                    self.AFF[pl.ds(z * 2 + y, 1), pl.ds(s * 128, 128)] = self.AFS[s, y, z]

    def moments(self, total, count, mean_ref, inv_ref):
        sums, squares = unpack(total, self.channels)
        mean = sums / count
        inv = lax.rsqrt(squares / count - mean * mean + EPSILON)
        mean_ref[...] = mean
        inv_ref[...] = inv
        return mean, inv

    def norm_one(self):
        mean, inv = self.moments(self.sum1.total(), self.CNT[0], self.MI.at[0], self.MI.at[1])
        self.AB[0] = inv * self.AFF[0:1]
        self.AB[1] = self.AFF[1:2] - mean * self.AB[0]

    def pool(self, hrs, first=0, last=None):
        col = self.cols(self.side_full)

        def one(n):
            for i, hr in enumerate(hrs):
                act = raw = None
                for k in range(2):
                    r = 2 * hr + k
                    inside = col < self.width(n, r)
                    u = self.IMG[n, r].astype(F32)
                    v = u * self.at(0, n) + self.at(1, n)
                    act = plus(act, jnp.where(inside, v * sigmoid(v), 0.0))
                    raw = plus(raw, jnp.where(inside, u, 0.0))
                for t in range(self.tiles):
                    lanes = slice(t * 128, t * 128 + 128)
                    self.T[i, t] = act[:, lanes]
                    self.T[i + 2, t] = raw[:, lanes]
            even, odd = pl.ds(0, self.side, stride=2), pl.ds(1, self.side, stride=2)
            for i, hr in enumerate(hrs):
                for t in range(self.tiles):
                    lanes = pl.ds(t * 128, 128)
                    v = self.T[i, t, even] + self.T[i, t, odd]
                    self.PO[hr + 1, n, :, lanes] = (v * 0.25).astype(BF16)
                    v = self.T[i + 2, t, even] + self.T[i + 2, t, odd]
                    self.SKIP[hr, n, :, lanes] = v * 0.25

        self.loop(one, first, last)


    def shift(self, src, rows):
        col = self.cols(self.side)

        def one(n):
            for r in rows:
                v = src[r, n].astype(F32)
                self.X[0, r, n] = jnp.where(col > 0, pltpu.roll(v, 1, 0), 0.0).astype(BF16)
                v = jnp.where(col < self.side - 1, pltpu.roll(v, self.side - 1, 0), 0.0)
                self.X[1, r, n] = v.astype(BF16)

        self.loop(one)

    def conv(self, center, base, row, back):
        count = self.ACC.shape[0]
        size = count * self.images * self.side
        total = None
        for a in range(3):
            for b in range(3):
                da, db = (2 - a, 2 - b) if back else (a, b)
                src = center if db == 1 else self.X.at[0 if db == 0 else 1]
                left = src[pl.ds(row + da, count)].reshape(size, self.channels)
                tap = self.W[pl.ds(base + (3 * a + b) * self.channels, self.channels)]
                dims = (((1,), (1 if back else 0,)), ((), ()))
                total = plus(total, lax.dot_general(left, tap, dims, preferred_element_type=F32))
        self.ACC[...] = total.reshape(self.ACC.shape)

    def tap_grad(self, center, grads, t):
        a, b = divmod(t, 3)
        size = self.rows * self.images * self.side
        src = center if b == 1 else self.X.at[0 if b == 0 else 1]
        left = src[pl.ds(a, self.rows)].reshape(size, self.channels)
        right = grads[pl.ds(1, self.rows)].reshape(size, self.channels)
        self.DW[pl.ds(t * self.channels, self.channels)] = lax.dot_general(
            left, right, (((0,), (0,)), ((), ())), preferred_element_type=F32
        ).astype(BF16)

    def mask_cot(self):
        col = self.cols(self.side)
        self.C2[...] = jnp.zeros_like(self.C2)

        def one(n):
            total = None
            for r in range(self.rows):
                v = jnp.where(col < self.half_width(n, r), self.COT[n, r].astype(F32), 0.0)
                self.G[r + 1, n] = v.astype(BF16)
                total = plus(total, fold(v))
            self.C2[...] += total

        self.loop(one)

    def inner_conv(self, row):
        col = self.cols(self.side)
        self.conv(self.PO, 0, row, False)

        def one(n):
            s = q = None
            for r in range(self.ACC.shape[0]):
                v = self.ACC[r, n] + self.AFF[2:3]
                v = jnp.where(col < self.half_width(n, row + r), v, 0.0).astype(BF16)
                self.INN[row + r, n] = v
                v = v.astype(F32)
                s, q = plus(s, fold(v)), plus(q, fold(v * v))
            self.add_sums(n, s, q)

        self.loop(one)


    def stats_two(self):
        self.ST2[self.p.sp] = pack(self.SS[:16], self.SS[16:])

    def norm_two(self):
        self.MI[4] = self.PX[5] + (self.AFF[3:4] + 1.0)
        self.MI[5] = self.PX[6] + self.AFF[4:5]
        mean, inv = self.moments(self.sum2.total(), self.CNT[1], self.MI.at[2], self.MI.at[3])
        self.AB[2] = inv
        self.AB[3] = -mean * inv
        self.AB[4] = self.AFF[5:6] * self.MI[4]
        self.AB[5] = self.AFF[6:7] * self.MI[4] + self.MI[5]

    def xhat_two(self, r, n):
        return self.INN[r, n].astype(F32) * self.at(2, n) + self.at(3, n)

    def activate(self, rs):
        col = self.cols(self.side)

        def one(n):
            for r in rs:
                v = self.xhat_two(r, n) * self.at(4, n) + self.at(5, n)
                v = jnp.where(col < self.half_width(n, r), v * sigmoid(v), 0.0)
                self.A2[r + 1, n] = v.astype(BF16)

        self.loop(one)

    def mixed_grad(self, row):
        col = self.cols(self.side)
        self.conv(self.G, self.kernel_rows, row, True)

        def one(n):
            s = q = None
            for r in range(self.ACC.shape[0]):
                v = self.ACC[r, n].astype(BF16).astype(F32)
                xhat = self.xhat_two(row + r, n)
                mixed = xhat * self.at(4, n) + self.at(5, n)
                v = jnp.where(col < self.half_width(n, row + r), v * slope(mixed), 0.0)
                self.GM[row + r, n] = v
                s, q = plus(s, fold(v)), plus(q, fold(v * xhat))
            self.add_sums(n, s, q)

        self.loop(one)

    def sums_two_back(self):
        p1, p2 = self.SS[:16], self.SS[16:]
        self.PS[0] = p1
        self.PS[1] = p2
        self.ST3[self.p.sp] = pack(p1 * self.AB[4], p2 * self.AB[4])
        scale = self.MI[4]
        self.AFP[0:3] = jnp.zeros_like(self.AFP[0:3])
        self.AFP[3:4] = jnp.sum(self.AFF[5:6] * p2 + self.AFF[6:7] * p1, axis=0, keepdims=True)
        self.AFP[4:5] = jnp.sum(p1, axis=0, keepdims=True)
        self.AFP[5:6] = jnp.sum(scale * p2, axis=0, keepdims=True)
        self.AFP[6:7] = jnp.sum(scale * p1, axis=0, keepdims=True)
        self.AFP[7:8] = jnp.sum(self.C2[...], axis=0, keepdims=True)

    def output(self, row):
        col = self.cols(self.side)
        self.conv(self.A2, self.kernel_rows, row, False)

        def one(n):
            for r in range(self.ACC.shape[0]):
                v = self.ACC[r, n] + self.AFF[7:8]
                v = jnp.where(col < self.half_width(n, row + r), v, 0.0)
                self.OUTV[n, row + r] = (self.SKIP[row + r, n] + v).astype(BF16)

        self.loop(one)

    def project_grad(self):
        p1, p2 = self.PS[5], self.PS[6]
        scale = self.AFF[5:6] * p2 + self.AFF[6:7] * p1
        self.GP[0] = scale
        self.GP[1] = p1
        self.GPA[self.p.y, self.p.z, 0] = scale.astype(BF16)
        self.GPA[self.p.y, self.p.z, 1] = p1.astype(BF16)

    def norm_two_back(self):
        first, second = unpack(self.sum3.total(), self.channels)
        inv = self.AB[2]
        self.AB[6] = inv * self.AB[4]
        self.AB[7] = inv * (first / self.CNT[1])
        self.AB[8] = inv * (second / self.CNT[1])
        self.C1[...] = jnp.zeros_like(self.C1)

    def inner_grad(self, rs):
        col = self.cols(self.side)

        def one(n):
            total = None
            for r in rs:
                v = self.GM[r, n] * self.at(6, n) - self.at(7, n) - self.xhat_two(r, n) * self.at(8, n)
                v = jnp.where(col < self.half_width(n, r), v, 0.0).astype(BF16)
                self.GB[r + 1, n] = v
                total = plus(total, fold(v.astype(F32)))
            self.C1[...] += total

        self.loop(one)


    def embedding_part(self):
        gp = jnp.concatenate([self.GP[0], self.GP[1]], axis=1)
        gp = jnp.concatenate(thirds(gp), axis=0)
        v = lax.dot_general(gp, self.EZ[...], (((1,), (1,)), ((), ())), preferred_element_type=F32)
        v = v[:16] + v[16:32] + v[32:]
        self.PE[0] = v[:, : self.channels]
        self.PE[1] = v[:, self.channels :]

    def embedding_grad(self):
        v = jnp.concatenate([self.PE[5], self.PE[6]], axis=1)[: self.images]
        self.ge[...] = v * slope(self.EP[pl.ds(0, self.images)])

    def embedding_weights(self):
        p = self.p
        left = jnp.concatenate([self.EZT[p.y].reshape(64, 128), self.EY[...].reshape(64, 128)], axis=0)
        for i in range(2):
            right = [self.GPA[y, :, i].reshape(64, self.channels) for y in (p.y, 1 - p.y)]
            self.EW[:, pl.ds(i * self.channels, self.channels)] = lax.dot_general(
                left, jnp.concatenate(right, axis=0), (((0,), (0,)), ((), ())), preferred_element_type=F32
            )
        self.ewg[...] = self.EW[pl.ds(many(p.sp * 32, 32), 32)]


    def doubled(self, value, slot):
        for t in range(self.tiles):
            v = value[:, t * 128 : t * 128 + 128]
            self.T[slot, t, pl.ds(0, self.side, stride=2)] = v
            self.T[slot, t, pl.ds(1, self.side, stride=2)] = v
        return jnp.concatenate([self.T[slot, t] for t in range(self.tiles)], axis=1)

    def prepare_one_back(self):
        self.AB[2] = self.MI[1]
        self.AB[3] = -self.MI[0] * self.MI[1]
        self.clear_sums()

    def norm_one_grad(self, n, r, grad):
        v = self.IMG[n, r].astype(F32)
        xhat = v * self.at(2, n) + self.at(3, n)
        v = v * self.at(0, n) + self.at(1, n)
        return xhat, jnp.where(self.cols(self.side_full) < self.width(n, r), grad * slope(v), 0.0)

    def pooled_conv(self, row):
        self.conv(self.GB, 0, row, True)
        self.GM[pl.ds(row, self.ACC.shape[0])] = self.ACC[...] * 0.25

    def pooled_grad(self, row, first=0, last=None):
        def one(n):
            s = q = None
            for r in range(self.ACC.shape[0]):
                grad = self.doubled(self.GM[row + r, n], r)
                for k in range(2):
                    xhat, v = self.norm_one_grad(n, 2 * (row + r) + k, grad)
                    s, q = plus(s, fold(v)), plus(q, fold(v * xhat))
            self.add_sums(n, s, q)

        self.loop(one, first, last)

    def sums_one_back(self):
        self.AFP[0:1] = jnp.sum(self.SS[16:32], axis=0, keepdims=True)
        self.AFP[1:2] = jnp.sum(self.SS[0:16], axis=0, keepdims=True)
        self.AFP[2:3] = jnp.sum(self.C1[...], axis=0, keepdims=True)
        self.AFR[self.p.sp] = self.AFP[...]
        self.ST4[self.p.sp] = pack(self.SS[:16] * self.AFF[0:1], self.SS[16:] * self.AFF[0:1])

    def affine_y(self):
        self.AFY[0] = self.asum.total()
        self.w.put(self.AFY.at[0], self.AFY.at[1], self.p.yn, self.afy)

    def affine_z(self):
        self.w.got(self.AFY.at[1], self.afy, self.p.yn)
        self.AFZ[self.p.z] = self.AFY[0] + self.AFY[1]
        for k in range(3):
            self.w.put(self.AFZ.at[self.p.z], self.AFZ.at[self.p.z], self.p.zs[k], self.afz + k)

    def affine_done(self):
        for k in range(3):
            self.w.got(self.AFZ.at[self.p.z_off(3 - k)], self.afz + k, self.p.zs[k])
        self.AFP[...] = self.AFZ[0] + self.AFZ[1] + self.AFZ[2] + self.AFZ[3]
        tile = self.AFP[:, pl.ds(many(self.p.sp * 128, 128), 128)]
        line = lax.broadcasted_iota(jnp.int32, tile.shape, 0) == self.p.img
        self.ag[...] = jnp.sum(jnp.where(line, tile, 0.0), axis=0, keepdims=True)

    def norm_one_back(self):
        first, second = unpack(self.sum4.total(), self.channels)
        self.AB[4] = self.MI[1] * self.AFF[0:1]
        self.AB[5] = self.MI[1] * (first / self.CNT[0])
        self.AB[6] = self.MI[1] * (second / self.CNT[0])

    def image_grad(self, first, last):
        col = self.cols(self.side_full)

        def one(n):
            for hr in range(self.rows):
                grad = self.doubled(self.GM[hr, n], 0)
                cell = self.doubled(self.COT[n, hr].astype(F32) * 0.25, 1)
                for k in range(2):
                    r = 2 * hr + k
                    xhat, v = self.norm_one_grad(n, r, grad)
                    v = v * self.at(4, n) - self.at(5, n) - xhat * self.at(6, n) + cell
                    self.IMG[n, r] = jnp.where(col < self.width(n, r), v, 0.0).astype(BF16)

        self.loop(one, first, last)


    def update(self, weight, moment, average, total, new_weight, new_moment, new_average):
        mean = total[...] * self.inverse
        m = MOMENTUM * moment[...] + mean
        w = weight[...] - LEARN_RATE * (mean + MOMENTUM * m)
        new_weight[...] = w
        new_moment[...] = m
        new_average[...] = EMA_DECAY * average[...] + (1.0 - EMA_DECAY) * w

    def update_small(self):
        self.loaded(4)
        self.loaded(5)
        self.update(self.ew, self.EM, self.EE, self.ewg, self.new, self.nem, self.nee)
        self.update(self.aff, self.am, self.ae, self.ag, self.naw, self.nam, self.nae)

    def update_conv(self):
        self.loaded(2)
        self.loaded(3)
        step = 32
        arrays = (self.cw, self.CM, self.CE, self.RES, self.ncw, self.ncm, self.nce)

        def piece(i, _):
            at = pl.ds(pl.multiple_of(i * step, step), step)
            self.update(*(r.at[at] for r in arrays))
            return 0

        lax.fori_loop(0, self.cw.shape[0] // step, piece, 0)


def mix(works, ticks):
    done = 0
    for i, work in enumerate(works):
        work()
        upto = (i + 1) * len(ticks) // len(works)
        for tick in ticks[done:upto]:
            tick()
        done = upto
    for tick in ticks[done:]:
        tick()


def pairs(*lists):
    return [item for group in zip(*lists) for item in group]


def schedule(s):
    p, g, z = s.p, s.g, s.p.z
    pieces = list(range(PIECES))
    edge, middle = (0, s.rows - 1), range(1, s.rows - 1)
    inside, outside = range(1, s.rim - 1), (0, s.rim - 1)
    lead = choose(z == 0, 0, 1)
    other = choose(z == 1, 0, 1)
    tail = 1 - lead
    lead_two = choose(z == 3, 3, 2)
    tail_two = 5 - lead_two
    n = s.images

    def come(b, j, when=None):
        def run():
            g.arrive(b, j, when)
            g.own(b, j, when)

        return run

    def call(method, *args):
        return lambda: method(*args)

    def steps(scatter, k, b):
        return [call(scatter.step, k, b, j) for j in pieces]

    def run(calls):
        for item in calls:
            item()

    def taken(scatter, b):
        for yy in range(2):
            for xx in range(2):
                scatter.take(b, yy, xx)

    s.load()
    s.own_weights()
    s.w.greet(p)
    s.aff_img.send()
    for j in pieces:
        g.along(z, j, z < 2, z > 0)
        g.own(z, j, z < 2)
    s.own_embedding()
    s.counts()
    s.clear_sums()
    s.loaded(0)
    s.stats_one(0, n // 2)
    come(other, 0)()
    s.stats_one(n // 2, n)
    s.stats_one_end()
    s.sum1.send()
    s.aff_img.turn()
    come(other, 1)()
    g.turn(lead, 0)
    come(other, 2)()
    s.aff_img.wait()
    s.aff_sp.send()
    g.turn(lead, 1)
    for j in pieces:
        g.arrive(3, j, z == 2)
    come(0, 0, z >= 2)()
    g.turn(lead, 2)
    s.sum1.wait()
    s.aff_sp.wait()
    s.affine_rows()
    s.norm_one()
    s.ez_send()
    works = [call(s.pool, edge, i, i + 4) for i in range(0, n, 4)] + [s.halo_p.send]
    works += [call(s.pool, middle, i, i + 4) for i in range(0, n, 4)]
    works += [call(s.loaded, 1), s.mask_cot, call(s.shift, s.PO, inside)]
    ticks = [come(0, j, z >= 2) for j in pieces[1:]]
    ticks += [call(g.arrive, 2, j, z == 1) for j in pieces]
    ticks += pairs([call(g.last, lead, j) for j in pieces], [call(g.turn, tail, j) for j in pieces])
    mix(works, ticks)

    def next_two(j):
        g.arrive(2, j, z == 0)
        g.own(lead_two, j)

    def tail_two_on(j):
        g.arrive(tail_two, j, (z == 0) | (z == 3))
        g.own(tail_two, j)

    for j in pieces:
        g.arrive(3, j, z == 1)
    s.ez_turn()
    next_two(0)
    for j in pieces:
        g.last(tail, j)
    next_two(1)
    s.halo_p.wait()
    s.shift(s.PO, outside)
    for j in pieces:
        g.along(2, j, z == 2, z > 3)
    g.done(lead)
    g.done(tail)
    next_two(2)
    sent = s.w.started()
    s.clear_sums()
    s.ea_send()
    s.inner_conv(0)
    g.turn(lead_two, 0)
    s.ez_wait()
    s.project()
    s.proj.send()
    tail_two_on(0)
    s.proj.cross()
    g.turn(lead_two, 1)
    s.inner_conv(2)
    s.proj.back()
    s.stats_two()
    s.sum2.send()
    tail_two_on(1)
    s.proj.wait()
    s.sum2.wait()
    s.norm_two()
    s.activate(edge)
    s.halo_a.send()
    s.activate(middle)
    tail_two_on(2)
    g.turn(lead_two, 2)
    s.shift(s.A2, inside)
    s.halo_g.send()
    s.ea_turn()
    s.w.left(sent)
    s.halo_a.wait()
    s.shift(s.A2, outside)

    def tap_two(t):
        s.tap_grad(s.A2, s.G, t)
        s.r2.give((t + 1) * s.channels)

    between = [[]] + [[call(g.last, lead_two, j), call(g.turn, tail_two, j)] for j in pieces]
    between += [[], []] + [[call(g.last, tail_two, j)] for j in pieces]
    between[6] += [call(taken, s.r2, 0)] + steps(s.r2, 0, 0)
    between[7] += steps(s.r2, 1, 0)
    for t in range(9):
        tap_two(t)
        run(between[t])

    s.shift(s.G, inside)
    s.halo_g.wait()
    s.shift(s.G, outside)
    s.clear_sums()
    taken(s.r2, 1)
    run(steps(s.r2, 0, 1))
    g.done(2)
    g.done(3)
    s.mixed_grad(0)
    run(steps(s.r2, 2, 0))
    s.mixed_grad(2)
    s.sums_two_back()
    s.sum3.send()
    run(steps(s.r2, 1, 1))
    run(steps(s.r2, 2, 1))
    s.psum.send()
    s.shift(s.PO, range(s.rim))
    s.sum3.wait()
    s.norm_two_back()
    s.inner_grad(edge)
    s.halo_b.send()
    s.inner_grad(middle)
    s.psum.cross()
    s.r2.given()

    def tap_one(t):
        s.tap_grad(s.PO, s.GB, t)
        s.r1.give((t + 1) * s.channels)

    def r1(*which):
        for k, b, j in which:
            if j < PIECES:
                s.r1.step(k, b, j)

    between = [[item] for item in steps(s.r2, 3, 0)] + [[], [], []]
    between += [
        [call(taken, s.r1, 0), call(r1, (0, 0, 0), (0, 0, 1))],
        [call(r1, (0, 0, 2), (1, 0, 0))],
        [call(s.r1.step, 1, 0, 1), s.psum.back],
    ]
    for t in range(9):
        tap_one(t)
        run(between[t])

    sent = s.w.started()
    s.halo_b.wait()
    s.shift(s.GB, range(s.rim))
    s.prepare_one_back()
    taken(s.r1, 1)
    r1((2, 0, 0), (0, 1, 0), (1, 0, 2))
    run(steps(s.r2, 3, 1))
    s.pooled_conv(0)
    r1((2, 0, 1), (0, 1, 1), (1, 1, 0))
    s.psum.wait()
    s.project_grad()
    s.spread_g.send()
    run(steps(s.r2, 4, 0))
    s.pooled_conv(2)
    r1((2, 0, 2), (0, 1, 2), (1, 1, 1))
    half = n // 2
    s.pooled_grad(0, 0, half)
    r1((2, 1, 0), (1, 1, 2), (3, 0, 0))
    s.pooled_grad(0, half, n)
    r1((2, 1, 1), (3, 0, 1))
    s.pooled_grad(2, 0, half)
    r1((2, 1, 2), (3, 0, 2))
    s.pooled_grad(2, half, n)
    s.sums_one_back()
    s.sum4.send()
    s.asum.send()
    r1((3, 1, 0), (4, 0, 0))
    s.spread_g.turn()
    s.embedding_part()
    s.esum.send()
    r1((3, 1, 1), (4, 0, 1))
    s.shift(s.A2, range(s.rim))
    s.w.left(sent)
    s.sum4.wait()
    s.norm_one_back()
    r1((3, 1, 2), (4, 0, 2))
    s.asum.wait()
    s.affine_y()
    s.esum.cross()
    s.output(0)
    s.r1.step(4, 1, 0)
    s.r1.step(4, 1, 1)
    s.affine_z()
    s.esum.back()
    s.image_grad(0, n // 3)
    s.r1.step(4, 1, 2)
    run(steps(s.r2, 4, 1))
    s.output(2)
    s.image_grad(n // 3, 2 * (n // 3))
    run(steps(s.r2, 5, 0))
    run(steps(s.r1, 5, 0))
    s.image_grad(2 * (n // 3), n)
    run(steps(s.r2, 5, 1))
    s.spread_g.wait()
    s.ea_wait()
    s.embedding_weights()
    s.affine_done()
    s.esum.wait()
    s.embedding_grad()
    s.update_small()
    run(steps(s.r1, 5, 1))
    s.update_conv()
    s.w.close()


def whole_kernel(names, image_total, *refs):
    refs = dict(zip(names, refs))
    place = Place(lax.axis_index("img"), lax.axis_index("sp"))
    wire = Wire(refs.pop("ssem"), refs.pop("rsem"))
    schedule(Step(place, wire, refs, image_total))


def shapes(images, cotangent, conv_w, emb_w):
    n, rows_full, side_full, c = images
    _, rows, side, _ = cotangent
    shard = conv_w[0]
    rim = (rows + 2, n, side, c)
    band = (rows, n, side, c)
    out = dict(
        RES=(conv_w, F32), ag=((1, 128), F32), ewg=(emb_w, F32),
        CM=(conv_w, F32), CE=(conv_w, F32), EM=(emb_w, F32), EE=(emb_w, F32),
        COT=(cotangent, BF16), W=((32 * shard, c), BF16), EZ=((emb_w[1], emb_w[1]), BF16),
        PO=(rim, BF16), G=(rim, BF16), A2=(rim, BF16), GB=(rim, BF16), X=((2,) + rim, BF16),
        INN=(band, BF16), SKIP=(band, F32), GM=(band, F32), ACC=((2,) + band[1:], F32),
        DW=((16 * shard, c), BF16), T=((4, c // 128, side_full, 128), F32), SS=((32, c), F32),
        CNT=((2, 16, c), F32), MI=((6, 16, c), F32), AB=((9, 16, c), F32), AFF=((8, c), F32), AFP=((8, c), F32),
        C1=((8, c), F32), C2=((8, c), F32), AFS=((4, 2, 4, 1, 128), F32), AFR=((4, 8, c), F32),
        AFY=((2, 8, c), F32), AFZ=((4, 8, c), F32), EP=((16, 2 * c), F32), EA=((16, 2 * c), BF16), ET=((4, 2, 16, 128), BF16), EZT=((2, 4, 16, 128), BF16),
        EY=((4, 16, 128), BF16),
        GPA=((2, 4, 2, 16, c), BF16), GP=((2, 16, c), F32), EW=((128, 2 * c), F32), PX=((7, 16, c), F32), PE=((7, 16, c), F32),
        ST1=((4, 16, 128), F32), ST2=((4, 16, 128), F32), ST3=((4, 16, 128), F32), PS=((7, 16, c), F32), ST4=((4, 16, 128), F32),
    )
    for k in "AB":
        for i, v in enumerate(Scatter.scratch(shard, c)):
            out["R%s%d" % (k, i)] = v
    return out


WIRES = 360
VM = pl.BlockSpec(memory_space=pltpu.VMEM)
ANY = pl.BlockSpec(memory_space=pl.ANY)
SM = pl.BlockSpec(memory_space=pltpu.SMEM)


def place_kernel(*refs):
    count = len(refs) // 2
    sem = refs[-1]
    copies = [pltpu.make_async_copy(refs[i], refs[count + i], sem.at[i]) for i in range(count)]
    for copy in copies:
        copy.start()
    for copy in copies:
        copy.wait()


def local_kernels(image_total, images, embedding, extent, cotangent, conv_w, emb_w, affine,
                  conv_mom, emb_mom, affine_mom, conv_ema, emb_ema, affine_ema):
    line = lambda v: v.reshape(1, 128)
    scratch = shapes(images.shape, cotangent.shape, conv_w.shape, emb_w.shape)
    inputs = ["ext", "img", "cot", "emb", "cw", "ew", "aff", "cm_in", "ce_in", "em_in", "ee_in", "am", "ae"]
    trio = [(conv_w.shape, F32), (emb_w.shape, F32), ((1, 128), F32)]
    outputs = {"OUTV": (cotangent.shape, BF16), "IMG": (images.shape, BF16), "ge": (embedding.shape, F32)}
    outputs |= zip(("ncw", "new", "naw", "ncm", "nem", "nam", "nce", "nee", "nae"), trio * 3)
    names = inputs + list(outputs) + list(scratch) + ["lsem", "ssem", "rsem"]
    held = pl.pallas_call(
        lambda *refs: whole_kernel(names, image_total, *refs),
        name="resblock_step",
        out_shape=[pltpu.VMEM(*v) for v in outputs.values()],
        in_specs=[SM, ANY, ANY, VM, VM, VM, VM] + [ANY] * 4 + [VM] * 2,
        out_specs=[VM] * len(outputs),
        scratch_shapes=[pltpu.VMEM(*v) for v in scratch.values()]
        + [pltpu.SemaphoreType.DMA((8,)), pltpu.SemaphoreType.DMA((WIRES,)), pltpu.SemaphoreType.DMA((WIRES,))],
        compiler_params=pltpu.CompilerParams(
            collective_id=1, has_side_effects=True, vmem_limit_bytes=54 << 20
        ),
    )(extent.T, images, cotangent, embedding, conv_w, emb_w, line(affine), conv_mom, conv_ema, emb_mom, emb_ema,
      line(affine_mom), line(affine_ema))
    held = [pltpu.with_memory_space_constraint(v, pltpu.VMEM) for v in held]
    count = len(held)
    out, gi, ge, ncw, new, naw, ncm, nem, nam, nce, nee, nae = pl.pallas_call(
        place_kernel,
        name="place",
        out_shape=[jax.ShapeDtypeStruct(v.shape, v.dtype) for v in held],
        in_specs=[VM] * count,
        out_specs=[ANY] * count,
        scratch_shapes=[pltpu.SemaphoreType.DMA((count,))],
        compiler_params=pltpu.CompilerParams(vmem_limit_bytes=16 << 20),
    )(*held)
    flat = lambda v: v.reshape(-1)
    return out, gi, ge, ncw, new, flat(naw), ncm, nem, flat(nam), nce, nee, flat(nae)


def padded_2(cells, sides, width):
    for axis, dim in sides:
        count = lax.axis_size(axis)
        ends = count - 1
        head = lax.slice_in_dim(cells, 0, width, axis=dim)
        tail = lax.slice_in_dim(cells, cells.shape[dim] - width, cells.shape[dim], axis=dim)
        cells = jnp.concatenate(
            [
                lax.ppermute(tail, axis, [(i, (i + 1) % count) for i in range(ends)]),
                cells,
                lax.ppermute(head, axis, [((i + 1) % count, i) for i in range(ends)]),
            ],
            axis=dim,
        )
    return cells


def band_mask(extent, first_row, band_rows, band_cols, halved):
    height = extent[:, 0]
    breadth = extent[:, 1]
    if halved:
        height = height // 2
        breadth = breadth // 2
    row_ids = first_row + jnp.arange(band_rows, dtype=jnp.int32)
    col_ids = jnp.arange(band_cols, dtype=jnp.int32)
    inside = (row_ids[None, :, None] < height[:, None, None]) & (
        col_ids[None, None, :] < breadth[:, None, None]
    )
    return inside.astype(jnp.float32)[..., None]


def per_group_sums(values, group_count):
    shaped = values.reshape(values.shape[:3] + (group_count, values.shape[3] // group_count))
    return jnp.sum(shaped, axis=(1, 2, 4))


def spread_to_channels(stat, channels_per_group):
    return jnp.repeat(stat, channels_per_group, axis=1)[:, None, None, :]


def pool_cells(values):
    shaped = values.reshape(
        values.shape[0], values.shape[1] // 2, 2, values.shape[2] // 2, 2, values.shape[3]
    )
    return jnp.sum(shaped, axis=(2, 4)) * 0.25


def spread_cells(values):
    return jnp.repeat(jnp.repeat(values, 2, axis=1), 2, axis=2) * 0.25


def silu_slope(values):
    sigma = jax.nn.sigmoid(values)
    return sigma * (1.0 + values * (1.0 - sigma))


def conv_rows(padded, kernel, layout):
    return lax.conv_general_dilated(
        padded,
        kernel,
        (1, 1),
        ((0, 0), (1, 1)),
        dimension_numbers=("NHWC", "HWIO", layout),
        preferred_element_type=jnp.float32,
    )


def conv_back(padded, kernel):
    return lax.conv_general_dilated(
        padded,
        jnp.flip(kernel, (0, 1)),
        (1, 1),
        ((0, 0), (1, 1)),
        dimension_numbers=("NHWC", "HWOI", "NHWC"),
        preferred_element_type=jnp.float32,
    )


def tap_grads(padded, grads):
    window = jnp.pad(padded, ((0, 0), (0, 0), (1, 1), (0, 0)))
    band_rows = grads.shape[1]
    band_cols = grads.shape[2]
    kernel_rows = []
    for tap_row in range(3):
        taps = []
        for tap_col in range(3):
            source = window[:, tap_row : tap_row + band_rows, tap_col : tap_col + band_cols, :]
            taps.append(
                jnp.einsum("brci,brco->io", source, grads, preferred_element_type=jnp.float32)
            )
        kernel_rows.append(jnp.stack(taps))
    return jnp.stack(kernel_rows)


def band_rim(values):
    return padded_2(values, (("sp", 1),), 1)


def other_rim(values):
    return padded_2(values, (("sp", 1),), 1)


def update(weight, moment, average, total, image_total):
    grad_mean = total / image_total
    new_moment = MOMENTUM * moment + grad_mean
    new_weight = weight - LEARN_RATE * (grad_mean + MOMENTUM * new_moment)
    new_average = EMA_DECAY * average + (1.0 - EMA_DECAY) * new_weight
    return (new_weight, new_moment, new_average)


def local(
    images,
    embedding,
    extent,
    cotangent,
    conv_w,
    emb_w,
    affine,
    conv_mom,
    emb_mom,
    affine_mom,
    conv_ema,
    emb_ema,
    affine_ema,
):
    conv_all, emb_all, affine_all = (
        lax.all_gather(conv_w.astype(jnp.bfloat16), ("img", "sp"), axis=0, tiled=True),
        lax.all_gather(emb_w.astype(jnp.bfloat16), ("img", "sp"), axis=0, tiled=True),
        lax.all_gather(affine.astype(jnp.bfloat16), ("img", "sp"), axis=0, tiled=True),
    )
    channels = conv_all.shape[1]
    first_kernel = conv_all[: 9 * channels].reshape(3, 3, channels, channels)
    second_kernel = conv_all[9 * channels :].reshape(3, 3, channels, channels)
    parameters = affine_all.astype(jnp.float32).reshape(8, channels)
    image_count = images.shape[0]
    band_rows = images.shape[1]
    grid_side = images.shape[2]
    half_band = band_rows // 2
    half_side = grid_side // 2
    sp_size = lax.axis_size("sp")
    sp_index = lax.axis_index("sp")
    local_channels = channels // sp_size
    first_channels = sp_index * local_channels
    channels_per_group = channels // NORM_GROUPS
    groups_on_device = local_channels // channels_per_group
    full_mask = band_mask(extent, sp_index * band_rows, band_rows, grid_side, False)
    half_mask = band_mask(extent, sp_index * half_band, half_band, half_side, True)
    whole_half = band_mask(extent, 0, half_side, half_side, True)
    full_pixel_count = (extent[:, 0] * extent[:, 1] * channels_per_group).astype(jnp.float32)[
        :, None
    ]
    half_pixel_count = (extent[:, 0] // 2 * (extent[:, 1] // 2) * channels_per_group).astype(
        jnp.float32
    )[:, None]
    masked_values = images.astype(jnp.float32) * full_mask
    sums_one, squares_one = lax.psum(
        (
            per_group_sums(masked_values, NORM_GROUPS),
            per_group_sums(masked_values * masked_values, NORM_GROUPS),
        ),
        "sp",
    )
    first_group_mean = sums_one / full_pixel_count
    first_inverse_deviation = lax.rsqrt(
        squares_one / full_pixel_count - first_group_mean * first_group_mean + EPSILON
    )
    first_normalized = (
        masked_values - spread_to_channels(first_group_mean, channels_per_group)
    ) * spread_to_channels(first_inverse_deviation, channels_per_group)
    first_group_norm = first_normalized * parameters[0] + parameters[1]
    pooled = pool_cells(jax.nn.silu(first_group_norm) * full_mask).astype(jnp.bfloat16)
    skip_path = pool_cells(masked_values)
    pooled_rim = band_rim(pooled)
    inner_act = ((conv_rows(pooled_rim, first_kernel, "NHWC") + parameters[2]) * half_mask).astype(
        jnp.bfloat16
    )
    emb_act = jax.nn.silu(embedding.astype(jnp.float32)).astype(jnp.bfloat16)

    def place_local(values):
        return lax.dynamic_update_slice_in_dim(
            jnp.zeros((channels,), jnp.float32), values, first_channels, 0
        )

    inner_channels = lax.all_to_all(
        inner_act, "sp", split_axis=3, concat_axis=1, tiled=True
    ).astype(jnp.float32)
    emb_cols = jnp.concatenate(
        [
            lax.dynamic_slice_in_dim(emb_all, first_channels, local_channels, 1),
            lax.dynamic_slice_in_dim(emb_all, channels + first_channels, local_channels, 1),
        ],
        axis=1,
    )
    emb_bias = jnp.concatenate(
        [
            lax.dynamic_slice_in_dim(parameters[3], first_channels, local_channels, 0),
            lax.dynamic_slice_in_dim(parameters[4], first_channels, local_channels, 0),
        ]
    )
    emb_proj = jnp.dot(emb_act, emb_cols, preferred_element_type=jnp.float32) + emb_bias
    ada_scale = 1.0 + emb_proj[:, :local_channels][:, None, None, :]
    ada_shift = emb_proj[:, local_channels:][:, None, None, :]
    sums_two = per_group_sums(inner_channels, groups_on_device)
    squares_two = per_group_sums(inner_channels * inner_channels, groups_on_device)
    second_group_mean = sums_two / half_pixel_count
    second_inverse_deviation = lax.rsqrt(
        squares_two / half_pixel_count - second_group_mean * second_group_mean + EPSILON
    )
    second_normalized = (
        inner_channels - spread_to_channels(second_group_mean, channels_per_group)
    ) * spread_to_channels(second_inverse_deviation, channels_per_group)
    second_gain = lax.dynamic_slice_in_dim(parameters[5], first_channels, local_channels, 0)
    second_group_norm = second_normalized * second_gain + lax.dynamic_slice_in_dim(
        parameters[6], first_channels, local_channels, 0
    )
    mixed_act = second_group_norm * ada_scale + ada_shift
    act_two = (jax.nn.silu(mixed_act) * whole_half).astype(jnp.bfloat16)
    act_rows = lax.all_to_all(act_two, "sp", split_axis=1, concat_axis=3, tiled=True)
    act_rim = other_rim(act_rows)
    branch = conv_rows(act_rim, second_kernel, "NHWC") + parameters[7]
    output = (skip_path + branch * half_mask).astype(jnp.bfloat16)
    grad_branch = (cotangent.astype(jnp.float32) * half_mask).astype(jnp.bfloat16)
    bias_two_grad = jnp.sum(grad_branch.astype(jnp.float32), axis=(0, 1, 2))
    grad_rim = other_rim(grad_branch)
    kernel_two = tap_grads(act_rim, grad_branch)
    grad_band = conv_back(grad_rim, second_kernel).astype(jnp.bfloat16)
    grad_act = lax.all_to_all(grad_band, "sp", split_axis=3, concat_axis=1, tiled=True)
    grad_mixed = grad_act.astype(jnp.float32) * whole_half * silu_slope(mixed_act)
    grad_proj = jnp.concatenate(
        [jnp.sum(grad_mixed * second_group_norm, axis=(1, 2)), jnp.sum(grad_mixed, axis=(1, 2))],
        axis=1,
    )
    second_norm_gradient = grad_mixed * ada_scale
    second_gain_gradient = jnp.sum(second_norm_gradient * second_normalized, axis=(0, 1, 2))
    bias_norm_two_grad = jnp.sum(second_norm_gradient, axis=(0, 1, 2))
    second_normalized_gradient = second_norm_gradient * second_gain
    first_total_count = (
        per_group_sums(second_normalized_gradient, groups_on_device) / half_pixel_count
    )
    second_total_count = (
        per_group_sums(second_normalized_gradient * second_normalized, groups_on_device)
        / half_pixel_count
    )
    grad_inner = spread_to_channels(second_inverse_deviation, channels_per_group) * (
        second_normalized_gradient
        - spread_to_channels(first_total_count, channels_per_group)
        - second_normalized * spread_to_channels(second_total_count, channels_per_group)
    )
    grad_inner_rows = lax.all_to_all(
        grad_inner.astype(jnp.bfloat16), "sp", split_axis=1, concat_axis=3, tiled=True
    )
    emb_grad_cols = jnp.einsum(
        "be,bk->ek", emb_act.astype(jnp.float32), grad_proj, precision=HIGHEST
    )
    emb_kernel = jnp.zeros((emb_all.shape[0], 2 * channels), jnp.float32)
    emb_kernel = lax.dynamic_update_slice_in_dim(
        emb_kernel, emb_grad_cols[:, :local_channels], first_channels, 1
    )
    emb_kernel = lax.dynamic_update_slice_in_dim(
        emb_kernel, emb_grad_cols[:, local_channels:], channels + first_channels, 1
    )
    silu_part = jnp.einsum("bk,ek->be", grad_proj, emb_cols.astype(jnp.float32), precision=HIGHEST)
    silu_grad = lax.psum(silu_part.astype(jnp.bfloat16), "sp").astype(jnp.float32)
    emb_bias_grad = jnp.sum(grad_proj, axis=0)
    coarse_affine = [
        place_local(emb_bias_grad[:local_channels]),
        place_local(emb_bias_grad[local_channels:]),
        place_local(second_gain_gradient),
        place_local(bias_norm_two_grad),
    ]
    grad_embedding = silu_grad * silu_slope(embedding.astype(jnp.float32))
    grad_raw = (grad_inner_rows.astype(jnp.float32) * half_mask).astype(jnp.bfloat16)
    bias_one_grad = jnp.sum(grad_raw.astype(jnp.float32), axis=(0, 1, 2))
    kernel_one = tap_grads(pooled_rim, grad_raw)
    grad_pooled = conv_back(band_rim(grad_raw), first_kernel)
    first_norm_gradient = spread_cells(grad_pooled) * full_mask * silu_slope(first_group_norm)
    first_gain_gradient = jnp.sum(first_norm_gradient * first_normalized, axis=(0, 1, 2))
    bias_norm_one_grad = jnp.sum(first_norm_gradient, axis=(0, 1, 2))
    first_normalized_gradient = first_norm_gradient * parameters[0]
    back_one, second_backward = lax.psum(
        (
            per_group_sums(first_normalized_gradient, NORM_GROUPS),
            per_group_sums(first_normalized_gradient * first_normalized, NORM_GROUPS),
        ),
        "sp",
    )
    grad_masked = spread_to_channels(first_inverse_deviation, channels_per_group) * (
        first_normalized_gradient
        - spread_to_channels(back_one / full_pixel_count, channels_per_group)
        - first_normalized
        * spread_to_channels(second_backward / full_pixel_count, channels_per_group)
    ) + spread_cells(cotangent.astype(jnp.float32))
    grad_images = (grad_masked * full_mask).astype(jnp.bfloat16)
    affine_grad = jnp.concatenate(
        [first_gain_gradient, bias_norm_one_grad, bias_one_grad] + coarse_affine + [bias_two_grad]
    )
    conv_grad = jnp.concatenate(
        [kernel_one.reshape(9 * channels, channels), kernel_two.reshape(9 * channels, channels)]
    )
    conv_sum, emb_sum, affine_sum = (
        lax.psum_scatter(conv_grad, ("img", "sp"), scatter_dimension=0, tiled=True),
        lax.psum_scatter(emb_kernel, ("img", "sp"), scatter_dimension=0, tiled=True),
        lax.psum_scatter(affine_grad, ("img", "sp"), scatter_dimension=0, tiled=True),
    )
    image_total = float(image_count * lax.axis_size("img"))
    new_conv, conv_moment, conv_average = update(conv_w, conv_mom, conv_ema, conv_sum, image_total)
    new_emb, emb_moment, emb_average = update(emb_w, emb_mom, emb_ema, emb_sum, image_total)
    new_affine, affine_moment, affine_average = update(
        affine, affine_mom, affine_ema, affine_sum, image_total
    )
    return (
        output,
        grad_images,
        grad_embedding,
        new_conv,
        new_emb,
        new_affine,
        conv_moment,
        emb_moment,
        affine_moment,
        conv_average,
        emb_average,
        affine_average,
    )


def kernels_or_ops(images, embedding, extent, cotangent, conv_w, *rest):
    arrays = (images, embedding, extent, cotangent, conv_w) + rest
    n, rows, side, channels = images.shape
    if n > 16 or rows != 8 or side != 32 or channels != 512 or conv_w.shape[0] != 288:
        return local(*arrays)
    return local_kernels(float(n * lax.axis_size("img")), *arrays)


def solution(mesh):
    in_specs = (
        P("img", "sp", None, None),
        P("img", None),
        P("img", None),
        P("img", "sp", None, None),
        P(("img", "sp"), None),
        P(("img", "sp"), None),
        P(("img", "sp")),
        P(("img", "sp"), None),
        P(("img", "sp"), None),
        P(("img", "sp")),
        P(("img", "sp"), None),
        P(("img", "sp"), None),
        P(("img", "sp")),
    )
    out_specs = (
        P("img", "sp", None, None),
        P("img", "sp", None, None),
        P("img", None),
        P(("img", "sp"), None),
        P(("img", "sp"), None),
        P(("img", "sp")),
        P(("img", "sp"), None),
        P(("img", "sp"), None),
        P(("img", "sp")),
        P(("img", "sp"), None),
        P(("img", "sp"), None),
        P(("img", "sp")),
    )
    fits = dict(mesh.shape) == {"img": 8, "sp": 4}
    return jax.shard_map(kernels_or_ops if fits else local, mesh=mesh, in_specs=in_specs, out_specs=out_specs, check_vma=False)
```

```python
import jax
import jax.numpy as jnp
from jax import lax
from jax.experimental import pallas as pl
from jax.experimental.pallas import tpu as pltpu
from jax.sharding import PartitionSpec as P

F32 = jnp.float32
BF16 = jnp.bfloat16
HIGHEST = lax.Precision.HIGHEST
MESH = pl.DeviceIdType.MESH
EPSILON = 1e-05
LEARN_RATE = 0.03
MOMENTUM = 0.5
EMA_DECAY = 0.5
NORM_GROUPS = 32
PIECES = 3


def choose(cond, a, b):
    if isinstance(cond, bool):
        return a if cond else b
    return jnp.where(cond, a, b)


def many(value, factor):
    return value if isinstance(value, int) else pl.multiple_of(value, factor)


class Place:
    def __init__(self, img, sp):
        self.img, self.sp = img, sp
        if isinstance(img, int):
            self.z, self.y, self.x, self.c = img // 2, img % 2, sp // 2, sp % 2
        else:
            self.z, self.y = lax.div(img, 2), lax.rem(img, 2)
            self.x, self.c = lax.div(sp, 2), lax.rem(sp, 2)
        z, y, x, c = self.z, self.y, self.x, self.c
        self.core = self.at(z, y, x, 1 - c)
        self.xn = self.at(z, y, 1 - x, c)
        self.yn = self.at(z, 1 - y, x, c)
        self.up, self.down = self.at(z + 1, y, x, c), self.at(z - 1, y, x, c)
        self.pair = self.at(z + 1 - 2 * self.odd(z), y, x, c)
        self.gate = self.at(choose(z < 2, 2, 1), y, x, c)
        self.zs = [self.at(self.z_off(k), y, x, c) for k in (1, 2, 3)]
        self.sps = [(img, self.sp_off(k)) for k in (1, 2, 3)]

    def at(self, z, y, x, c):
        return (z * 2 + y, x * 2 + c)

    def odd(self, value):
        return value % 2 if isinstance(value, int) else lax.rem(value, 2)

    def off(self, value, k):
        value = value + k
        return value % 4 if isinstance(value, int) else lax.rem(value, 4)

    def z_off(self, k):
        return self.off(self.z, k)

    def sp_off(self, k):
        return self.off(self.sp, k)


class Wire:
    def __init__(self, ssem, rsem):
        self.ssem, self.rsem = ssem, rsem
        self.used = 0
        self.open = []

    def take(self, count=1):
        first = self.used
        self.used += count
        return first

    def when(self, cond, do):
        if cond is None:
            do()
        else:
            pl.when(cond)(do)

    def copy(self, src, dst, peer, send, recv):
        return pltpu.make_async_remote_copy(
            src_ref=src, dst_ref=dst, send_sem=self.ssem.at[send], recv_sem=self.rsem.at[recv],
            device_id=peer, device_id_type=MESH,
        )

    def put(self, src, dst, peer, send, recv=None, when=None):
        def make():
            return self.copy(src, dst, peer, send, send if recv is None else recv)

        self.when(when, lambda: make().start())
        self.open.append((make, when))
        return self.open[-1]

    def left(self, copies):
        for make, when in copies:
            self.when(when, lambda make=make: make().wait_send())
        gone = [id(copy) for copy in copies]
        self.open = [item for item in self.open if id(item) not in gone]

    def got(self, ref, recv, peer, when=None):
        self.when(when, lambda: self.copy(ref, ref, peer, recv, recv).wait_recv())

    def started(self):
        return list(self.open)

    def close(self):
        self.left(self.started())

    def greet(self, place):
        barrier = pltpu.get_barrier_semaphore()
        peers = place.sps + [place.yn] + place.zs
        for peer in peers:
            pl.semaphore_signal(barrier, inc=1, device_id=peer, device_id_type=MESH)
        pl.semaphore_wait(barrier, len(peers))


class Gather:
    def __init__(self, wire, place, W, rows):
        self.wire, self.place, self.W, self.rows = wire, place, W, rows
        self.piece = rows // PIECES
        count = 4 * PIECES
        self.sems = {k: wire.take(count) for k in ("z", "u", "d", "x", "y", "xy", "yx")}
        self.core = wire.take(16)

    def sem(self, kind, b, j):
        return self.sems[kind] + b * PIECES + j

    def ref(self, b, y, x, c, j, half=None):
        start = self.rows * ((b * 2 + y) * 4 + x * 2 + c) + j * self.piece
        size = self.piece
        if half is not None:
            size = size // 2
            start = start + half * size
        return self.W.at[pl.ds(many(start, 16), size)]

    def along(self, b, j, up, down):
        p, wire = self.place, self.wire
        r = self.ref(b, p.y, p.x, p.c, j)
        wire.put(r, r, p.up, self.sem("u", b, j), self.sem("z", b, j), when=up)
        wire.put(r, r, p.down, self.sem("d", b, j), self.sem("z", b, j), when=down)

    def arrive(self, b, j, when=None):
        p = self.place
        both = lambda cond: cond if when is None else when & cond
        self.wire.got(self.ref(b, p.y, p.x, p.c, j), self.sem("z", b, j), p.up, when=when)
        self.along(b, j, both((b < p.z) & (p.z < 3)), both((b > p.z) & (p.z > 0)))

    def block(self, b, y, x, c):
        start = self.rows * ((b * 2 + y) * 4 + x * 2 + c)
        return self.W.at[pl.ds(many(start, 16), self.rows)]

    def share(self, b, k, y, x, when=None):
        r = self.block(b, y, x, self.place.c)
        self.wire.put(r, r, self.place.core, self.core + b * 4 + k, when=when)

    def own(self, b, j, when=None):
        p, wire = self.place, self.wire
        r = self.ref(b, p.y, p.x, p.c, j)
        wire.put(r, r, p.xn, self.sem("x", b, j), when=when)
        wire.put(r, r, p.yn, self.sem("y", b, j), when=when)
        if j == PIECES - 1:
            self.share(b, 0, p.y, p.x, when)

    def turn(self, b, j):
        p, wire = self.place, self.wire
        wire.got(self.ref(b, p.y, 1 - p.x, p.c, j), self.sem("x", b, j), p.xn)
        h = self.ref(b, p.y, 1 - p.x, p.c, j, 0)
        wire.put(h, h, p.yn, self.sem("xy", b, j))
        wire.got(self.ref(b, 1 - p.y, p.x, p.c, j), self.sem("y", b, j), p.yn)
        h = self.ref(b, 1 - p.y, p.x, p.c, j, 1)
        wire.put(h, h, p.xn, self.sem("yx", b, j))
        if j == PIECES - 1:
            self.share(b, 1, p.y, 1 - p.x)
            self.share(b, 2, 1 - p.y, p.x)

    def last(self, b, j):
        p, wire = self.place, self.wire
        wire.got(self.ref(b, 1 - p.y, 1 - p.x, p.c, j, 0), self.sem("xy", b, j), p.yn)
        wire.got(self.ref(b, 1 - p.y, 1 - p.x, p.c, j, 1), self.sem("yx", b, j), p.xn)
        if j == PIECES - 1:
            self.share(b, 3, 1 - p.y, 1 - p.x)

    def done(self, b):
        p, wire = self.place, self.wire
        for k, y, x in ((0, p.y, p.x), (1, p.y, 1 - p.x), (2, 1 - p.y, p.x), (3, 1 - p.y, 1 - p.x)):
            wire.got(self.block(b, y, x, 1 - p.c), self.core + b * 4 + k, p.core)


class Scatter:
    def __init__(self, wire, place, grad, bufs, out, first):
        self.wire, self.place, self.grad, self.out, self.first = wire, place, grad, out, first
        self.SB, self.CR, self.DR, self.NR, self.ZR, self.R, self.FR = bufs
        self.rows = self.SB.shape[3]
        self.piece = self.rows // PIECES
        self.half = self.piece // 2
        count = 2 * PIECES
        self.core = wire.take(8)
        self.sems = {k: wire.take(count) for k in ("da", "db", "xa", "xb", "ya", "yb", "u", "v", "d")}
        self.sent = []

    def sem(self, kind, b, j):
        return self.sems[kind] + b * PIECES + j

    def block(self, b, y, x, c, j=0, size=None):
        start = self.rows * ((b * 2 + y) * 4 + x * 2 + c) + j * self.piece
        return self.grad.at[pl.ds(many(start, 16), self.rows if size is None else size)]

    def give(self, ready):
        p = self.place
        while len(self.sent) < 8 and (2 * len(self.sent) + 2) * self.rows <= ready:
            i = len(self.sent)
            b, y, x = i // 4, i // 2 % 2, i % 2
            src = self.block(b, y, x, 1 - p.c)
            self.sent.append(self.wire.put(src, self.CR.at[b, y, x], p.core, self.core + i))

    def given(self):
        self.wire.left(self.sent)

    def take(self, b, y, x):
        self.wire.got(self.CR.at[b, y, x], self.core + b * 4 + y * 2 + x, self.place.core)

    def span(self, j, h=None):
        if h is None:
            return pl.ds(j * self.piece, self.piece)
        return pl.ds(j * self.piece + h * self.half, self.half)

    def add_core(self, b, y, x, j):
        mine = self.block(b, y, x, self.place.c, j, self.piece)
        v = mine[...].astype(F32) + self.CR[b, y, x, self.span(j)].astype(F32)
        self.SB[b, y, x, self.span(j)] = v.astype(BF16)

    def add_pass(self, b, y, x, j, h):
        at = self.span(j, h)
        v = self.SB[b, y, x, at].astype(F32) + self.DR[b, h, pl.ds(j * self.half, self.half)].astype(F32)
        self.SB[b, y, x, at] = v.astype(BF16)

    def add_plane(self, b, j):
        p, at = self.place, self.span(j)
        self.R[b, at] = (self.SB[b, p.y, p.x, at].astype(F32) + self.NR[b, 0, at].astype(F32)
                         + self.NR[b, 1, at].astype(F32))

    def back(self, b, j):
        at = self.span(j)
        self.SB[b, self.place.y, self.place.x, at] = self.R[b, at].astype(BF16)

    def add_far(self, b, j):
        at = self.span(j)
        self.R[b, at] += self.ZR[b, 0, at].astype(F32)

    def final(self, b, j):
        at = self.span(j)
        v = self.R[b, at] + (self.ZR[b, 0, at].astype(F32) + self.ZR[b, 1, at].astype(F32))
        if self.straight(b, j):
            v = v + self.FR[...].astype(F32)
        self.out[at] = v

    def straight(self, b, j):
        return self.first == 0 and b == 1 and j == PIECES - 1

    def step(self, k, b, j):
        p, wire = self.place, self.wire
        y, x = p.y, p.x
        owner = self.first + b
        far, mid = (0, 1) if self.first == 2 else (3, 2)
        if k == 0:
            self.add_core(b, 1 - y, 1 - x, j)
            at = pl.ds(j * self.half, self.half)
            src = self.SB.at[b, 1 - y, 1 - x]
            wire.put(src.at[self.span(j, 0)], self.DR.at[b, 0, at], p.yn, self.sem("da", b, j))
            wire.put(src.at[self.span(j, 1)], self.DR.at[b, 1, at], p.xn, self.sem("db", b, j))
        elif k == 1:
            self.add_core(b, y, 1 - x, j)
            at = self.span(j, 1)
            wire.put(self.SB.at[b, y, 1 - x, at], self.NR.at[b, 0, at], p.xn, self.sem("xb", b, j))
            self.add_core(b, 1 - y, x, j)
            at = self.span(j, 0)
            wire.put(self.SB.at[b, 1 - y, x, at], self.NR.at[b, 1, at], p.yn, self.sem("ya", b, j))
            self.add_core(b, y, x, j)
        elif k == 2:
            got = pl.ds(j * self.half, self.half)
            wire.got(self.DR.at[b, 0, got], self.sem("da", b, j), p.yn)
            self.add_pass(b, y, 1 - x, j, 0)
            at = self.span(j, 0)
            wire.put(self.SB.at[b, y, 1 - x, at], self.NR.at[b, 0, at], p.xn, self.sem("xa", b, j))
            wire.got(self.DR.at[b, 1, got], self.sem("db", b, j), p.xn)
            self.add_pass(b, 1 - y, x, j, 1)
            at = self.span(j, 1)
            wire.put(self.SB.at[b, 1 - y, x, at], self.NR.at[b, 1, at], p.yn, self.sem("yb", b, j))
        elif k == 3:
            wire.got(self.NR.at[b, 0, self.span(j, 1)], self.sem("xb", b, j), p.xn)
            wire.got(self.NR.at[b, 1, self.span(j, 0)], self.sem("ya", b, j), p.yn)
            wire.got(self.NR.at[b, 0, self.span(j, 0)], self.sem("xa", b, j), p.xn)
            wire.got(self.NR.at[b, 1, self.span(j, 1)], self.sem("yb", b, j), p.yn)
            self.add_plane(b, j)
            at = self.span(j)
            mine = self.SB.at[b, y, x, at]
            side = 2 * self.first + 1 - owner
            if self.straight(b, j):
                wire.when(p.z != owner, lambda: self.back(b, j))
                peer = p.at(owner, y, x, p.c)
                wire.put(mine, self.FR, peer, self.sem("u", b, j), when=p.z == far)
                wire.put(mine, self.ZR.at[b, 0, at], peer, self.sem("v", b, j), when=p.z == mid)
            else:
                wire.when((p.z == far) | (p.z == side), lambda: self.back(b, j))
                wire.put(mine, self.ZR.at[b, 0, at], p.pair, self.sem("u", b, j), when=p.z == far)
            wire.put(mine, self.ZR.at[b, 1, at], p.pair, self.sem("d", b, j), when=p.z == side)
        elif k == 4:
            if self.straight(b, j):
                return
            at = self.span(j)

            def on():
                self.add_far(b, j)
                self.back(b, j)

            wire.got(self.ZR.at[b, 0, at], self.sem("u", b, j), p.pair, when=p.z == mid)
            wire.when(p.z == mid, on)
            peer = p.at(owner, y, x, p.c)
            wire.put(self.SB.at[b, y, x, at], self.ZR.at[b, 0, at], peer, self.sem("v", b, j), when=p.z == mid)
        else:
            at = self.span(j)
            wire.got(self.ZR.at[b, 0, at], self.sem("v", b, j), p.gate, when=p.z == owner)
            wire.got(self.ZR.at[b, 1, at], self.sem("d", b, j), p.pair, when=p.z == owner)
            if self.straight(b, j):
                wire.got(self.FR, self.sem("u", b, j), p.gate, when=p.z == owner)
            wire.when(p.z == owner, lambda: self.final(b, j))

    @staticmethod
    def scratch(rows, channels):
        return [
            ((2, 2, 2, rows, channels), BF16),
            ((2, 2, 2, rows, channels), BF16),
            ((2, 2, rows // 2, channels), BF16),
            ((2, 2, rows, channels), BF16),
            ((2, 2, rows, channels), BF16),
            ((2, rows, channels), F32),
            ((rows // PIECES, channels), BF16),
        ]


class Halo:
    def __init__(self, wire, place, buf):
        self.wire, self.place, self.buf = wire, place, buf
        self.up, self.down = wire.take(), wire.take()

    def send(self):
        p, wire, buf = self.place, self.wire, self.buf
        last = buf.shape[0] - 1
        wire.put(buf.at[1], buf.at[last], (p.img, p.sp - 1), self.up, when=p.sp > 0)
        wire.put(buf.at[last - 1], buf.at[0], (p.img, p.sp + 1), self.down, when=p.sp < 3)
        wire.when(p.sp == 0, lambda: self.clear(0))
        wire.when(p.sp == 3, lambda: self.clear(last))

    def clear(self, row):
        self.buf[row] = jnp.zeros_like(self.buf[row])

    def wait(self):
        p, wire, buf = self.place, self.wire, self.buf
        last = buf.shape[0] - 1
        wire.got(buf.at[last], self.up, (p.img, p.sp + 1), when=p.sp < 3)
        wire.got(buf.at[0], self.down, (p.img, p.sp - 1), when=p.sp > 0)


class BandSum:
    def __init__(self, wire, place, slots):
        self.wire, self.place, self.slots = wire, place, slots
        self.first = wire.take(3)

    def send(self):
        p = self.place
        for k in range(3):
            self.wire.put(self.slots.at[p.sp], self.slots.at[p.sp], p.sps[k], self.first + k)

    def wait(self):
        for k in range(3):
            slot = self.slots.at[self.place.sp_off(3 - k)]
            self.wire.got(slot, self.first + k, self.place.sps[k])

    def total(self):
        return self.slots[0] + self.slots[1] + self.slots[2] + self.slots[3]


class SplitSum:
    def __init__(self, wire, place, slots):
        self.wire, self.place, self.slots = wire, place, slots
        self.sems = wire.take(3)

    def send(self):
        p, s = self.place, self.slots
        self.wire.put(s.at[1 - p.c], s.at[2], p.core, self.sems)

    def add(self, out, a, b):
        self.slots[out] = self.slots[a] + self.slots[b]

    def cross(self):
        p, s = self.place, self.slots
        self.wire.got(s.at[2], self.sems, p.core)
        self.add(3, p.c, 2)
        self.wire.put(s.at[3], s.at[4], p.xn, self.sems + 1)

    def back(self):
        p, s = self.place, self.slots
        self.wire.got(s.at[4], self.sems + 1, p.xn)
        self.add(5 + p.c, 3, 4)
        self.wire.put(s.at[5 + p.c], s.at[5 + p.c], p.core, self.sems + 2)

    def wait(self):
        self.wire.got(self.slots.at[6 - self.place.c], self.sems + 2, self.place.core)


class Spread:
    def __init__(self, wire, place, slots):
        self.wire, self.place, self.slots = wire, place, slots
        self.z, self.y = wire.take(3), wire.take()

    def send(self):
        p = self.place
        for k in range(3):
            self.wire.put(self.slots.at[p.y, p.z], self.slots.at[p.y, p.z], p.zs[k], self.z + k)

    def turn(self):
        p = self.place
        for k in range(3):
            self.wire.got(self.slots.at[p.y, p.z_off(3 - k)], self.z + k, p.zs[k])
        self.wire.put(self.slots.at[p.y], self.slots.at[p.y], p.yn, self.y)

    def wait(self):
        self.wire.got(self.slots.at[1 - self.place.y], self.y, self.place.yn)


def group_matrix(channels, across, first):
    per = channels // NORM_GROUPS
    shape = (channels, 128) if across else (128, channels)
    c = lax.broadcasted_iota(jnp.int32, shape, 0 if across else 1)
    g = lax.broadcasted_iota(jnp.int32, shape, 1 if across else 0)
    return (lax.div(c, per) + first == g).astype(F32)


def exact_dot(a, b):
    return jnp.dot(a, b, precision=HIGHEST, preferred_element_type=F32)


def pack(a, b):
    return exact_dot(a, group_matrix(a.shape[1], True, 0)) + exact_dot(b, group_matrix(b.shape[1], True, 64))


def unpack(v, channels):
    return exact_dot(v, group_matrix(channels, False, 0)), exact_dot(v, group_matrix(channels, False, 64))


def sigmoid(v):
    return 0.5 * jnp.tanh(0.5 * v) + 0.5


def slope(v):
    s = sigmoid(v)
    return s * (1.0 + v * (1.0 - s))


def thirds(v):
    high = v.astype(BF16)
    v = v - high.astype(F32)
    mid = v.astype(BF16)
    return high, mid, (v - mid.astype(F32)).astype(BF16)


def fold(v):
    return jnp.sum(v.reshape(v.shape[0] // 8, 8, v.shape[1]), axis=0)


def plus(total, v):
    return v if total is None else total + v


class Step:
    def __init__(self, place, wire, refs, image_total):
        self.__dict__.update(refs)
        self.inverse = 1.0 / image_total
        self.p, self.w = place, wire
        self.images, self.rows_full, self.side_full, self.channels = self.IMG.shape
        self.rim, _, self.side, _ = self.PO.shape
        self.rows = self.rim - 2
        self.per = self.channels // NORM_GROUPS
        self.tiles = self.channels // 128
        shard = self.cw.shape[0]
        self.kernel_rows = 16 * shard
        self.g = Gather(wire, place, self.W, shard)
        self.r2 = Scatter(wire, place, self.DW, [self.__dict__["RA%d" % i] for i in range(6)] + [None], self.RES, 2)
        self.r1 = Scatter(wire, place, self.DW, [self.__dict__["RB%d" % i] for i in range(7)], self.RES, 0)
        self.halo_p = Halo(wire, place, self.PO)
        self.halo_g = Halo(wire, place, self.G)
        self.halo_a = Halo(wire, place, self.A2)
        self.halo_b = Halo(wire, place, self.GB)
        self.aff_img = Spread(wire, place, self.AFS.at[place.sp])
        self.aff_sp = BandSum(wire, place, self.AFS)
        self.sum1 = BandSum(wire, place, self.ST1)
        self.sum2 = BandSum(wire, place, self.ST2)
        self.sum3 = BandSum(wire, place, self.ST3)
        self.sum4 = BandSum(wire, place, self.ST4)
        self.psum = SplitSum(wire, place, self.PS)
        self.proj = SplitSum(wire, place, self.PX)
        self.esum = SplitSum(wire, place, self.PE)
        self.asum = BandSum(wire, place, self.AFR)
        self.spread_g = Spread(wire, place, self.GPA)
        self.ea = wire.take(6), wire.take()
        self.ez = wire.take(3), wire.take(4)
        self.afy = wire.take()
        self.afz = wire.take(3)


    def loop(self, body, first=0, last=None):
        def one(n, _):
            body(n)
            return 0

        lax.fori_loop(first, self.images if last is None else last, one, 0)

    def width(self, n, r):
        return jnp.where(self.p.sp * self.rows_full + r < self.ext[0, n], self.ext[1, n], 0)

    def half_width(self, n, r):
        inside = self.p.sp * self.rows + r < lax.div(self.ext[0, n], 2)
        return jnp.where(inside, lax.div(self.ext[1, n], 2), 0)

    def cols(self, side):
        return lax.broadcasted_iota(jnp.int32, (side, self.channels), 0)

    def at(self, k, n):
        return self.AB[k, pl.ds(n, 1)]

    def clear_sums(self):
        self.SS[...] = jnp.zeros_like(self.SS)

    def add_sums(self, n, s, q):
        self.SS[pl.ds(n, 1)] += jnp.sum(s, axis=0, keepdims=True)
        self.SS[pl.ds(n + 16, 1)] += jnp.sum(q, axis=0, keepdims=True)

    def eslot(self, z, y):
        rows = self.ew.shape[0]
        start = ((z * 2 + y) * 4 + self.p.sp) * rows
        return self.EZ.at[pl.ds(many(start, 32), rows)]


    def load(self):
        self.copies = [
            pltpu.make_async_copy(self.img, self.IMG, self.lsem.at[0]),
            pltpu.make_async_copy(self.cot, self.COT, self.lsem.at[1]),
        ]
        late = ((self.cm_in, self.CM), (self.ce_in, self.CE), (self.em_in, self.EM), (self.ee_in, self.EE))
        for i, (src, dst) in enumerate(late):
            self.copies.append(pltpu.make_async_copy(src, dst, self.lsem.at[2 + i]))
        for copy in self.copies:
            copy.start()

    def loaded(self, k):
        self.copies[k].wait()

    def own_weights(self):
        p = self.p
        rows = self.cw.shape[0]
        self.W[pl.ds(many(rows * (p.img * 4 + p.sp), 16), rows)] = self.cw[...].astype(BF16)
        low = self.aff[...].astype(BF16).astype(F32)
        self.AFS[p.sp, p.y, p.z] = low

    def own_embedding(self):
        p = self.p
        rows = self.ew.shape[0]
        zero = jnp.zeros((rows, self.EZ.shape[1]), BF16)
        for i in range(8):
            for sp in p.sps:
                self.EZ[pl.ds(many((i * 4 + sp[1]) * rows, 32), rows)] = zero
        self.EZ[pl.ds(many((p.img * 4 + p.sp) * rows, 32), rows)] = self.ew[...].astype(BF16)
        self.EP[...] = jnp.zeros_like(self.EP)
        self.EP[pl.ds(0, self.images)] = self.emb[...].astype(F32)
        e = self.EP[...]
        act = (e * sigmoid(e)).astype(BF16)
        self.EA[...] = act
        for i in range(8):
            self.ET[i // 2, i % 2] = act[:, i * 128 : i * 128 + 128]
        for y in range(2):
            self.EZT[y, p.z] = self.ET[p.z, y]

    def counts(self):
        self.CNT[...] = jnp.ones_like(self.CNT)

        def one(n):
            h, w = self.ext[0, n], self.ext[1, n]
            for i, number in enumerate((h * w, lax.div(h, 2) * lax.div(w, 2))):
                number = jnp.full((1, self.channels), number * self.per, jnp.int32)
                self.CNT[i, pl.ds(n, 1)] = number.astype(F32)

        self.loop(one)


    def ez_send(self):
        p = self.p
        for k in range(3):
            self.w.put(self.eslot(p.z, p.y), self.eslot(p.z, p.y), p.zs[k], self.ez[0] + k)

    def ez_turn(self):
        p = self.p
        for k in range(3):
            self.w.got(self.eslot(p.z_off(3 - k), p.y), self.ez[0] + k, p.zs[k])
        for k in range(4):
            self.w.put(self.eslot(k, p.y), self.eslot(k, p.y), p.yn, self.ez[1] + k)

    def ez_wait(self):
        for k in range(4):
            self.w.got(self.eslot(k, 1 - self.p.y), self.ez[1] + k, self.p.yn)


    def ea_send(self):
        p = self.p
        for k in range(3):
            for y in range(2):
                src = self.ET.at[p.z_off(k + 1), y]
                self.w.put(src, self.EZT.at[y, p.z], p.zs[k], self.ea[0] + 2 * k + y)

    def ea_turn(self):
        p = self.p
        for k in range(3):
            for y in range(2):
                self.w.got(self.EZT.at[y, p.z_off(3 - k)], self.ea[0] + 2 * k + y, p.zs[k])
        self.w.put(self.EZT.at[1 - p.y], self.EY, p.yn, self.ea[1])

    def ea_wait(self):
        self.w.got(self.EY, self.ea[1], self.p.yn)

    def project(self):
        v = jnp.dot(self.EA[...], self.EZ[...], preferred_element_type=F32)
        self.PX[0] = v[:, : self.channels]
        self.PX[1] = v[:, self.channels :]


    def stats_one(self, first, last):
        col = self.cols(self.side_full)

        def one(n):
            s = q = None
            for r in range(self.rows_full):
                v = jnp.where(col < self.width(n, r), self.IMG[n, r].astype(F32), 0.0)
                s, q = plus(s, fold(v)), plus(q, fold(v * v))
            self.add_sums(n, s, q)

        self.loop(one, first, last)

    def stats_one_end(self):
        self.ST1[self.p.sp] = pack(self.SS[:16], self.SS[16:])

    def affine_rows(self):
        for s in range(4):
            for y in range(2):
                for z in range(4):
                    self.AFF[pl.ds(z * 2 + y, 1), pl.ds(s * 128, 128)] = self.AFS[s, y, z]

    def moments(self, total, count, mean_ref, inv_ref):
        sums, squares = unpack(total, self.channels)
        mean = sums / count
        inv = lax.rsqrt(squares / count - mean * mean + EPSILON)
        mean_ref[...] = mean
        inv_ref[...] = inv
        return mean, inv

    def norm_one(self):
        mean, inv = self.moments(self.sum1.total(), self.CNT[0], self.MI.at[0], self.MI.at[1])
        self.AB[0] = inv * self.AFF[0:1]
        self.AB[1] = self.AFF[1:2] - mean * self.AB[0]

    def pool(self, hrs, first=0, last=None):
        col = self.cols(self.side_full)

        def one(n):
            for i, hr in enumerate(hrs):
                act = raw = None
                for k in range(2):
                    r = 2 * hr + k
                    inside = col < self.width(n, r)
                    u = self.IMG[n, r].astype(F32)
                    v = u * self.at(0, n) + self.at(1, n)
                    act = plus(act, jnp.where(inside, v * sigmoid(v), 0.0))
                    raw = plus(raw, jnp.where(inside, u, 0.0))
                for t in range(self.tiles):
                    lanes = slice(t * 128, t * 128 + 128)
                    self.T[i, t] = act[:, lanes]
                    self.T[i + 2, t] = raw[:, lanes]
            even, odd = pl.ds(0, self.side, stride=2), pl.ds(1, self.side, stride=2)
            for i, hr in enumerate(hrs):
                for t in range(self.tiles):
                    lanes = pl.ds(t * 128, 128)
                    v = self.T[i, t, even] + self.T[i, t, odd]
                    self.PO[hr + 1, n, :, lanes] = (v * 0.25).astype(BF16)
                    v = self.T[i + 2, t, even] + self.T[i + 2, t, odd]
                    self.SKIP[hr, n, :, lanes] = v * 0.25

        self.loop(one, first, last)


    def sides(self, src):
        return self.XP if src is self.PO else self.XA if src is self.A2 else self.XG

    def shift(self, src, rows):
        col = self.cols(self.side)
        X = self.sides(src)

        def one(n):
            for r in rows:
                v = src[r, n].astype(F32)
                X[0, r, n] = jnp.where(col > 0, pltpu.roll(v, 1, 0), 0.0).astype(BF16)
                v = jnp.where(col < self.side - 1, pltpu.roll(v, self.side - 1, 0), 0.0)
                X[1, r, n] = v.astype(BF16)

        self.loop(one)

    def conv(self, center, base, row, back):
        count = self.ACC.shape[0]
        size = count * self.images * self.side
        total = None
        for a in range(3):
            for b in range(3):
                da, db = (2 - a, 2 - b) if back else (a, b)
                src = center if db == 1 else self.sides(center).at[0 if db == 0 else 1]
                left = src[pl.ds(row + da, count)].reshape(size, self.channels)
                tap = self.W[pl.ds(base + (3 * a + b) * self.channels, self.channels)]
                dims = (((1,), (1 if back else 0,)), ((), ()))
                total = plus(total, lax.dot_general(left, tap, dims, preferred_element_type=F32))
        self.ACC[...] = total.reshape(self.ACC.shape)

    def tap_grad(self, center, grads, t):
        a, b = divmod(t, 3)
        size = self.rows * self.images * self.side
        src = center if b == 1 else self.sides(center).at[0 if b == 0 else 1]
        left = src[pl.ds(a, self.rows)].reshape(size, self.channels)
        right = grads[pl.ds(1, self.rows)].reshape(size, self.channels)
        self.DW[pl.ds(t * self.channels, self.channels)] = lax.dot_general(
            left, right, (((0,), (0,)), ((), ())), preferred_element_type=F32
        ).astype(BF16)

    def mask_cot(self):
        col = self.cols(self.side)
        self.C2[...] = jnp.zeros_like(self.C2)

        def one(n):
            total = None
            for r in range(self.rows):
                v = jnp.where(col < self.half_width(n, r), self.COT[n, r].astype(F32), 0.0)
                self.G[r + 1, n] = v.astype(BF16)
                total = plus(total, fold(v))
            self.C2[...] += total

        self.loop(one)

    def inner_conv(self, row):
        col = self.cols(self.side)
        self.conv(self.PO, 0, row, False)

        def one(n):
            s = q = None
            for r in range(self.ACC.shape[0]):
                v = self.ACC[r, n] + self.AFF[2:3]
                v = jnp.where(col < self.half_width(n, row + r), v, 0.0).astype(BF16)
                self.INN[row + r, n] = v
                v = v.astype(F32)
                s, q = plus(s, fold(v)), plus(q, fold(v * v))
            self.add_sums(n, s, q)

        self.loop(one)


    def stats_two(self):
        self.ST2[self.p.sp] = pack(self.SS[:16], self.SS[16:])

    def norm_two(self):
        self.MI[4] = self.PX[5] + (self.AFF[3:4] + 1.0)
        self.MI[5] = self.PX[6] + self.AFF[4:5]
        mean, inv = self.moments(self.sum2.total(), self.CNT[1], self.MI.at[2], self.MI.at[3])
        self.AB[2] = inv
        self.AB[3] = -mean * inv
        self.AB[4] = self.AFF[5:6] * self.MI[4]
        self.AB[5] = self.AFF[6:7] * self.MI[4] + self.MI[5]

    def xhat_two(self, r, n):
        return self.INN[r, n].astype(F32) * self.at(2, n) + self.at(3, n)

    def activate(self, rs):
        col = self.cols(self.side)

        def one(n):
            for r in rs:
                v = self.xhat_two(r, n) * self.at(4, n) + self.at(5, n)
                v = jnp.where(col < self.half_width(n, r), v * sigmoid(v), 0.0)
                self.A2[r + 1, n] = v.astype(BF16)

        self.loop(one)

    def mixed_grad(self, row):
        col = self.cols(self.side)
        self.conv(self.G, self.kernel_rows, row, True)

        def one(n):
            s = q = None
            for r in range(self.ACC.shape[0]):
                v = self.ACC[r, n].astype(BF16).astype(F32)
                xhat = self.xhat_two(row + r, n)
                mixed = xhat * self.at(4, n) + self.at(5, n)
                v = jnp.where(col < self.half_width(n, row + r), v * slope(mixed), 0.0)
                self.GM[row + r, n] = v
                s, q = plus(s, fold(v)), plus(q, fold(v * xhat))
            self.add_sums(n, s, q)

        self.loop(one)

    def sums_two_back(self):
        p1, p2 = self.SS[:16], self.SS[16:]
        self.PS[0] = p1
        self.PS[1] = p2
        self.ST3[self.p.sp] = pack(p1 * self.AB[4], p2 * self.AB[4])
        scale = self.MI[4]
        self.AFP[0:3] = jnp.zeros_like(self.AFP[0:3])
        self.AFP[3:4] = jnp.sum(self.AFF[5:6] * p2 + self.AFF[6:7] * p1, axis=0, keepdims=True)
        self.AFP[4:5] = jnp.sum(p1, axis=0, keepdims=True)
        self.AFP[5:6] = jnp.sum(scale * p2, axis=0, keepdims=True)
        self.AFP[6:7] = jnp.sum(scale * p1, axis=0, keepdims=True)
        self.AFP[7:8] = jnp.sum(self.C2[...], axis=0, keepdims=True)

    def output(self, row):
        col = self.cols(self.side)
        self.conv(self.A2, self.kernel_rows, row, False)

        def one(n):
            for r in range(self.ACC.shape[0]):
                v = self.ACC[r, n] + self.AFF[7:8]
                v = jnp.where(col < self.half_width(n, row + r), v, 0.0)
                self.OUTV[n, row + r] = (self.SKIP[row + r, n] + v).astype(BF16)

        self.loop(one)

    def project_grad(self):
        p1, p2 = self.PS[5], self.PS[6]
        scale = self.AFF[5:6] * p2 + self.AFF[6:7] * p1
        self.GP[0] = scale
        self.GP[1] = p1
        self.GPA[self.p.y, self.p.z, 0] = scale.astype(BF16)
        self.GPA[self.p.y, self.p.z, 1] = p1.astype(BF16)

    def norm_two_back(self):
        first, second = unpack(self.sum3.total(), self.channels)
        inv = self.AB[2]
        self.AB[6] = inv * self.AB[4]
        self.AB[7] = inv * (first / self.CNT[1])
        self.AB[8] = inv * (second / self.CNT[1])
        self.C1[...] = jnp.zeros_like(self.C1)

    def inner_grad(self, rs):
        col = self.cols(self.side)

        def one(n):
            total = None
            for r in rs:
                v = self.GM[r, n] * self.at(6, n) - self.at(7, n) - self.xhat_two(r, n) * self.at(8, n)
                v = jnp.where(col < self.half_width(n, r), v, 0.0).astype(BF16)
                self.GB[r + 1, n] = v
                total = plus(total, fold(v.astype(F32)))
            self.C1[...] += total

        self.loop(one)


    def embedding_part(self):
        gp = jnp.concatenate([self.GP[0], self.GP[1]], axis=1)
        gp = jnp.concatenate(thirds(gp), axis=0)
        v = lax.dot_general(gp, self.EZ[...], (((1,), (1,)), ((), ())), preferred_element_type=F32)
        v = v[:16] + v[16:32] + v[32:]
        self.PE[0] = v[:, : self.channels]
        self.PE[1] = v[:, self.channels :]

    def embedding_grad(self):
        v = jnp.concatenate([self.PE[5], self.PE[6]], axis=1)[: self.images]
        self.ge[...] = v * slope(self.EP[pl.ds(0, self.images)])

    def embedding_weights(self):
        p = self.p
        left = jnp.concatenate([self.EZT[p.y].reshape(64, 128), self.EY[...].reshape(64, 128)], axis=0)
        for i in range(2):
            right = [self.GPA[y, :, i].reshape(64, self.channels) for y in (p.y, 1 - p.y)]
            self.EW[:, pl.ds(i * self.channels, self.channels)] = lax.dot_general(
                left, jnp.concatenate(right, axis=0), (((0,), (0,)), ((), ())), preferred_element_type=F32
            )
        self.ewg[...] = self.EW[pl.ds(many(p.sp * 32, 32), 32)]


    def doubled(self, value, slot):
        for t in range(self.tiles):
            v = value[:, t * 128 : t * 128 + 128]
            self.T[slot, t, pl.ds(0, self.side, stride=2)] = v
            self.T[slot, t, pl.ds(1, self.side, stride=2)] = v
        return jnp.concatenate([self.T[slot, t] for t in range(self.tiles)], axis=1)

    def prepare_one_back(self):
        self.AB[2] = self.MI[1]
        self.AB[3] = -self.MI[0] * self.MI[1]
        self.clear_sums()

    def norm_one_grad(self, n, r, grad):
        v = self.IMG[n, r].astype(F32)
        xhat = v * self.at(2, n) + self.at(3, n)
        v = v * self.at(0, n) + self.at(1, n)
        return xhat, jnp.where(self.cols(self.side_full) < self.width(n, r), grad * slope(v), 0.0)

    def pooled_conv(self, row):
        self.conv(self.GB, 0, row, True)
        self.GM[pl.ds(row, self.ACC.shape[0])] = self.ACC[...] * 0.25

    def pooled_grad(self, row, first=0, last=None):
        def one(n):
            s = q = None
            for r in range(self.ACC.shape[0]):
                grad = self.doubled(self.GM[row + r, n], r)
                for k in range(2):
                    xhat, v = self.norm_one_grad(n, 2 * (row + r) + k, grad)
                    s, q = plus(s, fold(v)), plus(q, fold(v * xhat))
            self.add_sums(n, s, q)

        self.loop(one, first, last)

    def sums_one_back(self):
        self.AFP[0:1] = jnp.sum(self.SS[16:32], axis=0, keepdims=True)
        self.AFP[1:2] = jnp.sum(self.SS[0:16], axis=0, keepdims=True)
        self.AFP[2:3] = jnp.sum(self.C1[...], axis=0, keepdims=True)
        self.AFZ[self.p.z] = self.AFP[...]
        self.ST4[self.p.sp] = pack(self.SS[:16] * self.AFF[0:1], self.SS[16:] * self.AFF[0:1])

    def affine_z(self):
        for k in range(3):
            self.w.put(self.AFZ.at[self.p.z], self.AFZ.at[self.p.z], self.p.zs[k], self.afz + k)

    def affine_sp(self):
        for k in range(3):
            self.w.got(self.AFZ.at[self.p.z_off(3 - k)], self.afz + k, self.p.zs[k])
        self.add_affine()
        self.asum.send()

    def add_affine(self):
        self.AFR[self.p.sp] = self.AFZ[0] + self.AFZ[1] + self.AFZ[2] + self.AFZ[3]

    def affine_y(self):
        self.asum.wait()
        self.total_affine()
        self.w.put(self.AFY.at[0], self.AFY.at[1], self.p.yn, self.afy)

    def total_affine(self):
        self.AFY[0] = self.asum.total()

    def affine_done(self):
        self.w.got(self.AFY.at[1], self.afy, self.p.yn)
        self.own_affine()

    def own_affine(self):
        self.AFP[...] = self.AFY[0] + self.AFY[1]
        tile = self.AFP[:, pl.ds(many(self.p.sp * 128, 128), 128)]
        line = lax.broadcasted_iota(jnp.int32, tile.shape, 0) == self.p.img
        self.ag[...] = jnp.sum(jnp.where(line, tile, 0.0), axis=0, keepdims=True)

    def norm_one_back(self):
        first, second = unpack(self.sum4.total(), self.channels)
        self.AB[4] = self.MI[1] * self.AFF[0:1]
        self.AB[5] = self.MI[1] * (first / self.CNT[0])
        self.AB[6] = self.MI[1] * (second / self.CNT[0])

    def image_grad(self, first, last):
        col = self.cols(self.side_full)

        def one(n):
            for hr in range(self.rows):
                grad = self.doubled(self.GM[hr, n], 0)
                cell = self.doubled(self.COT[n, hr].astype(F32) * 0.25, 1)
                for k in range(2):
                    r = 2 * hr + k
                    xhat, v = self.norm_one_grad(n, r, grad)
                    v = v * self.at(4, n) - self.at(5, n) - xhat * self.at(6, n) + cell
                    self.IMG[n, r] = jnp.where(col < self.width(n, r), v, 0.0).astype(BF16)

        self.loop(one, first, last)


    def update(self, weight, moment, average, total, new_weight, new_moment, new_average):
        mean = total[...] * self.inverse
        m = MOMENTUM * moment[...] + mean
        w = weight[...] - LEARN_RATE * (mean + MOMENTUM * m)
        new_weight[...] = w
        new_moment[...] = m
        new_average[...] = EMA_DECAY * average[...] + (1.0 - EMA_DECAY) * w

    def update_small(self):
        self.loaded(4)
        self.loaded(5)
        self.update(self.ew, self.EM, self.EE, self.ewg, self.new, self.nem, self.nee)
        self.update(self.aff, self.am, self.ae, self.ag, self.naw, self.nam, self.nae)

    def update_conv(self):
        self.loaded(2)
        self.loaded(3)
        step = 32
        arrays = (self.cw, self.CM, self.CE, self.RES, self.ncw, self.ncm, self.nce)

        def piece(i, _):
            at = pl.ds(pl.multiple_of(i * step, step), step)
            self.update(*(r.at[at] for r in arrays))
            return 0

        lax.fori_loop(0, self.cw.shape[0] // step, piece, 0)


def mix(works, ticks):
    done = 0
    for i, work in enumerate(works):
        work()
        upto = (i + 1) * len(ticks) // len(works)
        for tick in ticks[done:upto]:
            tick()
        done = upto
    for tick in ticks[done:]:
        tick()


def pairs(*lists):
    return [item for group in zip(*lists) for item in group]


def schedule(s):
    p, g, z = s.p, s.g, s.p.z
    pieces = list(range(PIECES))
    edge, middle = (0, s.rows - 1), range(1, s.rows - 1)
    inside, outside = range(1, s.rim - 1), (0, s.rim - 1)
    lead = choose(z == 0, 0, 1)
    other = choose(z == 1, 0, 1)
    tail = 1 - lead
    lead_two = choose(z == 3, 3, 2)
    tail_two = 5 - lead_two
    n = s.images

    def come(b, j, when=None):
        def run():
            g.arrive(b, j, when)
            g.own(b, j, when)

        return run

    def call(method, *args):
        return lambda: method(*args)

    def steps(scatter, k, b):
        return [call(scatter.step, k, b, j) for j in pieces]

    def run(calls):
        for item in calls:
            item()

    def taken(scatter, b):
        for yy in range(2):
            for xx in range(2):
                scatter.take(b, yy, xx)

    s.load()
    s.own_weights()
    s.w.greet(p)
    s.aff_img.send()
    for j in pieces:
        g.along(z, j, z < 2, z > 0)
        g.own(z, j, z < 2)
    s.own_embedding()
    s.counts()
    s.clear_sums()
    s.loaded(0)
    s.stats_one(0, n // 2)
    come(other, 0)()
    s.stats_one(n // 2, n)
    s.stats_one_end()
    s.sum1.send()
    s.aff_img.turn()
    come(other, 1)()
    g.turn(lead, 0)
    come(other, 2)()
    s.aff_img.wait()
    s.aff_sp.send()
    g.turn(lead, 1)
    for j in pieces:
        g.arrive(3, j, z == 2)
    come(0, 0, z >= 2)()
    g.turn(lead, 2)
    s.sum1.wait()
    s.aff_sp.wait()
    s.affine_rows()
    s.norm_one()
    s.ez_send()
    works = [call(s.pool, edge, i, i + 4) for i in range(0, n, 4)] + [s.halo_p.send]
    works += [call(s.pool, middle, i, i + 4) for i in range(0, n, 4)]
    works += [call(s.loaded, 1), s.mask_cot, call(s.shift, s.PO, inside)]
    ticks = [come(0, j, z >= 2) for j in pieces[1:]]
    ticks += [call(g.arrive, 2, j, z == 1) for j in pieces]
    ticks += pairs([call(g.last, lead, j) for j in pieces], [call(g.turn, tail, j) for j in pieces])
    mix(works, ticks)

    def next_two(j):
        g.arrive(2, j, z == 0)
        g.own(lead_two, j)

    def tail_two_on(j):
        g.arrive(tail_two, j, (z == 0) | (z == 3))
        g.own(tail_two, j)

    for j in pieces:
        g.arrive(3, j, z == 1)
    s.ez_turn()
    next_two(0)
    for j in pieces:
        g.last(tail, j)
    next_two(1)
    s.halo_p.wait()
    s.shift(s.PO, outside)
    for j in pieces:
        g.along(2, j, z == 2, z > 3)
    g.done(lead)
    g.done(tail)
    next_two(2)
    s.clear_sums()
    s.ea_send()
    s.inner_conv(0)
    s.ez_wait()
    s.project()
    s.proj.send()
    tail_two_on(0)
    s.inner_conv(2)
    s.proj.cross()
    s.stats_two()
    s.sum2.send()
    s.shift(s.G, inside)
    g.turn(lead_two, 0)
    g.turn(lead_two, 1)
    s.proj.back()
    s.sum2.wait()
    s.proj.wait()
    s.norm_two()
    s.activate(edge)
    s.halo_a.send()
    s.activate(middle)
    s.shift(s.A2, inside)
    tail_two_on(1)
    tail_two_on(2)
    g.turn(lead_two, 2)
    s.halo_g.send()
    s.ea_turn()

    order = [3, 4, 5, 0, 1, 2, 6, 7, 8]
    between = [
        [],
        [call(g.last, lead_two, 0), call(g.turn, tail_two, 0)],
        [s.halo_a.wait, call(s.shift, s.A2, outside)],
        [call(g.last, lead_two, 1), call(g.turn, tail_two, 1)],
        [call(g.last, lead_two, 2), call(g.turn, tail_two, 2)],
        [],
        [call(g.last, tail_two, 0)],
        [call(g.last, tail_two, 1)],
        [call(g.last, tail_two, 2), call(taken, s.r2, 0)] + steps(s.r2, 0, 0) + steps(s.r2, 1, 0),
    ]
    for i, t in enumerate(order):
        s.tap_grad(s.A2, s.G, t)
        if i >= 5:
            s.r2.give((t + 1) * s.channels if i > 5 else 6 * s.channels)
        run(between[i])

    s.halo_g.wait()
    s.shift(s.G, outside)
    s.clear_sums()
    g.done(2)
    g.done(3)
    s.output(0)
    s.mixed_grad(0)
    run(steps(s.r2, 2, 0))
    s.mixed_grad(2)
    s.sums_two_back()
    s.sum3.send()
    taken(s.r2, 1)
    run(steps(s.r2, 0, 1))
    run(steps(s.r2, 1, 1))
    s.psum.send()
    s.sum3.wait()
    s.norm_two_back()
    s.inner_grad(edge)
    s.halo_b.send()
    s.inner_grad(middle)
    s.psum.cross()
    s.r2.given()

    def tap_one(t):
        s.tap_grad(s.PO, s.GB, t)
        s.r1.give((t + 1) * s.channels)

    def r1(*which):
        for k, b, j in which:
            if j < PIECES:
                s.r1.step(k, b, j)

    between = [[item] for item in steps(s.r2, 2, 1)] + [[item] for item in steps(s.r2, 3, 0)]
    between += [
        [call(taken, s.r1, 0), call(r1, (0, 0, 0), (0, 0, 1))],
        [call(r1, (0, 0, 2), (1, 0, 0))],
        [call(s.r1.step, 1, 0, 1), s.psum.back],
    ]
    for t in range(9):
        tap_one(t)
        run(between[t])

    sent = s.w.started()
    s.output(2)
    s.halo_b.wait()
    s.shift(s.GB, range(s.rim))
    s.prepare_one_back()
    taken(s.r1, 1)
    r1((2, 0, 0), (0, 1, 0), (1, 0, 2))
    run(steps(s.r2, 3, 1))
    s.pooled_conv(0)
    r1((2, 0, 1), (0, 1, 1), (1, 1, 0))
    s.psum.wait()
    s.project_grad()
    s.spread_g.send()
    run(steps(s.r2, 4, 0))
    s.pooled_conv(2)
    r1((2, 0, 2), (0, 1, 2), (1, 1, 1))
    half = n // 2
    run(steps(s.r2, 4, 1))
    s.pooled_grad(0, 0, half)
    r1((2, 1, 0), (1, 1, 2), (3, 0, 0))
    s.pooled_grad(0, half, n)
    r1((2, 1, 1), (3, 0, 1))
    s.pooled_grad(2, 0, half)
    r1((2, 1, 2), (3, 0, 2))
    s.pooled_grad(2, half, n)
    s.sums_one_back()
    s.sum4.send()
    s.affine_z()
    r1((3, 1, 0), (4, 0, 0))
    s.spread_g.turn()
    s.embedding_part()
    s.esum.send()
    r1((3, 1, 1), (4, 0, 1))
    s.w.left(sent)
    s.sum4.wait()
    s.norm_one_back()
    r1((3, 1, 2), (4, 0, 2))
    quarter = n // 4
    s.image_grad(0, quarter)
    s.r1.step(4, 1, 0)
    s.image_grad(quarter, 2 * quarter)
    s.r1.step(4, 1, 1)
    s.affine_sp()
    s.esum.cross()
    s.image_grad(2 * quarter, 3 * quarter)
    s.esum.back()
    run(steps(s.r2, 5, 0))
    run(steps(s.r2, 5, 1))
    s.affine_y()
    s.image_grad(3 * quarter, n)
    run(steps(s.r1, 5, 0))
    s.spread_g.wait()
    s.ea_wait()
    s.embedding_weights()
    s.affine_done()
    s.esum.wait()
    s.embedding_grad()
    s.update_small()
    run(steps(s.r1, 5, 1))
    s.update_conv()
    s.w.close()


def whole_kernel(names, image_total, *refs):
    refs = dict(zip(names, refs))
    place = Place(lax.axis_index("img"), lax.axis_index("sp"))
    wire = Wire(refs.pop("ssem"), refs.pop("rsem"))
    schedule(Step(place, wire, refs, image_total))


def shapes(images, cotangent, conv_w, emb_w):
    n, rows_full, side_full, c = images
    _, rows, side, _ = cotangent
    shard = conv_w[0]
    rim = (rows + 2, n, side, c)
    band = (rows, n, side, c)
    out = dict(
        RES=(conv_w, F32), ag=((1, 128), F32), ewg=(emb_w, F32),
        CM=(conv_w, F32), CE=(conv_w, F32), EM=(emb_w, F32), EE=(emb_w, F32),
        COT=(cotangent, BF16), W=((32 * shard, c), BF16), EZ=((emb_w[1], emb_w[1]), BF16),
        PO=(rim, BF16), G=(rim, BF16), A2=(rim, BF16), GB=(rim, BF16), XP=((2,) + rim, BF16), XA=((2,) + rim, BF16), XG=((2,) + rim, BF16),
        INN=(band, BF16), SKIP=(band, F32), GM=(band, F32), ACC=((2,) + band[1:], F32),
        DW=((16 * shard, c), BF16), T=((4, c // 128, side_full, 128), F32), SS=((32, c), F32),
        CNT=((2, 16, c), F32), MI=((6, 16, c), F32), AB=((9, 16, c), F32), AFF=((8, c), F32), AFP=((8, c), F32),
        C1=((8, c), F32), C2=((8, c), F32), AFS=((4, 2, 4, 1, 128), F32), AFR=((4, 8, c), F32),
        AFY=((2, 8, c), F32), AFZ=((4, 8, c), F32), EP=((16, 2 * c), F32), EA=((16, 2 * c), BF16), ET=((4, 2, 16, 128), BF16), EZT=((2, 4, 16, 128), BF16),
        EY=((4, 16, 128), BF16),
        GPA=((2, 4, 2, 16, c), BF16), GP=((2, 16, c), F32), EW=((128, 2 * c), F32), PX=((7, 16, c), F32), PE=((7, 16, c), F32),
        ST1=((4, 16, 128), F32), ST2=((4, 16, 128), F32), ST3=((4, 16, 128), F32), PS=((7, 16, c), F32), ST4=((4, 16, 128), F32),
    )
    for k in "AB":
        for i, v in enumerate(Scatter.scratch(shard, c)):
            if k == "B" or i < 6:
                out["R%s%d" % (k, i)] = v
    return out


WIRES = 360
VM = pl.BlockSpec(memory_space=pltpu.VMEM)
ANY = pl.BlockSpec(memory_space=pl.ANY)
SM = pl.BlockSpec(memory_space=pltpu.SMEM)


def place_kernel(*refs):
    count = len(refs) // 2
    sem = refs[-1]
    copies = [pltpu.make_async_copy(refs[i], refs[count + i], sem.at[i]) for i in range(count)]
    for copy in copies:
        copy.start()
    for copy in copies:
        copy.wait()


def local_kernels(image_total, images, embedding, extent, cotangent, conv_w, emb_w, affine,
                  conv_mom, emb_mom, affine_mom, conv_ema, emb_ema, affine_ema):
    line = lambda v: v.reshape(1, 128)
    scratch = shapes(images.shape, cotangent.shape, conv_w.shape, emb_w.shape)
    inputs = ["ext", "img", "cot", "emb", "cw", "ew", "aff", "cm_in", "ce_in", "em_in", "ee_in", "am", "ae"]
    trio = [(conv_w.shape, F32), (emb_w.shape, F32), ((1, 128), F32)]
    outputs = {"OUTV": (cotangent.shape, BF16), "IMG": (images.shape, BF16), "ge": (embedding.shape, F32)}
    outputs |= zip(("ncw", "new", "naw", "ncm", "nem", "nam", "nce", "nee", "nae"), trio * 3)
    names = inputs + list(outputs) + list(scratch) + ["lsem", "ssem", "rsem"]
    held = pl.pallas_call(
        lambda *refs: whole_kernel(names, image_total, *refs),
        name="resblock_step",
        out_shape=[pltpu.VMEM(*v) for v in outputs.values()],
        in_specs=[SM, ANY, ANY, VM, VM, VM, VM] + [ANY] * 4 + [VM] * 2,
        out_specs=[VM] * len(outputs),
        scratch_shapes=[pltpu.VMEM(*v) for v in scratch.values()]
        + [pltpu.SemaphoreType.DMA((8,)), pltpu.SemaphoreType.DMA((WIRES,)), pltpu.SemaphoreType.DMA((WIRES,))],
        compiler_params=pltpu.CompilerParams(
            collective_id=1, has_side_effects=True, vmem_limit_bytes=113 << 19
        ),
    )(extent.T, images, cotangent, embedding, conv_w, emb_w, line(affine), conv_mom, conv_ema, emb_mom, emb_ema,
      line(affine_mom), line(affine_ema))
    held = [pltpu.with_memory_space_constraint(v, pltpu.VMEM) for v in held]
    count = len(held)
    out, gi, ge, ncw, new, naw, ncm, nem, nam, nce, nee, nae = pl.pallas_call(
        place_kernel,
        name="place",
        out_shape=[jax.ShapeDtypeStruct(v.shape, v.dtype) for v in held],
        in_specs=[VM] * count,
        out_specs=[ANY] * count,
        scratch_shapes=[pltpu.SemaphoreType.DMA((count,))],
        compiler_params=pltpu.CompilerParams(vmem_limit_bytes=16 << 20),
    )(*held)
    flat = lambda v: v.reshape(-1)
    return out, gi, ge, ncw, new, flat(naw), ncm, nem, flat(nam), nce, nee, flat(nae)


def padded_2(cells, sides, width):
    for axis, dim in sides:
        count = lax.axis_size(axis)
        ends = count - 1
        head = lax.slice_in_dim(cells, 0, width, axis=dim)
        tail = lax.slice_in_dim(cells, cells.shape[dim] - width, cells.shape[dim], axis=dim)
        cells = jnp.concatenate(
            [
                lax.ppermute(tail, axis, [(i, (i + 1) % count) for i in range(ends)]),
                cells,
                lax.ppermute(head, axis, [((i + 1) % count, i) for i in range(ends)]),
            ],
            axis=dim,
        )
    return cells


def band_mask(extent, first_row, band_rows, band_cols, halved):
    height = extent[:, 0]
    breadth = extent[:, 1]
    if halved:
        height = height // 2
        breadth = breadth // 2
    row_ids = first_row + jnp.arange(band_rows, dtype=jnp.int32)
    col_ids = jnp.arange(band_cols, dtype=jnp.int32)
    inside = (row_ids[None, :, None] < height[:, None, None]) & (
        col_ids[None, None, :] < breadth[:, None, None]
    )
    return inside.astype(jnp.float32)[..., None]


def per_group_sums(values, group_count):
    shaped = values.reshape(values.shape[:3] + (group_count, values.shape[3] // group_count))
    return jnp.sum(shaped, axis=(1, 2, 4))


def spread_to_channels(stat, channels_per_group):
    return jnp.repeat(stat, channels_per_group, axis=1)[:, None, None, :]


def pool_cells(values):
    shaped = values.reshape(
        values.shape[0], values.shape[1] // 2, 2, values.shape[2] // 2, 2, values.shape[3]
    )
    return jnp.sum(shaped, axis=(2, 4)) * 0.25


def spread_cells(values):
    return jnp.repeat(jnp.repeat(values, 2, axis=1), 2, axis=2) * 0.25


def silu_slope(values):
    sigma = jax.nn.sigmoid(values)
    return sigma * (1.0 + values * (1.0 - sigma))


def conv_rows(padded, kernel, layout):
    return lax.conv_general_dilated(
        padded,
        kernel,
        (1, 1),
        ((0, 0), (1, 1)),
        dimension_numbers=("NHWC", "HWIO", layout),
        preferred_element_type=jnp.float32,
    )


def conv_back(padded, kernel):
    return lax.conv_general_dilated(
        padded,
        jnp.flip(kernel, (0, 1)),
        (1, 1),
        ((0, 0), (1, 1)),
        dimension_numbers=("NHWC", "HWOI", "NHWC"),
        preferred_element_type=jnp.float32,
    )


def tap_grads(padded, grads):
    window = jnp.pad(padded, ((0, 0), (0, 0), (1, 1), (0, 0)))
    band_rows = grads.shape[1]
    band_cols = grads.shape[2]
    kernel_rows = []
    for tap_row in range(3):
        taps = []
        for tap_col in range(3):
            source = window[:, tap_row : tap_row + band_rows, tap_col : tap_col + band_cols, :]
            taps.append(
                jnp.einsum("brci,brco->io", source, grads, preferred_element_type=jnp.float32)
            )
        kernel_rows.append(jnp.stack(taps))
    return jnp.stack(kernel_rows)


def band_rim(values):
    return padded_2(values, (("sp", 1),), 1)


def other_rim(values):
    return padded_2(values, (("sp", 1),), 1)


def update(weight, moment, average, total, image_total):
    grad_mean = total / image_total
    new_moment = MOMENTUM * moment + grad_mean
    new_weight = weight - LEARN_RATE * (grad_mean + MOMENTUM * new_moment)
    new_average = EMA_DECAY * average + (1.0 - EMA_DECAY) * new_weight
    return (new_weight, new_moment, new_average)


def local(
    images,
    embedding,
    extent,
    cotangent,
    conv_w,
    emb_w,
    affine,
    conv_mom,
    emb_mom,
    affine_mom,
    conv_ema,
    emb_ema,
    affine_ema,
):
    conv_all, emb_all, affine_all = (
        lax.all_gather(conv_w.astype(jnp.bfloat16), ("img", "sp"), axis=0, tiled=True),
        lax.all_gather(emb_w.astype(jnp.bfloat16), ("img", "sp"), axis=0, tiled=True),
        lax.all_gather(affine.astype(jnp.bfloat16), ("img", "sp"), axis=0, tiled=True),
    )
    channels = conv_all.shape[1]
    first_kernel = conv_all[: 9 * channels].reshape(3, 3, channels, channels)
    second_kernel = conv_all[9 * channels :].reshape(3, 3, channels, channels)
    parameters = affine_all.astype(jnp.float32).reshape(8, channels)
    image_count = images.shape[0]
    band_rows = images.shape[1]
    grid_side = images.shape[2]
    half_band = band_rows // 2
    half_side = grid_side // 2
    sp_size = lax.axis_size("sp")
    sp_index = lax.axis_index("sp")
    local_channels = channels // sp_size
    first_channels = sp_index * local_channels
    channels_per_group = channels // NORM_GROUPS
    groups_on_device = local_channels // channels_per_group
    full_mask = band_mask(extent, sp_index * band_rows, band_rows, grid_side, False)
    half_mask = band_mask(extent, sp_index * half_band, half_band, half_side, True)
    whole_half = band_mask(extent, 0, half_side, half_side, True)
    full_pixel_count = (extent[:, 0] * extent[:, 1] * channels_per_group).astype(jnp.float32)[
        :, None
    ]
    half_pixel_count = (extent[:, 0] // 2 * (extent[:, 1] // 2) * channels_per_group).astype(
        jnp.float32
    )[:, None]
    masked_values = images.astype(jnp.float32) * full_mask
    sums_one, squares_one = lax.psum(
        (
            per_group_sums(masked_values, NORM_GROUPS),
            per_group_sums(masked_values * masked_values, NORM_GROUPS),
        ),
        "sp",
    )
    first_group_mean = sums_one / full_pixel_count
    first_inverse_deviation = lax.rsqrt(
        squares_one / full_pixel_count - first_group_mean * first_group_mean + EPSILON
    )
    first_normalized = (
        masked_values - spread_to_channels(first_group_mean, channels_per_group)
    ) * spread_to_channels(first_inverse_deviation, channels_per_group)
    first_group_norm = first_normalized * parameters[0] + parameters[1]
    pooled = pool_cells(jax.nn.silu(first_group_norm) * full_mask).astype(jnp.bfloat16)
    skip_path = pool_cells(masked_values)
    pooled_rim = band_rim(pooled)
    inner_act = ((conv_rows(pooled_rim, first_kernel, "NHWC") + parameters[2]) * half_mask).astype(
        jnp.bfloat16
    )
    emb_act = jax.nn.silu(embedding.astype(jnp.float32)).astype(jnp.bfloat16)

    def place_local(values):
        return lax.dynamic_update_slice_in_dim(
            jnp.zeros((channels,), jnp.float32), values, first_channels, 0
        )

    inner_channels = lax.all_to_all(
        inner_act, "sp", split_axis=3, concat_axis=1, tiled=True
    ).astype(jnp.float32)
    emb_cols = jnp.concatenate(
        [
            lax.dynamic_slice_in_dim(emb_all, first_channels, local_channels, 1),
            lax.dynamic_slice_in_dim(emb_all, channels + first_channels, local_channels, 1),
        ],
        axis=1,
    )
    emb_bias = jnp.concatenate(
        [
            lax.dynamic_slice_in_dim(parameters[3], first_channels, local_channels, 0),
            lax.dynamic_slice_in_dim(parameters[4], first_channels, local_channels, 0),
        ]
    )
    emb_proj = jnp.dot(emb_act, emb_cols, preferred_element_type=jnp.float32) + emb_bias
    ada_scale = 1.0 + emb_proj[:, :local_channels][:, None, None, :]
    ada_shift = emb_proj[:, local_channels:][:, None, None, :]
    sums_two = per_group_sums(inner_channels, groups_on_device)
    squares_two = per_group_sums(inner_channels * inner_channels, groups_on_device)
    second_group_mean = sums_two / half_pixel_count
    second_inverse_deviation = lax.rsqrt(
        squares_two / half_pixel_count - second_group_mean * second_group_mean + EPSILON
    )
    second_normalized = (
        inner_channels - spread_to_channels(second_group_mean, channels_per_group)
    ) * spread_to_channels(second_inverse_deviation, channels_per_group)
    second_gain = lax.dynamic_slice_in_dim(parameters[5], first_channels, local_channels, 0)
    second_group_norm = second_normalized * second_gain + lax.dynamic_slice_in_dim(
        parameters[6], first_channels, local_channels, 0
    )
    mixed_act = second_group_norm * ada_scale + ada_shift
    act_two = (jax.nn.silu(mixed_act) * whole_half).astype(jnp.bfloat16)
    act_rows = lax.all_to_all(act_two, "sp", split_axis=1, concat_axis=3, tiled=True)
    act_rim = other_rim(act_rows)
    branch = conv_rows(act_rim, second_kernel, "NHWC") + parameters[7]
    output = (skip_path + branch * half_mask).astype(jnp.bfloat16)
    grad_branch = (cotangent.astype(jnp.float32) * half_mask).astype(jnp.bfloat16)
    bias_two_grad = jnp.sum(grad_branch.astype(jnp.float32), axis=(0, 1, 2))
    grad_rim = other_rim(grad_branch)
    kernel_two = tap_grads(act_rim, grad_branch)
    grad_band = conv_back(grad_rim, second_kernel).astype(jnp.bfloat16)
    grad_act = lax.all_to_all(grad_band, "sp", split_axis=3, concat_axis=1, tiled=True)
    grad_mixed = grad_act.astype(jnp.float32) * whole_half * silu_slope(mixed_act)
    grad_proj = jnp.concatenate(
        [jnp.sum(grad_mixed * second_group_norm, axis=(1, 2)), jnp.sum(grad_mixed, axis=(1, 2))],
        axis=1,
    )
    second_norm_gradient = grad_mixed * ada_scale
    second_gain_gradient = jnp.sum(second_norm_gradient * second_normalized, axis=(0, 1, 2))
    bias_norm_two_grad = jnp.sum(second_norm_gradient, axis=(0, 1, 2))
    second_normalized_gradient = second_norm_gradient * second_gain
    first_total_count = (
        per_group_sums(second_normalized_gradient, groups_on_device) / half_pixel_count
    )
    second_total_count = (
        per_group_sums(second_normalized_gradient * second_normalized, groups_on_device)
        / half_pixel_count
    )
    grad_inner = spread_to_channels(second_inverse_deviation, channels_per_group) * (
        second_normalized_gradient
        - spread_to_channels(first_total_count, channels_per_group)
        - second_normalized * spread_to_channels(second_total_count, channels_per_group)
    )
    grad_inner_rows = lax.all_to_all(
        grad_inner.astype(jnp.bfloat16), "sp", split_axis=1, concat_axis=3, tiled=True
    )
    emb_grad_cols = jnp.einsum(
        "be,bk->ek", emb_act.astype(jnp.float32), grad_proj, precision=HIGHEST
    )
    emb_kernel = jnp.zeros((emb_all.shape[0], 2 * channels), jnp.float32)
    emb_kernel = lax.dynamic_update_slice_in_dim(
        emb_kernel, emb_grad_cols[:, :local_channels], first_channels, 1
    )
    emb_kernel = lax.dynamic_update_slice_in_dim(
        emb_kernel, emb_grad_cols[:, local_channels:], channels + first_channels, 1
    )
    silu_part = jnp.einsum("bk,ek->be", grad_proj, emb_cols.astype(jnp.float32), precision=HIGHEST)
    silu_grad = lax.psum(silu_part.astype(jnp.bfloat16), "sp").astype(jnp.float32)
    emb_bias_grad = jnp.sum(grad_proj, axis=0)
    coarse_affine = [
        place_local(emb_bias_grad[:local_channels]),
        place_local(emb_bias_grad[local_channels:]),
        place_local(second_gain_gradient),
        place_local(bias_norm_two_grad),
    ]
    grad_embedding = silu_grad * silu_slope(embedding.astype(jnp.float32))
    grad_raw = (grad_inner_rows.astype(jnp.float32) * half_mask).astype(jnp.bfloat16)
    bias_one_grad = jnp.sum(grad_raw.astype(jnp.float32), axis=(0, 1, 2))
    kernel_one = tap_grads(pooled_rim, grad_raw)
    grad_pooled = conv_back(band_rim(grad_raw), first_kernel)
    first_norm_gradient = spread_cells(grad_pooled) * full_mask * silu_slope(first_group_norm)
    first_gain_gradient = jnp.sum(first_norm_gradient * first_normalized, axis=(0, 1, 2))
    bias_norm_one_grad = jnp.sum(first_norm_gradient, axis=(0, 1, 2))
    first_normalized_gradient = first_norm_gradient * parameters[0]
    back_one, second_backward = lax.psum(
        (
            per_group_sums(first_normalized_gradient, NORM_GROUPS),
            per_group_sums(first_normalized_gradient * first_normalized, NORM_GROUPS),
        ),
        "sp",
    )
    grad_masked = spread_to_channels(first_inverse_deviation, channels_per_group) * (
        first_normalized_gradient
        - spread_to_channels(back_one / full_pixel_count, channels_per_group)
        - first_normalized
        * spread_to_channels(second_backward / full_pixel_count, channels_per_group)
    ) + spread_cells(cotangent.astype(jnp.float32))
    grad_images = (grad_masked * full_mask).astype(jnp.bfloat16)
    affine_grad = jnp.concatenate(
        [first_gain_gradient, bias_norm_one_grad, bias_one_grad] + coarse_affine + [bias_two_grad]
    )
    conv_grad = jnp.concatenate(
        [kernel_one.reshape(9 * channels, channels), kernel_two.reshape(9 * channels, channels)]
    )
    conv_sum, emb_sum, affine_sum = (
        lax.psum_scatter(conv_grad, ("img", "sp"), scatter_dimension=0, tiled=True),
        lax.psum_scatter(emb_kernel, ("img", "sp"), scatter_dimension=0, tiled=True),
        lax.psum_scatter(affine_grad, ("img", "sp"), scatter_dimension=0, tiled=True),
    )
    image_total = float(image_count * lax.axis_size("img"))
    new_conv, conv_moment, conv_average = update(conv_w, conv_mom, conv_ema, conv_sum, image_total)
    new_emb, emb_moment, emb_average = update(emb_w, emb_mom, emb_ema, emb_sum, image_total)
    new_affine, affine_moment, affine_average = update(
        affine, affine_mom, affine_ema, affine_sum, image_total
    )
    return (
        output,
        grad_images,
        grad_embedding,
        new_conv,
        new_emb,
        new_affine,
        conv_moment,
        emb_moment,
        affine_moment,
        conv_average,
        emb_average,
        affine_average,
    )


def kernels_or_ops(images, embedding, extent, cotangent, conv_w, *rest):
    arrays = (images, embedding, extent, cotangent, conv_w) + rest
    n, rows, side, channels = images.shape
    if n > 16 or rows != 8 or side != 32 or channels != 512 or conv_w.shape[0] != 288:
        return local(*arrays)
    return local_kernels(float(n * lax.axis_size("img")), *arrays)


def solution(mesh):
    in_specs = (
        P("img", "sp", None, None),
        P("img", None),
        P("img", None),
        P("img", "sp", None, None),
        P(("img", "sp"), None),
        P(("img", "sp"), None),
        P(("img", "sp")),
        P(("img", "sp"), None),
        P(("img", "sp"), None),
        P(("img", "sp")),
        P(("img", "sp"), None),
        P(("img", "sp"), None),
        P(("img", "sp")),
    )
    out_specs = (
        P("img", "sp", None, None),
        P("img", "sp", None, None),
        P("img", None),
        P(("img", "sp"), None),
        P(("img", "sp"), None),
        P(("img", "sp")),
        P(("img", "sp"), None),
        P(("img", "sp"), None),
        P(("img", "sp")),
        P(("img", "sp"), None),
        P(("img", "sp"), None),
        P(("img", "sp")),
    )
    fits = dict(mesh.shape) == {"img": 8, "sp": 4}
    return jax.shard_map(kernels_or_ops if fits else local, mesh=mesh, in_specs=in_specs, out_specs=out_specs, check_vma=False)
```

```python
import jax
import jax.numpy as jnp
from jax import lax
from jax.experimental import pallas as pl
from jax.experimental.pallas import tpu as pltpu
from jax.sharding import PartitionSpec as P

F32 = jnp.float32
BF16 = jnp.bfloat16
HIGHEST = lax.Precision.HIGHEST
MESH = pl.DeviceIdType.MESH
EPSILON = 1e-05
LEARN_RATE = 0.03
MOMENTUM = 0.5
EMA_DECAY = 0.5
NORM_GROUPS = 32
PIECES = 3


def choose(cond, a, b):
    if isinstance(cond, bool):
        return a if cond else b
    return jnp.where(cond, a, b)


def many(value, factor):
    return value if isinstance(value, int) else pl.multiple_of(value, factor)


class Place:
    def __init__(self, img, sp):
        self.img, self.sp = img, sp
        if isinstance(img, int):
            self.z, self.y, self.x, self.c = img // 2, img % 2, sp // 2, sp % 2
        else:
            self.z, self.y = lax.div(img, 2), lax.rem(img, 2)
            self.x, self.c = lax.div(sp, 2), lax.rem(sp, 2)
        z, y, x, c = self.z, self.y, self.x, self.c
        self.core = self.at(z, y, x, 1 - c)
        self.xn = self.at(z, y, 1 - x, c)
        self.yn = self.at(z, 1 - y, x, c)
        self.up, self.down = self.at(z + 1, y, x, c), self.at(z - 1, y, x, c)
        self.pair = self.at(z + 1 - 2 * self.odd(z), y, x, c)
        self.gate = self.at(choose(z < 2, 2, 1), y, x, c)
        self.zs = [self.at(self.z_off(k), y, x, c) for k in (1, 2, 3)]
        self.sps = [(img, self.sp_off(k)) for k in (1, 2, 3)]

    def at(self, z, y, x, c):
        return (z * 2 + y, x * 2 + c)

    def odd(self, value):
        return value % 2 if isinstance(value, int) else lax.rem(value, 2)

    def off(self, value, k):
        value = value + k
        return value % 4 if isinstance(value, int) else lax.rem(value, 4)

    def z_off(self, k):
        return self.off(self.z, k)

    def sp_off(self, k):
        return self.off(self.sp, k)


class Wire:
    def __init__(self, ssem, rsem):
        self.ssem, self.rsem = ssem, rsem
        self.used = 0
        self.open = []

    def take(self, count=1):
        first = self.used
        self.used += count
        return first

    def when(self, cond, do):
        if cond is None:
            do()
        else:
            pl.when(cond)(do)

    def copy(self, src, dst, peer, send, recv):
        return pltpu.make_async_remote_copy(
            src_ref=src, dst_ref=dst, send_sem=self.ssem.at[send], recv_sem=self.rsem.at[recv],
            device_id=peer, device_id_type=MESH,
        )

    def put(self, src, dst, peer, send, recv=None, when=None):
        def make():
            return self.copy(src, dst, peer, send, send if recv is None else recv)

        self.when(when, lambda: make().start())
        self.open.append((make, when))
        return self.open[-1]

    def left(self, copies):
        for make, when in copies:
            self.when(when, lambda make=make: make().wait_send())
        gone = [id(copy) for copy in copies]
        self.open = [item for item in self.open if id(item) not in gone]

    def got(self, ref, recv, peer, when=None):
        self.when(when, lambda: self.copy(ref, ref, peer, recv, recv).wait_recv())

    def started(self):
        return list(self.open)

    def close(self):
        self.left(self.started())

    def greet(self, place, meanwhile):
        barrier = pltpu.get_barrier_semaphore()
        peers = place.sps + [place.yn] + place.zs
        for peer in peers:
            pl.semaphore_signal(barrier, inc=1, device_id=peer, device_id_type=MESH)
        meanwhile()
        pl.semaphore_wait(barrier, len(peers))


class Gather:
    def __init__(self, wire, place, W, rows):
        self.wire, self.place, self.W, self.rows = wire, place, W, rows
        self.piece = rows // PIECES
        count = 4 * PIECES
        self.sems = {k: wire.take(count) for k in ("z", "u", "d", "x", "y", "xy", "yx")}
        self.core = wire.take(16)

    def sem(self, kind, b, j):
        return self.sems[kind] + b * PIECES + j

    def ref(self, b, y, x, c, j, half=None):
        start = self.rows * ((b * 2 + y) * 4 + x * 2 + c) + j * self.piece
        size = self.piece
        if half is not None:
            size = size // 2
            start = start + half * size
        return self.W.at[pl.ds(many(start, 16), size)]

    def along(self, b, j, up, down):
        p, wire = self.place, self.wire
        r = self.ref(b, p.y, p.x, p.c, j)
        wire.put(r, r, p.up, self.sem("u", b, j), self.sem("z", b, j), when=up)
        wire.put(r, r, p.down, self.sem("d", b, j), self.sem("z", b, j), when=down)

    def arrive(self, b, j, when=None):
        p = self.place
        both = lambda cond: cond if when is None else when & cond
        self.wire.got(self.ref(b, p.y, p.x, p.c, j), self.sem("z", b, j), p.up, when=when)
        self.along(b, j, both((b < p.z) & (p.z < 3)), both((b > p.z) & (p.z > 0)))

    def block(self, b, y, x, c):
        start = self.rows * ((b * 2 + y) * 4 + x * 2 + c)
        return self.W.at[pl.ds(many(start, 16), self.rows)]

    def share(self, b, k, y, x, when=None):
        r = self.block(b, y, x, self.place.c)
        self.wire.put(r, r, self.place.core, self.core + b * 4 + k, when=when)

    def own(self, b, j, when=None):
        p, wire = self.place, self.wire
        r = self.ref(b, p.y, p.x, p.c, j)
        wire.put(r, r, p.xn, self.sem("x", b, j), when=when)
        wire.put(r, r, p.yn, self.sem("y", b, j), when=when)
        if j == PIECES - 1:
            self.share(b, 0, p.y, p.x, when)

    def turn(self, b, j):
        p, wire = self.place, self.wire
        wire.got(self.ref(b, p.y, 1 - p.x, p.c, j), self.sem("x", b, j), p.xn)
        h = self.ref(b, p.y, 1 - p.x, p.c, j, 0)
        wire.put(h, h, p.yn, self.sem("xy", b, j))
        wire.got(self.ref(b, 1 - p.y, p.x, p.c, j), self.sem("y", b, j), p.yn)
        h = self.ref(b, 1 - p.y, p.x, p.c, j, 1)
        wire.put(h, h, p.xn, self.sem("yx", b, j))
        if j == PIECES - 1:
            self.share(b, 1, p.y, 1 - p.x)
            self.share(b, 2, 1 - p.y, p.x)

    def last(self, b, j):
        p, wire = self.place, self.wire
        wire.got(self.ref(b, 1 - p.y, 1 - p.x, p.c, j, 0), self.sem("xy", b, j), p.yn)
        wire.got(self.ref(b, 1 - p.y, 1 - p.x, p.c, j, 1), self.sem("yx", b, j), p.xn)
        if j == PIECES - 1:
            self.share(b, 3, 1 - p.y, 1 - p.x)

    def done(self, b):
        p, wire = self.place, self.wire
        for k, y, x in ((0, p.y, p.x), (1, p.y, 1 - p.x), (2, 1 - p.y, p.x), (3, 1 - p.y, 1 - p.x)):
            wire.got(self.block(b, y, x, 1 - p.c), self.core + b * 4 + k, p.core)


class Scatter:
    def __init__(self, wire, place, grad, bufs, out, first):
        self.wire, self.place, self.grad, self.out, self.first = wire, place, grad, out, first
        self.SB, self.CR, self.DR, self.NR, self.ZR, self.R, self.FR = bufs
        self.rows = self.SB.shape[3]
        self.piece = self.rows // PIECES
        self.half = self.piece // 2
        count = 2 * PIECES
        self.core = wire.take(8)
        self.sems = {k: wire.take(count) for k in ("da", "db", "xa", "xb", "ya", "yb", "u", "v", "d")}
        self.sent = []

    def sem(self, kind, b, j):
        return self.sems[kind] + b * PIECES + j

    def block(self, b, y, x, c, j=0, size=None):
        start = self.rows * ((b * 2 + y) * 4 + x * 2 + c) + j * self.piece
        return self.grad.at[pl.ds(many(start, 16), self.rows if size is None else size)]

    def give(self, ready):
        p = self.place
        while len(self.sent) < 8 and (2 * len(self.sent) + 2) * self.rows <= ready:
            i = len(self.sent)
            b, y, x = i // 4, i // 2 % 2, i % 2
            src = self.block(b, y, x, 1 - p.c)
            self.sent.append(self.wire.put(src, self.CR.at[b, y, x], p.core, self.core + i))

    def given(self):
        self.wire.left(self.sent)

    def take(self, b, y, x):
        self.wire.got(self.CR.at[b, y, x], self.core + b * 4 + y * 2 + x, self.place.core)

    def span(self, j, h=None):
        if h is None:
            return pl.ds(j * self.piece, self.piece)
        return pl.ds(j * self.piece + h * self.half, self.half)

    def add_core(self, b, y, x, j):
        mine = self.block(b, y, x, self.place.c, j, self.piece)
        v = mine[...].astype(F32) + self.CR[b, y, x, self.span(j)].astype(F32)
        self.SB[b, y, x, self.span(j)] = v.astype(BF16)

    def add_pass(self, b, y, x, j, h):
        at = self.span(j, h)
        v = self.SB[b, y, x, at].astype(F32) + self.DR[b, h, pl.ds(j * self.half, self.half)].astype(F32)
        self.SB[b, y, x, at] = v.astype(BF16)

    def add_plane(self, b, j):
        p, at = self.place, self.span(j)
        self.R[b, at] = (self.SB[b, p.y, p.x, at].astype(F32) + self.NR[b, 0, at].astype(F32)
                         + self.NR[b, 1, at].astype(F32))

    def back(self, b, j):
        at = self.span(j)
        self.SB[b, self.place.y, self.place.x, at] = self.R[b, at].astype(BF16)

    def add_far(self, b, j):
        at = self.span(j)
        self.R[b, at] += self.ZR[b, 0, at].astype(F32)

    def final(self, b, j):
        at = self.span(j)
        v = self.R[b, at] + (self.ZR[b, 0, at].astype(F32) + self.ZR[b, 1, at].astype(F32))
        if self.straight(b, j):
            v = v + self.FR[...].astype(F32)
        self.out[at] = v

    def straight(self, b, j):
        return self.first == 0 and b == 1 and j == PIECES - 1

    def step(self, k, b, j):
        p, wire = self.place, self.wire
        y, x = p.y, p.x
        owner = self.first + b
        far, mid = (0, 1) if self.first == 2 else (3, 2)
        if k == 0:
            self.add_core(b, 1 - y, 1 - x, j)
            at = pl.ds(j * self.half, self.half)
            src = self.SB.at[b, 1 - y, 1 - x]
            wire.put(src.at[self.span(j, 0)], self.DR.at[b, 0, at], p.yn, self.sem("da", b, j))
            wire.put(src.at[self.span(j, 1)], self.DR.at[b, 1, at], p.xn, self.sem("db", b, j))
        elif k == 1:
            self.add_core(b, y, 1 - x, j)
            at = self.span(j, 1)
            wire.put(self.SB.at[b, y, 1 - x, at], self.NR.at[b, 0, at], p.xn, self.sem("xb", b, j))
            self.add_core(b, 1 - y, x, j)
            at = self.span(j, 0)
            wire.put(self.SB.at[b, 1 - y, x, at], self.NR.at[b, 1, at], p.yn, self.sem("ya", b, j))
            self.add_core(b, y, x, j)
        elif k == 2:
            got = pl.ds(j * self.half, self.half)
            wire.got(self.DR.at[b, 0, got], self.sem("da", b, j), p.yn)
            self.add_pass(b, y, 1 - x, j, 0)
            at = self.span(j, 0)
            wire.put(self.SB.at[b, y, 1 - x, at], self.NR.at[b, 0, at], p.xn, self.sem("xa", b, j))
            wire.got(self.DR.at[b, 1, got], self.sem("db", b, j), p.xn)
            self.add_pass(b, 1 - y, x, j, 1)
            at = self.span(j, 1)
            wire.put(self.SB.at[b, 1 - y, x, at], self.NR.at[b, 1, at], p.yn, self.sem("yb", b, j))
        elif k == 3:
            wire.got(self.NR.at[b, 0, self.span(j, 1)], self.sem("xb", b, j), p.xn)
            wire.got(self.NR.at[b, 1, self.span(j, 0)], self.sem("ya", b, j), p.yn)
            wire.got(self.NR.at[b, 0, self.span(j, 0)], self.sem("xa", b, j), p.xn)
            wire.got(self.NR.at[b, 1, self.span(j, 1)], self.sem("yb", b, j), p.yn)
            self.add_plane(b, j)
            at = self.span(j)
            mine = self.SB.at[b, y, x, at]
            side = 2 * self.first + 1 - owner
            if self.straight(b, j):
                wire.when(p.z != owner, lambda: self.back(b, j))
                peer = p.at(owner, y, x, p.c)
                wire.put(mine, self.FR, peer, self.sem("u", b, j), when=p.z == far)
                wire.put(mine, self.ZR.at[b, 0, at], peer, self.sem("v", b, j), when=p.z == mid)
            else:
                wire.when((p.z == far) | (p.z == side), lambda: self.back(b, j))
                wire.put(mine, self.ZR.at[b, 0, at], p.pair, self.sem("u", b, j), when=p.z == far)
            wire.put(mine, self.ZR.at[b, 1, at], p.pair, self.sem("d", b, j), when=p.z == side)
        elif k == 4:
            if self.straight(b, j):
                return
            at = self.span(j)

            def on():
                self.add_far(b, j)
                self.back(b, j)

            wire.got(self.ZR.at[b, 0, at], self.sem("u", b, j), p.pair, when=p.z == mid)
            wire.when(p.z == mid, on)
            peer = p.at(owner, y, x, p.c)
            wire.put(self.SB.at[b, y, x, at], self.ZR.at[b, 0, at], peer, self.sem("v", b, j), when=p.z == mid)
        else:
            at = self.span(j)
            wire.got(self.ZR.at[b, 0, at], self.sem("v", b, j), p.gate, when=p.z == owner)
            wire.got(self.ZR.at[b, 1, at], self.sem("d", b, j), p.pair, when=p.z == owner)
            if self.straight(b, j):
                wire.got(self.FR, self.sem("u", b, j), p.gate, when=p.z == owner)
            wire.when(p.z == owner, lambda: self.final(b, j))

    @staticmethod
    def scratch(rows, channels):
        return [
            ((2, 2, 2, rows, channels), BF16),
            ((2, 2, 2, rows, channels), BF16),
            ((2, 2, rows // 2, channels), BF16),
            ((2, 2, rows, channels), BF16),
            ((2, 2, rows, channels), BF16),
            ((2, rows, channels), F32),
            ((rows // PIECES, channels), BF16),
        ]


class Halo:
    def __init__(self, wire, place, buf):
        self.wire, self.place, self.buf = wire, place, buf
        self.up, self.down = wire.take(), wire.take()

    def send(self):
        p, wire, buf = self.place, self.wire, self.buf
        last = buf.shape[0] - 1
        wire.put(buf.at[1], buf.at[last], (p.img, p.sp - 1), self.up, when=p.sp > 0)
        wire.put(buf.at[last - 1], buf.at[0], (p.img, p.sp + 1), self.down, when=p.sp < 3)
        wire.when(p.sp == 0, lambda: self.clear(0))
        wire.when(p.sp == 3, lambda: self.clear(last))

    def clear(self, row):
        self.buf[row] = jnp.zeros_like(self.buf[row])

    def wait(self):
        p, wire, buf = self.place, self.wire, self.buf
        last = buf.shape[0] - 1
        wire.got(buf.at[last], self.up, (p.img, p.sp + 1), when=p.sp < 3)
        wire.got(buf.at[0], self.down, (p.img, p.sp - 1), when=p.sp > 0)


class BandSum:
    def __init__(self, wire, place, slots):
        self.wire, self.place, self.slots = wire, place, slots
        self.first = wire.take(3)

    def send(self):
        p = self.place
        for k in range(3):
            self.wire.put(self.slots.at[p.sp], self.slots.at[p.sp], p.sps[k], self.first + k)

    def wait(self):
        for k in range(3):
            slot = self.slots.at[self.place.sp_off(3 - k)]
            self.wire.got(slot, self.first + k, self.place.sps[k])

    def total(self):
        return self.slots[0] + self.slots[1] + self.slots[2] + self.slots[3]


class SplitSum:
    def __init__(self, wire, place, slots):
        self.wire, self.place, self.slots = wire, place, slots
        self.sems = wire.take(3)

    def send(self):
        p, s = self.place, self.slots
        self.wire.put(s.at[1 - p.c], s.at[2], p.core, self.sems)

    def add(self, out, a, b):
        self.slots[out] = self.slots[a] + self.slots[b]

    def cross(self):
        p, s = self.place, self.slots
        self.wire.got(s.at[2], self.sems, p.core)
        self.add(3, p.c, 2)
        self.wire.put(s.at[3], s.at[4], p.xn, self.sems + 1)

    def back(self):
        p, s = self.place, self.slots
        self.wire.got(s.at[4], self.sems + 1, p.xn)
        self.add(5 + p.c, 3, 4)
        self.wire.put(s.at[5 + p.c], s.at[5 + p.c], p.core, self.sems + 2)

    def wait(self):
        self.wire.got(self.slots.at[6 - self.place.c], self.sems + 2, self.place.core)


class Spread:
    def __init__(self, wire, place, slots):
        self.wire, self.place, self.slots = wire, place, slots
        self.z, self.y = wire.take(3), wire.take()

    def send(self):
        p = self.place
        for k in range(3):
            self.wire.put(self.slots.at[p.y, p.z], self.slots.at[p.y, p.z], p.zs[k], self.z + k)

    def turn(self):
        p = self.place
        for k in range(3):
            self.wire.got(self.slots.at[p.y, p.z_off(3 - k)], self.z + k, p.zs[k])
        self.wire.put(self.slots.at[p.y], self.slots.at[p.y], p.yn, self.y)

    def wait(self):
        self.wire.got(self.slots.at[1 - self.place.y], self.y, self.place.yn)


def group_matrix(channels, across, first):
    per = channels // NORM_GROUPS
    shape = (channels, 128) if across else (128, channels)
    c = lax.broadcasted_iota(jnp.int32, shape, 0 if across else 1)
    g = lax.broadcasted_iota(jnp.int32, shape, 1 if across else 0)
    return (lax.div(c, per) + first == g).astype(F32)


def exact_dot(a, b):
    return jnp.dot(a, b, precision=HIGHEST, preferred_element_type=F32)


def pack(a, b):
    return exact_dot(a, group_matrix(a.shape[1], True, 0)) + exact_dot(b, group_matrix(b.shape[1], True, 64))


def unpack(v, channels):
    return exact_dot(v, group_matrix(channels, False, 0)), exact_dot(v, group_matrix(channels, False, 64))


def sigmoid(v):
    return 0.5 * jnp.tanh(0.5 * v) + 0.5


def slope(v):
    s = sigmoid(v)
    return s * (1.0 + v * (1.0 - s))


def thirds(v):
    high = v.astype(BF16)
    v = v - high.astype(F32)
    mid = v.astype(BF16)
    return high, mid, (v - mid.astype(F32)).astype(BF16)


def fold(v):
    return jnp.sum(v.reshape(v.shape[0] // 8, 8, v.shape[1]), axis=0)


def plus(total, v):
    return v if total is None else total + v


class Step:
    def __init__(self, place, wire, refs, image_total):
        self.__dict__.update(refs)
        self.inverse = 1.0 / image_total
        self.p, self.w = place, wire
        self.images, self.rows_full, self.side_full, self.channels = self.IMG.shape
        self.rim, _, self.side, _ = self.PO.shape
        self.rows = self.rim - 2
        self.per = self.channels // NORM_GROUPS
        self.tiles = self.channels // 128
        shard = self.cw.shape[0]
        self.kernel_rows = 16 * shard
        self.g = Gather(wire, place, self.W, shard)
        self.r2 = Scatter(wire, place, self.DW, [self.__dict__["RA%d" % i] for i in range(6)] + [None], self.RES, 2)
        self.r1 = Scatter(wire, place, self.DW, [self.__dict__["RB%d" % i] for i in range(7)], self.RES, 0)
        self.halo_p = Halo(wire, place, self.PO)
        self.halo_g = Halo(wire, place, self.G)
        self.halo_a = Halo(wire, place, self.A2)
        self.halo_b = Halo(wire, place, self.GB)
        self.aff_img = Spread(wire, place, self.AFS.at[place.sp])
        self.aff_sp = BandSum(wire, place, self.AFS)
        self.sum1 = BandSum(wire, place, self.ST1)
        self.sum2 = BandSum(wire, place, self.ST2)
        self.sum3 = BandSum(wire, place, self.ST3)
        self.sum4 = BandSum(wire, place, self.ST4)
        self.psum = SplitSum(wire, place, self.PS)
        self.proj = SplitSum(wire, place, self.PX)
        self.esum = SplitSum(wire, place, self.PE)
        self.asum = BandSum(wire, place, self.AFR)
        self.spread_g = Spread(wire, place, self.GPA)
        self.ea = wire.take(6), wire.take()
        self.ez = wire.take(3), wire.take(4)
        self.afy = wire.take()
        self.afz = wire.take(3)


    def loop(self, body, first=0, last=None):
        def one(n, _):
            body(n)
            return 0

        lax.fori_loop(first, self.images if last is None else last, one, 0)

    def width(self, n, r):
        return jnp.where(self.p.sp * self.rows_full + r < self.ext[0, n], self.ext[1, n], 0)

    def half_width(self, n, r):
        inside = self.p.sp * self.rows + r < lax.div(self.ext[0, n], 2)
        return jnp.where(inside, lax.div(self.ext[1, n], 2), 0)

    def cols(self, side):
        return lax.broadcasted_iota(jnp.int32, (side, self.channels), 0)

    def at(self, k, n):
        return self.AB[k, pl.ds(n, 1)]

    def clear_sums(self):
        self.SS[...] = jnp.zeros_like(self.SS)

    def add_sums(self, n, s, q):
        self.SS[pl.ds(n, 1)] += jnp.sum(s, axis=0, keepdims=True)
        self.SS[pl.ds(n + 16, 1)] += jnp.sum(q, axis=0, keepdims=True)

    def eslot(self, z, y):
        rows = self.ew.shape[0]
        start = ((z * 2 + y) * 4 + self.p.sp) * rows
        return self.EZ.at[pl.ds(many(start, 32), rows)]


    def load(self):
        self.copies = [
            pltpu.make_async_copy(self.img, self.IMG, self.lsem.at[0]),
            pltpu.make_async_copy(self.cot, self.COT, self.lsem.at[1]),
        ]
        late = ((self.cm_in, self.CM), (self.ce_in, self.CE), (self.em_in, self.EM), (self.ee_in, self.EE))
        for i, (src, dst) in enumerate(late):
            self.copies.append(pltpu.make_async_copy(src, dst, self.lsem.at[2 + i]))
        for copy in self.copies:
            copy.start()

    def loaded(self, k):
        self.copies[k].wait()

    def own_weights(self):
        p = self.p
        rows = self.cw.shape[0]
        self.W[pl.ds(many(rows * (p.img * 4 + p.sp), 16), rows)] = self.cw[...].astype(BF16)
        low = self.aff[...].astype(BF16).astype(F32)
        self.AFS[p.sp, p.y, p.z] = low

    def own_embedding(self):
        p = self.p
        rows = self.ew.shape[0]
        zero = jnp.zeros((rows, self.EZ.shape[1]), BF16)
        for i in range(8):
            for sp in p.sps:
                self.EZ[pl.ds(many((i * 4 + sp[1]) * rows, 32), rows)] = zero
        self.EZ[pl.ds(many((p.img * 4 + p.sp) * rows, 32), rows)] = self.ew[...].astype(BF16)
        self.EP[...] = jnp.zeros_like(self.EP)
        self.EP[pl.ds(0, self.images)] = self.emb[...].astype(F32)
        e = self.EP[...]
        act = (e * sigmoid(e)).astype(BF16)
        self.EA[...] = act
        for i in range(8):
            self.ET[i // 2, i % 2] = act[:, i * 128 : i * 128 + 128]
        for y in range(2):
            self.EZT[y, p.z] = self.ET[p.z, y]

    def counts(self):
        self.CNT[...] = jnp.ones_like(self.CNT)

        def one(n):
            h, w = self.ext[0, n], self.ext[1, n]
            for i, number in enumerate((h * w, lax.div(h, 2) * lax.div(w, 2))):
                number = jnp.full((1, self.channels), number * self.per, jnp.int32)
                self.CNT[i, pl.ds(n, 1)] = number.astype(F32)

        self.loop(one)


    def ez_send(self):
        p = self.p
        for k in range(3):
            self.w.put(self.eslot(p.z, p.y), self.eslot(p.z, p.y), p.zs[k], self.ez[0] + k)

    def ez_turn(self):
        p = self.p
        for k in range(3):
            self.w.got(self.eslot(p.z_off(3 - k), p.y), self.ez[0] + k, p.zs[k])
        for k in range(4):
            self.w.put(self.eslot(k, p.y), self.eslot(k, p.y), p.yn, self.ez[1] + k)

    def ez_wait(self):
        for k in range(4):
            self.w.got(self.eslot(k, 1 - self.p.y), self.ez[1] + k, self.p.yn)


    def ea_send(self):
        p = self.p
        for k in range(3):
            for y in range(2):
                src = self.ET.at[p.z_off(k + 1), y]
                self.w.put(src, self.EZT.at[y, p.z], p.zs[k], self.ea[0] + 2 * k + y)

    def ea_turn(self):
        p = self.p
        for k in range(3):
            for y in range(2):
                self.w.got(self.EZT.at[y, p.z_off(3 - k)], self.ea[0] + 2 * k + y, p.zs[k])
        self.w.put(self.EZT.at[1 - p.y], self.EY, p.yn, self.ea[1])

    def ea_wait(self):
        self.w.got(self.EY, self.ea[1], self.p.yn)

    def project(self):
        v = jnp.dot(self.EA[...], self.EZ[...], preferred_element_type=F32)
        self.PX[0] = v[:, : self.channels]
        self.PX[1] = v[:, self.channels :]


    def stats_one(self, first, last):
        col = self.cols(self.side_full)

        def one(n):
            s = q = None
            for r in range(self.rows_full):
                v = jnp.where(col < self.width(n, r), self.IMG[n, r].astype(F32), 0.0)
                s, q = plus(s, fold(v)), plus(q, fold(v * v))
            self.add_sums(n, s, q)

        self.loop(one, first, last)

    def stats_one_end(self):
        self.ST1[self.p.sp] = pack(self.SS[:16], self.SS[16:])

    def affine_rows(self):
        for s in range(4):
            for y in range(2):
                for z in range(4):
                    self.AFF[pl.ds(z * 2 + y, 1), pl.ds(s * 128, 128)] = self.AFS[s, y, z]

    def moments(self, total, count, mean_ref, inv_ref):
        sums, squares = unpack(total, self.channels)
        mean = sums / count
        inv = lax.rsqrt(squares / count - mean * mean + EPSILON)
        mean_ref[...] = mean
        inv_ref[...] = inv
        return mean, inv

    def norm_one(self):
        mean, inv = self.moments(self.sum1.total(), self.CNT[0], self.MI.at[0], self.MI.at[1])
        self.AB[0] = inv * self.AFF[0:1]
        self.AB[1] = self.AFF[1:2] - mean * self.AB[0]

    def pool(self, hrs, first=0, last=None):
        col = self.cols(self.side_full)

        def one(n):
            for i, hr in enumerate(hrs):
                act = raw = None
                for k in range(2):
                    r = 2 * hr + k
                    inside = col < self.width(n, r)
                    u = self.IMG[n, r].astype(F32)
                    v = u * self.at(0, n) + self.at(1, n)
                    act = plus(act, jnp.where(inside, v * sigmoid(v), 0.0))
                    raw = plus(raw, jnp.where(inside, u, 0.0))
                for t in range(self.tiles):
                    lanes = slice(t * 128, t * 128 + 128)
                    self.T[i, t] = act[:, lanes]
                    self.T[i + 2, t] = raw[:, lanes]
            even, odd = pl.ds(0, self.side, stride=2), pl.ds(1, self.side, stride=2)
            for i, hr in enumerate(hrs):
                for t in range(self.tiles):
                    lanes = pl.ds(t * 128, 128)
                    v = self.T[i, t, even] + self.T[i, t, odd]
                    self.PO[hr + 1, n, :, lanes] = (v * 0.25).astype(BF16)
                    v = self.T[i + 2, t, even] + self.T[i + 2, t, odd]
                    self.SKIP[hr, n, :, lanes] = v * 0.25

        self.loop(one, first, last)


    def sides(self, src):
        return self.XP if src is self.PO else self.XA if src is self.A2 else self.XG

    def shift(self, src, rows):
        col = self.cols(self.side)
        X = self.sides(src)

        def one(n):
            for r in rows:
                v = src[r, n].astype(F32)
                X[0, r, n] = jnp.where(col > 0, pltpu.roll(v, 1, 0), 0.0).astype(BF16)
                v = jnp.where(col < self.side - 1, pltpu.roll(v, self.side - 1, 0), 0.0)
                X[1, r, n] = v.astype(BF16)

        self.loop(one)

    def conv(self, center, base, row, back):
        count = self.ACC.shape[0]
        size = count * self.images * self.side
        total = None
        for a in range(3):
            for b in range(3):
                da, db = (2 - a, 2 - b) if back else (a, b)
                src = center if db == 1 else self.sides(center).at[0 if db == 0 else 1]
                left = src[pl.ds(row + da, count)].reshape(size, self.channels)
                tap = self.W[pl.ds(base + (3 * a + b) * self.channels, self.channels)]
                dims = (((1,), (1 if back else 0,)), ((), ()))
                total = plus(total, lax.dot_general(left, tap, dims, preferred_element_type=F32))
        self.ACC[...] = total.reshape(self.ACC.shape)

    def tap_grad(self, center, grads, t):
        a, b = divmod(t, 3)
        size = self.rows * self.images * self.side
        src = center if b == 1 else self.sides(center).at[0 if b == 0 else 1]
        left = src[pl.ds(a, self.rows)].reshape(size, self.channels)
        right = grads[pl.ds(1, self.rows)].reshape(size, self.channels)
        self.DW[pl.ds(t * self.channels, self.channels)] = lax.dot_general(
            left, right, (((0,), (0,)), ((), ())), preferred_element_type=F32
        ).astype(BF16)

    def mask_cot(self):
        col = self.cols(self.side)
        self.C2[...] = jnp.zeros_like(self.C2)

        def one(n):
            total = None
            for r in range(self.rows):
                v = jnp.where(col < self.half_width(n, r), self.COT[n, r].astype(F32), 0.0)
                self.G[r + 1, n] = v.astype(BF16)
                total = plus(total, fold(v))
            self.C2[...] += total

        self.loop(one)

    def inner_conv(self, row):
        col = self.cols(self.side)
        self.conv(self.PO, 0, row, False)

        def one(n):
            s = q = None
            for r in range(self.ACC.shape[0]):
                v = self.ACC[r, n] + self.AFF[2:3]
                v = jnp.where(col < self.half_width(n, row + r), v, 0.0).astype(BF16)
                self.INN[row + r, n] = v
                v = v.astype(F32)
                s, q = plus(s, fold(v)), plus(q, fold(v * v))
            self.add_sums(n, s, q)

        self.loop(one)


    def stats_two(self):
        self.ST2[self.p.sp] = pack(self.SS[:16], self.SS[16:])

    def norm_two(self):
        self.MI[4] = self.PX[5] + (self.AFF[3:4] + 1.0)
        self.MI[5] = self.PX[6] + self.AFF[4:5]
        mean, inv = self.moments(self.sum2.total(), self.CNT[1], self.MI.at[2], self.MI.at[3])
        self.AB[2] = inv
        self.AB[3] = -mean * inv
        self.AB[4] = self.AFF[5:6] * self.MI[4]
        self.AB[5] = self.AFF[6:7] * self.MI[4] + self.MI[5]

    def xhat_two(self, r, n):
        return self.INN[r, n].astype(F32) * self.at(2, n) + self.at(3, n)

    def activate(self, rs):
        col = self.cols(self.side)

        def one(n):
            for r in rs:
                v = self.xhat_two(r, n) * self.at(4, n) + self.at(5, n)
                v = jnp.where(col < self.half_width(n, r), v * sigmoid(v), 0.0)
                self.A2[r + 1, n] = v.astype(BF16)

        self.loop(one)

    def mixed_grad(self, row):
        col = self.cols(self.side)
        self.conv(self.G, self.kernel_rows, row, True)

        def one(n):
            s = q = None
            for r in range(self.ACC.shape[0]):
                v = self.ACC[r, n].astype(BF16).astype(F32)
                xhat = self.xhat_two(row + r, n)
                mixed = xhat * self.at(4, n) + self.at(5, n)
                v = jnp.where(col < self.half_width(n, row + r), v * slope(mixed), 0.0)
                self.GM[row + r, n] = v
                s, q = plus(s, fold(v)), plus(q, fold(v * xhat))
            self.add_sums(n, s, q)

        self.loop(one)

    def sums_two_back(self):
        p1, p2 = self.SS[:16], self.SS[16:]
        self.PS[0] = p1
        self.PS[1] = p2
        self.ST3[self.p.sp] = pack(p1 * self.AB[4], p2 * self.AB[4])
        scale = self.MI[4]
        self.AFP[0:3] = jnp.zeros_like(self.AFP[0:3])
        self.AFP[3:4] = jnp.sum(self.AFF[5:6] * p2 + self.AFF[6:7] * p1, axis=0, keepdims=True)
        self.AFP[4:5] = jnp.sum(p1, axis=0, keepdims=True)
        self.AFP[5:6] = jnp.sum(scale * p2, axis=0, keepdims=True)
        self.AFP[6:7] = jnp.sum(scale * p1, axis=0, keepdims=True)
        self.AFP[7:8] = jnp.sum(self.C2[...], axis=0, keepdims=True)

    def output(self, row):
        col = self.cols(self.side)
        self.conv(self.A2, self.kernel_rows, row, False)

        def one(n):
            for r in range(self.ACC.shape[0]):
                v = self.ACC[r, n] + self.AFF[7:8]
                v = jnp.where(col < self.half_width(n, row + r), v, 0.0)
                self.OUTV[n, row + r] = (self.SKIP[row + r, n] + v).astype(BF16)

        self.loop(one)

    def project_grad(self):
        p1, p2 = self.PS[5], self.PS[6]
        scale = self.AFF[5:6] * p2 + self.AFF[6:7] * p1
        self.GP[0] = scale
        self.GP[1] = p1
        self.GPA[self.p.y, self.p.z, 0] = scale.astype(BF16)
        self.GPA[self.p.y, self.p.z, 1] = p1.astype(BF16)

    def norm_two_back(self):
        first, second = unpack(self.sum3.total(), self.channels)
        inv = self.AB[2]
        self.AB[6] = inv * self.AB[4]
        self.AB[7] = inv * (first / self.CNT[1])
        self.AB[8] = inv * (second / self.CNT[1])
        self.C1[...] = jnp.zeros_like(self.C1)

    def inner_grad(self, rs):
        col = self.cols(self.side)

        def one(n):
            total = None
            for r in rs:
                v = self.GM[r, n] * self.at(6, n) - self.at(7, n) - self.xhat_two(r, n) * self.at(8, n)
                v = jnp.where(col < self.half_width(n, r), v, 0.0).astype(BF16)
                self.GB[r + 1, n] = v
                total = plus(total, fold(v.astype(F32)))
            self.C1[...] += total

        self.loop(one)


    def embedding_part(self):
        gp = jnp.concatenate([self.GP[0], self.GP[1]], axis=1)
        gp = jnp.concatenate(thirds(gp), axis=0)
        v = lax.dot_general(gp, self.EZ[...], (((1,), (1,)), ((), ())), preferred_element_type=F32)
        v = v[:16] + v[16:32] + v[32:]
        self.PE[0] = v[:, : self.channels]
        self.PE[1] = v[:, self.channels :]

    def embedding_grad(self):
        v = jnp.concatenate([self.PE[5], self.PE[6]], axis=1)[: self.images]
        self.ge[...] = v * slope(self.EP[pl.ds(0, self.images)])

    def embedding_weights(self):
        p = self.p
        left = jnp.concatenate([self.EZT[p.y].reshape(64, 128), self.EY[...].reshape(64, 128)], axis=0)
        for i in range(2):
            right = [self.GPA[y, :, i].reshape(64, self.channels) for y in (p.y, 1 - p.y)]
            self.EW[:, pl.ds(i * self.channels, self.channels)] = lax.dot_general(
                left, jnp.concatenate(right, axis=0), (((0,), (0,)), ((), ())), preferred_element_type=F32
            )
        self.ewg[...] = self.EW[pl.ds(many(p.sp * 32, 32), 32)]


    def doubled(self, value, slot):
        for t in range(self.tiles):
            v = value[:, t * 128 : t * 128 + 128]
            self.T[slot, t, pl.ds(0, self.side, stride=2)] = v
            self.T[slot, t, pl.ds(1, self.side, stride=2)] = v
        return jnp.concatenate([self.T[slot, t] for t in range(self.tiles)], axis=1)

    def prepare_one_back(self):
        self.AB[2] = self.MI[1]
        self.AB[3] = -self.MI[0] * self.MI[1]
        self.clear_sums()

    def norm_one_grad(self, n, r, grad):
        v = self.IMG[n, r].astype(F32)
        xhat = v * self.at(2, n) + self.at(3, n)
        v = v * self.at(0, n) + self.at(1, n)
        return xhat, jnp.where(self.cols(self.side_full) < self.width(n, r), grad * slope(v), 0.0)

    def pooled_conv(self, row):
        self.conv(self.GB, 0, row, True)
        self.GM[pl.ds(row, self.ACC.shape[0])] = self.ACC[...] * 0.25

    def pooled_grad(self, row, first=0, last=None):
        def one(n):
            s = q = None
            for r in range(self.ACC.shape[0]):
                grad = self.doubled(self.GM[row + r, n], r)
                for k in range(2):
                    xhat, v = self.norm_one_grad(n, 2 * (row + r) + k, grad)
                    s, q = plus(s, fold(v)), plus(q, fold(v * xhat))
            self.add_sums(n, s, q)

        self.loop(one, first, last)

    def sums_one_back(self):
        self.AFP[0:1] = jnp.sum(self.SS[16:32], axis=0, keepdims=True)
        self.AFP[1:2] = jnp.sum(self.SS[0:16], axis=0, keepdims=True)
        self.AFP[2:3] = jnp.sum(self.C1[...], axis=0, keepdims=True)
        self.AFZ[self.p.z] = self.AFP[...]
        self.ST4[self.p.sp] = pack(self.SS[:16] * self.AFF[0:1], self.SS[16:] * self.AFF[0:1])

    def affine_z(self):
        for k in range(3):
            self.w.put(self.AFZ.at[self.p.z], self.AFZ.at[self.p.z], self.p.zs[k], self.afz + k)

    def affine_sp(self):
        for k in range(3):
            self.w.got(self.AFZ.at[self.p.z_off(3 - k)], self.afz + k, self.p.zs[k])
        self.add_affine()
        self.asum.send()

    def add_affine(self):
        self.AFR[self.p.sp] = self.AFZ[0] + self.AFZ[1] + self.AFZ[2] + self.AFZ[3]

    def affine_y(self):
        self.asum.wait()
        self.total_affine()
        self.w.put(self.AFY.at[0], self.AFY.at[1], self.p.yn, self.afy)

    def total_affine(self):
        self.AFY[0] = self.asum.total()

    def affine_done(self):
        self.w.got(self.AFY.at[1], self.afy, self.p.yn)
        self.own_affine()

    def own_affine(self):
        self.AFP[...] = self.AFY[0] + self.AFY[1]
        tile = self.AFP[:, pl.ds(many(self.p.sp * 128, 128), 128)]
        line = lax.broadcasted_iota(jnp.int32, tile.shape, 0) == self.p.img
        self.ag[...] = jnp.sum(jnp.where(line, tile, 0.0), axis=0, keepdims=True)

    def norm_one_back(self):
        first, second = unpack(self.sum4.total(), self.channels)
        self.AB[4] = self.MI[1] * self.AFF[0:1]
        self.AB[5] = self.MI[1] * (first / self.CNT[0])
        self.AB[6] = self.MI[1] * (second / self.CNT[0])

    def image_grad(self, first, last):
        col = self.cols(self.side_full)

        def one(n):
            for hr in range(self.rows):
                grad = self.doubled(self.GM[hr, n], 0)
                cell = self.doubled(self.COT[n, hr].astype(F32) * 0.25, 1)
                for k in range(2):
                    r = 2 * hr + k
                    xhat, v = self.norm_one_grad(n, r, grad)
                    v = v * self.at(4, n) - self.at(5, n) - xhat * self.at(6, n) + cell
                    self.IMG[n, r] = jnp.where(col < self.width(n, r), v, 0.0).astype(BF16)

        self.loop(one, first, last)


    def update(self, weight, moment, average, total, new_weight, new_moment, new_average):
        mean = total[...] * self.inverse
        m = MOMENTUM * moment[...] + mean
        w = weight[...] - LEARN_RATE * (mean + MOMENTUM * m)
        new_weight[...] = w
        new_moment[...] = m
        new_average[...] = EMA_DECAY * average[...] + (1.0 - EMA_DECAY) * w

    def update_small(self):
        self.loaded(4)
        self.loaded(5)
        self.update(self.ew, self.EM, self.EE, self.ewg, self.new, self.nem, self.nee)
        self.update(self.aff, self.am, self.ae, self.ag, self.naw, self.nam, self.nae)

    def update_conv(self):
        self.loaded(2)
        self.loaded(3)
        step = 32
        arrays = (self.cw, self.CM, self.CE, self.RES, self.ncw, self.ncm, self.nce)

        def piece(i, _):
            at = pl.ds(pl.multiple_of(i * step, step), step)
            self.update(*(r.at[at] for r in arrays))
            return 0

        lax.fori_loop(0, self.cw.shape[0] // step, piece, 0)


def mix(works, ticks):
    done = 0
    for i, work in enumerate(works):
        work()
        upto = (i + 1) * len(ticks) // len(works)
        for tick in ticks[done:upto]:
            tick()
        done = upto
    for tick in ticks[done:]:
        tick()


def pairs(*lists):
    return [item for group in zip(*lists) for item in group]


def schedule(s):
    p, g, z = s.p, s.g, s.p.z
    pieces = list(range(PIECES))
    edge, middle = (0, s.rows - 1), range(1, s.rows - 1)
    inside, outside = range(1, s.rim - 1), (0, s.rim - 1)
    lead = choose(z == 0, 0, 1)
    other = choose(z == 1, 0, 1)
    tail = 1 - lead
    lead_two = choose(z == 3, 3, 2)
    tail_two = 5 - lead_two
    n = s.images

    def come(b, j, when=None):
        def run():
            g.arrive(b, j, when)
            g.own(b, j, when)

        return run

    def call(method, *args):
        return lambda: method(*args)

    def steps(scatter, k, b):
        return [call(scatter.step, k, b, j) for j in pieces]

    def run(calls):
        for item in calls:
            item()

    def taken(scatter, b):
        for yy in range(2):
            for xx in range(2):
                scatter.take(b, yy, xx)

    s.load()

    def prepare():
        s.own_weights()
        s.own_embedding()
        s.counts()
        s.clear_sums()

    s.w.greet(p, prepare)
    s.aff_img.send()
    for j in pieces:
        g.along(z, j, z < 2, z > 0)
        g.own(z, j, z < 2)
    s.loaded(0)
    s.stats_one(0, n // 2)
    come(other, 0)()
    s.stats_one(n // 2, n)
    s.stats_one_end()
    s.sum1.send()
    s.aff_img.turn()
    come(other, 1)()
    g.turn(lead, 0)
    come(other, 2)()
    s.aff_img.wait()
    s.aff_sp.send()
    g.turn(lead, 1)
    for j in pieces:
        g.arrive(3, j, z == 2)
    come(0, 0, z >= 2)()
    g.turn(lead, 2)
    s.sum1.wait()
    s.aff_sp.wait()
    s.affine_rows()
    s.norm_one()
    s.ez_send()
    works = [call(s.pool, edge, i, i + 4) for i in range(0, n, 4)] + [s.halo_p.send]
    works += [call(s.pool, middle, i, i + 4) for i in range(0, n, 4)]
    works += [call(s.loaded, 1), s.mask_cot, call(s.shift, s.PO, inside)]
    ticks = [come(0, j, z >= 2) for j in pieces[1:]]
    ticks += [call(g.arrive, 2, j, z == 1) for j in pieces]
    ticks += pairs([call(g.last, lead, j) for j in pieces], [call(g.turn, tail, j) for j in pieces])
    mix(works, ticks)

    def next_two(j):
        g.arrive(2, j, z == 0)
        g.own(lead_two, j)

    def tail_two_on(j):
        g.arrive(tail_two, j, (z == 0) | (z == 3))
        g.own(tail_two, j)

    for j in pieces:
        g.arrive(3, j, z == 1)
    s.ez_turn()
    next_two(0)
    for j in pieces:
        g.last(tail, j)
    next_two(1)
    s.halo_p.wait()
    s.shift(s.PO, outside)
    for j in pieces:
        g.along(2, j, z == 2, z > 3)
    g.done(lead)
    g.done(tail)
    next_two(2)
    s.clear_sums()
    s.ea_send()
    s.inner_conv(0)
    s.ez_wait()
    s.project()
    s.proj.send()
    tail_two_on(0)
    s.inner_conv(2)
    s.proj.cross()
    s.stats_two()
    s.sum2.send()
    s.shift(s.G, inside)
    g.turn(lead_two, 0)
    g.turn(lead_two, 1)
    s.proj.back()
    s.sum2.wait()
    s.proj.wait()
    s.norm_two()
    s.activate(edge)
    s.halo_a.send()
    s.activate(middle)
    s.shift(s.A2, inside)
    tail_two_on(1)
    tail_two_on(2)
    g.turn(lead_two, 2)
    s.halo_g.send()
    s.ea_turn()

    order = [3, 4, 5, 0, 1, 2, 6, 7, 8]
    between = [
        [],
        [call(g.last, lead_two, 0), call(g.turn, tail_two, 0)],
        [s.halo_a.wait, call(s.shift, s.A2, outside)],
        [call(g.last, lead_two, 1), call(g.turn, tail_two, 1)],
        [call(g.last, lead_two, 2), call(g.turn, tail_two, 2)],
        [],
        [call(g.last, tail_two, 0)],
        [call(g.last, tail_two, 1)],
        [call(g.last, tail_two, 2), call(taken, s.r2, 0)] + steps(s.r2, 0, 0) + steps(s.r2, 1, 0),
    ]
    for i, t in enumerate(order):
        s.tap_grad(s.A2, s.G, t)
        if i >= 5:
            s.r2.give((t + 1) * s.channels if i > 5 else 6 * s.channels)
        run(between[i])

    s.halo_g.wait()
    s.shift(s.G, outside)
    s.clear_sums()
    g.done(2)
    g.done(3)
    s.output(0)
    s.mixed_grad(0)
    run(steps(s.r2, 2, 0))
    s.mixed_grad(2)
    s.sums_two_back()
    s.sum3.send()
    taken(s.r2, 1)
    run(steps(s.r2, 0, 1))
    run(steps(s.r2, 1, 1))
    s.psum.send()
    s.sum3.wait()
    s.norm_two_back()
    s.inner_grad(edge)
    s.halo_b.send()
    s.inner_grad(middle)
    s.psum.cross()
    s.r2.given()

    def tap_one(t):
        s.tap_grad(s.PO, s.GB, t)
        s.r1.give((t + 1) * s.channels)

    def r1(*which):
        for k, b, j in which:
            if j < PIECES:
                s.r1.step(k, b, j)

    between = [[item] for item in steps(s.r2, 2, 1)] + [[item] for item in steps(s.r2, 3, 0)]
    between += [
        [call(taken, s.r1, 0), call(r1, (0, 0, 0), (0, 0, 1))],
        [call(r1, (0, 0, 2), (1, 0, 0))],
        [call(s.r1.step, 1, 0, 1), s.psum.back],
    ]
    for t in range(9):
        tap_one(t)
        run(between[t])

    sent = s.w.started()
    s.output(2)
    s.halo_b.wait()
    s.shift(s.GB, range(s.rim))
    s.prepare_one_back()
    taken(s.r1, 1)
    r1((2, 0, 0), (0, 1, 0), (1, 0, 2))
    run(steps(s.r2, 3, 1))
    s.pooled_conv(0)
    r1((2, 0, 1), (0, 1, 1), (1, 1, 0))
    s.psum.wait()
    s.project_grad()
    s.spread_g.send()
    run(steps(s.r2, 4, 0))
    s.pooled_conv(2)
    r1((2, 0, 2), (0, 1, 2), (1, 1, 1))
    half = n // 2
    run(steps(s.r2, 4, 1))
    s.pooled_grad(0, 0, half)
    r1((2, 1, 0), (1, 1, 2), (3, 0, 0))
    s.pooled_grad(0, half, n)
    r1((2, 1, 1), (3, 0, 1))
    s.pooled_grad(2, 0, half)
    r1((2, 1, 2), (3, 0, 2))
    s.pooled_grad(2, half, n)
    s.sums_one_back()
    s.sum4.send()
    s.affine_z()
    r1((3, 1, 0), (4, 0, 0))
    s.spread_g.turn()
    s.embedding_part()
    s.esum.send()
    r1((3, 1, 1), (4, 0, 1))
    s.w.left(sent)
    s.sum4.wait()
    s.norm_one_back()
    r1((3, 1, 2), (4, 0, 2))
    quarter = n // 4
    s.image_grad(0, quarter)
    s.r1.step(4, 1, 0)
    s.image_grad(quarter, 2 * quarter)
    s.r1.step(4, 1, 1)
    s.affine_sp()
    s.esum.cross()
    s.image_grad(2 * quarter, 3 * quarter)
    s.esum.back()
    run(steps(s.r2, 5, 0))
    run(steps(s.r2, 5, 1))
    s.affine_y()
    s.image_grad(3 * quarter, n)
    run(steps(s.r1, 5, 0))
    s.spread_g.wait()
    s.ea_wait()
    s.embedding_weights()
    s.affine_done()
    s.esum.wait()
    s.embedding_grad()
    s.update_small()
    run(steps(s.r1, 5, 1))
    s.update_conv()
    s.w.close()


def whole_kernel(names, image_total, *refs):
    refs = dict(zip(names, refs))
    place = Place(lax.axis_index("img"), lax.axis_index("sp"))
    wire = Wire(refs.pop("ssem"), refs.pop("rsem"))
    schedule(Step(place, wire, refs, image_total))


def shapes(images, cotangent, conv_w, emb_w):
    n, rows_full, side_full, c = images
    _, rows, side, _ = cotangent
    shard = conv_w[0]
    rim = (rows + 2, n, side, c)
    band = (rows, n, side, c)
    out = dict(
        RES=(conv_w, F32), ag=((1, 128), F32), ewg=(emb_w, F32),
        CM=(conv_w, F32), CE=(conv_w, F32), EM=(emb_w, F32), EE=(emb_w, F32),
        COT=(cotangent, BF16), W=((32 * shard, c), BF16), EZ=((emb_w[1], emb_w[1]), BF16),
        PO=(rim, BF16), G=(rim, BF16), A2=(rim, BF16), GB=(rim, BF16), XP=((2,) + rim, BF16), XA=((2,) + rim, BF16), XG=((2,) + rim, BF16),
        INN=(band, BF16), SKIP=(band, F32), GM=(band, F32), ACC=((2,) + band[1:], F32),
        DW=((16 * shard, c), BF16), T=((4, c // 128, side_full, 128), F32), SS=((32, c), F32),
        CNT=((2, 16, c), F32), MI=((6, 16, c), F32), AB=((9, 16, c), F32), AFF=((8, c), F32), AFP=((8, c), F32),
        C1=((8, c), F32), C2=((8, c), F32), AFS=((4, 2, 4, 1, 128), F32), AFR=((4, 8, c), F32),
        AFY=((2, 8, c), F32), AFZ=((4, 8, c), F32), EP=((16, 2 * c), F32), EA=((16, 2 * c), BF16), ET=((4, 2, 16, 128), BF16), EZT=((2, 4, 16, 128), BF16),
        EY=((4, 16, 128), BF16),
        GPA=((2, 4, 2, 16, c), BF16), GP=((2, 16, c), F32), EW=((128, 2 * c), F32), PX=((7, 16, c), F32), PE=((7, 16, c), F32),
        ST1=((4, 16, 128), F32), ST2=((4, 16, 128), F32), ST3=((4, 16, 128), F32), PS=((7, 16, c), F32), ST4=((4, 16, 128), F32),
    )
    for k in "AB":
        for i, v in enumerate(Scatter.scratch(shard, c)):
            if k == "B" or i < 6:
                out["R%s%d" % (k, i)] = v
    return out


WIRES = 360
VM = pl.BlockSpec(memory_space=pltpu.VMEM)
ANY = pl.BlockSpec(memory_space=pl.ANY)
SM = pl.BlockSpec(memory_space=pltpu.SMEM)


def place_kernel(*refs):
    count = len(refs) // 2
    sem = refs[-1]
    copies = [pltpu.make_async_copy(refs[i], refs[count + i], sem.at[i]) for i in range(count)]
    for copy in copies:
        copy.start()
    for copy in copies:
        copy.wait()


def local_kernels(image_total, images, embedding, extent, cotangent, conv_w, emb_w, affine,
                  conv_mom, emb_mom, affine_mom, conv_ema, emb_ema, affine_ema):
    line = lambda v: v.reshape(1, 128)
    scratch = shapes(images.shape, cotangent.shape, conv_w.shape, emb_w.shape)
    inputs = ["ext", "img", "cot", "emb", "cw", "ew", "aff", "cm_in", "ce_in", "em_in", "ee_in", "am", "ae"]
    trio = [(conv_w.shape, F32), (emb_w.shape, F32), ((1, 128), F32)]
    outputs = {"OUTV": (cotangent.shape, BF16), "IMG": (images.shape, BF16), "ge": (embedding.shape, F32)}
    outputs |= zip(("ncw", "new", "naw", "ncm", "nem", "nam", "nce", "nee", "nae"), trio * 3)
    names = inputs + list(outputs) + list(scratch) + ["lsem", "ssem", "rsem"]
    held = pl.pallas_call(
        lambda *refs: whole_kernel(names, image_total, *refs),
        name="resblock_step",
        out_shape=[pltpu.VMEM(*v) for v in outputs.values()],
        in_specs=[SM, ANY, ANY, VM, VM, VM, VM] + [ANY] * 4 + [VM] * 2,
        out_specs=[VM] * len(outputs),
        scratch_shapes=[pltpu.VMEM(*v) for v in scratch.values()]
        + [pltpu.SemaphoreType.DMA((8,)), pltpu.SemaphoreType.DMA((WIRES,)), pltpu.SemaphoreType.DMA((WIRES,))],
        compiler_params=pltpu.CompilerParams(
            collective_id=1, has_side_effects=True, vmem_limit_bytes=113 << 19
        ),
    )(extent.T, images, cotangent, embedding, conv_w, emb_w, line(affine), conv_mom, conv_ema, emb_mom, emb_ema,
      line(affine_mom), line(affine_ema))
    held = [pltpu.with_memory_space_constraint(v, pltpu.VMEM) for v in held]
    count = len(held)
    out, gi, ge, ncw, new, naw, ncm, nem, nam, nce, nee, nae = pl.pallas_call(
        place_kernel,
        name="place",
        out_shape=[jax.ShapeDtypeStruct(v.shape, v.dtype) for v in held],
        in_specs=[VM] * count,
        out_specs=[ANY] * count,
        scratch_shapes=[pltpu.SemaphoreType.DMA((count,))],
        compiler_params=pltpu.CompilerParams(vmem_limit_bytes=16 << 20),
    )(*held)
    flat = lambda v: v.reshape(-1)
    return out, gi, ge, ncw, new, flat(naw), ncm, nem, flat(nam), nce, nee, flat(nae)


def padded_2(cells, sides, width):
    for axis, dim in sides:
        count = lax.axis_size(axis)
        ends = count - 1
        head = lax.slice_in_dim(cells, 0, width, axis=dim)
        tail = lax.slice_in_dim(cells, cells.shape[dim] - width, cells.shape[dim], axis=dim)
        cells = jnp.concatenate(
            [
                lax.ppermute(tail, axis, [(i, (i + 1) % count) for i in range(ends)]),
                cells,
                lax.ppermute(head, axis, [((i + 1) % count, i) for i in range(ends)]),
            ],
            axis=dim,
        )
    return cells


def band_mask(extent, first_row, band_rows, band_cols, halved):
    height = extent[:, 0]
    breadth = extent[:, 1]
    if halved:
        height = height // 2
        breadth = breadth // 2
    row_ids = first_row + jnp.arange(band_rows, dtype=jnp.int32)
    col_ids = jnp.arange(band_cols, dtype=jnp.int32)
    inside = (row_ids[None, :, None] < height[:, None, None]) & (
        col_ids[None, None, :] < breadth[:, None, None]
    )
    return inside.astype(jnp.float32)[..., None]


def per_group_sums(values, group_count):
    shaped = values.reshape(values.shape[:3] + (group_count, values.shape[3] // group_count))
    return jnp.sum(shaped, axis=(1, 2, 4))


def spread_to_channels(stat, channels_per_group):
    return jnp.repeat(stat, channels_per_group, axis=1)[:, None, None, :]


def pool_cells(values):
    shaped = values.reshape(
        values.shape[0], values.shape[1] // 2, 2, values.shape[2] // 2, 2, values.shape[3]
    )
    return jnp.sum(shaped, axis=(2, 4)) * 0.25


def spread_cells(values):
    return jnp.repeat(jnp.repeat(values, 2, axis=1), 2, axis=2) * 0.25


def silu_slope(values):
    sigma = jax.nn.sigmoid(values)
    return sigma * (1.0 + values * (1.0 - sigma))


def conv_rows(padded, kernel, layout):
    return lax.conv_general_dilated(
        padded,
        kernel,
        (1, 1),
        ((0, 0), (1, 1)),
        dimension_numbers=("NHWC", "HWIO", layout),
        preferred_element_type=jnp.float32,
    )


def conv_back(padded, kernel):
    return lax.conv_general_dilated(
        padded,
        jnp.flip(kernel, (0, 1)),
        (1, 1),
        ((0, 0), (1, 1)),
        dimension_numbers=("NHWC", "HWOI", "NHWC"),
        preferred_element_type=jnp.float32,
    )


def tap_grads(padded, grads):
    window = jnp.pad(padded, ((0, 0), (0, 0), (1, 1), (0, 0)))
    band_rows = grads.shape[1]
    band_cols = grads.shape[2]
    kernel_rows = []
    for tap_row in range(3):
        taps = []
        for tap_col in range(3):
            source = window[:, tap_row : tap_row + band_rows, tap_col : tap_col + band_cols, :]
            taps.append(
                jnp.einsum("brci,brco->io", source, grads, preferred_element_type=jnp.float32)
            )
        kernel_rows.append(jnp.stack(taps))
    return jnp.stack(kernel_rows)


def band_rim(values):
    return padded_2(values, (("sp", 1),), 1)


def other_rim(values):
    return padded_2(values, (("sp", 1),), 1)


def update(weight, moment, average, total, image_total):
    grad_mean = total / image_total
    new_moment = MOMENTUM * moment + grad_mean
    new_weight = weight - LEARN_RATE * (grad_mean + MOMENTUM * new_moment)
    new_average = EMA_DECAY * average + (1.0 - EMA_DECAY) * new_weight
    return (new_weight, new_moment, new_average)


def local(
    images,
    embedding,
    extent,
    cotangent,
    conv_w,
    emb_w,
    affine,
    conv_mom,
    emb_mom,
    affine_mom,
    conv_ema,
    emb_ema,
    affine_ema,
):
    conv_all, emb_all, affine_all = (
        lax.all_gather(conv_w.astype(jnp.bfloat16), ("img", "sp"), axis=0, tiled=True),
        lax.all_gather(emb_w.astype(jnp.bfloat16), ("img", "sp"), axis=0, tiled=True),
        lax.all_gather(affine.astype(jnp.bfloat16), ("img", "sp"), axis=0, tiled=True),
    )
    channels = conv_all.shape[1]
    first_kernel = conv_all[: 9 * channels].reshape(3, 3, channels, channels)
    second_kernel = conv_all[9 * channels :].reshape(3, 3, channels, channels)
    parameters = affine_all.astype(jnp.float32).reshape(8, channels)
    image_count = images.shape[0]
    band_rows = images.shape[1]
    grid_side = images.shape[2]
    half_band = band_rows // 2
    half_side = grid_side // 2
    sp_size = lax.axis_size("sp")
    sp_index = lax.axis_index("sp")
    local_channels = channels // sp_size
    first_channels = sp_index * local_channels
    channels_per_group = channels // NORM_GROUPS
    groups_on_device = local_channels // channels_per_group
    full_mask = band_mask(extent, sp_index * band_rows, band_rows, grid_side, False)
    half_mask = band_mask(extent, sp_index * half_band, half_band, half_side, True)
    whole_half = band_mask(extent, 0, half_side, half_side, True)
    full_pixel_count = (extent[:, 0] * extent[:, 1] * channels_per_group).astype(jnp.float32)[
        :, None
    ]
    half_pixel_count = (extent[:, 0] // 2 * (extent[:, 1] // 2) * channels_per_group).astype(
        jnp.float32
    )[:, None]
    masked_values = images.astype(jnp.float32) * full_mask
    sums_one, squares_one = lax.psum(
        (
            per_group_sums(masked_values, NORM_GROUPS),
            per_group_sums(masked_values * masked_values, NORM_GROUPS),
        ),
        "sp",
    )
    first_group_mean = sums_one / full_pixel_count
    first_inverse_deviation = lax.rsqrt(
        squares_one / full_pixel_count - first_group_mean * first_group_mean + EPSILON
    )
    first_normalized = (
        masked_values - spread_to_channels(first_group_mean, channels_per_group)
    ) * spread_to_channels(first_inverse_deviation, channels_per_group)
    first_group_norm = first_normalized * parameters[0] + parameters[1]
    pooled = pool_cells(jax.nn.silu(first_group_norm) * full_mask).astype(jnp.bfloat16)
    skip_path = pool_cells(masked_values)
    pooled_rim = band_rim(pooled)
    inner_act = ((conv_rows(pooled_rim, first_kernel, "NHWC") + parameters[2]) * half_mask).astype(
        jnp.bfloat16
    )
    emb_act = jax.nn.silu(embedding.astype(jnp.float32)).astype(jnp.bfloat16)

    def place_local(values):
        return lax.dynamic_update_slice_in_dim(
            jnp.zeros((channels,), jnp.float32), values, first_channels, 0
        )

    inner_channels = lax.all_to_all(
        inner_act, "sp", split_axis=3, concat_axis=1, tiled=True
    ).astype(jnp.float32)
    emb_cols = jnp.concatenate(
        [
            lax.dynamic_slice_in_dim(emb_all, first_channels, local_channels, 1),
            lax.dynamic_slice_in_dim(emb_all, channels + first_channels, local_channels, 1),
        ],
        axis=1,
    )
    emb_bias = jnp.concatenate(
        [
            lax.dynamic_slice_in_dim(parameters[3], first_channels, local_channels, 0),
            lax.dynamic_slice_in_dim(parameters[4], first_channels, local_channels, 0),
        ]
    )
    emb_proj = jnp.dot(emb_act, emb_cols, preferred_element_type=jnp.float32) + emb_bias
    ada_scale = 1.0 + emb_proj[:, :local_channels][:, None, None, :]
    ada_shift = emb_proj[:, local_channels:][:, None, None, :]
    sums_two = per_group_sums(inner_channels, groups_on_device)
    squares_two = per_group_sums(inner_channels * inner_channels, groups_on_device)
    second_group_mean = sums_two / half_pixel_count
    second_inverse_deviation = lax.rsqrt(
        squares_two / half_pixel_count - second_group_mean * second_group_mean + EPSILON
    )
    second_normalized = (
        inner_channels - spread_to_channels(second_group_mean, channels_per_group)
    ) * spread_to_channels(second_inverse_deviation, channels_per_group)
    second_gain = lax.dynamic_slice_in_dim(parameters[5], first_channels, local_channels, 0)
    second_group_norm = second_normalized * second_gain + lax.dynamic_slice_in_dim(
        parameters[6], first_channels, local_channels, 0
    )
    mixed_act = second_group_norm * ada_scale + ada_shift
    act_two = (jax.nn.silu(mixed_act) * whole_half).astype(jnp.bfloat16)
    act_rows = lax.all_to_all(act_two, "sp", split_axis=1, concat_axis=3, tiled=True)
    act_rim = other_rim(act_rows)
    branch = conv_rows(act_rim, second_kernel, "NHWC") + parameters[7]
    output = (skip_path + branch * half_mask).astype(jnp.bfloat16)
    grad_branch = (cotangent.astype(jnp.float32) * half_mask).astype(jnp.bfloat16)
    bias_two_grad = jnp.sum(grad_branch.astype(jnp.float32), axis=(0, 1, 2))
    grad_rim = other_rim(grad_branch)
    kernel_two = tap_grads(act_rim, grad_branch)
    grad_band = conv_back(grad_rim, second_kernel).astype(jnp.bfloat16)
    grad_act = lax.all_to_all(grad_band, "sp", split_axis=3, concat_axis=1, tiled=True)
    grad_mixed = grad_act.astype(jnp.float32) * whole_half * silu_slope(mixed_act)
    grad_proj = jnp.concatenate(
        [jnp.sum(grad_mixed * second_group_norm, axis=(1, 2)), jnp.sum(grad_mixed, axis=(1, 2))],
        axis=1,
    )
    second_norm_gradient = grad_mixed * ada_scale
    second_gain_gradient = jnp.sum(second_norm_gradient * second_normalized, axis=(0, 1, 2))
    bias_norm_two_grad = jnp.sum(second_norm_gradient, axis=(0, 1, 2))
    second_normalized_gradient = second_norm_gradient * second_gain
    first_total_count = (
        per_group_sums(second_normalized_gradient, groups_on_device) / half_pixel_count
    )
    second_total_count = (
        per_group_sums(second_normalized_gradient * second_normalized, groups_on_device)
        / half_pixel_count
    )
    grad_inner = spread_to_channels(second_inverse_deviation, channels_per_group) * (
        second_normalized_gradient
        - spread_to_channels(first_total_count, channels_per_group)
        - second_normalized * spread_to_channels(second_total_count, channels_per_group)
    )
    grad_inner_rows = lax.all_to_all(
        grad_inner.astype(jnp.bfloat16), "sp", split_axis=1, concat_axis=3, tiled=True
    )
    emb_grad_cols = jnp.einsum(
        "be,bk->ek", emb_act.astype(jnp.float32), grad_proj, precision=HIGHEST
    )
    emb_kernel = jnp.zeros((emb_all.shape[0], 2 * channels), jnp.float32)
    emb_kernel = lax.dynamic_update_slice_in_dim(
        emb_kernel, emb_grad_cols[:, :local_channels], first_channels, 1
    )
    emb_kernel = lax.dynamic_update_slice_in_dim(
        emb_kernel, emb_grad_cols[:, local_channels:], channels + first_channels, 1
    )
    silu_part = jnp.einsum("bk,ek->be", grad_proj, emb_cols.astype(jnp.float32), precision=HIGHEST)
    silu_grad = lax.psum(silu_part.astype(jnp.bfloat16), "sp").astype(jnp.float32)
    emb_bias_grad = jnp.sum(grad_proj, axis=0)
    coarse_affine = [
        place_local(emb_bias_grad[:local_channels]),
        place_local(emb_bias_grad[local_channels:]),
        place_local(second_gain_gradient),
        place_local(bias_norm_two_grad),
    ]
    grad_embedding = silu_grad * silu_slope(embedding.astype(jnp.float32))
    grad_raw = (grad_inner_rows.astype(jnp.float32) * half_mask).astype(jnp.bfloat16)
    bias_one_grad = jnp.sum(grad_raw.astype(jnp.float32), axis=(0, 1, 2))
    kernel_one = tap_grads(pooled_rim, grad_raw)
    grad_pooled = conv_back(band_rim(grad_raw), first_kernel)
    first_norm_gradient = spread_cells(grad_pooled) * full_mask * silu_slope(first_group_norm)
    first_gain_gradient = jnp.sum(first_norm_gradient * first_normalized, axis=(0, 1, 2))
    bias_norm_one_grad = jnp.sum(first_norm_gradient, axis=(0, 1, 2))
    first_normalized_gradient = first_norm_gradient * parameters[0]
    back_one, second_backward = lax.psum(
        (
            per_group_sums(first_normalized_gradient, NORM_GROUPS),
            per_group_sums(first_normalized_gradient * first_normalized, NORM_GROUPS),
        ),
        "sp",
    )
    grad_masked = spread_to_channels(first_inverse_deviation, channels_per_group) * (
        first_normalized_gradient
        - spread_to_channels(back_one / full_pixel_count, channels_per_group)
        - first_normalized
        * spread_to_channels(second_backward / full_pixel_count, channels_per_group)
    ) + spread_cells(cotangent.astype(jnp.float32))
    grad_images = (grad_masked * full_mask).astype(jnp.bfloat16)
    affine_grad = jnp.concatenate(
        [first_gain_gradient, bias_norm_one_grad, bias_one_grad] + coarse_affine + [bias_two_grad]
    )
    conv_grad = jnp.concatenate(
        [kernel_one.reshape(9 * channels, channels), kernel_two.reshape(9 * channels, channels)]
    )
    conv_sum, emb_sum, affine_sum = (
        lax.psum_scatter(conv_grad, ("img", "sp"), scatter_dimension=0, tiled=True),
        lax.psum_scatter(emb_kernel, ("img", "sp"), scatter_dimension=0, tiled=True),
        lax.psum_scatter(affine_grad, ("img", "sp"), scatter_dimension=0, tiled=True),
    )
    image_total = float(image_count * lax.axis_size("img"))
    new_conv, conv_moment, conv_average = update(conv_w, conv_mom, conv_ema, conv_sum, image_total)
    new_emb, emb_moment, emb_average = update(emb_w, emb_mom, emb_ema, emb_sum, image_total)
    new_affine, affine_moment, affine_average = update(
        affine, affine_mom, affine_ema, affine_sum, image_total
    )
    return (
        output,
        grad_images,
        grad_embedding,
        new_conv,
        new_emb,
        new_affine,
        conv_moment,
        emb_moment,
        affine_moment,
        conv_average,
        emb_average,
        affine_average,
    )


def kernels_or_ops(images, embedding, extent, cotangent, conv_w, *rest):
    arrays = (images, embedding, extent, cotangent, conv_w) + rest
    n, rows, side, channels = images.shape
    if n > 16 or rows != 8 or side != 32 or channels != 512 or conv_w.shape[0] != 288:
        return local(*arrays)
    return local_kernels(float(n * lax.axis_size("img")), *arrays)


def solution(mesh):
    in_specs = (
        P("img", "sp", None, None),
        P("img", None),
        P("img", None),
        P("img", "sp", None, None),
        P(("img", "sp"), None),
        P(("img", "sp"), None),
        P(("img", "sp")),
        P(("img", "sp"), None),
        P(("img", "sp"), None),
        P(("img", "sp")),
        P(("img", "sp"), None),
        P(("img", "sp"), None),
        P(("img", "sp")),
    )
    out_specs = (
        P("img", "sp", None, None),
        P("img", "sp", None, None),
        P("img", None),
        P(("img", "sp"), None),
        P(("img", "sp"), None),
        P(("img", "sp")),
        P(("img", "sp"), None),
        P(("img", "sp"), None),
        P(("img", "sp")),
        P(("img", "sp"), None),
        P(("img", "sp"), None),
        P(("img", "sp")),
    )
    fits = dict(mesh.shape) == {"img": 8, "sp": 4}
    return jax.shard_map(kernels_or_ops if fits else local, mesh=mesh, in_specs=in_specs, out_specs=out_specs, check_vma=False)
```
